32 devices in a mesh: dp: 2 (over y), ctx: 4 (over z), mp: 4 (over x, core).
Axes of the slice: x: 2, y: 2, z: 4, core: 2. Of those that a mesh axis runs over, the one named last changes fastest.
Arguments:
- inputs: bfloat16 [8, 1024, 1024], P('dp', 'ctx'), may hold values from -6 to 6
- segment_ids: int32 [8, 1024], P('dp'), may hold values from 0 to 2, as said below
- norm_attn_one: bfloat16 [1024], P(('dp', 'ctx')), may hold values from 0.25 to 1.75
- query_one: bfloat16 [1024, 1024], P(('dp', 'ctx'), 'mp'), may hold values from -0.1875 to 0.1875
- key_one: bfloat16 [1024, 1024], P(('dp', 'ctx'), 'mp'), may hold values from -0.1875 to 0.1875
- value_one: bfloat16 [1024, 1024], P(('dp', 'ctx'), 'mp'), may hold values from -0.1875 to 0.1875
- output_one: bfloat16 [1024, 1024], P('mp', ('dp', 'ctx')), may hold values from -1.5 to 1.5
- norm_ffn_one: bfloat16 [1024], P(('dp', 'ctx')), may hold values from 0.25 to 1.75
- gate_one: bfloat16 [1024, 2816], P(('dp', 'ctx'), 'mp'), may hold values from -0.1875 to 0.1875
- up_one: bfloat16 [1024, 2816], P(('dp', 'ctx'), 'mp'), may hold values from -0.1875 to 0.1875
- down_one: bfloat16 [2816, 1024], P('mp', ('dp', 'ctx')), may hold values from -0.109375 to 0.109375
- norm_attn_two: bfloat16 [1024], P(('dp', 'ctx')), may hold values from 0.25 to 1.75
- query_two: bfloat16 [1024, 1024], P(('dp', 'ctx'), 'mp'), may hold values from -0.1875 to 0.1875
- key_two: bfloat16 [1024, 1024], P(('dp', 'ctx'), 'mp'), may hold values from -0.1875 to 0.1875
- value_two: bfloat16 [1024, 1024], P(('dp', 'ctx'), 'mp'), may hold values from -0.1875 to 0.1875
- output_two: bfloat16 [1024, 1024], P('mp', ('dp', 'ctx')), may hold values from -1.5 to 1.5
- norm_ffn_two: bfloat16 [1024], P(('dp', 'ctx')), may hold values from 0.25 to 1.75
- gate_two: bfloat16 [1024, 2816], P(('dp', 'ctx'), 'mp'), may hold values from -0.1875 to 0.1875
- up_two: bfloat16 [1024, 2816], P(('dp', 'ctx'), 'mp'), may hold values from -0.1875 to 0.1875
- down_two: bfloat16 [2816, 1024], P('mp', ('dp', 'ctx')), may hold values from -0.109375 to 0.109375
- cotangent: bfloat16 [8, 1024, 1024], P('dp', 'ctx'), may hold values from -6 to 6
Outputs:
- layer_one_out: bfloat16 [8, 1024, 1024], P('dp', 'ctx')
- layer_two_out: bfloat16 [8, 1024, 1024], P('dp', 'ctx')
- input_grad: float32 [8, 1024, 1024], P('dp', 'ctx')
- norm_attn_one_grad: float32 [1024], P(('dp', 'ctx'))
- query_one_grad: float32 [1024, 1024], P(('dp', 'ctx'), 'mp')
- key_one_grad: float32 [1024, 1024], P(('dp', 'ctx'), 'mp')
- value_one_grad: float32 [1024, 1024], P(('dp', 'ctx'), 'mp')
- output_one_grad: float32 [1024, 1024], P('mp', ('dp', 'ctx'))
- norm_ffn_one_grad: float32 [1024], P(('dp', 'ctx'))
- gate_one_grad: float32 [1024, 2816], P(('dp', 'ctx'), 'mp')
- up_one_grad: float32 [1024, 2816], P(('dp', 'ctx'), 'mp')
- down_one_grad: float32 [2816, 1024], P('mp', ('dp', 'ctx'))
- norm_attn_two_grad: float32 [1024], P(('dp', 'ctx'))
- query_two_grad: float32 [1024, 1024], P(('dp', 'ctx'), 'mp')
- key_two_grad: float32 [1024, 1024], P(('dp', 'ctx'), 'mp')
- value_two_grad: float32 [1024, 1024], P(('dp', 'ctx'), 'mp')
- output_two_grad: float32 [1024, 1024], P('mp', ('dp', 'ctx'))
- norm_ffn_two_grad: float32 [1024], P(('dp', 'ctx'))
- gate_two_grad: float32 [1024, 2816], P(('dp', 'ctx'), 'mp')
- up_two_grad: float32 [1024, 2816], P(('dp', 'ctx'), 'mp')
- down_two_grad: float32 [2816, 1024], P('mp', ('dp', 'ctx'))
The draws below stay inside these ranges and needn't reach their ends.
Inputs may be any that keep to these rules, and one draw needn't show every extreme that they name: `segment_ids`: within each sequence the ids start at 0 and never fall along the positions.
All inputs are finite; a program needn't handle non-finite values.
Results may differ from the reference program's by a relative error of at most 0.04.
Values may be sent and summed in bfloat16 or wider, within the bound.
A program may use at most 256 MiB of HBM per device.

```python
import math
import jax
import jax.numpy as jnp
from jax import lax

D = 1024
HEADS = 16
HEAD_DIM = 64
FF = 2816
SEQS = 4
SEQ_LEN = 1024
SEQUENCES = 8


def draw_segment_ids(key, part):
    doc_low = max(4, min(200, SEQ_LEN // 8))
    doc_high = max(doc_low + 2, min(2001, SEQ_LEN // 2))
    doc_slots = SEQ_LEN // doc_low + 1
    group_count = SEQUENCES // SEQS
    id_limit = min(SEQS - 1, 1) * ((SEQ_LEN - 1) // (doc_high - 1))
    length_key, long_key = jax.random.split(key)
    lengths = jax.random.randint(length_key, (SEQUENCES, doc_slots), doc_low, doc_high)
    doc_ends = jnp.cumsum(lengths, axis=1)
    places = jnp.arange(SEQ_LEN, dtype=jnp.int32)
    doc_ids = jnp.sum((doc_ends[:, None, :] <= places[None, :, None]).astype(jnp.int32), axis=2)
    doc_ids = jnp.minimum(doc_ids, id_limit)
    chosen = jax.random.randint(long_key, (group_count,), 0, SEQS)
    row_numbers = jnp.arange(SEQUENCES, dtype=jnp.int32)
    single = row_numbers % SEQS == chosen[row_numbers // SEQS]
    return jnp.where(single[:, None], 0, doc_ids).astype(jnp.int32)


def raised(entries, key, source, target, blocks, factor):
    def block_of(position):
        return (jnp.arange(entries.shape[position]) // (entries.shape[position] // blocks)).reshape((-1,) + (1,) * (entries.ndim - 1 - position))

    one_side = jax.random.permutation(key, blocks)[block_of(target)]
    far = (block_of(target) + blocks // 2) % blocks
    return jnp.where((block_of(source) == one_side) | (block_of(source) == far), factor * entries, entries)


def shard_levels(key, extent, shards, smallest, high):
    def one(position, parts):
        heights = jax.random.uniform(jax.random.fold_in(jax.random.fold_in(key, 6), position), (parts,), jnp.float32, smallest / len(shards), high / len(shards))
        return jnp.repeat(jnp.exp(heights), extent[position] // parts).reshape((-1,) + (1,) * (len(extent) - position - 1))

    level = one(*shards[0])
    for cut in shards[1:]:
        level = level * one(*cut)
    return level


def normal_values(own_key, dims, spread, most, cuts=(), kind=jnp.bfloat16):
    loudness = shard_levels(own_key, dims, cuts, -0.22, 0.18) if cuts else 1.0
    drawn = jax.random.normal(own_key, dims, jnp.float32) * spread * loudness
    return jnp.minimum(jnp.maximum(drawn, -most), most).astype(kind)


def bell_draw_with(own_key, extent, scale, limit, cuts, heavy, kind=jnp.bfloat16):
    values = scale * jax.random.normal(own_key, extent, jnp.float32)
    if cuts:
        values = values * shard_levels(own_key, extent, cuts, -0.22, 0.18)
    return jnp.clip(raised(values, jax.random.fold_in(own_key, 3), *heavy), -limit, limit).astype(kind)


def setup_inputs(seed: int = 0) -> dict:
    key_of = jax.random.split(jax.random.key(seed), 22)
    return {
        "inputs": normal_values(key_of[0], (SEQUENCES, SEQ_LEN, D), 1.0, 6.0, ((0, 2), (1, 4))),
        "segment_ids": draw_segment_ids(jax.random.fold_in(key_of[21], 71), 0),
        "norm_attn_one": jnp.clip(1.0 + 0.15 * jax.random.normal(key_of[2], (D,), jnp.float32), 0.25, 1.75).astype(jnp.bfloat16),
        "query_one": normal_values(key_of[3], (D, D), D ** -0.5, 0.1875, ((0, 8), (1, 4))),
        "key_one": normal_values(key_of[4], (D, D), D ** -0.5, 0.1875, ((0, 8), (1, 4))),
        "value_one": normal_values(key_of[5], (D, D), D ** -0.5, 0.1875, ((0, 8), (1, 4))),
        "output_one": normal_values(key_of[6], (D, D), (D // 64) ** -0.5, 1.5, ((0, 4), (1, 8))),
        "norm_ffn_one": jnp.clip(1.0 + 0.15 * jax.random.normal(key_of[7], (D,), jnp.float32), 0.25, 1.75).astype(jnp.bfloat16),
        "gate_one": normal_values(key_of[8], (D, FF), D ** -0.5, 0.1875, ((0, 8), (1, 4))),
        "up_one": normal_values(key_of[9], (D, FF), D ** -0.5, 0.1875, ((0, 8), (1, 4))),
        "down_one": normal_values(key_of[10], (FF, D), FF ** -0.5, 0.109375, ((0, 4), (1, 8))),
        "norm_attn_two": jnp.clip(1.0 + 0.15 * jax.random.normal(key_of[11], (D,), jnp.float32), 0.25, 1.75).astype(jnp.bfloat16),
        "query_two": normal_values(key_of[12], (D, D), D ** -0.5, 0.1875, ((0, 8), (1, 4))),
        "key_two": normal_values(key_of[13], (D, D), D ** -0.5, 0.1875, ((0, 8), (1, 4))),
        "value_two": normal_values(key_of[14], (D, D), D ** -0.5, 0.1875, ((0, 8), (1, 4))),
        "output_two": normal_values(key_of[15], (D, D), (D // 64) ** -0.5, 1.5, ((0, 4), (1, 8))),
        "norm_ffn_two": jnp.clip(1.0 + 0.15 * jax.random.normal(key_of[16], (D,), jnp.float32), 0.25, 1.75).astype(jnp.bfloat16),
        "gate_two": normal_values(key_of[17], (D, FF), D ** -0.5, 0.1875, ((0, 8), (1, 4))),
        "up_two": normal_values(key_of[18], (D, FF), D ** -0.5, 0.1875, ((0, 8), (1, 4))),
        "down_two": normal_values(key_of[19], (FF, D), FF ** -0.5, 0.109375, ((0, 4), (1, 8))),
        "cotangent": bell_draw_with(key_of[20], (SEQUENCES, SEQ_LEN, D), 1.0, 6.0, ((0, 2), (1, 4)), (1, 2, 4, 2.0)),
    }


largest_score = lax.Precision.HIGHEST
neg_large = -1e+30

@jax.custom_vjp
def low(v):
    return lax.optimization_barrier(v.astype(jnp.bfloat16)).astype(jnp.float32)

@jax.custom_vjp
def low_back(v):
    return v

def low_keep(v):
    return (low(v), None)

def low_pass(kept, grad):
    return (grad,)

def back_keep(v):
    return (v, None)

def back_low(kept, grad):
    return (low(grad),)
low.defvjp(low_keep, low_pass)
low_back.defvjp(back_keep, back_low)

def project(left_operand, right_operand):
    return jnp.einsum('kfi,ih->kfh', left_operand, right_operand, precision=largest_score)

def rms_norm(stream, gain_row):
    return stream * lax.rsqrt(lax.optimization_barrier(jnp.mean(stream * stream, axis=-1, keepdims=True)) + 1e-05) * gain_row

def rotary(packed):
    seq_count = packed.shape[0]
    length = packed.shape[1]
    per_head = packed.reshape(seq_count, length, HEADS, HEAD_DIM)
    half_width = HEAD_DIM // 2
    frequency = 10000.0 ** (-jnp.arange(half_width, dtype=jnp.float32) / half_width)
    angles = jnp.arange(length, dtype=jnp.float32)[:, None] * frequency[None, :]
    cosine = jnp.cos(angles)[None, :, None, :]
    sine_table = jnp.sin(angles)[None, :, None, :]
    first_half = per_head[..., :half_width]
    second_half = per_head[..., half_width:]
    turned = jnp.concatenate([first_half * cosine - second_half * sine_table, first_half * sine_table + second_half * cosine], axis=-1)
    return turned.reshape(packed.shape)

def attend_sequence(operands):
    query_seq, key_seq, value_seq, segment_seq = operands
    block_rows = math.gcd(SEQ_LEN, 512)
    key_places = jnp.arange(SEQ_LEN, dtype=jnp.int32)
    score_scale = HEAD_DIM ** (-0.5)

    def one_block(block_index):
        first_row = (block_index * block_rows).astype(jnp.int32)
        query_block = lax.dynamic_slice_in_dim(query_seq, first_row, block_rows, 0)
        query_places = first_row + jnp.arange(block_rows, dtype=jnp.int32)
        query_document_ids = lax.dynamic_slice_in_dim(segment_seq, first_row, block_rows, 0)
        scores = low_back(jnp.einsum('qhe,khe->hqk', query_block, key_seq, precision=largest_score) * score_scale)
        visible = (key_places[None, :] <= query_places[:, None]) & (segment_seq[None, :] == query_document_ids[:, None])
        masked = jnp.where(visible[None], scores, neg_large)
        row_top = lax.optimization_barrier(jnp.max(masked, axis=-1, keepdims=True))
        exponent = jnp.exp(masked - row_top)
        probabilities = exponent / lax.optimization_barrier(jnp.sum(exponent, axis=-1, keepdims=True))
        return jnp.einsum('hqk,khe->qhe', low(probabilities), value_seq, precision=largest_score)
    blocks = lax.map(jax.checkpoint(one_block), jnp.arange(SEQ_LEN // block_rows, dtype=jnp.int32))
    return blocks.reshape(SEQ_LEN, HEADS, HEAD_DIM)

def layer(stream, first_values, params, segment_ids):
    norm_attn, w_query, w_key, w_value, w_output, norm_ffn, w_gate, w_up, w_down = params
    seq_count = stream.shape[0]
    normed = low(rms_norm(stream, norm_attn))
    queries = low(rotary(low_back(project(normed, w_query))))
    key_rows = low(rotary(low_back(project(normed, w_key))))
    own_values = low_back(project(normed, w_value))
    if first_values is None:
        mixed = low(own_values)
    else:
        mixed = low(0.5 * own_values + 0.5 * first_values)
    split_shape = (seq_count, SEQ_LEN, HEADS, HEAD_DIM)
    attended = lax.map(attend_sequence, (queries.reshape(split_shape), key_rows.reshape(split_shape), mixed.reshape(split_shape), segment_ids))
    attended = low(low_back(attended.reshape(stream.shape)))
    hidden_one = stream + low_back(project(attended, w_output))
    normed_two = low(rms_norm(hidden_one, norm_ffn))
    gate_values = low_back(project(normed_two, w_gate))
    up_values = low_back(project(normed_two, w_up))
    activated = low(jax.nn.silu(gate_values) * up_values)
    result = hidden_one + low_back(project(activated, w_down))
    return (result, own_values)

def reference(inputs, segment_ids, norm_attn_one, query_one, key_one, value_one, output_one, norm_ffn_one, gate_one, up_one, down_one, norm_attn_two, query_two, key_two, value_two, output_two, norm_ffn_two, gate_two, up_two, down_two, cotangent):
    params = tuple((weight_arg.astype(jnp.float32) for weight_arg in (norm_attn_one, query_one, key_one, value_one, output_one, norm_ffn_one, gate_one, up_one, down_one, norm_attn_two, query_two, key_two, value_two, output_two, norm_ffn_two, gate_two, up_two, down_two)))

    def forward(stream, *flat_params):
        first_layer_output, first_values = layer(stream, None, flat_params[:9], segment_ids)
        out_two, unused = layer(first_layer_output, first_values, flat_params[9:], segment_ids)
        return (out_two, first_layer_output)
    out_two, pullback, first_layer_output = jax.vjp(forward, inputs.astype(jnp.float32), *params, has_aux=True)
    grads = pullback(cotangent.astype(jnp.float32))
    return (first_layer_output.astype(jnp.bfloat16), out_two.astype(jnp.bfloat16), grads[0], grads[1], grads[2], grads[3], grads[4], grads[5], grads[6], grads[7], grads[8], grads[9], grads[10], grads[11], grads[12], grads[13], grads[14], grads[15], grads[16], grads[17], grads[18])
```

```python
import functools
import math

import jax
import jax.numpy as jnp
from jax import lax
from jax.experimental import pallas as pl
from jax.experimental.pallas import tpu as pltpu
from jax.sharding import PartitionSpec as P

MESH = pl.DeviceIdType.MESH

HEAD_DIM = 64


epsilon = 1e-05
neg_large = -1e30


def project(left_operand, right_operand):
    return jnp.einsum(
        "sbd,de->sbe", left_operand, right_operand, preferred_element_type=jnp.float32
    )


def project_back(left_operand, right_operand):
    return jnp.einsum(
        "sbe,de->sbd", left_operand, right_operand, preferred_element_type=jnp.float32
    )


def weight_term(left_operand, right_operand):
    return jnp.einsum(
        "sbd,sbe->de", left_operand, right_operand, preferred_element_type=jnp.float32
    )


def head_sum_kernel(
    chunks, x_ref, o_ref, near, half_sum, far, send_a, recv_a, send_b, recv_b, send_c, recv_c
):
    dp, ctx, mp = (lax.axis_index(name) for name in ("dp", "ctx", "mp"))
    side = lax.rem(mp, 2)
    pair = (dp, ctx, mp + 1 - 2 * side)
    cross = (dp, ctx, lax.rem(mp + 2, 4))
    barrier = pltpu.get_barrier_semaphore()
    for peer in (pair, cross):
        pl.semaphore_signal(barrier, inc=1, device_id=peer, device_id_type=MESH)
    pl.semaphore_wait(barrier, 2)
    rows = x_ref.shape[0] // chunks
    half = rows // 2

    def copy(source, target, send, recv, i, peer):
        return pltpu.make_async_remote_copy(
            src_ref=source,
            dst_ref=target,
            send_sem=send.at[i],
            recv_sem=recv.at[i],
            device_id=peer,
            device_id_type=MESH,
        )

    def first(i):
        theirs = x_ref.at[pl.ds(i * rows + (1 - side) * half, half)]
        return copy(theirs, near.at[i], send_a, recv_a, i, pair)

    def second(i):
        return copy(half_sum.at[i], far.at[i], send_b, recv_b, i, cross)

    def third(i):
        mine = o_ref.at[pl.ds(i * rows + side * half, half)]
        return copy(mine, mine, send_c, recv_c, i, pair)

    for i in range(chunks):
        first(i).start()
    for i in range(chunks):
        first(i).wait()
        mine = x_ref[pl.ds(i * rows + side * half, half)].astype(jnp.float32)
        half_sum[i] = (mine + near[i].astype(jnp.float32)).astype(jnp.bfloat16)
        second(i).start()
    for i in range(chunks):
        second(i).wait()
        total = half_sum[i].astype(jnp.float32) + far[i].astype(jnp.float32)
        o_ref[pl.ds(i * rows + side * half, half)] = total.astype(jnp.bfloat16)
        third(i).start()
    for i in range(chunks):
        third(i).wait()


def head_sum(partial_sum, number):
    flat = partial_sum.astype(jnp.bfloat16).reshape(-1, partial_sum.shape[-1])
    count, width = flat.shape
    chunks = 4
    half = count // chunks // 2
    total = pl.pallas_call(
        functools.partial(head_sum_kernel, chunks),
        out_shape=jax.ShapeDtypeStruct((count, width), jnp.bfloat16),
        in_specs=[pl.BlockSpec(memory_space=pltpu.VMEM)],
        out_specs=pl.BlockSpec(memory_space=pltpu.VMEM),
        scratch_shapes=[pltpu.VMEM((chunks, half, width), jnp.bfloat16)] * 3
        + [pltpu.SemaphoreType.DMA((chunks,))] * 6,
        compiler_params=pltpu.CompilerParams(
            collective_id=0, has_side_effects=True, vmem_limit_bytes=32 << 20
        ),
    )(flat)
    return total.reshape(partial_sum.shape).astype(jnp.float32)


def head_total(partial_sum):
    return head_sum(partial_sum, 0)


def head_back(partial_sum):
    return head_sum(partial_sum, 0)


def rotary_tables(first_place, count_of_rows):
    half_width = HEAD_DIM // 2
    frequency = 10000.0 ** (-jnp.arange(half_width, dtype=jnp.float32) / half_width)
    places = (first_place + jnp.arange(count_of_rows, dtype=jnp.int32)).astype(jnp.float32)
    angles = places[:, None] * frequency[None, :]
    return (jnp.cos(angles)[None, :, None, :], jnp.sin(angles)[None, :, None, :])


def rotate(split_heads, cosine, sine_table):
    half_width = HEAD_DIM // 2
    first_half = split_heads[..., :half_width]
    second_half = split_heads[..., half_width:]
    return jnp.concatenate(
        [
            first_half * cosine - second_half * sine_table,
            first_half * sine_table + second_half * cosine,
        ],
        axis=-1,
    )


def rotate_back(split_heads, cosine, sine_table):
    half_width = HEAD_DIM // 2
    first_half = split_heads[..., :half_width]
    second_half = split_heads[..., half_width:]
    return jnp.concatenate(
        [
            first_half * cosine + second_half * sine_table,
            second_half * cosine - first_half * sine_table,
        ],
        axis=-1,
    )


def norm_forward(stream, gain_row):
    inverse = lax.rsqrt(jnp.mean(stream * stream, axis=-1, keepdims=True) + epsilon)
    normed = (stream * inverse * gain_row.astype(jnp.float32)).astype(jnp.bfloat16)
    return (normed, inverse)


def norm_backward(grad_normed, stream, inverse, gain_row):
    scaled = stream * inverse
    grad_scaled = grad_normed * gain_row.astype(jnp.float32)
    gain_grad = jnp.sum(grad_normed * scaled, axis=(0, 1))
    grad_stream = inverse * (
        grad_scaled - scaled * jnp.mean(grad_scaled * scaled, axis=-1, keepdims=True)
    )
    return (grad_stream, gain_grad)


def block_grads(
    query_block,
    grad_block,
    lse_block,
    delta_block,
    query_places,
    query_document_ids,
    key_block,
    value_block,
    key_places,
    key_segments,
):
    score_scale = HEAD_DIM ** (-0.5)
    scores = (
        jnp.einsum("sqhe,skhe->shqk", query_block, key_block, preferred_element_type=jnp.float32)
        * score_scale
    )
    visible = (
        (key_places[None, :] <= query_places[:, None])[None]
        & (key_segments[:, None, :] == query_document_ids[:, :, None])
    )[:, None]
    probabilities = jnp.where(visible, jnp.exp(scores - lse_block[..., None]), 0.0)
    grad_probs = jnp.einsum(
        "sqhe,skhe->shqk", grad_block, value_block, preferred_element_type=jnp.float32
    )
    grad_scores = (probabilities * (grad_probs - delta_block[..., None]) * score_scale).astype(
        jnp.bfloat16
    )
    query_grad = jnp.einsum(
        "shqk,skhe->sqhe", grad_scores, key_block, preferred_element_type=jnp.float32
    )
    key_grad = jnp.einsum(
        "shqk,sqhe->skhe", grad_scores, query_block, preferred_element_type=jnp.float32
    )
    value_grad = jnp.einsum(
        "shqk,sqhe->skhe",
        probabilities.astype(jnp.bfloat16),
        grad_block,
        preferred_element_type=jnp.float32,
    )
    return (query_grad, key_grad, value_grad)


def attend_forward(queries, key_rows, value_rows, segments, query_places):
    seq_count, count_of_rows, head_count, head_width = queries.shape
    score_scale = head_width ** (-0.5)
    query_document_ids = lax.dynamic_slice_in_dim(segments, query_places[0], count_of_rows, 1)
    last_query = query_places[count_of_rows - 1]
    initial = (
        jnp.full((seq_count, head_count, count_of_rows), neg_large, jnp.float32),
        jnp.zeros((seq_count, head_count, count_of_rows), jnp.float32),
        jnp.zeros((seq_count, count_of_rows, head_count, head_width), jnp.float32),
    )
    key_piece = lax.all_gather(key_rows, "ctx", axis=1, tiled=True)
    value_piece = lax.all_gather(value_rows, "ctx", axis=1, tiled=True)
    piece_rows = key_piece.shape[1]
    block_rows = math.gcd(piece_rows, 512)
    key_split = key_piece.reshape(seq_count, piece_rows, head_count, head_width)
    value_split = value_piece.reshape(seq_count, piece_rows, head_count, head_width)

    def absorb_visit(running, block_index):
        first_key = block_index * block_rows

        def absorb_compute(current):
            row_max, row_total, weighted = current
            key_block = lax.dynamic_slice_in_dim(key_split, first_key, block_rows, 1)
            value_block = lax.dynamic_slice_in_dim(value_split, first_key, block_rows, 1)
            key_places = first_key + jnp.arange(block_rows, dtype=jnp.int32)
            key_segments = lax.dynamic_slice_in_dim(segments, first_key, block_rows, 1)
            scores = (
                jnp.einsum(
                    "sqhe,skhe->shqk", queries, key_block, preferred_element_type=jnp.float32
                )
                * score_scale
            )
            visible = (
                (key_places[None, :] <= query_places[:, None])[None]
                & (key_segments[:, None, :] == query_document_ids[:, :, None])
            )[:, None]
            new_max = jnp.maximum(row_max, jnp.max(jnp.where(visible, scores, neg_large), axis=-1))
            exponent = jnp.where(visible, jnp.exp(scores - new_max[..., None]), 0.0)
            factor = jnp.exp(row_max - new_max)
            new_total = row_total * factor + jnp.sum(exponent, axis=-1)
            update = jnp.einsum(
                "shqk,skhe->sqhe",
                exponent.astype(jnp.bfloat16),
                value_block,
                preferred_element_type=jnp.float32,
            )
            new_weighted = weighted * jnp.transpose(factor, (0, 2, 1))[..., None] + update
            return (new_max, new_total, new_weighted)

        def absorb_keep(current):
            return current

        return (lax.cond(first_key <= last_query, absorb_compute, absorb_keep, running), None)

    result, unused = lax.scan(
        absorb_visit, initial, jnp.arange(piece_rows // block_rows, dtype=jnp.int32)
    )
    row_max, row_total, weighted = result
    attended = weighted / jnp.transpose(row_total, (0, 2, 1))[..., None]
    return (attended, row_max + jnp.log(row_total))


def attend_back_gather(
    queries, grad_attended, log_normalizer, row_delta, key_rows, value_rows, segments, query_places
):
    seq_count, count_of_rows, head_count, head_width = queries.shape
    query_document_ids = lax.dynamic_slice_in_dim(segments, query_places[0], count_of_rows, 1)
    last_query = query_places[count_of_rows - 1]
    all_keys, all_values = (
        lax.all_gather(key_rows, "ctx", axis=1, tiled=True),
        lax.all_gather(value_rows, "ctx", axis=1, tiled=True),
    )
    length = all_keys.shape[1]
    block_rows = math.gcd(length, 512)
    key_split = all_keys.reshape(seq_count, length, head_count, head_width)
    value_split = all_values.reshape(seq_count, length, head_count, head_width)
    initial = (
        jnp.zeros((seq_count, count_of_rows, head_count, head_width), jnp.float32),
        jnp.zeros((seq_count, length, head_count, head_width), jnp.float32),
        jnp.zeros((seq_count, length, head_count, head_width), jnp.float32),
    )

    def attend_visit(state_now, block_index):
        first_key = block_index * block_rows

        def attend_compute(current):
            query_acc, key_acc, value_acc = current
            key_block = lax.dynamic_slice_in_dim(key_split, first_key, block_rows, 1)
            value_block = lax.dynamic_slice_in_dim(value_split, first_key, block_rows, 1)
            key_places = first_key + jnp.arange(block_rows, dtype=jnp.int32)
            key_segments = lax.dynamic_slice_in_dim(segments, first_key, block_rows, 1)
            query_part, key_part, value_part = block_grads(
                queries,
                grad_attended,
                log_normalizer,
                row_delta,
                query_places,
                query_document_ids,
                key_block,
                value_block,
                key_places,
                key_segments,
            )
            key_acc = lax.dynamic_update_slice_in_dim(key_acc, key_part, first_key, 1)
            value_acc = lax.dynamic_update_slice_in_dim(value_acc, value_part, first_key, 1)
            return (query_acc + query_part, key_acc, value_acc)

        def attend_keep(current):
            return current

        return (lax.cond(first_key <= last_query, attend_compute, attend_keep, state_now), None)

    totals, unused = lax.scan(
        attend_visit, initial, jnp.arange(length // block_rows, dtype=jnp.int32)
    )
    query_grad, key_grad, value_grad = totals
    key_home, value_home = (
        lax.psum_scatter(
            key_grad.reshape(seq_count, length, -1).astype(jnp.bfloat16),
            "ctx",
            scatter_dimension=1,
            tiled=True,
        ).astype(jnp.float32),
        lax.psum_scatter(
            value_grad.reshape(seq_count, length, -1).astype(jnp.bfloat16),
            "ctx",
            scatter_dimension=1,
            tiled=True,
        ).astype(jnp.float32),
    )
    split_shape = (seq_count, count_of_rows, head_count, head_width)
    return (query_grad, key_home.reshape(split_shape), value_home.reshape(split_shape))


def forward_layer(stream, first_values, weights, segments, cosine, sine_table, query_places):
    norm_attn, w_query, w_key, w_value, w_output, norm_ffn, w_gate, w_up, w_down = weights
    seq_count, count_of_rows, model_width = stream.shape
    head_count = w_query.shape[1] // HEAD_DIM
    split_shape = (seq_count, count_of_rows, head_count, HEAD_DIM)
    normed, inverse_one = norm_forward(stream, norm_attn)
    queries = rotate(project(normed, w_query).reshape(split_shape), cosine, sine_table).astype(
        jnp.bfloat16
    )
    key_rows = (
        rotate(project(normed, w_key).reshape(split_shape), cosine, sine_table)
        .astype(jnp.bfloat16)
        .reshape(seq_count, count_of_rows, -1)
    )
    own_values = project(normed, w_value)
    if first_values is None:
        mixed = own_values.astype(jnp.bfloat16)
    else:
        mixed = (0.5 * own_values + 0.5 * first_values).astype(jnp.bfloat16)
    attended, log_normalizer = attend_forward(queries, key_rows, mixed, segments, query_places)
    attended_low = attended.reshape(seq_count, count_of_rows, -1).astype(jnp.bfloat16)
    hidden_one = stream + head_total(project(attended_low, w_output))
    normed_two, inverse_two = norm_forward(hidden_one, norm_ffn)
    gate_values = project(normed_two, w_gate)
    up_values = project(normed_two, w_up)
    activated = (jax.nn.silu(gate_values) * up_values).astype(jnp.bfloat16)
    result = hidden_one + head_total(project(activated, w_down))
    saved_state = (
        stream,
        inverse_one,
        normed,
        queries,
        key_rows,
        mixed,
        attended,
        log_normalizer,
        attended_low,
        hidden_one,
        inverse_two,
        normed_two,
        gate_values,
        up_values,
        activated,
    )
    return (result, saved_state, own_values)


def backward_layer(
    grad_out, value_extra, saved_state, weights, segments, cosine, sine_table, query_places, mixes
):
    (
        stream,
        inverse_one,
        normed,
        queries,
        key_rows,
        mixed,
        attended,
        log_normalizer,
        attended_low,
        hidden_one,
        inverse_two,
        normed_two,
        gate_values,
        up_values,
        activated,
    ) = saved_state
    norm_attn, w_query, w_key, w_value, w_output, norm_ffn, w_gate, w_up, w_down = weights
    seq_count, count_of_rows, head_count, head_width = queries.shape
    grad_branch = grad_out.astype(jnp.bfloat16)
    down_grad = weight_term(activated, grad_branch)
    grad_active = project_back(grad_branch, w_down)
    gate_sigmoid = jax.nn.sigmoid(gate_values)
    grad_gate = (
        grad_active * up_values * gate_sigmoid * (1.0 + gate_values * (1.0 - gate_sigmoid))
    ).astype(jnp.bfloat16)
    grad_up = (grad_active * gate_values * gate_sigmoid).astype(jnp.bfloat16)
    gate_grad = weight_term(normed_two, grad_gate)
    up_grad = weight_term(normed_two, grad_up)
    grad_normed_two = head_back(project_back(grad_gate, w_gate) + project_back(grad_up, w_up))
    grad_norm_two, ffn_gain_grad = norm_backward(grad_normed_two, hidden_one, inverse_two, norm_ffn)
    grad_hidden = grad_out + grad_norm_two
    grad_attn = grad_hidden.astype(jnp.bfloat16)
    output_grad = weight_term(attended_low, grad_attn)
    grad_attended = (
        project_back(grad_attn, w_output)
        .astype(jnp.bfloat16)
        .reshape(seq_count, count_of_rows, head_count, head_width)
    )
    row_delta = jnp.transpose(
        jnp.sum(grad_attended.astype(jnp.float32) * attended, axis=-1), (0, 2, 1)
    )
    query_rot, key_rot, value_mix = attend_back_gather(
        queries, grad_attended, log_normalizer, row_delta, key_rows, mixed, segments, query_places
    )
    query_low = (
        rotate_back(query_rot, cosine, sine_table)
        .astype(jnp.bfloat16)
        .reshape(seq_count, count_of_rows, -1)
    )
    key_low = (
        rotate_back(key_rot, cosine, sine_table)
        .astype(jnp.bfloat16)
        .reshape(seq_count, count_of_rows, -1)
    )
    value_mix = value_mix.reshape(seq_count, count_of_rows, -1)
    if mixes:
        value_low = (0.5 * value_mix).astype(jnp.bfloat16)
        passed_on = 0.5 * value_mix
    else:
        value_low = (value_mix + value_extra).astype(jnp.bfloat16)
        passed_on = value_extra
    query_grad = weight_term(normed, query_low)
    key_grad = weight_term(normed, key_low)
    value_grad = weight_term(normed, value_low)
    grad_normed = head_back(
        project_back(query_low, w_query)
        + project_back(key_low, w_key)
        + project_back(value_low, w_value)
    )
    grad_norm_one, attn_gain_grad = norm_backward(grad_normed, stream, inverse_one, norm_attn)
    grad_stream = grad_hidden + grad_norm_one
    grad_terms = (
        attn_gain_grad,
        query_grad,
        key_grad,
        value_grad,
        output_grad,
        ffn_gain_grad,
        gate_grad,
        up_grad,
        down_grad,
    )
    return (grad_stream, passed_on, grad_terms)


def on_device(
    inputs,
    segment_ids,
    norm_attn_one,
    query_one,
    key_one,
    value_one,
    output_one,
    norm_ffn_one,
    gate_one,
    up_one,
    down_one,
    norm_attn_two,
    query_two,
    key_two,
    value_two,
    output_two,
    norm_ffn_two,
    gate_two,
    up_two,
    down_two,
    cotangent,
):
    def gather_layer(gain_attn, query, key, value, output, gain_ffn, gate, up, down):
        both = ("dp", "ctx")
        packed = jnp.concatenate([query, key, value, output.T, gate, up, down.T], axis=1)
        whole = lax.all_gather(packed, both, axis=0, tiled=True)
        gains = lax.all_gather(jnp.stack([gain_attn, gain_ffn]), both, axis=1, tiled=True)
        cuts = []
        for part in (query, key, value, output.T, gate, up, down.T):
            cuts.append((cuts[-1] if cuts else 0) + part.shape[1])
        w_q, w_k, w_v, w_o, w_g, w_u, w_d = jnp.split(whole, cuts[:-1], axis=1)
        return (gains[0], w_q, w_k, w_v, w_o.T, gains[1], w_g, w_u, w_d.T)

    def scatter_layer(grads, outs):
        both = ("dp", "ctx")
        gain_attn, query, key, value, output, gain_ffn, gate, up, down = grads
        pieces = [query, key, value, output.T, gate, up, down.T]
        packed = jnp.concatenate([part.astype(jnp.bfloat16) for part in pieces], axis=1)
        mine = lax.psum_scatter(packed, both, scatter_dimension=0, tiled=True)
        gains = lax.psum_scatter(
            jnp.stack([gain_attn, gain_ffn]).astype(jnp.bfloat16),
            both,
            scatter_dimension=1,
            tiled=True,
        ).astype(jnp.float32)
        cuts = []
        for part in pieces:
            cuts.append((cuts[-1] if cuts else 0) + part.shape[1])
        g_q, g_k, g_v, g_o, g_g, g_u, g_d = (
            part.astype(jnp.float32) for part in jnp.split(mine, cuts[:-1], axis=1)
        )
        return (gains[0], g_q, g_k, g_v, g_o.T, gains[1], g_g, g_u, g_d.T)

    gathered = gather_layer(
        norm_attn_one,
        query_one,
        key_one,
        value_one,
        output_one,
        norm_ffn_one,
        gate_one,
        up_one,
        down_one,
    ) + gather_layer(
        norm_attn_two,
        query_two,
        key_two,
        value_two,
        output_two,
        norm_ffn_two,
        gate_two,
        up_two,
        down_two,
    )
    weights_one = gathered[:9]
    weights_two = gathered[9:]
    seq_count, count_of_rows, model_width = inputs.shape
    query_places = lax.axis_index("ctx") * count_of_rows + jnp.arange(
        count_of_rows, dtype=jnp.int32
    )
    cosine, sine_table = rotary_tables(query_places[0], count_of_rows)
    layer_one, saved_one, first_values = forward_layer(
        inputs.astype(jnp.float32), None, weights_one, segment_ids, cosine, sine_table, query_places
    )
    layer_two, saved_two, unused = forward_layer(
        layer_one, first_values, weights_two, segment_ids, cosine, sine_table, query_places
    )
    grad_middle, value_extra, grads_two = backward_layer(
        cotangent.astype(jnp.float32),
        None,
        saved_two,
        weights_two,
        segment_ids,
        cosine,
        sine_table,
        query_places,
        True,
    )
    grad_input, unused_extra, grads_one = backward_layer(
        grad_middle,
        value_extra,
        saved_one,
        weights_one,
        segment_ids,
        cosine,
        sine_table,
        query_places,
        False,
    )
    totals = scatter_layer(grads_one, None) + scatter_layer(grads_two, None)
    return (
        layer_one.astype(jnp.bfloat16),
        layer_two.astype(jnp.bfloat16),
        grad_input,
        totals[0],
        totals[1],
        totals[2],
        totals[3],
        totals[4],
        totals[5],
        totals[6],
        totals[7],
        totals[8],
        totals[9],
        totals[10],
        totals[11],
        totals[12],
        totals[13],
        totals[14],
        totals[15],
        totals[16],
        totals[17],
    )


def solution(mesh):
    placed = (
        P("dp", "ctx", None),
        P("dp", None),
        P(("dp", "ctx")),
        P(("dp", "ctx"), "mp"),
        P(("dp", "ctx"), "mp"),
        P(("dp", "ctx"), "mp"),
        P("mp", ("dp", "ctx")),
        P(("dp", "ctx")),
        P(("dp", "ctx"), "mp"),
        P(("dp", "ctx"), "mp"),
        P("mp", ("dp", "ctx")),
        P(("dp", "ctx")),
        P(("dp", "ctx"), "mp"),
        P(("dp", "ctx"), "mp"),
        P(("dp", "ctx"), "mp"),
        P("mp", ("dp", "ctx")),
        P(("dp", "ctx")),
        P(("dp", "ctx"), "mp"),
        P(("dp", "ctx"), "mp"),
        P("mp", ("dp", "ctx")),
        P("dp", "ctx", None),
    )
    return jax.shard_map(
        on_device,
        mesh=mesh,
        in_specs=placed,
        out_specs=(
            P("dp", "ctx", None),
            P("dp", "ctx", None),
            P("dp", "ctx", None),
            P(("dp", "ctx")),
            P(("dp", "ctx"), "mp"),
            P(("dp", "ctx"), "mp"),
            P(("dp", "ctx"), "mp"),
            P("mp", ("dp", "ctx")),
            P(("dp", "ctx")),
            P(("dp", "ctx"), "mp"),
            P(("dp", "ctx"), "mp"),
            P("mp", ("dp", "ctx")),
            P(("dp", "ctx")),
            P(("dp", "ctx"), "mp"),
            P(("dp", "ctx"), "mp"),
            P(("dp", "ctx"), "mp"),
            P("mp", ("dp", "ctx")),
            P(("dp", "ctx")),
            P(("dp", "ctx"), "mp"),
            P(("dp", "ctx"), "mp"),
            P("mp", ("dp", "ctx")),
        ),
        check_vma=False,
    )
```

```python
import functools
import math
from types import SimpleNamespace

import jax
import jax.numpy as jnp
from jax import lax
from jax.experimental import pallas as pl
from jax.experimental.pallas import tpu as pltpu
from jax.sharding import PartitionSpec as P

MESH = pl.DeviceIdType.MESH

HEAD_DIM = 64


epsilon = 1e-05
neg_large = -1e30


def project(left_operand, right_operand):
    return jnp.einsum(
        "sbd,de->sbe", left_operand, right_operand, preferred_element_type=jnp.float32
    )


def project_back(left_operand, right_operand):
    return jnp.einsum(
        "sbe,de->sbd", left_operand, right_operand, preferred_element_type=jnp.float32
    )


def weight_term(left_operand, right_operand):
    return jnp.einsum(
        "sbd,sbe->de", left_operand, right_operand, preferred_element_type=jnp.float32
    )


def head_sum_kernel(
    chunks, x_ref, o_ref, near, half_sum, far, send_a, recv_a, send_b, recv_b, send_c, recv_c
):
    dp, ctx, mp = (lax.axis_index(name) for name in ("dp", "ctx", "mp"))
    side = lax.rem(mp, 2)
    pair = (dp, ctx, mp + 1 - 2 * side)
    cross = (dp, ctx, lax.rem(mp + 2, 4))
    barrier = pltpu.get_barrier_semaphore()
    for peer in (pair, cross):
        pl.semaphore_signal(barrier, inc=1, device_id=peer, device_id_type=MESH)
    pl.semaphore_wait(barrier, 2)
    rows = x_ref.shape[0] // chunks
    half = rows // 2

    def copy(source, target, send, recv, i, peer):
        return pltpu.make_async_remote_copy(
            src_ref=source,
            dst_ref=target,
            send_sem=send.at[i],
            recv_sem=recv.at[i],
            device_id=peer,
            device_id_type=MESH,
        )

    def first(i):
        theirs = x_ref.at[pl.ds(i * rows + (1 - side) * half, half)]
        return copy(theirs, near.at[i], send_a, recv_a, i, pair)

    def second(i):
        return copy(half_sum.at[i], far.at[i], send_b, recv_b, i, cross)

    def third(i):
        mine = o_ref.at[pl.ds(i * rows + side * half, half)]
        return copy(mine, mine, send_c, recv_c, i, pair)

    for i in range(chunks):
        first(i).start()
    for i in range(chunks):
        first(i).wait()
        mine = x_ref[pl.ds(i * rows + side * half, half)].astype(jnp.float32)
        half_sum[i] = (mine + near[i].astype(jnp.float32)).astype(jnp.bfloat16)
        second(i).start()
    for i in range(chunks):
        second(i).wait()
        total = half_sum[i].astype(jnp.float32) + far[i].astype(jnp.float32)
        o_ref[pl.ds(i * rows + side * half, half)] = total.astype(jnp.bfloat16)
        third(i).start()
    for i in range(chunks):
        third(i).wait()


def head_sum(partial_sum, number):
    flat = partial_sum.astype(jnp.bfloat16).reshape(-1, partial_sum.shape[-1])
    count, width = flat.shape
    chunks = 4
    half = count // chunks // 2
    total = pl.pallas_call(
        functools.partial(head_sum_kernel, chunks),
        out_shape=jax.ShapeDtypeStruct((count, width), jnp.bfloat16),
        in_specs=[pl.BlockSpec(memory_space=pltpu.VMEM)],
        out_specs=pl.BlockSpec(memory_space=pltpu.VMEM),
        scratch_shapes=[pltpu.VMEM((chunks, half, width), jnp.bfloat16)] * 3
        + [pltpu.SemaphoreType.DMA((chunks,))] * 6,
        compiler_params=pltpu.CompilerParams(
            collective_id=0, has_side_effects=True, vmem_limit_bytes=32 << 20
        ),
    )(flat)
    return total.reshape(partial_sum.shape).astype(jnp.float32)


def head_total(partial_sum):
    return head_sum(partial_sum, 0)


def head_back(partial_sum):
    return head_sum(partial_sum, 0)


def rotary_tables(first_place, count_of_rows):
    half_width = HEAD_DIM // 2
    frequency = 10000.0 ** (-jnp.arange(half_width, dtype=jnp.float32) / half_width)
    places = (first_place + jnp.arange(count_of_rows, dtype=jnp.int32)).astype(jnp.float32)
    angles = places[:, None] * frequency[None, :]
    return (jnp.cos(angles)[None, :, None, :], jnp.sin(angles)[None, :, None, :])


def rotate(split_heads, cosine, sine_table):
    half_width = HEAD_DIM // 2
    first_half = split_heads[..., :half_width]
    second_half = split_heads[..., half_width:]
    return jnp.concatenate(
        [
            first_half * cosine - second_half * sine_table,
            first_half * sine_table + second_half * cosine,
        ],
        axis=-1,
    )


def rotate_back(split_heads, cosine, sine_table):
    half_width = HEAD_DIM // 2
    first_half = split_heads[..., :half_width]
    second_half = split_heads[..., half_width:]
    return jnp.concatenate(
        [
            first_half * cosine + second_half * sine_table,
            second_half * cosine - first_half * sine_table,
        ],
        axis=-1,
    )


def norm_forward(stream, gain_row):
    inverse = lax.rsqrt(jnp.mean(stream * stream, axis=-1, keepdims=True) + epsilon)
    normed = (stream * inverse * gain_row.astype(jnp.float32)).astype(jnp.bfloat16)
    return (normed, inverse)


def norm_backward(grad_normed, stream, inverse, gain_row):
    scaled = stream * inverse
    grad_scaled = grad_normed * gain_row.astype(jnp.float32)
    gain_grad = jnp.sum(grad_normed * scaled, axis=(0, 1))
    grad_stream = inverse * (
        grad_scaled - scaled * jnp.mean(grad_scaled * scaled, axis=-1, keepdims=True)
    )
    return (grad_stream, gain_grad)


def block_grads(
    query_block,
    grad_block,
    lse_block,
    delta_block,
    query_places,
    query_document_ids,
    key_block,
    value_block,
    key_places,
    key_segments,
):
    score_scale = HEAD_DIM ** (-0.5)
    scores = (
        jnp.einsum("sqhe,skhe->shqk", query_block, key_block, preferred_element_type=jnp.float32)
        * score_scale
    )
    visible = (
        (key_places[None, :] <= query_places[:, None])[None]
        & (key_segments[:, None, :] == query_document_ids[:, :, None])
    )[:, None]
    probabilities = jnp.where(visible, jnp.exp(scores - lse_block[..., None]), 0.0)
    grad_probs = jnp.einsum(
        "sqhe,skhe->shqk", grad_block, value_block, preferred_element_type=jnp.float32
    )
    grad_scores = (probabilities * (grad_probs - delta_block[..., None]) * score_scale).astype(
        jnp.bfloat16
    )
    query_grad = jnp.einsum(
        "shqk,skhe->sqhe", grad_scores, key_block, preferred_element_type=jnp.float32
    )
    key_grad = jnp.einsum(
        "shqk,sqhe->skhe", grad_scores, query_block, preferred_element_type=jnp.float32
    )
    value_grad = jnp.einsum(
        "shqk,sqhe->skhe",
        probabilities.astype(jnp.bfloat16),
        grad_block,
        preferred_element_type=jnp.float32,
    )
    return (query_grad, key_grad, value_grad)


def attend_forward(queries, key_rows, value_rows, segments, query_places):
    seq_count, count_of_rows, head_count, head_width = queries.shape
    score_scale = head_width ** (-0.5)
    query_document_ids = lax.dynamic_slice_in_dim(segments, query_places[0], count_of_rows, 1)
    last_query = query_places[count_of_rows - 1]
    initial = (
        jnp.full((seq_count, head_count, count_of_rows), neg_large, jnp.float32),
        jnp.zeros((seq_count, head_count, count_of_rows), jnp.float32),
        jnp.zeros((seq_count, count_of_rows, head_count, head_width), jnp.float32),
    )
    key_piece = lax.all_gather(key_rows, "ctx", axis=1, tiled=True)
    value_piece = lax.all_gather(value_rows, "ctx", axis=1, tiled=True)
    piece_rows = key_piece.shape[1]
    block_rows = math.gcd(piece_rows, 512)
    key_split = key_piece.reshape(seq_count, piece_rows, head_count, head_width)
    value_split = value_piece.reshape(seq_count, piece_rows, head_count, head_width)

    def absorb_visit(running, block_index):
        first_key = block_index * block_rows

        def absorb_compute(current):
            row_max, row_total, weighted = current
            key_block = lax.dynamic_slice_in_dim(key_split, first_key, block_rows, 1)
            value_block = lax.dynamic_slice_in_dim(value_split, first_key, block_rows, 1)
            key_places = first_key + jnp.arange(block_rows, dtype=jnp.int32)
            key_segments = lax.dynamic_slice_in_dim(segments, first_key, block_rows, 1)
            scores = (
                jnp.einsum(
                    "sqhe,skhe->shqk", queries, key_block, preferred_element_type=jnp.float32
                )
                * score_scale
            )
            visible = (
                (key_places[None, :] <= query_places[:, None])[None]
                & (key_segments[:, None, :] == query_document_ids[:, :, None])
            )[:, None]
            new_max = jnp.maximum(row_max, jnp.max(jnp.where(visible, scores, neg_large), axis=-1))
            exponent = jnp.where(visible, jnp.exp(scores - new_max[..., None]), 0.0)
            factor = jnp.exp(row_max - new_max)
            new_total = row_total * factor + jnp.sum(exponent, axis=-1)
            update = jnp.einsum(
                "shqk,skhe->sqhe",
                exponent.astype(jnp.bfloat16),
                value_block,
                preferred_element_type=jnp.float32,
            )
            new_weighted = weighted * jnp.transpose(factor, (0, 2, 1))[..., None] + update
            return (new_max, new_total, new_weighted)

        def absorb_keep(current):
            return current

        return (lax.cond(first_key <= last_query, absorb_compute, absorb_keep, running), None)

    result, unused = lax.scan(
        absorb_visit, initial, jnp.arange(piece_rows // block_rows, dtype=jnp.int32)
    )
    row_max, row_total, weighted = result
    attended = weighted / jnp.transpose(row_total, (0, 2, 1))[..., None]
    return (attended, row_max + jnp.log(row_total))


def attend_back_gather(
    queries, grad_attended, log_normalizer, row_delta, key_rows, value_rows, segments, query_places
):
    seq_count, count_of_rows, head_count, head_width = queries.shape
    query_document_ids = lax.dynamic_slice_in_dim(segments, query_places[0], count_of_rows, 1)
    last_query = query_places[count_of_rows - 1]
    all_keys, all_values = (
        lax.all_gather(key_rows, "ctx", axis=1, tiled=True),
        lax.all_gather(value_rows, "ctx", axis=1, tiled=True),
    )
    length = all_keys.shape[1]
    block_rows = math.gcd(length, 512)
    key_split = all_keys.reshape(seq_count, length, head_count, head_width)
    value_split = all_values.reshape(seq_count, length, head_count, head_width)
    initial = (
        jnp.zeros((seq_count, count_of_rows, head_count, head_width), jnp.float32),
        jnp.zeros((seq_count, length, head_count, head_width), jnp.float32),
        jnp.zeros((seq_count, length, head_count, head_width), jnp.float32),
    )

    def attend_visit(state_now, block_index):
        first_key = block_index * block_rows

        def attend_compute(current):
            query_acc, key_acc, value_acc = current
            key_block = lax.dynamic_slice_in_dim(key_split, first_key, block_rows, 1)
            value_block = lax.dynamic_slice_in_dim(value_split, first_key, block_rows, 1)
            key_places = first_key + jnp.arange(block_rows, dtype=jnp.int32)
            key_segments = lax.dynamic_slice_in_dim(segments, first_key, block_rows, 1)
            query_part, key_part, value_part = block_grads(
                queries,
                grad_attended,
                log_normalizer,
                row_delta,
                query_places,
                query_document_ids,
                key_block,
                value_block,
                key_places,
                key_segments,
            )
            key_acc = lax.dynamic_update_slice_in_dim(key_acc, key_part, first_key, 1)
            value_acc = lax.dynamic_update_slice_in_dim(value_acc, value_part, first_key, 1)
            return (query_acc + query_part, key_acc, value_acc)

        def attend_keep(current):
            return current

        return (lax.cond(first_key <= last_query, attend_compute, attend_keep, state_now), None)

    totals, unused = lax.scan(
        attend_visit, initial, jnp.arange(length // block_rows, dtype=jnp.int32)
    )
    query_grad, key_grad, value_grad = totals
    key_home, value_home = (
        lax.psum_scatter(
            key_grad.reshape(seq_count, length, -1).astype(jnp.bfloat16),
            "ctx",
            scatter_dimension=1,
            tiled=True,
        ).astype(jnp.float32),
        lax.psum_scatter(
            value_grad.reshape(seq_count, length, -1).astype(jnp.bfloat16),
            "ctx",
            scatter_dimension=1,
            tiled=True,
        ).astype(jnp.float32),
    )
    split_shape = (seq_count, count_of_rows, head_count, head_width)
    return (query_grad, key_home.reshape(split_shape), value_home.reshape(split_shape))


def forward_layer(stream, first_values, weights, segments, cosine, sine_table, query_places):
    norm_attn, w_query, w_key, w_value, w_output, norm_ffn, w_gate, w_up, w_down = weights
    seq_count, count_of_rows, model_width = stream.shape
    head_count = w_query.shape[1] // HEAD_DIM
    split_shape = (seq_count, count_of_rows, head_count, HEAD_DIM)
    normed, inverse_one = norm_forward(stream, norm_attn)
    queries = rotate(project(normed, w_query).reshape(split_shape), cosine, sine_table).astype(
        jnp.bfloat16
    )
    key_rows = (
        rotate(project(normed, w_key).reshape(split_shape), cosine, sine_table)
        .astype(jnp.bfloat16)
        .reshape(seq_count, count_of_rows, -1)
    )
    own_values = project(normed, w_value)
    if first_values is None:
        mixed = own_values.astype(jnp.bfloat16)
    else:
        mixed = (0.5 * own_values + 0.5 * first_values).astype(jnp.bfloat16)
    attended, log_normalizer = attend_forward(queries, key_rows, mixed, segments, query_places)
    attended_low = attended.reshape(seq_count, count_of_rows, -1).astype(jnp.bfloat16)
    hidden_one = stream + head_total(project(attended_low, w_output))
    normed_two, inverse_two = norm_forward(hidden_one, norm_ffn)
    gate_values = project(normed_two, w_gate)
    up_values = project(normed_two, w_up)
    activated = (jax.nn.silu(gate_values) * up_values).astype(jnp.bfloat16)
    result = hidden_one + head_total(project(activated, w_down))
    saved_state = (
        stream,
        inverse_one,
        normed,
        queries,
        key_rows,
        mixed,
        attended,
        log_normalizer,
        attended_low,
        hidden_one,
        inverse_two,
        normed_two,
        gate_values,
        up_values,
        activated,
    )
    return (result, saved_state, own_values)


def backward_layer(
    grad_out, value_extra, saved_state, weights, segments, cosine, sine_table, query_places, mixes
):
    (
        stream,
        inverse_one,
        normed,
        queries,
        key_rows,
        mixed,
        attended,
        log_normalizer,
        attended_low,
        hidden_one,
        inverse_two,
        normed_two,
        gate_values,
        up_values,
        activated,
    ) = saved_state
    norm_attn, w_query, w_key, w_value, w_output, norm_ffn, w_gate, w_up, w_down = weights
    seq_count, count_of_rows, head_count, head_width = queries.shape
    grad_branch = grad_out.astype(jnp.bfloat16)
    down_grad = weight_term(activated, grad_branch)
    grad_active = project_back(grad_branch, w_down)
    gate_sigmoid = jax.nn.sigmoid(gate_values)
    grad_gate = (
        grad_active * up_values * gate_sigmoid * (1.0 + gate_values * (1.0 - gate_sigmoid))
    ).astype(jnp.bfloat16)
    grad_up = (grad_active * gate_values * gate_sigmoid).astype(jnp.bfloat16)
    gate_grad = weight_term(normed_two, grad_gate)
    up_grad = weight_term(normed_two, grad_up)
    grad_normed_two = head_back(project_back(grad_gate, w_gate) + project_back(grad_up, w_up))
    grad_norm_two, ffn_gain_grad = norm_backward(grad_normed_two, hidden_one, inverse_two, norm_ffn)
    grad_hidden = grad_out + grad_norm_two
    grad_attn = grad_hidden.astype(jnp.bfloat16)
    output_grad = weight_term(attended_low, grad_attn)
    grad_attended = (
        project_back(grad_attn, w_output)
        .astype(jnp.bfloat16)
        .reshape(seq_count, count_of_rows, head_count, head_width)
    )
    row_delta = jnp.transpose(
        jnp.sum(grad_attended.astype(jnp.float32) * attended, axis=-1), (0, 2, 1)
    )
    query_rot, key_rot, value_mix = attend_back_gather(
        queries, grad_attended, log_normalizer, row_delta, key_rows, mixed, segments, query_places
    )
    query_low = (
        rotate_back(query_rot, cosine, sine_table)
        .astype(jnp.bfloat16)
        .reshape(seq_count, count_of_rows, -1)
    )
    key_low = (
        rotate_back(key_rot, cosine, sine_table)
        .astype(jnp.bfloat16)
        .reshape(seq_count, count_of_rows, -1)
    )
    value_mix = value_mix.reshape(seq_count, count_of_rows, -1)
    if mixes:
        value_low = (0.5 * value_mix).astype(jnp.bfloat16)
        passed_on = 0.5 * value_mix
    else:
        value_low = (value_mix + value_extra).astype(jnp.bfloat16)
        passed_on = value_extra
    query_grad = weight_term(normed, query_low)
    key_grad = weight_term(normed, key_low)
    value_grad = weight_term(normed, value_low)
    grad_normed = head_back(
        project_back(query_low, w_query)
        + project_back(key_low, w_key)
        + project_back(value_low, w_value)
    )
    grad_norm_one, attn_gain_grad = norm_backward(grad_normed, stream, inverse_one, norm_attn)
    grad_stream = grad_hidden + grad_norm_one
    grad_terms = (
        attn_gain_grad,
        query_grad,
        key_grad,
        value_grad,
        output_grad,
        ffn_gain_grad,
        gate_grad,
        up_grad,
        down_grad,
    )
    return (grad_stream, passed_on, grad_terms)


def on_device(
    inputs,
    segment_ids,
    norm_attn_one,
    query_one,
    key_one,
    value_one,
    output_one,
    norm_ffn_one,
    gate_one,
    up_one,
    down_one,
    norm_attn_two,
    query_two,
    key_two,
    value_two,
    output_two,
    norm_ffn_two,
    gate_two,
    up_two,
    down_two,
    cotangent,
):
    def gather_layer(gain_attn, query, key, value, output, gain_ffn, gate, up, down):
        both = ("dp", "ctx")
        packed = jnp.concatenate([query, key, value, output.T, gate, up, down.T], axis=1)
        whole = lax.all_gather(packed, both, axis=0, tiled=True)
        gains = lax.all_gather(jnp.stack([gain_attn, gain_ffn]), both, axis=1, tiled=True)
        cuts = []
        for part in (query, key, value, output.T, gate, up, down.T):
            cuts.append((cuts[-1] if cuts else 0) + part.shape[1])
        w_q, w_k, w_v, w_o, w_g, w_u, w_d = jnp.split(whole, cuts[:-1], axis=1)
        return (gains[0], w_q, w_k, w_v, w_o.T, gains[1], w_g, w_u, w_d.T)

    def scatter_layer(grads, outs):
        both = ("dp", "ctx")
        gain_attn, query, key, value, output, gain_ffn, gate, up, down = grads
        pieces = [query, key, value, output.T, gate, up, down.T]
        packed = jnp.concatenate([part.astype(jnp.bfloat16) for part in pieces], axis=1)
        mine = lax.psum_scatter(packed, both, scatter_dimension=0, tiled=True)
        gains = lax.psum_scatter(
            jnp.stack([gain_attn, gain_ffn]).astype(jnp.bfloat16),
            both,
            scatter_dimension=1,
            tiled=True,
        ).astype(jnp.float32)
        cuts = []
        for part in pieces:
            cuts.append((cuts[-1] if cuts else 0) + part.shape[1])
        g_q, g_k, g_v, g_o, g_g, g_u, g_d = (
            part.astype(jnp.float32) for part in jnp.split(mine, cuts[:-1], axis=1)
        )
        return (gains[0], g_q, g_k, g_v, g_o.T, gains[1], g_g, g_u, g_d.T)

    gathered = gather_layer(
        norm_attn_one,
        query_one,
        key_one,
        value_one,
        output_one,
        norm_ffn_one,
        gate_one,
        up_one,
        down_one,
    ) + gather_layer(
        norm_attn_two,
        query_two,
        key_two,
        value_two,
        output_two,
        norm_ffn_two,
        gate_two,
        up_two,
        down_two,
    )
    weights_one = gathered[:9]
    weights_two = gathered[9:]
    seq_count, count_of_rows, model_width = inputs.shape
    query_places = lax.axis_index("ctx") * count_of_rows + jnp.arange(
        count_of_rows, dtype=jnp.int32
    )
    cosine, sine_table = rotary_tables(query_places[0], count_of_rows)
    layer_one, saved_one, first_values = forward_layer(
        inputs.astype(jnp.float32), None, weights_one, segment_ids, cosine, sine_table, query_places
    )
    layer_two, saved_two, unused = forward_layer(
        layer_one, first_values, weights_two, segment_ids, cosine, sine_table, query_places
    )
    grad_middle, value_extra, grads_two = backward_layer(
        cotangent.astype(jnp.float32),
        None,
        saved_two,
        weights_two,
        segment_ids,
        cosine,
        sine_table,
        query_places,
        True,
    )
    grad_input, unused_extra, grads_one = backward_layer(
        grad_middle,
        value_extra,
        saved_one,
        weights_one,
        segment_ids,
        cosine,
        sine_table,
        query_places,
        False,
    )
    totals = scatter_layer(grads_one, None) + scatter_layer(grads_two, None)
    return (
        layer_one.astype(jnp.bfloat16),
        layer_two.astype(jnp.bfloat16),
        grad_input,
        totals[0],
        totals[1],
        totals[2],
        totals[3],
        totals[4],
        totals[5],
        totals[6],
        totals[7],
        totals[8],
        totals[9],
        totals[10],
        totals[11],
        totals[12],
        totals[13],
        totals[14],
        totals[15],
        totals[16],
        totals[17],
    )


class Call:
    def __init__(self, number):
        self.number = number
        self.operands, self.in_names, self.in_specs = [], [], []
        self.out_names, self.out_shapes, self.out_specs = [], [], []
        self.scratch_names, self.scratch = [], []
        self.scratch_bytes = 0
        self.far = False

    def take(self, name, array, space=pltpu.VMEM):
        self.in_names.append(name)
        self.operands.append(array)
        self.in_specs.append(pl.BlockSpec(memory_space=space))

    def give(self, name, shape, dtype, space=pltpu.VMEM):
        self.out_names.append(name)
        self.out_shapes.append(jax.ShapeDtypeStruct(shape, dtype))
        self.out_specs.append(pl.BlockSpec(memory_space=space))

    def hold(self, name, shape, dtype):
        self.scratch_names.append(name)
        self.scratch.append(pltpu.VMEM(shape, dtype))
        padded = shape[:-2] + (-(-shape[-2] // 16) * 16, -(-shape[-1] // 128) * 128)
        self.scratch_bytes += math.prod(padded) * jnp.dtype(dtype).itemsize

    def flags(self, name, count):
        self.scratch_names.append(name)
        self.scratch.append(pltpu.SemaphoreType.DMA((count,)))

    def run(self, body):
        names = self.in_names + self.out_names + self.scratch_names

        def kernel(*refs):
            body(SimpleNamespace(**dict(zip(names, refs))))

        results = pl.pallas_call(
            kernel,
            out_shape=tuple(self.out_shapes),
            in_specs=self.in_specs,
            out_specs=tuple(self.out_specs),
            scratch_shapes=self.scratch,
            compiler_params=pltpu.CompilerParams(
                collective_id=self.number,
                has_side_effects=True,
                vmem_limit_bytes=self.scratch_bytes + (14 << 20),
            ),
        )(*self.operands)
        return SimpleNamespace(**dict(zip(self.out_names, results)))


class Place:
    def __init__(self):
        self.dp, self.ctx, self.mp = (lax.axis_index(a) for a in ("dp", "ctx", "mp"))
        self.ctx_size = lax.axis_size("ctx")
        self.side = lax.rem(self.mp, 2)
        self.pair = (self.dp, self.ctx, self.mp + 1 - 2 * self.side)
        self.cross = (self.dp, self.ctx, lax.rem(self.mp + 2, 4))
        self.other = (1 - self.dp, self.ctx, self.mp)

    def ahead(self, step):
        return lax.rem(self.ctx + step, self.ctx_size)

    def behind(self, step):
        return lax.rem(self.ctx + self.ctx_size - step, self.ctx_size)

    def along(self, index):
        return (self.dp, index, self.mp)

    def enter(self, far):
        peers = [self.pair, self.cross]
        if far:
            peers.append(self.other)
            peers += [self.along(self.ahead(s)) for s in range(1, self.ctx_size)]
        barrier = pltpu.get_barrier_semaphore()
        for peer in peers:
            pl.semaphore_signal(barrier, inc=1, device_id=peer, device_id_type=MESH)
        pl.semaphore_wait(barrier, len(peers))


def remote(source, target, send, recv, peer):
    return pltpu.make_async_remote_copy(
        src_ref=source,
        dst_ref=target,
        send_sem=send,
        recv_sem=recv,
        device_id=peer,
        device_id_type=MESH,
    )


class HeadSum:
    def __init__(self, call, blocks, rows, width):
        self.rows, self.half = rows, rows // 2
        self.blocks = blocks
        call.hold("hs_part", (blocks, rows, width), jnp.bfloat16)
        for name in ("hs_near", "hs_far", "hs_rest"):
            call.hold(name, (blocks, rows // 2, width), jnp.bfloat16)
        for name in ("hs_sa", "hs_ra", "hs_sb", "hs_rb", "hs_sc", "hs_rc"):
            call.flags(name, blocks)

    def bind(self, n, place):
        self.n, self.place = n, place

    def own(self):
        return pl.ds(pl.multiple_of(self.place.side * self.half, self.half), self.half)

    def theirs(self):
        start = (1 - self.place.side) * self.half
        return pl.ds(pl.multiple_of(start, self.half), self.half)

    def first(self, i):
        n = self.n
        source = n.hs_part.at[i, self.theirs()]
        return remote(source, n.hs_near.at[i], n.hs_sa.at[i], n.hs_ra.at[i], self.place.pair)

    def second(self, i):
        n = self.n
        return remote(
            n.hs_near.at[i], n.hs_far.at[i], n.hs_sb.at[i], n.hs_rb.at[i], self.place.cross
        )

    def third(self, i):
        n = self.n
        return remote(
            n.hs_far.at[i], n.hs_rest.at[i], n.hs_sc.at[i], n.hs_rc.at[i], self.place.pair
        )

    def send(self, i, partial_rows):
        self.n.hs_part[i] = partial_rows.astype(jnp.bfloat16)
        self.first(i).start()

    def middle(self, i):
        n = self.n
        self.first(i).wait()
        mine = n.hs_part[i, self.own()].astype(jnp.float32)
        n.hs_near[i] = (mine + n.hs_near[i].astype(jnp.float32)).astype(jnp.bfloat16)
        self.second(i).start()

    def last(self, i):
        n = self.n
        self.second(i).wait()
        total = n.hs_near[i].astype(jnp.float32) + n.hs_far[i].astype(jnp.float32)
        n.hs_far[i] = total.astype(jnp.bfloat16)
        self.third(i).start()

    def total(self, i):
        n = self.n
        self.third(i).wait()
        n.hs_part[i, self.own()] = n.hs_far[i]
        n.hs_part[i, self.theirs()] = n.hs_rest[i]
        return n.hs_part[i].astype(jnp.float32)


class Gather:
    def __init__(self, call, name, shard, places):
        self.name, self.parts = name, lax.axis_size("ctx")
        call.far = True
        call.take(name + "_shard", shard, pl.ANY)
        call.give(name, (places,) + shard.shape, shard.dtype, pl.ANY)
        for flag, count in (("_l", 1), ("_zs", 0), ("_zr", 0), ("_ys", 1), ("_yr", 1)):
            call.flags(name + flag, count if flag == "_l" else self.parts)
        self.steps = self.parts - 1

    def bind(self, n, place):
        self.place = place
        get = lambda suffix: getattr(n, self.name + suffix)
        self.shard, self.whole = get("_shard"), get("")
        self.l, self.zs, self.zr, self.ys, self.yr = (
            get(s) for s in ("_l", "_zs", "_zr", "_ys", "_yr")
        )

    def slot(self, dp, ctx):
        return self.whole.at[dp * self.parts + ctx]

    def local(self):
        p = self.place
        return pltpu.make_async_copy(self.shard, self.slot(p.dp, p.ctx), self.l.at[0])

    def along(self, s):
        p = self.place
        target = self.slot(p.dp, p.ctx)
        return remote(self.shard, target, self.zs.at[s], self.zr.at[s], p.along(p.ahead(s)))

    def across(self, s):
        p = self.place
        block = self.slot(p.dp, p.behind(s))
        source = self.shard if s == 0 else block
        return remote(source, block, self.ys.at[s], self.yr.at[s], p.other)

    def start(self):
        for s in range(self.parts - 1, 0, -1):
            self.along(s).start()
        self.across(0).start()
        self.local().start()

    def step(self, k):
        s = k + 1
        p = self.place
        block = self.slot(p.dp, p.behind(s))
        remote(block, block, self.zs.at[s], self.zr.at[s], p.along(p.ctx)).wait_recv()
        self.across(s).start()

    def finish(self):
        p = self.place
        self.local().wait()
        for s in range(1, self.parts):
            self.along(s).wait_send()
        for s in range(self.parts):
            self.across(s).wait_send()
            block = self.slot(1 - p.dp, p.behind(s))
            remote(block, block, self.ys.at[s], self.yr.at[s], p.other).wait_recv()


class Scatter:
    def __init__(self, call, name, blocks, dtype=jnp.bfloat16):
        self.name, self.parts = name, lax.axis_size("ctx")
        places, rows, width = blocks.shape
        self.dtype = blocks.dtype
        call.far = True
        call.take(name + "_in", blocks)
        call.give(name, (rows, width), jnp.float32)
        for suffix in ("_yb", "_zb"):
            call.hold(name + suffix, (self.parts, rows, width), blocks.dtype)
        for flag in ("_zs", "_zr", "_ys", "_yr"):
            call.flags(name + flag, self.parts)
        self.steps = self.parts

    def bind(self, n, place):
        self.place = place
        get = lambda suffix: getattr(n, self.name + suffix)
        self.blocks, self.out = get("_in"), get("")
        self.yb, self.zb = get("_yb"), get("_zb")
        self.zs, self.zr, self.ys, self.yr = (get(s) for s in ("_zs", "_zr", "_ys", "_yr"))

    def across(self, s):
        p = self.place
        block = self.blocks.at[(1 - p.dp) * self.parts + p.ahead(s)]
        return remote(block, self.yb.at[s], self.ys.at[s], self.yr.at[s], p.other)

    def along(self, s):
        p = self.place
        return remote(
            self.yb.at[s], self.zb.at[s], self.zs.at[s], self.zr.at[s], p.along(p.ahead(s))
        )

    def start(self):
        for s in list(range(self.parts - 1, 0, -1)) + [0]:
            self.across(s).start()

    def step(self, k):
        p = self.place
        s = self.parts - 1 - k
        self.across(s).wait()
        mine = self.blocks[p.dp * self.parts + p.ahead(s)].astype(jnp.float32)
        both = mine + self.yb[s].astype(jnp.float32)
        if s == 0:
            self.out[...] = both
        else:
            self.yb[s] = both.astype(self.dtype)
            self.along(s).start()

    def finish(self):
        total = self.out[...]
        for s in range(self.parts - 1, 0, -1):
            self.along(s).wait()
            total = total + self.zb[s].astype(jnp.float32)
        self.out[...] = total


class Deal:
    def __init__(self, call, name, blocks):
        self.name, self.parts = name, lax.axis_size("ctx")
        self.quarter = blocks.shape[1] // 4
        call.far = True
        call.take(name + "_from", blocks, pl.ANY)
        call.give(name, blocks.shape, blocks.dtype, pl.ANY)
        call.flags(name + "_l", 1)
        for flag in ("_zs", "_zr", "_xs", "_xr", "_as", "_ar", "_bs", "_br"):
            call.flags(name + flag, self.parts)
        self.steps = 2 * (self.parts - 1)

    def bind(self, n, place):
        self.place = place
        get = lambda suffix: getattr(n, self.name + suffix)
        self.source, self.target, self.l = get("_from"), get(""), get("_l")
        for flag in ("zs", "zr", "xs", "xr", "as", "ar", "bs", "br"):
            setattr(self, "f_" + flag, get("_" + flag))

    def rows(self, mp):
        return pl.ds(pl.multiple_of(mp * self.quarter, self.quarter), self.quarter)

    def local(self):
        p = self.place
        return pltpu.make_async_copy(self.source.at[p.ctx], self.target.at[p.ctx], self.l.at[0])

    def along(self, s):
        p = self.place
        rows = self.rows(p.mp)
        return remote(
            self.source.at[p.ahead(s), rows],
            self.target.at[p.ctx, rows],
            self.f_zs.at[s],
            self.f_zr.at[s],
            p.along(p.ahead(s)),
        )

    def piece(self, s, mp, send, recv, peer):
        ref = self.target.at[self.place.behind(s), self.rows(mp)]
        return remote(ref, ref, send.at[s], recv.at[s], peer)

    def start(self):
        for s in range(self.parts - 1, 0, -1):
            self.along(s).start()
        self.local().start()

    def step(self, k):
        p = self.place
        s = self.parts - 1 - k // 2
        far = lax.rem(p.mp + 2, 4)
        if k % 2 == 0:
            self.piece(s, p.mp, self.f_zs, self.f_zr, p.along(p.ctx)).wait_recv()
            self.piece(s, p.mp, self.f_xs, self.f_xr, p.cross).start()
            self.piece(s, p.mp, self.f_as, self.f_ar, p.pair).start()
        else:
            self.piece(s, far, self.f_xs, self.f_xr, p.cross).wait_recv()
            self.piece(s, far, self.f_bs, self.f_br, p.pair).start()

    def finish(self):
        p = self.place
        far = lax.rem(p.mp + 2, 4)
        near = p.mp + 1 - 2 * p.side
        near_far = lax.rem(near + 2, 4)
        self.local().wait()
        for s in range(1, self.parts):
            self.along(s).wait_send()
            self.piece(s, p.mp, self.f_xs, self.f_xr, p.cross).wait_send()
            self.piece(s, p.mp, self.f_as, self.f_ar, p.pair).wait_send()
            self.piece(s, far, self.f_bs, self.f_br, p.pair).wait_send()
            self.piece(s, near, self.f_as, self.f_ar, p.pair).wait_recv()
            self.piece(s, near_far, self.f_bs, self.f_br, p.pair).wait_recv()


class Jobs:
    def __init__(self, jobs):
        self.jobs = list(jobs)
        self.queue = []
        for k in range(max([job.steps for job in self.jobs], default=0)):
            self.queue += [(job, k) for job in self.jobs if k < job.steps]
        self.at = 0

    def bind(self, n, place):
        self.at = 0
        for job in self.jobs:
            job.bind(n, place)

    def start(self):
        for job in self.jobs:
            job.start()

    def advance(self, share):
        stop = min(len(self.queue), int(math.ceil(share * len(self.queue))))
        while self.at < stop:
            job, k = self.queue[self.at]
            job.step(k)
            self.at += 1

    def finish(self):
        self.advance(1.0)
        for job in self.jobs:
            job.finish()


def dot_nn(a, b):
    return lax.dot_general(a, b, (((1,), (0,)), ((), ())), preferred_element_type=jnp.float32)


def dot_nt(a, b):
    return lax.dot_general(a, b, (((1,), (1,)), ((), ())), preferred_element_type=jnp.float32)


def dot_tn(a, b):
    return lax.dot_general(a, b, (((0,), (0,)), ((), ())), preferred_element_type=jnp.float32)


def lane_number(width):
    return lax.broadcasted_iota(jnp.int32, (1, width), 1)


def turn(values, cosine, signed_sine, back):
    width = values.shape[1]
    half = HEAD_DIM // 2
    leading = lax.rem(lane_number(width), HEAD_DIM) < half
    swapped = jnp.where(leading, pltpu.roll(values, width - half, 1), pltpu.roll(values, half, 1))
    moved = swapped * signed_sine
    return values * cosine - moved if back else values * cosine + moved


BLOCKS = 4


def write_bias(n, i, rows, keys):
    query_at = i * rows + lax.broadcasted_iota(jnp.int32, (rows, 1), 0)
    key_at = lax.broadcasted_iota(jnp.int32, (1, keys), 1)
    same = n.seg_col[pl.ds(i * rows, rows), :] == n.seg_row[:, :keys]
    n.bias[:, :keys] = jnp.where(same & (key_at <= query_at), 0.0, neg_large)


def attention_layer(number, x, first_v, wa, gains, which, tables, jobs_of):
    count, width = x.shape
    hid = wa.shape[1] // 4
    heads = hid // HEAD_DIM
    rows = count // BLOCKS
    call = Call(number)
    call.take("x", x)
    call.take("wa", wa)
    call.take("gains", gains)
    for name, table in tables.items():
        call.take(name, table)
    if first_v is not None:
        call.take("first_v", first_v)
    call.give("x1", (count, width), jnp.float32)
    call.give("h", (count, width), jnp.bfloat16)
    for name in ("q", "k", "m", "o"):
        call.give(name, (count, hid), jnp.bfloat16)
    call.give("lse", (heads, count, 1), jnp.float32)
    if first_v is None:
        call.give("v", (count, hid), jnp.float32)
    call.hold("bias", (rows, count), jnp.float32)
    call.hold("acc", (rows, hid), jnp.float32)
    total = HeadSum(call, BLOCKS, rows, width)
    jobs = Jobs(jobs_of(call))

    def body(n):
        place = Place()
        place.enter(call.far)
        total.bind(n, place)
        jobs.bind(n, place)
        jobs.start()
        lane = lane_number(hid)
        for i in range(BLOCKS):
            at = pl.ds(i * rows, rows)
            stream = n.x[at, :].astype(jnp.float32)
            inverse = lax.rsqrt(jnp.mean(stream * stream, axis=-1, keepdims=True) + epsilon)
            normed = (stream * inverse * n.gains[which : which + 1, :]).astype(jnp.bfloat16)
            n.h[at, :] = normed
            projected = dot_nn(normed, n.wa[:, : 3 * hid])
            cosine, sine = n.cosine[at, :], n.sine[at, :]
            queries = turn(projected[:, :hid], cosine, sine, False).astype(jnp.bfloat16)
            n.q[at, :] = queries * jnp.bfloat16(HEAD_DIM**-0.5)
            n.k[at, :] = turn(projected[:, hid : 2 * hid], cosine, sine, False).astype(jnp.bfloat16)
            values = projected[:, 2 * hid :]
            if first_v is None:
                n.v[at, :] = values
            else:
                values = 0.5 * values + 0.5 * n.first_v[at, :]
            n.m[at, :] = values.astype(jnp.bfloat16)
            keys = (i + 1) * rows
            write_bias(n, i, rows, keys)

            def one_head(h, unused):
                mask = lane // HEAD_DIM == h
                query = jnp.where(mask, n.q[at, :], jnp.bfloat16(0))
                scores = dot_nt(query, n.k[:keys, :]) + n.bias[:, :keys]
                top = jnp.max(scores, axis=-1, keepdims=True)
                exponent = jnp.exp(scores - top)
                summed = jnp.sum(exponent, axis=-1, keepdims=True)
                weighted = dot_nn(exponent.astype(jnp.bfloat16), n.m[:keys, :])
                n.acc[...] = jnp.where(mask, weighted / summed, n.acc[...])
                n.lse[h, at, :] = top + jnp.log(summed)
                return unused

            lax.fori_loop(0, heads, one_head, 0)
            attended = n.acc[...].astype(jnp.bfloat16)
            n.o[at, :] = attended
            total.send(i, dot_nt(attended, n.wa[:, 3 * hid :]))
            if i:
                total.middle(i - 1)
            jobs.advance((i + 1) / (BLOCKS + 1))
        total.middle(BLOCKS - 1)
        for i in range(BLOCKS):
            total.last(i)
        for i in range(BLOCKS):
            at = pl.ds(i * rows, rows)
            n.x1[at, :] = n.x[at, :].astype(jnp.float32) + total.total(i)
        jobs.finish()

    return call.run(body)


def feed_forward_layer(number, x1, gate, up, down, gains, which, jobs_of):
    count, width = x1.shape
    units = gate.shape[1]
    rows = count // BLOCKS
    call = Call(number)
    for name, array in (("x1", x1), ("gate", gate), ("up", up), ("down", down), ("gains", gains)):
        call.take(name, array)
    call.give("y", (count, width), jnp.float32)
    call.give("y_low", (count, width), jnp.bfloat16)
    call.give("h2", (count, width), jnp.bfloat16)
    for name in ("z", "u", "a"):
        call.give(name, (count, units), jnp.bfloat16)
    total = HeadSum(call, BLOCKS, rows, width)
    jobs = Jobs(jobs_of(call))

    def body(n):
        place = Place()
        place.enter(call.far)
        total.bind(n, place)
        jobs.bind(n, place)
        jobs.start()
        for i in range(BLOCKS):
            at = pl.ds(i * rows, rows)
            stream = n.x1[at, :]
            inverse = lax.rsqrt(jnp.mean(stream * stream, axis=-1, keepdims=True) + epsilon)
            normed = (stream * inverse * n.gains[which : which + 1, :]).astype(jnp.bfloat16)
            n.h2[at, :] = normed
            z = dot_nn(normed, n.gate[...])
            u = dot_nn(normed, n.up[...])
            active = (z * lax.logistic(z) * u).astype(jnp.bfloat16)
            n.z[at, :] = z.astype(jnp.bfloat16)
            n.u[at, :] = u.astype(jnp.bfloat16)
            n.a[at, :] = active
            total.send(i, dot_nt(active, n.down[...]))
            if i:
                total.middle(i - 1)
            jobs.advance((i + 1) / (BLOCKS + 1))
        total.middle(BLOCKS - 1)
        for i in range(BLOCKS):
            total.last(i)
        for i in range(BLOCKS):
            at = pl.ds(i * rows, rows)
            y = n.x1[at, :] + total.total(i)
            n.y[at, :] = y
            n.y_low[at, :] = y.astype(jnp.bfloat16)
        jobs.finish()

    return call.run(body)


def norm_back(n, grad, stream, which, at, out, gain_sum):
    inverse = lax.rsqrt(jnp.mean(stream * stream, axis=-1, keepdims=True) + epsilon)
    scaled = stream * inverse
    grad_scaled = grad * n.gains[which : which + 1, :]
    products = jnp.mean(grad_scaled * scaled, axis=-1, keepdims=True)
    gain_sum = gain_sum + jnp.sum(grad * scaled, axis=0, keepdims=True)
    return inverse * (grad_scaled - scaled * products), gain_sum


def feed_forward_back(number, gy, x1, saved, gate, up, down, gains, which, jobs_of):
    count, width = x1.shape
    units = gate.shape[1]
    rows = count // BLOCKS
    call = Call(number)
    for name, array in (
        ("gy", gy),
        ("x1", x1),
        ("h2", saved.h2),
        ("z", saved.z),
        ("u", saved.u),
        ("a", saved.a),
        ("gate", gate),
        ("up", up),
        ("down", down),
        ("gains", gains),
    ):
        call.take(name, array)
    call.give("gx1", (count, width), jnp.float32)
    call.give("gain", (1, width), jnp.float32)
    for name in ("d_gate", "d_up", "d_down"):
        call.give(name, (width, units), jnp.bfloat16)
    call.hold("low", (count, width), jnp.bfloat16)
    call.hold("gz", (count, units), jnp.bfloat16)
    call.hold("gu", (count, units), jnp.bfloat16)
    total = HeadSum(call, BLOCKS, rows, width)
    jobs = Jobs(jobs_of(call))

    def body(n):
        place = Place()
        place.enter(call.far)
        total.bind(n, place)
        jobs.bind(n, place)
        jobs.start()
        for i in range(BLOCKS):
            at = pl.ds(i * rows, rows)
            low = n.gy[at, :].astype(jnp.bfloat16)
            n.low[at, :] = low
            ga = dot_nn(low, n.down[...])
            z = n.z[at, :].astype(jnp.float32)
            u = n.u[at, :].astype(jnp.float32)
            sigma = lax.logistic(z)
            gz = (ga * u * sigma * (1.0 + z * (1.0 - sigma))).astype(jnp.bfloat16)
            gu = (ga * z * sigma).astype(jnp.bfloat16)
            n.gz[at, :] = gz
            n.gu[at, :] = gu
            total.send(i, dot_nt(gz, n.gate[...]) + dot_nt(gu, n.up[...]))
            if i:
                total.middle(i - 1)
            jobs.advance((i + 1) / (BLOCKS + 3))
        total.middle(BLOCKS - 1)
        cols = width // 4
        for left, right, out in ((n.low, n.a, n.d_down), (n.h2, n.gz, n.d_gate), (n.h2, n.gu, n.d_up)):
            for j in range(4):
                part = dot_tn(left[:, j * cols : (j + 1) * cols], right[...])
                out[j * cols : (j + 1) * cols, :] = part.astype(jnp.bfloat16)
            jobs.advance((BLOCKS + 1) / (BLOCKS + 3))
        for i in range(BLOCKS):
            total.last(i)
        gain_sum = jnp.zeros((1, width), jnp.float32)
        for i in range(BLOCKS):
            at = pl.ds(i * rows, rows)
            step, gain_sum = norm_back(n, total.total(i), n.x1[at, :], which, at, n.gx1, gain_sum)
            n.gx1[at, :] = n.gy[at, :].astype(jnp.float32) + step
        n.gain[...] = gain_sum
        jobs.finish()

    return call.run(body)


def attention_back(number, gx1, x, saved, extra, wa, gains, which, tables, jobs_of):
    count, width = x.shape
    hid = wa.shape[1] // 4
    heads = hid // HEAD_DIM
    rows = count // BLOCKS
    call = Call(number)
    for name, array in (
        ("gx1", gx1),
        ("x", x),
        ("h", saved.h),
        ("q", saved.q),
        ("k", saved.k),
        ("m", saved.m),
        ("o", saved.o),
        ("lse", saved.lse),
        ("wa", wa),
        ("gains", gains),
    ):
        call.take(name, array)
    for name, table in tables.items():
        call.take(name, table)
    if extra is not None:
        call.take("extra", extra)
        call.give("gx", (count, width), jnp.bfloat16)
    else:
        call.give("gx", (count, width), jnp.float32)
        call.give("passed", (count, hid), jnp.float32)
    call.give("gain", (1, width), jnp.float32)
    call.give("d_wa", (width, 4 * hid), jnp.bfloat16)
    call.hold("low", (count, width), jnp.bfloat16)
    call.hold("bias", (rows, count), jnp.float32)
    call.hold("go", (rows, hid), jnp.bfloat16)
    call.hold("gq", (rows, hid), jnp.float32)
    call.hold("gk", (count, hid), jnp.float32)
    call.hold("gm", (count, hid), jnp.float32)
    call.hold("g3", (count, 3 * hid), jnp.bfloat16)
    total = HeadSum(call, BLOCKS, rows, width)
    jobs = Jobs(jobs_of(call))

    def body(n):
        place = Place()
        place.enter(call.far)
        total.bind(n, place)
        jobs.bind(n, place)
        jobs.start()
        lane = lane_number(hid)
        n.gk[...] = jnp.zeros_like(n.gk)
        n.gm[...] = jnp.zeros_like(n.gm)
        order = list(range(BLOCKS))[::-1]
        for turn_index, i in enumerate(order):
            at = pl.ds(i * rows, rows)
            low = n.gx1[at, :].astype(jnp.bfloat16)
            n.low[at, :] = low
            n.go[...] = dot_nn(low, n.wa[:, 3 * hid :]).astype(jnp.bfloat16)
            keys = (i + 1) * rows
            write_bias(n, i, rows, keys)
            n.gq[...] = jnp.zeros_like(n.gq)

            def one_head(h, unused):
                mask = lane // HEAD_DIM == h
                zero = jnp.bfloat16(0)
                query = jnp.where(mask, n.q[at, :], zero)
                grad = jnp.where(mask, n.go[...], zero)
                both = grad.astype(jnp.float32) * n.o[at, :].astype(jnp.float32)
                delta = jnp.sum(both, axis=-1, keepdims=True)
                scores = dot_nt(query, n.k[:keys, :]) + n.bias[:, :keys]
                prob = jnp.exp(scores - n.lse[h, at, :])
                grad_prob = dot_nt(grad, n.m[:keys, :])
                grad_score = (prob * (grad_prob - delta)).astype(jnp.bfloat16)
                part = dot_nn(grad_score, n.k[:keys, :])
                n.gq[...] = jnp.where(mask, part, n.gq[...])
                n.gk[:keys, :] += dot_tn(grad_score, query)
                n.gm[:keys, :] += dot_tn(prob.astype(jnp.bfloat16), grad)
                return unused

            lax.fori_loop(0, heads, one_head, 0)
            cosine, sine = n.cosine[at, :], n.sine[at, :]
            gq = turn(n.gq[...] * HEAD_DIM**-0.5, cosine, sine, True)
            gk = turn(n.gk[at, :], cosine, sine, True)
            gm = n.gm[at, :]
            if extra is None:
                gm = 0.5 * gm
                n.passed[at, :] = gm
            else:
                gm = gm + n.extra[at, :]
            n.g3[at, :hid] = gq.astype(jnp.bfloat16)
            n.g3[at, hid : 2 * hid] = gk.astype(jnp.bfloat16)
            n.g3[at, 2 * hid :] = gm.astype(jnp.bfloat16)
            total.send(i, dot_nt(n.g3[at, :], n.wa[:, : 3 * hid]))
            if turn_index:
                total.middle(order[turn_index - 1])
            jobs.advance((turn_index + 1) / (BLOCKS + 2))
        total.middle(order[-1])
        cols = width // 4
        for j in range(4):
            cut = slice(j * cols, (j + 1) * cols)
            n.d_wa[cut, : 3 * hid] = dot_tn(n.h[:, cut], n.g3[...]).astype(jnp.bfloat16)
            n.d_wa[cut, 3 * hid :] = dot_tn(n.low[:, cut], n.o[...]).astype(jnp.bfloat16)
        jobs.advance((BLOCKS + 1) / (BLOCKS + 2))
        for i in order:
            total.last(i)
        gain_sum = jnp.zeros((1, width), jnp.float32)
        for i in order:
            at = pl.ds(i * rows, rows)
            stream = n.x[at, :].astype(jnp.float32)
            step, gain_sum = norm_back(n, total.total(i), stream, which, at, n.gx, gain_sum)
            n.gx[at, :] = (n.gx1[at, :] + step).astype(n.gx.dtype)
        n.gain[...] = gain_sum
        jobs.finish()

    return call.run(body)


def transfers(number, jobs_of):
    call = Call(number)
    jobs = Jobs(jobs_of(call))

    def body(n):
        place = Place()
        place.enter(call.far)
        jobs.bind(n, place)
        jobs.start()
        jobs.finish()

    return call.run(body)


def dealt_device(
    inputs,
    segment_ids,
    norm_attn_one,
    query_one,
    key_one,
    value_one,
    output_one,
    norm_ffn_one,
    gate_one,
    up_one,
    down_one,
    norm_attn_two,
    query_two,
    key_two,
    value_two,
    output_two,
    norm_ffn_two,
    gate_two,
    up_two,
    down_two,
    cotangent,
):
    parts, length, width = inputs.shape
    count = parts * length
    hid = query_one.shape[1]
    places = lax.axis_size("dp") * lax.axis_size("ctx")
    shard = width // places
    wa_one = jnp.concatenate([query_one, key_one, value_one, output_one.T], axis=1)
    wa_two = jnp.concatenate([query_two, key_two, value_two, output_two.T], axis=1)
    down_one, down_two = down_one.T, down_two.T
    gain_rows = jnp.stack([norm_attn_one, norm_ffn_one, norm_attn_two, norm_ffn_two])
    gain_rows = jnp.concatenate([gain_rows, gain_rows]).astype(jnp.float32)

    own = lax.dynamic_index_in_dim(segment_ids, lax.axis_index("ctx"), 0, True)
    half_width = HEAD_DIM // 2
    frequency = 10000.0 ** (-jnp.arange(half_width, dtype=jnp.float32) / half_width)
    angles = jnp.arange(count, dtype=jnp.float32)[:, None] * frequency[None, :]
    cosine, sine = jnp.cos(angles), jnp.sin(angles)
    heads = hid // HEAD_DIM
    tables = {
        "cosine": jnp.tile(cosine, (1, 2 * heads)),
        "sine": jnp.tile(jnp.concatenate([-sine, sine], axis=1), (1, heads)),
        "seg_row": own,
        "seg_col": own.reshape(count, 1),
    }

    def flat(blocks):
        return blocks.reshape(-1, blocks.shape[-1])

    def split(array):
        return array.reshape(places, shard, array.shape[-1])

    def deal(array):
        return array.reshape(parts, length, width)

    entry = transfers(
        0,
        lambda c: [
            Gather(c, "wa", wa_one, places),
            Deal(c, "tokens", inputs),
            Gather(c, "gains", gain_rows, places),
        ],
    )
    gains = jnp.transpose(entry.gains, (1, 0, 2)).reshape(-1, width)
    x = flat(entry.tokens)
    wa_one = flat(entry.wa)
    attn_one = attention_layer(
        1,
        x,
        None,
        wa_one,
        gains,
        0,
        tables,
        lambda c: [
            Gather(c, "gate", gate_one, places),
            Gather(c, "up", up_one, places),
            Gather(c, "down", down_one, places),
        ],
    )
    ffn_one_w = (flat(attn_one.gate), flat(attn_one.up), flat(attn_one.down))
    ffn_one = feed_forward_layer(
        2, attn_one.x1, *ffn_one_w, gains, 1, lambda c: [Gather(c, "wa", wa_two, places)]
    )
    wa_two = flat(ffn_one.wa)
    attn_two = attention_layer(
        3,
        ffn_one.y,
        attn_one.v,
        wa_two,
        gains,
        2,
        tables,
        lambda c: [
            Gather(c, "gate", gate_two, places),
            Gather(c, "up", up_two, places),
            Gather(c, "down", down_two, places),
        ],
    )
    ffn_two_w = (flat(attn_two.gate), flat(attn_two.up), flat(attn_two.down))
    ffn_two = feed_forward_layer(
        4,
        attn_two.x1,
        *ffn_two_w,
        gains,
        3,
        lambda c: [Deal(c, "cot", cotangent), Deal(c, "out_one", deal(ffn_one.y_low))],
    )
    back_ffn_two = feed_forward_back(
        5,
        flat(ffn_two.cot),
        attn_two.x1,
        ffn_two,
        *ffn_two_w,
        gains,
        3,
        lambda c: [Deal(c, "out_two", deal(ffn_two.y_low))],
    )
    back_attn_two = attention_back(
        6,
        back_ffn_two.gx1,
        ffn_one.y,
        attn_two,
        None,
        wa_two,
        gains,
        2,
        tables,
        lambda c: [
            Scatter(c, "gate", split(back_ffn_two.d_gate)),
            Scatter(c, "up", split(back_ffn_two.d_up)),
            Scatter(c, "down", split(back_ffn_two.d_down)),
        ],
    )
    back_ffn_one = feed_forward_back(
        7,
        back_attn_two.gx,
        attn_one.x1,
        ffn_one,
        *ffn_one_w,
        gains,
        1,
        lambda c: [Scatter(c, "wa", split(back_attn_two.d_wa))],
    )
    back_attn_one = attention_back(
        8,
        back_ffn_one.gx1,
        x,
        attn_one,
        back_attn_two.passed,
        wa_one,
        gains,
        0,
        tables,
        lambda c: [
            Scatter(c, "gate", split(back_ffn_one.d_gate)),
            Scatter(c, "up", split(back_ffn_one.d_up)),
            Scatter(c, "down", split(back_ffn_one.d_down)),
        ],
    )
    gain_grads = jnp.concatenate(
        [back_attn_one.gain, back_ffn_one.gain, back_attn_two.gain, back_ffn_two.gain]
    )
    gain_grads = jnp.concatenate([gain_grads, gain_grads])
    gain_grads = jnp.transpose(gain_grads.reshape(-1, places, shard), (1, 0, 2))
    leave = transfers(
        9,
        lambda c: [
            Scatter(c, "wa", split(back_attn_one.d_wa)),
            Scatter(c, "gains", gain_grads),
            Deal(c, "grad", deal(back_attn_one.gx)),
        ],
    )

    def attention_grads(packed):
        query, key, value, output = jnp.split(packed, 4, axis=1)
        return query, key, value, output.T

    one = attention_grads(leave.wa)
    two = attention_grads(back_ffn_one.wa)
    return (
        ffn_two.out_one,
        back_ffn_two.out_two,
        leave.grad.astype(jnp.float32),
        leave.gains[0],
        *one,
        leave.gains[1],
        back_attn_one.gate,
        back_attn_one.up,
        back_attn_one.down.T,
        leave.gains[2],
        *two,
        leave.gains[3],
        back_attn_two.gate,
        back_attn_two.up,
        back_attn_two.down.T,
    )


def solution(mesh):
    placed = (
        P("dp", "ctx", None),
        P("dp", None),
        P(("dp", "ctx")),
        P(("dp", "ctx"), "mp"),
        P(("dp", "ctx"), "mp"),
        P(("dp", "ctx"), "mp"),
        P("mp", ("dp", "ctx")),
        P(("dp", "ctx")),
        P(("dp", "ctx"), "mp"),
        P(("dp", "ctx"), "mp"),
        P("mp", ("dp", "ctx")),
        P(("dp", "ctx")),
        P(("dp", "ctx"), "mp"),
        P(("dp", "ctx"), "mp"),
        P(("dp", "ctx"), "mp"),
        P("mp", ("dp", "ctx")),
        P(("dp", "ctx")),
        P(("dp", "ctx"), "mp"),
        P(("dp", "ctx"), "mp"),
        P("mp", ("dp", "ctx")),
        P("dp", "ctx", None),
    )
    sizes = dict(mesh.shape)

    def per_device(*operands):
        fits = sizes["dp"] == 2 and sizes["mp"] == 4 and operands[0].shape[0] == sizes["ctx"]
        return (dealt_device if fits else on_device)(*operands)

    return jax.shard_map(
        per_device,
        mesh=mesh,
        in_specs=placed,
        out_specs=(
            P("dp", "ctx", None),
            P("dp", "ctx", None),
            P("dp", "ctx", None),
            P(("dp", "ctx")),
            P(("dp", "ctx"), "mp"),
            P(("dp", "ctx"), "mp"),
            P(("dp", "ctx"), "mp"),
            P("mp", ("dp", "ctx")),
            P(("dp", "ctx")),
            P(("dp", "ctx"), "mp"),
            P(("dp", "ctx"), "mp"),
            P("mp", ("dp", "ctx")),
            P(("dp", "ctx")),
            P(("dp", "ctx"), "mp"),
            P(("dp", "ctx"), "mp"),
            P(("dp", "ctx"), "mp"),
            P("mp", ("dp", "ctx")),
            P(("dp", "ctx")),
            P(("dp", "ctx"), "mp"),
            P(("dp", "ctx"), "mp"),
            P("mp", ("dp", "ctx")),
        ),
        check_vma=False,
    )
```

```python
import functools
import math
from types import SimpleNamespace

import jax
import jax.numpy as jnp
import numpy as np
from jax import lax
from jax.experimental import pallas as pl
from jax.experimental.pallas import tpu as pltpu
from jax.sharding import PartitionSpec as P

MESH = pl.DeviceIdType.MESH

HEAD_DIM = 64
DP, CTX, MP = "dp", "ctx", "mp"


epsilon = 1e-05
neg_large = -1e30


def project(left_operand, right_operand):
    return jnp.einsum(
        "sbd,de->sbe", left_operand, right_operand, preferred_element_type=jnp.float32
    )


def project_back(left_operand, right_operand):
    return jnp.einsum(
        "sbe,de->sbd", left_operand, right_operand, preferred_element_type=jnp.float32
    )


def weight_term(left_operand, right_operand):
    return jnp.einsum(
        "sbd,sbe->de", left_operand, right_operand, preferred_element_type=jnp.float32
    )


def head_sum_kernel(
    chunks, x_ref, o_ref, near, half_sum, far, send_a, recv_a, send_b, recv_b, send_c, recv_c
):
    dp, ctx, mp = (lax.axis_index(name) for name in (DP, CTX, MP))
    side = lax.rem(mp, 2)
    pair = (dp, ctx, mp + 1 - 2 * side)
    cross = (dp, ctx, lax.rem(mp + 2, 4))
    barrier = pltpu.get_barrier_semaphore()
    for peer in (pair, cross):
        pl.semaphore_signal(barrier, inc=1, device_id=peer, device_id_type=MESH)
    pl.semaphore_wait(barrier, 2)
    rows = x_ref.shape[0] // chunks
    half = rows // 2

    def copy(source, target, send, recv, i, peer):
        return pltpu.make_async_remote_copy(
            src_ref=source,
            dst_ref=target,
            send_sem=send.at[i],
            recv_sem=recv.at[i],
            device_id=peer,
            device_id_type=MESH,
        )

    def first(i):
        theirs = x_ref.at[pl.ds(i * rows + (1 - side) * half, half)]
        return copy(theirs, near.at[i], send_a, recv_a, i, pair)

    def second(i):
        return copy(half_sum.at[i], far.at[i], send_b, recv_b, i, cross)

    def third(i):
        mine = o_ref.at[pl.ds(i * rows + side * half, half)]
        return copy(mine, mine, send_c, recv_c, i, pair)

    for i in range(chunks):
        first(i).start()
    for i in range(chunks):
        first(i).wait()
        mine = x_ref[pl.ds(i * rows + side * half, half)].astype(jnp.float32)
        half_sum[i] = (mine + near[i].astype(jnp.float32)).astype(jnp.bfloat16)
        second(i).start()
    for i in range(chunks):
        second(i).wait()
        total = half_sum[i].astype(jnp.float32) + far[i].astype(jnp.float32)
        o_ref[pl.ds(i * rows + side * half, half)] = total.astype(jnp.bfloat16)
        third(i).start()
    for i in range(chunks):
        third(i).wait()


def head_sum(partial_sum, number):
    flat = partial_sum.astype(jnp.bfloat16).reshape(-1, partial_sum.shape[-1])
    count, width = flat.shape
    chunks = 4
    half = count // chunks // 2
    total = pl.pallas_call(
        functools.partial(head_sum_kernel, chunks),
        out_shape=jax.ShapeDtypeStruct((count, width), jnp.bfloat16),
        in_specs=[pl.BlockSpec(memory_space=pltpu.VMEM)],
        out_specs=pl.BlockSpec(memory_space=pltpu.VMEM),
        scratch_shapes=[pltpu.VMEM((chunks, half, width), jnp.bfloat16)] * 3
        + [pltpu.SemaphoreType.DMA((chunks,))] * 6,
        compiler_params=pltpu.CompilerParams(
            collective_id=0, has_side_effects=True, vmem_limit_bytes=32 << 20
        ),
    )(flat)
    return total.reshape(partial_sum.shape).astype(jnp.float32)


def head_total(partial_sum):
    return head_sum(partial_sum, 0)


def head_back(partial_sum):
    return head_sum(partial_sum, 0)


def rotary_tables(first_place, count_of_rows):
    half_width = HEAD_DIM // 2
    frequency = 10000.0 ** (-jnp.arange(half_width, dtype=jnp.float32) / half_width)
    places = (first_place + jnp.arange(count_of_rows, dtype=jnp.int32)).astype(jnp.float32)
    angles = places[:, None] * frequency[None, :]
    return (jnp.cos(angles)[None, :, None, :], jnp.sin(angles)[None, :, None, :])


def rotate(split_heads, cosine, sine_table):
    half_width = HEAD_DIM // 2
    first_half = split_heads[..., :half_width]
    second_half = split_heads[..., half_width:]
    return jnp.concatenate(
        [
            first_half * cosine - second_half * sine_table,
            first_half * sine_table + second_half * cosine,
        ],
        axis=-1,
    )


def rotate_back(split_heads, cosine, sine_table):
    half_width = HEAD_DIM // 2
    first_half = split_heads[..., :half_width]
    second_half = split_heads[..., half_width:]
    return jnp.concatenate(
        [
            first_half * cosine + second_half * sine_table,
            second_half * cosine - first_half * sine_table,
        ],
        axis=-1,
    )


def norm_forward(stream, gain_row):
    inverse = lax.rsqrt(jnp.mean(stream * stream, axis=-1, keepdims=True) + epsilon)
    normed = (stream * inverse * gain_row.astype(jnp.float32)).astype(jnp.bfloat16)
    return (normed, inverse)


def norm_backward(grad_normed, stream, inverse, gain_row):
    scaled = stream * inverse
    grad_scaled = grad_normed * gain_row.astype(jnp.float32)
    gain_grad = jnp.sum(grad_normed * scaled, axis=(0, 1))
    grad_stream = inverse * (
        grad_scaled - scaled * jnp.mean(grad_scaled * scaled, axis=-1, keepdims=True)
    )
    return (grad_stream, gain_grad)


def block_grads(
    query_block,
    grad_block,
    lse_block,
    delta_block,
    query_places,
    query_document_ids,
    key_block,
    value_block,
    key_places,
    key_segments,
):
    score_scale = HEAD_DIM ** (-0.5)
    scores = (
        jnp.einsum("sqhe,skhe->shqk", query_block, key_block, preferred_element_type=jnp.float32)
        * score_scale
    )
    visible = (
        (key_places[None, :] <= query_places[:, None])[None]
        & (key_segments[:, None, :] == query_document_ids[:, :, None])
    )[:, None]
    probabilities = jnp.where(visible, jnp.exp(scores - lse_block[..., None]), 0.0)
    grad_probs = jnp.einsum(
        "sqhe,skhe->shqk", grad_block, value_block, preferred_element_type=jnp.float32
    )
    grad_scores = (probabilities * (grad_probs - delta_block[..., None]) * score_scale).astype(
        jnp.bfloat16
    )
    query_grad = jnp.einsum(
        "shqk,skhe->sqhe", grad_scores, key_block, preferred_element_type=jnp.float32
    )
    key_grad = jnp.einsum(
        "shqk,sqhe->skhe", grad_scores, query_block, preferred_element_type=jnp.float32
    )
    value_grad = jnp.einsum(
        "shqk,sqhe->skhe",
        probabilities.astype(jnp.bfloat16),
        grad_block,
        preferred_element_type=jnp.float32,
    )
    return (query_grad, key_grad, value_grad)


def attend_forward(queries, key_rows, value_rows, segments, query_places):
    seq_count, count_of_rows, head_count, head_width = queries.shape
    score_scale = head_width ** (-0.5)
    query_document_ids = lax.dynamic_slice_in_dim(segments, query_places[0], count_of_rows, 1)
    last_query = query_places[count_of_rows - 1]
    initial = (
        jnp.full((seq_count, head_count, count_of_rows), neg_large, jnp.float32),
        jnp.zeros((seq_count, head_count, count_of_rows), jnp.float32),
        jnp.zeros((seq_count, count_of_rows, head_count, head_width), jnp.float32),
    )
    key_piece = lax.all_gather(key_rows, CTX, axis=1, tiled=True)
    value_piece = lax.all_gather(value_rows, CTX, axis=1, tiled=True)
    piece_rows = key_piece.shape[1]
    block_rows = math.gcd(piece_rows, 512)
    key_split = key_piece.reshape(seq_count, piece_rows, head_count, head_width)
    value_split = value_piece.reshape(seq_count, piece_rows, head_count, head_width)

    def absorb_visit(running, block_index):
        first_key = block_index * block_rows

        def absorb_compute(current):
            row_max, row_total, weighted = current
            key_block = lax.dynamic_slice_in_dim(key_split, first_key, block_rows, 1)
            value_block = lax.dynamic_slice_in_dim(value_split, first_key, block_rows, 1)
            key_places = first_key + jnp.arange(block_rows, dtype=jnp.int32)
            key_segments = lax.dynamic_slice_in_dim(segments, first_key, block_rows, 1)
            scores = (
                jnp.einsum(
                    "sqhe,skhe->shqk", queries, key_block, preferred_element_type=jnp.float32
                )
                * score_scale
            )
            visible = (
                (key_places[None, :] <= query_places[:, None])[None]
                & (key_segments[:, None, :] == query_document_ids[:, :, None])
            )[:, None]
            new_max = jnp.maximum(row_max, jnp.max(jnp.where(visible, scores, neg_large), axis=-1))
            exponent = jnp.where(visible, jnp.exp(scores - new_max[..., None]), 0.0)
            factor = jnp.exp(row_max - new_max)
            new_total = row_total * factor + jnp.sum(exponent, axis=-1)
            update = jnp.einsum(
                "shqk,skhe->sqhe",
                exponent.astype(jnp.bfloat16),
                value_block,
                preferred_element_type=jnp.float32,
            )
            new_weighted = weighted * jnp.transpose(factor, (0, 2, 1))[..., None] + update
            return (new_max, new_total, new_weighted)

        def absorb_keep(current):
            return current

        return (lax.cond(first_key <= last_query, absorb_compute, absorb_keep, running), None)

    result, unused = lax.scan(
        absorb_visit, initial, jnp.arange(piece_rows // block_rows, dtype=jnp.int32)
    )
    row_max, row_total, weighted = result
    attended = weighted / jnp.transpose(row_total, (0, 2, 1))[..., None]
    return (attended, row_max + jnp.log(row_total))


def attend_back_gather(
    queries, grad_attended, log_normalizer, row_delta, key_rows, value_rows, segments, query_places
):
    seq_count, count_of_rows, head_count, head_width = queries.shape
    query_document_ids = lax.dynamic_slice_in_dim(segments, query_places[0], count_of_rows, 1)
    last_query = query_places[count_of_rows - 1]
    all_keys, all_values = (
        lax.all_gather(key_rows, CTX, axis=1, tiled=True),
        lax.all_gather(value_rows, CTX, axis=1, tiled=True),
    )
    length = all_keys.shape[1]
    block_rows = math.gcd(length, 512)
    key_split = all_keys.reshape(seq_count, length, head_count, head_width)
    value_split = all_values.reshape(seq_count, length, head_count, head_width)
    initial = (
        jnp.zeros((seq_count, count_of_rows, head_count, head_width), jnp.float32),
        jnp.zeros((seq_count, length, head_count, head_width), jnp.float32),
        jnp.zeros((seq_count, length, head_count, head_width), jnp.float32),
    )

    def attend_visit(state_now, block_index):
        first_key = block_index * block_rows

        def attend_compute(current):
            query_acc, key_acc, value_acc = current
            key_block = lax.dynamic_slice_in_dim(key_split, first_key, block_rows, 1)
            value_block = lax.dynamic_slice_in_dim(value_split, first_key, block_rows, 1)
            key_places = first_key + jnp.arange(block_rows, dtype=jnp.int32)
            key_segments = lax.dynamic_slice_in_dim(segments, first_key, block_rows, 1)
            query_part, key_part, value_part = block_grads(
                queries,
                grad_attended,
                log_normalizer,
                row_delta,
                query_places,
                query_document_ids,
                key_block,
                value_block,
                key_places,
                key_segments,
            )
            key_acc = lax.dynamic_update_slice_in_dim(key_acc, key_part, first_key, 1)
            value_acc = lax.dynamic_update_slice_in_dim(value_acc, value_part, first_key, 1)
            return (query_acc + query_part, key_acc, value_acc)

        def attend_keep(current):
            return current

        return (lax.cond(first_key <= last_query, attend_compute, attend_keep, state_now), None)

    totals, unused = lax.scan(
        attend_visit, initial, jnp.arange(length // block_rows, dtype=jnp.int32)
    )
    query_grad, key_grad, value_grad = totals
    key_home, value_home = (
        lax.psum_scatter(
            key_grad.reshape(seq_count, length, -1).astype(jnp.bfloat16),
            CTX,
            scatter_dimension=1,
            tiled=True,
        ).astype(jnp.float32),
        lax.psum_scatter(
            value_grad.reshape(seq_count, length, -1).astype(jnp.bfloat16),
            CTX,
            scatter_dimension=1,
            tiled=True,
        ).astype(jnp.float32),
    )
    split_shape = (seq_count, count_of_rows, head_count, head_width)
    return (query_grad, key_home.reshape(split_shape), value_home.reshape(split_shape))


def forward_layer(stream, first_values, weights, segments, cosine, sine_table, query_places):
    norm_attn, w_query, w_key, w_value, w_output, norm_ffn, w_gate, w_up, w_down = weights
    seq_count, count_of_rows, model_width = stream.shape
    head_count = w_query.shape[1] // HEAD_DIM
    split_shape = (seq_count, count_of_rows, head_count, HEAD_DIM)
    normed, inverse_one = norm_forward(stream, norm_attn)
    queries = rotate(project(normed, w_query).reshape(split_shape), cosine, sine_table).astype(
        jnp.bfloat16
    )
    key_rows = (
        rotate(project(normed, w_key).reshape(split_shape), cosine, sine_table)
        .astype(jnp.bfloat16)
        .reshape(seq_count, count_of_rows, -1)
    )
    own_values = project(normed, w_value)
    if first_values is None:
        mixed = own_values.astype(jnp.bfloat16)
    else:
        mixed = (0.5 * own_values + 0.5 * first_values).astype(jnp.bfloat16)
    attended, log_normalizer = attend_forward(queries, key_rows, mixed, segments, query_places)
    attended_low = attended.reshape(seq_count, count_of_rows, -1).astype(jnp.bfloat16)
    hidden_one = stream + head_total(project(attended_low, w_output))
    normed_two, inverse_two = norm_forward(hidden_one, norm_ffn)
    gate_values = project(normed_two, w_gate)
    up_values = project(normed_two, w_up)
    activated = (jax.nn.silu(gate_values) * up_values).astype(jnp.bfloat16)
    result = hidden_one + head_total(project(activated, w_down))
    saved_state = (
        stream,
        inverse_one,
        normed,
        queries,
        key_rows,
        mixed,
        attended,
        log_normalizer,
        attended_low,
        hidden_one,
        inverse_two,
        normed_two,
        gate_values,
        up_values,
        activated,
    )
    return (result, saved_state, own_values)


def backward_layer(
    grad_out, value_extra, saved_state, weights, segments, cosine, sine_table, query_places, mixes
):
    (
        stream,
        inverse_one,
        normed,
        queries,
        key_rows,
        mixed,
        attended,
        log_normalizer,
        attended_low,
        hidden_one,
        inverse_two,
        normed_two,
        gate_values,
        up_values,
        activated,
    ) = saved_state
    norm_attn, w_query, w_key, w_value, w_output, norm_ffn, w_gate, w_up, w_down = weights
    seq_count, count_of_rows, head_count, head_width = queries.shape
    grad_branch = grad_out.astype(jnp.bfloat16)
    down_grad = weight_term(activated, grad_branch)
    grad_active = project_back(grad_branch, w_down)
    gate_sigmoid = jax.nn.sigmoid(gate_values)
    grad_gate = (
        grad_active * up_values * gate_sigmoid * (1.0 + gate_values * (1.0 - gate_sigmoid))
    ).astype(jnp.bfloat16)
    grad_up = (grad_active * gate_values * gate_sigmoid).astype(jnp.bfloat16)
    gate_grad = weight_term(normed_two, grad_gate)
    up_grad = weight_term(normed_two, grad_up)
    grad_normed_two = head_back(project_back(grad_gate, w_gate) + project_back(grad_up, w_up))
    grad_norm_two, ffn_gain_grad = norm_backward(grad_normed_two, hidden_one, inverse_two, norm_ffn)
    grad_hidden = grad_out + grad_norm_two
    grad_attn = grad_hidden.astype(jnp.bfloat16)
    output_grad = weight_term(attended_low, grad_attn)
    grad_attended = (
        project_back(grad_attn, w_output)
        .astype(jnp.bfloat16)
        .reshape(seq_count, count_of_rows, head_count, head_width)
    )
    row_delta = jnp.transpose(
        jnp.sum(grad_attended.astype(jnp.float32) * attended, axis=-1), (0, 2, 1)
    )
    query_rot, key_rot, value_mix = attend_back_gather(
        queries, grad_attended, log_normalizer, row_delta, key_rows, mixed, segments, query_places
    )
    query_low = (
        rotate_back(query_rot, cosine, sine_table)
        .astype(jnp.bfloat16)
        .reshape(seq_count, count_of_rows, -1)
    )
    key_low = (
        rotate_back(key_rot, cosine, sine_table)
        .astype(jnp.bfloat16)
        .reshape(seq_count, count_of_rows, -1)
    )
    value_mix = value_mix.reshape(seq_count, count_of_rows, -1)
    if mixes:
        value_low = (0.5 * value_mix).astype(jnp.bfloat16)
        passed_on = 0.5 * value_mix
    else:
        value_low = (value_mix + value_extra).astype(jnp.bfloat16)
        passed_on = value_extra
    query_grad = weight_term(normed, query_low)
    key_grad = weight_term(normed, key_low)
    value_grad = weight_term(normed, value_low)
    grad_normed = head_back(
        project_back(query_low, w_query)
        + project_back(key_low, w_key)
        + project_back(value_low, w_value)
    )
    grad_norm_one, attn_gain_grad = norm_backward(grad_normed, stream, inverse_one, norm_attn)
    grad_stream = grad_hidden + grad_norm_one
    grad_terms = (
        attn_gain_grad,
        query_grad,
        key_grad,
        value_grad,
        output_grad,
        ffn_gain_grad,
        gate_grad,
        up_grad,
        down_grad,
    )
    return (grad_stream, passed_on, grad_terms)


def on_device(
    inputs,
    segment_ids,
    norm_attn_one,
    query_one,
    key_one,
    value_one,
    output_one,
    norm_ffn_one,
    gate_one,
    up_one,
    down_one,
    norm_attn_two,
    query_two,
    key_two,
    value_two,
    output_two,
    norm_ffn_two,
    gate_two,
    up_two,
    down_two,
    cotangent,
):
    def gather_layer(gain_attn, query, key, value, output, gain_ffn, gate, up, down):
        both = (DP, CTX)
        packed = jnp.concatenate([query, key, value, output.T, gate, up, down.T], axis=1)
        whole = lax.all_gather(packed, both, axis=0, tiled=True)
        gains = lax.all_gather(jnp.stack([gain_attn, gain_ffn]), both, axis=1, tiled=True)
        cuts = []
        for part in (query, key, value, output.T, gate, up, down.T):
            cuts.append((cuts[-1] if cuts else 0) + part.shape[1])
        w_q, w_k, w_v, w_o, w_g, w_u, w_d = jnp.split(whole, cuts[:-1], axis=1)
        return (gains[0], w_q, w_k, w_v, w_o.T, gains[1], w_g, w_u, w_d.T)

    def scatter_layer(grads, outs):
        both = (DP, CTX)
        gain_attn, query, key, value, output, gain_ffn, gate, up, down = grads
        pieces = [query, key, value, output.T, gate, up, down.T]
        packed = jnp.concatenate([part.astype(jnp.bfloat16) for part in pieces], axis=1)
        mine = lax.psum_scatter(packed, both, scatter_dimension=0, tiled=True)
        gains = lax.psum_scatter(
            jnp.stack([gain_attn, gain_ffn]).astype(jnp.bfloat16),
            both,
            scatter_dimension=1,
            tiled=True,
        ).astype(jnp.float32)
        cuts = []
        for part in pieces:
            cuts.append((cuts[-1] if cuts else 0) + part.shape[1])
        g_q, g_k, g_v, g_o, g_g, g_u, g_d = (
            part.astype(jnp.float32) for part in jnp.split(mine, cuts[:-1], axis=1)
        )
        return (gains[0], g_q, g_k, g_v, g_o.T, gains[1], g_g, g_u, g_d.T)

    gathered = gather_layer(
        norm_attn_one,
        query_one,
        key_one,
        value_one,
        output_one,
        norm_ffn_one,
        gate_one,
        up_one,
        down_one,
    ) + gather_layer(
        norm_attn_two,
        query_two,
        key_two,
        value_two,
        output_two,
        norm_ffn_two,
        gate_two,
        up_two,
        down_two,
    )
    weights_one = gathered[:9]
    weights_two = gathered[9:]
    seq_count, count_of_rows, model_width = inputs.shape
    query_places = lax.axis_index(CTX) * count_of_rows + jnp.arange(
        count_of_rows, dtype=jnp.int32
    )
    cosine, sine_table = rotary_tables(query_places[0], count_of_rows)
    layer_one, saved_one, first_values = forward_layer(
        inputs.astype(jnp.float32), None, weights_one, segment_ids, cosine, sine_table, query_places
    )
    layer_two, saved_two, unused = forward_layer(
        layer_one, first_values, weights_two, segment_ids, cosine, sine_table, query_places
    )
    grad_middle, value_extra, grads_two = backward_layer(
        cotangent.astype(jnp.float32),
        None,
        saved_two,
        weights_two,
        segment_ids,
        cosine,
        sine_table,
        query_places,
        True,
    )
    grad_input, unused_extra, grads_one = backward_layer(
        grad_middle,
        value_extra,
        saved_one,
        weights_one,
        segment_ids,
        cosine,
        sine_table,
        query_places,
        False,
    )
    totals = scatter_layer(grads_one, None) + scatter_layer(grads_two, None)
    return (
        layer_one.astype(jnp.bfloat16),
        layer_two.astype(jnp.bfloat16),
        grad_input,
        totals[0],
        totals[1],
        totals[2],
        totals[3],
        totals[4],
        totals[5],
        totals[6],
        totals[7],
        totals[8],
        totals[9],
        totals[10],
        totals[11],
        totals[12],
        totals[13],
        totals[14],
        totals[15],
        totals[16],
        totals[17],
    )


class Raw:
    def __init__(self, call, kind, index):
        self.call, self.kind, self.index = call, kind, index

    @property
    def ref(self):
        return self.call.refs[self.kind][self.index]

    @property
    def at(self):
        return self.ref.at

    @property
    def result(self):
        return self.call.results[self.index]


def cut_rows(ref, blocks, i):
    if blocks == 1:
        return ref
    rows = ref.shape[-2] // blocks
    part = pl.ds(i * rows, rows)
    return ref.at[part] if len(ref.shape) == 2 else ref.at[:, part]


class Store:
    def __init__(self, call, held, shape, dtype, blocks):
        self.held, self.blocks = held, blocks
        self.out = call.give(shape, dtype)
        self.flag = call.flags(blocks)
        call.stores.append(self)

    def copy(self, i):
        return pltpu.make_async_copy(
            cut_rows(self.held.ref, self.blocks, i),
            cut_rows(self.out.ref, self.blocks, i),
            self.flag.at[i],
        )

    def put(self, i=None):
        for k in range(self.blocks) if i is None else (i,):
            self.copy(k).start()

    def finish(self):
        for i in range(self.blocks):
            self.copy(i).wait()

    @property
    def result(self):
        return self.out.result


class Held:
    def __init__(self, call, shape, dtype):
        self.call, self.shape, self.dtype = call, shape, dtype
        self.slot = call.scratch_slot(pltpu.VMEM(shape, dtype))
        self.source = self.out = None
        self.blocks, self.waited = 1, set()

    @property
    def ref(self):
        return self.call.refs[2][self.slot]

    @property
    def at(self):
        return self.ref.at

    def __getitem__(self, key):
        return self.ref[key]

    def __setitem__(self, key, value):
        self.ref[key] = value

    def load_copy(self, i):
        return pltpu.make_async_copy(
            cut_rows(self.source.ref, self.blocks, i),
            cut_rows(self.ref, self.blocks, i),
            self.flag.at[i],
        )

    def need(self, i=None):
        if self.source is None:
            return
        for k in range(self.blocks) if i is None or self.blocks == 1 else (i,):
            if k not in self.waited:
                self.waited.add(k)
                self.load_copy(k).wait()

    def put(self, i=None):
        self.out.put(i)

    @property
    def result(self):
        return self.out.result


class Call:
    def __init__(self, number):
        self.number = number
        self.operands, self.shapes, self.scratch = [], [], []
        self.loads, self.stores, self.jobs = [], [], []
        self.far = False

    def take(self, array):
        self.operands.append(array)
        return Raw(self, 0, len(self.operands) - 1)

    def give(self, shape, dtype):
        self.shapes.append(jax.ShapeDtypeStruct(shape, dtype))
        return Raw(self, 1, len(self.shapes) - 1)

    def scratch_slot(self, kind):
        self.scratch.append(kind)
        return len(self.scratch) - 1

    def flags(self, count):
        return Raw(self, 2, self.scratch_slot(pltpu.SemaphoreType.DMA((count,))))

    def hold(self, shape, dtype):
        return Held(self, shape, dtype)

    def load(self, array, blocks=1):
        held = Held(self, array.shape, array.dtype)
        self.load_into(held, self.take(array), blocks)
        self.loads.append(held)
        return held

    def load_into(self, held, source, blocks):
        held.source, held.blocks, held.flag = source, blocks, self.flags(blocks)

    def store(self, shape, dtype, blocks=1):
        held = Held(self, shape, dtype)
        held.out = Store(self, held, shape, dtype, blocks)
        return held

    def store_from(self, held, shape, dtype, blocks=1):
        return Store(self, held, shape, dtype, blocks)

    def start_loads(self, backward=False):
        for k in range(max([held.blocks for held in self.loads], default=0)):
            for held in self.loads:
                if k < held.blocks:
                    held.load_copy(held.blocks - 1 - k if backward else k).start()

    def run(self, body, remote_ops=True):
        ins, outs = len(self.operands), len(self.operands) + len(self.shapes)

        def kernel(*refs):
            self.refs = (refs[:ins], refs[ins:outs], refs[outs:])
            for held in self.loads:
                held.waited = set()
            body()
            for held in self.loads:
                held.need()
            for store in self.stores:
                store.finish()

        space = pl.BlockSpec(memory_space=pltpu.HBM)
        self.results = pl.pallas_call(
            kernel,
            out_shape=tuple(self.shapes),
            in_specs=[space] * ins,
            out_specs=(space,) * len(self.shapes),
            scratch_shapes=self.scratch,
            compiler_params=pltpu.CompilerParams(
                has_side_effects=remote_ops,
                vmem_limit_bytes=62 << 20,
                collective_id=self.number if remote_ops else None,
            ),
        )(*self.operands)
        self.refs = None


class Place:
    def __init__(self):
        self.dp, self.ctx, self.mp = (lax.axis_index(a) for a in (DP, CTX, MP))
        self.ctx_size = lax.axis_size(CTX)
        self.side = lax.rem(self.mp, 2)
        self.pair = (self.dp, self.ctx, self.mp + 1 - 2 * self.side)
        self.cross = (self.dp, self.ctx, lax.rem(self.mp + 2, 4))
        self.other = (1 - self.dp, self.ctx, self.mp)

    def ahead(self, step):
        return lax.rem(self.ctx + step, self.ctx_size)

    def behind(self, step):
        return lax.rem(self.ctx + self.ctx_size - step, self.ctx_size)

    def along(self, index):
        return (self.dp, index, self.mp)

    def peers(self, far):
        peers = [self.pair, self.cross]
        if far:
            peers.append(self.other)
            peers += [self.along(self.ahead(s)) for s in range(1, self.ctx_size)]
        return peers

    def greet(self, far):
        barrier = pltpu.get_barrier_semaphore()
        for peer in self.peers(far):
            pl.semaphore_signal(barrier, inc=1, device_id=peer, device_id_type=MESH)

    def enter(self, far):
        pl.semaphore_wait(pltpu.get_barrier_semaphore(), len(self.peers(far)))


def remote(source, target, send, recv, peer):
    return pltpu.make_async_remote_copy(
        src_ref=source,
        dst_ref=target,
        send_sem=send,
        recv_sem=recv,
        device_id=peer,
        device_id_type=MESH,
    )


class HeadSum:
    def __init__(self, call, blocks, rows, width):
        self.half = rows // 2
        self.part = call.hold((blocks, rows, width), jnp.bfloat16)
        self.near, self.far, self.rest = (
            call.hold((blocks, rows // 2, width), jnp.bfloat16) for _ in range(3)
        )
        self.sa, self.ra, self.sb, self.rb, self.sc, self.rc = (
            call.flags(blocks) for _ in range(6)
        )

    def bind(self, place):
        self.place = place

    def own(self):
        return pl.ds(pl.multiple_of(self.place.side * self.half, self.half), self.half)

    def theirs(self):
        start = (1 - self.place.side) * self.half
        return pl.ds(pl.multiple_of(start, self.half), self.half)

    def first(self, i):
        source = self.part.at[i, self.theirs()]
        return remote(source, self.near.at[i], self.sa.at[i], self.ra.at[i], self.place.pair)

    def second(self, i):
        return remote(
            self.near.at[i], self.far.at[i], self.sb.at[i], self.rb.at[i], self.place.cross
        )

    def third(self, i):
        return remote(
            self.far.at[i], self.rest.at[i], self.sc.at[i], self.rc.at[i], self.place.pair
        )

    def send(self, i, partial_rows):
        self.part[i] = partial_rows.astype(jnp.bfloat16)
        self.first(i).start()

    def middle(self, i):
        self.first(i).wait()
        mine = self.part[i, self.own()].astype(jnp.float32)
        self.near[i] = (mine + self.near[i].astype(jnp.float32)).astype(jnp.bfloat16)
        self.second(i).start()

    def last(self, i):
        self.second(i).wait()
        total = self.near[i].astype(jnp.float32) + self.far[i].astype(jnp.float32)
        self.far[i] = total.astype(jnp.bfloat16)
        self.third(i).start()

    def total(self, i):
        self.third(i).wait()
        self.part[i, self.own()] = self.far[i]
        self.part[i, self.theirs()] = self.rest[i]
        return self.part[i].astype(jnp.float32)


class Gather:
    def __init__(self, call, shard, places):
        self.parts = lax.axis_size(CTX)
        call.far = True
        self.shard = shard if isinstance(shard, Held) else call.load(shard)
        self.whole = call.give((places,) + shard.shape, shard.dtype)
        self.zs, self.zr, self.ys, self.yr = (call.flags(self.parts) for _ in range(4))
        self.l = call.flags(1)
        self.relayed = self.parts == 4
        self.order = (2, 1, 3) if self.relayed else tuple(range(self.parts - 1, 0, -1))
        self.steps = len(self.order)

    def bind(self, place):
        self.place = place

    def slot(self, dp, ctx):
        return self.whole.at[dp * self.parts + ctx]

    def local(self):
        p = self.place
        return pltpu.make_async_copy(self.shard.ref, self.slot(p.dp, p.ctx), self.l.at[0])

    def along(self, s):
        p = self.place
        target = self.slot(p.dp, p.ctx)
        return remote(self.shard.ref, target, self.zs.at[s], self.zr.at[s], p.along(p.ahead(s)))

    def direct(self, s, act):
        if self.relayed and s != 2:
            pl.when(self.place.ctx != (0 if s == 3 else 3))(lambda: act(self.along(s)))
        else:
            act(self.along(s))

    def relay(self, act):
        p = self.place
        block = self.slot(p.dp, p.behind(2))
        for middle, end, s in ((2, 3, 3), (1, 0, 1)):
            copy = remote(block, block, self.zs.at[0], self.zr.at[s], p.along(end))
            pl.when(p.ctx == middle)(lambda copy=copy: act(copy))

    def across(self, s):
        p = self.place
        block = self.slot(p.dp, p.behind(s))
        source = self.shard.ref if s == 0 else block
        return remote(source, block, self.ys.at[s], self.yr.at[s], p.other)

    def start(self):
        self.shard.need()
        for s in self.order:
            self.direct(s, lambda copy: copy.start())
        self.across(0).start()
        self.local().start()

    def step(self, k):
        s = self.order[k]
        p = self.place
        block = self.slot(p.dp, p.behind(s))
        remote(block, block, self.zs.at[s], self.zr.at[s], p.along(p.ctx)).wait_recv()
        if self.relayed and s == 2:
            self.relay(lambda copy: copy.start())
        self.across(s).start()

    def finish(self):
        p = self.place
        self.local().wait()
        for s in self.order:
            self.direct(s, lambda copy: copy.wait_send())
        if self.relayed:
            self.relay(lambda copy: copy.wait_send())
        for s in range(self.parts):
            self.across(s).wait_send()
            block = self.slot(1 - p.dp, p.behind(s))
            remote(block, block, self.ys.at[s], self.yr.at[s], p.other).wait_recv()

    @property
    def result(self):
        whole = self.whole.result
        return whole.reshape(-1, whole.shape[-1])


class Scatter:
    def __init__(self, call, blocks):
        self.parts = lax.axis_size(CTX)
        places, rows, width = blocks.shape
        self.dtype = blocks.dtype
        call.far = True
        self.late = isinstance(blocks, Held)
        self.blocks = blocks if self.late else call.take(blocks)
        self.out = call.store((rows, width), jnp.float32)
        if not self.late:
            self.mb = call.hold((self.parts, rows, width), blocks.dtype)
        self.yb = call.hold((self.parts, rows, width), blocks.dtype)
        self.zb = call.hold((self.parts - 1, rows, width), blocks.dtype)
        self.zs, self.zr, self.ys, self.yr = (call.flags(self.parts) for _ in range(4))
        self.l = call.flags(1)
        self.relayed = self.parts == 4
        self.order = (3, 1, 2, 0) if self.relayed else tuple(range(self.parts - 1, -1, -1))
        if self.relayed:
            self.rb = call.hold((rows, width), blocks.dtype)
        self.steps = self.parts

    def bind(self, place):
        self.place = place

    def local(self):
        mine = self.blocks.at[pl.ds(self.place.dp * self.parts, self.parts)]
        return pltpu.make_async_copy(mine, self.mb.ref, self.l.at[0])

    def across(self, s):
        p = self.place
        block = self.blocks.at[(1 - p.dp) * self.parts + p.ahead(s)]
        return remote(block, self.yb.at[s], self.ys.at[s], self.yr.at[s], p.other)

    def along(self, s, act):
        p = self.place
        target = self.zb.at[s - 1]
        copy = remote(self.yb.at[s], target, self.zs.at[s], self.zr.at[s], p.along(p.ahead(s)))
        if not self.relayed or s == 2:
            act(copy)
            return
        end, middle = (0, 1) if s == 3 else (3, 2)
        way = remote(self.yb.at[s], self.rb.ref, self.zs.at[s], self.zr.at[0], p.along(middle))
        pl.when(p.ctx != end)(lambda: act(copy))
        pl.when(p.ctx == end)(lambda: act(way))

    def start(self):
        for s in self.order:
            self.across(s).start()
        if not self.late:
            self.local().start()

    def step(self, k):
        p = self.place
        s = self.order[k]
        if k == 0 and not self.late:
            self.local().wait()
        self.across(s).wait()
        if self.late:
            mine = self.blocks[p.dp * self.parts + p.ahead(s)]
        else:
            mine = self.mb[p.ahead(s)]
        both = mine.astype(jnp.float32) + self.yb[s].astype(jnp.float32)
        if s == 0:
            self.out[...] = both
            return
        self.yb[s] = both.astype(self.dtype)
        if self.relayed and s == 2:

            def add_ends():
                way = remote(self.rb.ref, self.rb.ref, self.zs.at[0], self.zr.at[0], p.other)
                way.wait_recv()
                through = self.yb[s].astype(jnp.float32) + self.rb[...].astype(jnp.float32)
                self.yb[s] = through.astype(self.dtype)

            pl.when((p.ctx == 1) | (p.ctx == 2))(add_ends)
        self.along(s, lambda copy: copy.start())

    def finish(self):
        p = self.place

        def add(s):
            block = self.zb.at[s - 1]
            remote(block, block, self.zs.at[s], self.zr.at[s], p.other).wait_recv()
            self.out[...] += self.zb[s - 1].astype(jnp.float32)

        for s in self.order:
            if s == 0:
                continue
            self.along(s, lambda copy: copy.wait_send())
            if self.relayed and s != 2:
                pl.when(p.ctx != (3 if s == 3 else 0))(functools.partial(add, s))
            else:
                add(s)
        self.out.put()

    @property
    def result(self):
        return self.out.result


class Deal:
    def __init__(self, call, blocks, wide=False):
        self.parts, self.wide = lax.axis_size(CTX), wide
        self.share = blocks.shape[1] // (2 if wide else 4)
        call.far = True
        self.source = call.take(blocks)
        self.target = call.give(blocks.shape, blocks.dtype)
        self.held = call.hold(blocks.shape[1:], blocks.dtype)
        self.l = call.flags(2)
        self.zf, self.af, self.xf, self.bf = (
            tuple(call.flags(self.parts) for _ in range(2)) for _ in range(4)
        )
        self.steps = (self.parts - 1) * (1 if wide else 2)

    def bind(self, place):
        self.place = place
        self.own = place.side if self.wide else place.mp

    def rows(self, index):
        return pl.ds(pl.multiple_of(index * self.share, self.share), self.share)

    def local(self, k):
        p = self.place
        refs = (self.source.at[p.ctx], self.held.ref, self.target.at[p.ctx])
        return pltpu.make_async_copy(refs[k], refs[k + 1], self.l.at[k])

    def along(self, s):
        p = self.place
        rows = self.rows(self.own)
        return remote(
            self.source.at[p.ahead(s), rows],
            self.target.at[p.ctx, rows],
            self.zf[0].at[s],
            self.zf[1].at[s],
            p.along(p.ahead(s)),
        )

    def piece(self, s, index, flags, peer):
        ref = self.target.at[self.place.behind(s), self.rows(index)]
        return remote(ref, ref, flags[0].at[s], flags[1].at[s], peer)

    def start(self):
        for s in range(self.parts - 1, 0, -1):
            self.along(s).start()
        self.local(0).start()

    def step(self, k):
        p = self.place
        if k == 0:
            self.local(0).wait()
            self.local(1).start()
        if self.wide:
            s = self.parts - 1 - k
            self.piece(s, self.own, self.zf, p.along(p.ctx)).wait_recv()
            self.piece(s, self.own, self.af, p.pair).start()
            return
        s = self.parts - 1 - k // 2
        far = lax.rem(p.mp + 2, 4)
        if k % 2 == 0:
            self.piece(s, p.mp, self.zf, p.along(p.ctx)).wait_recv()
            self.piece(s, p.mp, self.xf, p.cross).start()
            self.piece(s, p.mp, self.af, p.pair).start()
        else:
            self.piece(s, far, self.xf, p.cross).wait_recv()
            self.piece(s, far, self.bf, p.pair).start()

    def finish(self):
        p = self.place
        self.local(1).wait()
        if self.wide:
            for s in range(1, self.parts):
                self.along(s).wait_send()
                self.piece(s, self.own, self.af, p.pair).wait_send()
                self.piece(s, 1 - self.own, self.af, p.pair).wait_recv()
            return
        far = lax.rem(p.mp + 2, 4)
        near = p.mp + 1 - 2 * p.side
        near_far = lax.rem(near + 2, 4)
        for s in range(1, self.parts):
            self.along(s).wait_send()
            self.piece(s, p.mp, self.xf, p.cross).wait_send()
            self.piece(s, p.mp, self.af, p.pair).wait_send()
            self.piece(s, far, self.bf, p.pair).wait_send()
            self.piece(s, near, self.af, p.pair).wait_recv()
            self.piece(s, near_far, self.bf, p.pair).wait_recv()

    @property
    def result(self):
        whole = self.target.result
        return whole.reshape(-1, whole.shape[-1])


LATE = "late"


class Jobs:
    def __init__(self, jobs, span=40.0, order=None):
        self.jobs = list(jobs)
        self.queue = [(job, k) for job in self.jobs for k in range(job.steps)]
        if order is not None:
            left = [list(range(job.steps)) for job in self.jobs]
            self.queue = [(self.jobs[j], left[j].pop(0)) for j in order]
        self.span, self.at = span, 0

    def start(self, place):
        self.at = 0
        for job in self.jobs:
            job.bind(place)
        for job in self.jobs:
            if not getattr(job, LATE, False):
                job.start()

    def advance(self, reached):
        stop = min(len(self.queue), int(len(self.queue) * reached / self.span))
        while self.at < stop:
            job, k = self.queue[self.at]
            job.step(k)
            self.at += 1

    def finish(self):
        self.advance(self.span)
        for job in self.jobs:
            job.finish()


def begin(call, total, jobs, backward=False):
    place = Place()
    if total is not None:
        total.bind(place)
    place.greet(call.far)
    call.start_loads(backward)
    place.enter(call.far)
    jobs.start(place)


def dot_nn(a, b):
    return lax.dot_general(a, b, (((1,), (0,)), ((), ())), preferred_element_type=jnp.float32)


def dot_nt(a, b):
    return lax.dot_general(a, b, (((1,), (1,)), ((), ())), preferred_element_type=jnp.float32)


def dot_tn(a, b):
    return lax.dot_general(a, b, (((0,), (0,)), ((), ())), preferred_element_type=jnp.float32)


def lane_number(width):
    return lax.broadcasted_iota(jnp.int32, (1, width), 1)


LANES = 128
BLOCKS = 4


def turn(values, cosine, signed_sine, back):
    half = HEAD_DIM // 2
    leading = lax.rem(lane_number(LANES), HEAD_DIM) < half
    pieces = []
    for at in range(0, values.shape[1], LANES):
        piece = values[:, at : at + LANES]
        swapped = jnp.where(leading, pltpu.roll(piece, LANES - half, 1), pltpu.roll(piece, half, 1))
        moved = swapped * signed_sine
        pieces.append(piece * cosine - moved if back else piece * cosine + moved)
    return jnp.concatenate(pieces, axis=1)


def write_bias(bias, seg_col, seg_row, i, rows, keys):
    query_at = i * rows + lax.broadcasted_iota(jnp.int32, (rows, 1), 0)
    key_at = lax.broadcasted_iota(jnp.int32, (1, keys), 1)
    same = seg_col[pl.ds(i * rows, rows), :1] == seg_row[:1, :keys]
    bias[:, :keys] = jnp.where(same & (key_at <= query_at), 0.0, neg_large)


class Opening:
    def __init__(self, call, inputs, segment_ids, layers, gain_rows, angle_row, places):
        self.call, self.places = call, places
        parts, length, width = inputs.shape
        self.count = count = parts * length
        (q1, k1, v1, o1, *tall1), (q2, k2, v2, o2, *tall2) = layers
        self.shard, self.hid = shard, hid = q1.shape
        units = tall1[0].shape[0]
        low = jnp.bfloat16
        self.first = [call.load(array) for array in (q1, k1, v1, o1)]
        self.gain_rows = call.load(gain_rows)
        self.ids, self.angle = call.load(segment_ids), call.load(angle_row)
        self.tall = [call.load(array) for array in tall1]
        self.second = [call.load(array) for array in (q2, k2, v2, o2)]
        self.tall += [call.load(array) for array in tall2]
        self.shards_one = [call.hold((shard, units), low) for _ in tall1]
        self.shards_two = [call.store((shard, units), low) for _ in tall2]
        self.wa_one = call.hold((shard, 4 * hid), low)
        self.wa_two = call.store((shard, 4 * hid), low)
        self.gains_wide = call.hold(gain_rows.shape, jnp.float32)
        self.cosine, self.sine, self.seg_col = (
            call.store((count, LANES), jnp.float32, BLOCKS) for _ in range(3)
        )
        self.seg_row = call.store((8, count), jnp.float32)
        self.gather = Gather(call, self.wa_one, places)
        self.deal = Deal(call, inputs)
        self.gather_gains = Gather(call, self.gains_wide, places)
        self.jobs = Jobs([self.gather_gains, self.deal, self.gather])
        self.x = call.hold((count, width), low)
        self.wa = call.hold((width, 4 * hid), low)
        self.gain_blocks = call.hold((places,) + gain_rows.shape, jnp.float32)
        self.gains = call.store((gain_rows.shape[0], width), jnp.float32)
        self.flag = call.flags(2 + 2 * parts)

    def tables(self):
        return (self.cosine, self.sine, self.seg_col, self.seg_row)

    def run(self, total, jobs):
        call, hid = self.call, self.hid
        place = Place()
        total.bind(place)
        place.greet(call.far)
        call.start_loads()
        for j, held in enumerate(self.first):
            held.need()
            values = held[...]
            self.wa_one[:, j * hid : (j + 1) * hid] = values.T if j == 3 else values
        self.gain_rows.need()
        self.gains_wide[...] = self.gain_rows[...].astype(jnp.float32)
        place.enter(call.far)
        self.jobs.start(place)
        for tall, shard in zip(self.tall, self.shards_one + self.shards_two):
            tall.need()
            shard[...] = tall[...].T
            if shard.out is not None:
                shard.put()
        for j, held in enumerate(self.second):
            held.need()
            values = held[...]
            self.wa_two[:, j * hid : (j + 1) * hid] = values.T if j == 3 else values
        self.wa_two.put()
        self.ids.need()
        self.angle.need()
        ids = self.ids[...].astype(jnp.float32)
        mine = lax.broadcasted_iota(jnp.int32, ids.shape, 0) == place.ctx
        own = jnp.sum(jnp.where(mine, ids, 0.0), axis=0, keepdims=True)
        self.seg_row[...] = jnp.broadcast_to(own, self.seg_row.shape)
        self.seg_row.put()
        self.seg_col[...] = jnp.broadcast_to(own, (LANES, self.count)).T
        self.seg_col.put()
        rows = self.count // BLOCKS
        for i in range(BLOCKS):
            at = pl.ds(i * rows, rows)
            index = i * rows + lax.broadcasted_iota(jnp.int32, (rows, 1), 0)
            angles = index.astype(jnp.float32) * self.angle[:1, :]
            self.cosine[at, :] = jnp.cos(angles)
            self.sine[at, :] = jnp.sin(angles) * self.angle[1:2, :]
        self.cosine.put()
        self.sine.put()
        self.jobs.advance(self.jobs.span)
        jobs.start(place)
        self.jobs.finish()
        shard = self.shard
        copies = [
            pltpu.make_async_copy(
                self.gather_gains.whole.ref, self.gain_blocks.ref, self.flag.at[0]
            )
        ]
        parts = self.deal.parts
        length = self.count // parts
        for k in range(parts):
            copies.append(
                pltpu.make_async_copy(
                    self.deal.target.at[k],
                    self.x.at[pl.ds(k * length, length)],
                    self.flag.at[1 + k],
                )
            )
        for k in range(self.places):
            copies.append(
                pltpu.make_async_copy(
                    self.gather.whole.at[k],
                    self.wa.at[pl.ds(k * shard, shard)],
                    self.flag.at[1 + parts],
                )
            )
        for copy in copies:
            copy.start()
        for copy in copies:
            copy.wait()
        for k in range(self.places):
            self.gains[:, k * shard : (k + 1) * shard] = self.gain_blocks[k]
        self.gains.put()


def attention_layer(number, x, first_v, wa, gains, which, tables, jobs_of, opening=None, span=40.0):
    call = Call(number)
    if opening is None:
        start = None
        x, gains, wa = call.load(x, BLOCKS), call.load(gains), call.load(wa)
        cosine, sine, seg_col = (call.load(table, BLOCKS) for table in tables[:3])
        seg_row = call.load(tables[3])
    else:
        start = opening(call)
        x, gains, wa = start.x, start.gains, start.wa
        cosine, sine, seg_col, seg_row = start.tables()
    count, width = x.shape
    hid = wa.shape[1] // 4
    heads = hid // HEAD_DIM
    rows = count // BLOCKS
    if first_v is not None:
        first_v = call.load(first_v, BLOCKS)
    else:
        v = call.store((count, hid), jnp.float32, BLOCKS)
    x1 = call.store((count, width), jnp.float32, BLOCKS)
    h = call.store((count, width), jnp.bfloat16, BLOCKS)
    q, k, m, o = (call.store((count, hid), jnp.bfloat16, BLOCKS) for _ in range(4))
    lse = call.store((heads, count, 1), jnp.float32, BLOCKS)
    bias = call.hold((rows, count), jnp.float32)
    acc = call.hold((rows, hid), jnp.float32)
    total = HeadSum(call, BLOCKS, rows, width)
    carried = jobs_of(call, start)
    jobs = Jobs(carried, span)

    def body():
        if start is None:
            begin(call, total, jobs)
        else:
            start.run(total, jobs)
        lane = lane_number(hid)
        for i in range(BLOCKS):
            at = pl.ds(i * rows, rows)
            x.need(i)
            gains.need()
            stream = x[at, :].astype(jnp.float32)
            inverse = lax.rsqrt(jnp.mean(stream * stream, axis=-1, keepdims=True) + epsilon)
            normed = (stream * inverse * gains[which : which + 1, :]).astype(jnp.bfloat16)
            h[at, :] = normed
            h.put(i)
            wa.need()
            projected = dot_nn(normed, wa[:, : 3 * hid])
            cosine.need(i)
            sine.need(i)
            cos, sin = cosine[at, :], sine[at, :]
            queries = turn(projected[:, :hid], cos, sin, False).astype(jnp.bfloat16)
            q[at, :] = queries * jnp.bfloat16(HEAD_DIM**-0.5)
            k[at, :] = turn(projected[:, hid : 2 * hid], cos, sin, False).astype(jnp.bfloat16)
            values = projected[:, 2 * hid :]
            if first_v is None:
                v[at, :] = values
                v.put(i)
            else:
                first_v.need(i)
                values = 0.5 * values + 0.5 * first_v[at, :]
            m[at, :] = values.astype(jnp.bfloat16)
            for held in (q, k, m):
                held.put(i)
            keys = (i + 1) * rows
            seg_col.need(i)
            seg_row.need()
            write_bias(bias, seg_col, seg_row, i, rows, keys)
            jobs.advance(5.0 * i + 3.0)

            def one_head(index, unused):
                mask = lane // HEAD_DIM == index
                query = jnp.where(mask, q[at, :], jnp.bfloat16(0))
                scores = dot_nt(query, k[:keys, :]) + bias[:, :keys]
                top = jnp.max(scores, axis=-1, keepdims=True)
                exponent = jnp.exp(scores - top)
                summed = jnp.sum(exponent, axis=-1, keepdims=True)
                weighted = dot_nn(exponent.astype(jnp.bfloat16), m[:keys, :])
                acc[...] = jnp.where(mask, weighted / summed, acc[...])
                lse[index, at, :] = top + jnp.log(summed)
                return unused

            lax.fori_loop(0, heads, one_head, 0)
            attended = acc[...].astype(jnp.bfloat16)
            o[at, :] = attended
            o.put(i)
            lse.put(i)
            total.send(i, dot_nt(attended, wa[:, 3 * hid :]))
            if i:
                total.middle(i - 1)
            jobs.advance(5.0 * i + 5.5)
        total.middle(BLOCKS - 1)
        for i in range(BLOCKS):
            total.last(i)
            jobs.advance(23.0 + 4.0 * i)
        for i in range(BLOCKS):
            at = pl.ds(i * rows, rows)
            x1[at, :] = x[at, :].astype(jnp.float32) + total.total(i)
            x1.put(i)
        jobs.finish()

    call.run(body)
    return SimpleNamespace(
        x1=x1.result,
        h=h.result,
        q=q.result,
        k=k.result,
        m=m.result,
        o=o.result,
        lse=lse.result,
        v=v.result if first_v is None else None,
        carried=[job.result for job in carried],
        start=start,
    )


def feed_forward_layer(number, x1, gate, up, down, gains, which, jobs_of, span=30.0):
    count, width = x1.shape
    units = gate.shape[1]
    rows = count // BLOCKS
    call = Call(number)
    x1 = call.load(x1, BLOCKS)
    gains, gate, up, down = (call.load(array) for array in (gains, gate, up, down))
    y = call.store_from(x1, (count, width), jnp.float32, BLOCKS)
    y_low, h2 = (call.store((count, width), jnp.bfloat16, BLOCKS) for _ in range(2))
    z, u, a = (call.store((count, units), jnp.bfloat16, BLOCKS) for _ in range(3))
    total = HeadSum(call, BLOCKS, rows, width)
    carried = jobs_of(call)
    jobs = Jobs(carried, span)

    def body():
        begin(call, total, jobs)
        for i in range(BLOCKS):
            at = pl.ds(i * rows, rows)
            x1.need(i)
            gains.need()
            stream = x1[at, :]
            inverse = lax.rsqrt(jnp.mean(stream * stream, axis=-1, keepdims=True) + epsilon)
            normed = (stream * inverse * gains[which : which + 1, :]).astype(jnp.bfloat16)
            h2[at, :] = normed
            gate.need()
            gated = dot_nn(normed, gate[...])
            up.need()
            raised = dot_nn(normed, up[...])
            active = (gated * lax.logistic(gated) * raised).astype(jnp.bfloat16)
            z[at, :] = gated.astype(jnp.bfloat16)
            u[at, :] = raised.astype(jnp.bfloat16)
            a[at, :] = active
            for held in (h2, z, u, a):
                held.put(i)
            down.need()
            total.send(i, dot_nt(active, down[...]))
            if i:
                total.middle(i - 1)
            jobs.advance(2.5 * i + 4.0)
        total.middle(BLOCKS - 1)
        for i in range(BLOCKS):
            total.last(i)
            jobs.advance(14.0 + 5.0 * i)
        for i in range(BLOCKS):
            at = pl.ds(i * rows, rows)
            result = x1[at, :] + total.total(i)
            x1[at, :] = result
            y_low[at, :] = result.astype(jnp.bfloat16)
            y.put(i)
            y_low.put(i)
        jobs.finish()

    call.run(body)
    return SimpleNamespace(
        y=y.result,
        y_low=y_low.result,
        h2=h2.result,
        z=z.result,
        u=u.result,
        a=a.result,
        carried=[job.result for job in carried],
    )


def norm_back(gain, grad, stream, gain_sum):
    inverse = lax.rsqrt(jnp.mean(stream * stream, axis=-1, keepdims=True) + epsilon)
    scaled = stream * inverse
    grad_scaled = grad * gain
    products = jnp.mean(grad_scaled * scaled, axis=-1, keepdims=True)
    gain_sum = gain_sum + jnp.sum(grad * scaled, axis=0, keepdims=True)
    return inverse * (grad_scaled - scaled * products), gain_sum


def feed_forward_back(number, gy, x1, saved, gate, up, down, gains, which, jobs_of, span=30.0):
    count, width = x1.shape
    units = gate.shape[1]
    rows = count // BLOCKS
    call = Call(number)
    gy = call.load(gy, BLOCKS)
    a, down = call.load(saved.a), call.load(down)
    z, u = call.load(saved.z, BLOCKS), call.load(saved.u, BLOCKS)
    gate, up, h2, gains = (call.load(w) for w in (gate, up, saved.h2, gains))
    x1 = call.load(x1, BLOCKS)
    gx1 = call.store_from(x1, (count, width), jnp.float32, BLOCKS)
    gain = call.store((1, width), jnp.float32)
    d_gate, d_up = (call.store((width, units), jnp.bfloat16, 4) for _ in range(2))
    places = lax.axis_size(DP) * lax.axis_size(CTX)
    shard = width // places
    d_down = call.hold((places, shard, units), jnp.bfloat16)
    low = call.hold((count, width), jnp.bfloat16)
    gz, gu = (call.hold((count, units), jnp.bfloat16) for _ in range(2))
    total = HeadSum(call, BLOCKS, rows, width)
    down_sum = Scatter(call, d_down)
    carried = jobs_of(call, down_sum)
    jobs = Jobs(carried, span)

    def body():
        begin(call, total, jobs)
        for i in range(BLOCKS):
            at = pl.ds(i * rows, rows)
            gy.need(i)
            low[at, :] = gy[at, :].astype(jnp.bfloat16)
        a.need()
        for j in range(places // 2):
            cut = slice(j * 2 * shard, (j + 1) * 2 * shard)
            part = dot_tn(low[:, cut], a[...]).astype(jnp.bfloat16)
            d_down[2 * j : 2 * j + 2] = part.reshape(2, shard, units)
        down_sum.start()
        for i in range(BLOCKS):
            at = pl.ds(i * rows, rows)
            down.need()
            ga = dot_nn(low[at, :], down[...])
            z.need(i)
            u.need(i)
            gated = z[at, :].astype(jnp.float32)
            sigma = lax.logistic(gated)
            raised = u[at, :].astype(jnp.float32)
            slope = sigma * (1.0 + gated * (1.0 - sigma))
            gz[at, :] = (ga * raised * slope).astype(jnp.bfloat16)
            gu[at, :] = (ga * gated * sigma).astype(jnp.bfloat16)
            gate.need()
            up.need()
            total.send(i, dot_nt(gz[at, :], gate[...]) + dot_nt(gu[at, :], up[...]))
            if i:
                total.middle(i - 1)
            jobs.advance(2.5 * i + 6.0)
        total.middle(BLOCKS - 1)
        cols = width // 4
        h2.need()
        for reached, left, right, out in ((17.0, h2, gz, d_gate), (20.0, h2, gu, d_up)):
            for j in range(4):
                cut = slice(j * cols, (j + 1) * cols)
                out[cut, :] = dot_tn(left[:, cut], right[...]).astype(jnp.bfloat16)
                out.put(j)
            jobs.advance(reached)
        gains.need()
        for i in range(BLOCKS):
            total.last(i)
            jobs.advance(22.0 + 4.0 * i)
        gain_sum = jnp.zeros((1, width), jnp.float32)
        for i in range(BLOCKS):
            at = pl.ds(i * rows, rows)
            x1.need(i)
            step, gain_sum = norm_back(
                gains[which : which + 1, :], total.total(i), x1[at, :], gain_sum
            )
            x1[at, :] = gy[at, :].astype(jnp.float32) + step
            gx1.put(i)
        gain[...] = gain_sum
        gain.put()
        jobs.finish()

    call.run(body)
    return SimpleNamespace(
        gx1=gx1.result,
        gain=gain.result,
        d_gate=d_gate.result,
        d_up=d_up.result,
        carried=[job.result for job in carried],
    )


def attention_back(number, gx1, x, saved, extra, wa, gains, which, tables, jobs_of, span=50.0):
    count, width = x.shape
    hid = wa.shape[1] // 4
    heads = hid // HEAD_DIM
    rows = count // BLOCKS
    call = Call(number)
    gx1, wa = call.load(gx1, BLOCKS), call.load(wa)
    q, k, m, o = (
        call.load(array, blocks)
        for array, blocks in ((saved.q, BLOCKS), (saved.k, 1), (saved.m, 1), (saved.o, BLOCKS))
    )
    lse = call.load(saved.lse, BLOCKS)
    cosine, sine, seg_col = (call.load(table, BLOCKS) for table in tables[:3])
    seg_row = call.load(tables[3])
    if extra is not None:
        extra = call.load(extra, BLOCKS)
    h, gains, x = call.load(saved.h), call.load(gains), call.load(x, BLOCKS)
    if extra is not None:
        gx = call.store((count, width), jnp.bfloat16, BLOCKS)
        gx_held = gx
    else:
        gx_held = gx1
        gx = call.store_from(gx1, (count, width), jnp.float32, BLOCKS)
        passed = call.store((count, hid), jnp.float32, BLOCKS)
    gain = call.store((1, width), jnp.float32)
    d_wa = call.store((width, 4 * hid), jnp.bfloat16, 4)
    low = call.hold((count, width), jnp.bfloat16)
    bias = call.hold((rows, count), jnp.float32)
    go = call.hold((rows, hid), jnp.bfloat16)
    gq = call.hold((rows, hid), jnp.float32)
    gk, gm = (call.hold((count, hid), jnp.float32) for _ in range(2))
    g3 = call.hold((count, 3 * hid), jnp.bfloat16)
    total = HeadSum(call, BLOCKS, rows, width)
    carried = jobs_of(call)
    jobs = Jobs(carried, span)

    def body():
        begin(call, total, jobs, True)
        lane = lane_number(hid)
        gk[...] = jnp.zeros(gk.shape, gk.dtype)
        gm[...] = jnp.zeros(gm.shape, gm.dtype)
        order = list(range(BLOCKS))[::-1]
        for turn_index, i in enumerate(order):
            at = pl.ds(i * rows, rows)
            gx1.need(i)
            low[at, :] = gx1[at, :].astype(jnp.bfloat16)
            wa.need()
            go[...] = dot_nn(low[at, :], wa[:, 3 * hid :]).astype(jnp.bfloat16)
            keys = (i + 1) * rows
            for held in (seg_row, seg_col, q, o, lse, k, m):
                held.need(i)
            write_bias(bias, seg_col, seg_row, i, rows, keys)
            gq[...] = jnp.zeros(gq.shape, gq.dtype)

            def one_head(index, unused):
                mask = lane // HEAD_DIM == index
                zero = jnp.bfloat16(0)
                query = jnp.where(mask, q[at, :], zero)
                grad = jnp.where(mask, go[...], zero)
                both = grad.astype(jnp.float32) * o[at, :].astype(jnp.float32)
                delta = jnp.sum(both, axis=-1, keepdims=True)
                scores = dot_nt(query, k[:keys, :]) + bias[:, :keys]
                prob = jnp.exp(scores - lse[index, at, :])
                grad_prob = dot_nt(grad, m[:keys, :])
                grad_score = (prob * (grad_prob - delta)).astype(jnp.bfloat16)
                part = dot_nn(grad_score, k[:keys, :])
                gq[...] = jnp.where(mask, part, gq[...])
                gk[:keys, :] += dot_tn(grad_score, query)
                gm[:keys, :] += dot_tn(prob.astype(jnp.bfloat16), grad)
                return unused

            lax.fori_loop(0, heads, one_head, 0)
            cosine.need(i)
            sine.need(i)
            cos, sin = cosine[at, :], sine[at, :]
            values = gm[at, :]
            if extra is None:
                values = 0.5 * values
                passed[at, :] = values
                passed.put(i)
            else:
                extra.need(i)
                values = values + extra[at, :]
            back = turn(gq[...] * HEAD_DIM**-0.5, cos, sin, True)
            g3[at, :hid] = back.astype(jnp.bfloat16)
            g3[at, hid : 2 * hid] = turn(gk[at, :], cos, sin, True).astype(jnp.bfloat16)
            g3[at, 2 * hid :] = values.astype(jnp.bfloat16)
            total.send(i, dot_nt(g3[at, :], wa[:, : 3 * hid]))
            if turn_index:
                total.middle(order[turn_index - 1])
            jobs.advance((8.0, 14.0, 18.0, 21.0)[turn_index])
        total.middle(order[-1])
        cols = width // 4
        h.need()
        for j in range(4):
            cut = slice(j * cols, (j + 1) * cols)
            d_wa[cut, : 3 * hid] = dot_tn(h[:, cut], g3[...]).astype(jnp.bfloat16)
            d_wa[cut, 3 * hid :] = dot_tn(low[:, cut], o[...]).astype(jnp.bfloat16)
            d_wa.put(j)
        jobs.advance(25.0)
        gains.need()
        for turn_index, i in enumerate(order):
            total.last(i)
            jobs.advance(28.0 + 4.0 * turn_index)
        gain_sum = jnp.zeros((1, width), jnp.float32)
        for i in order:
            at = pl.ds(i * rows, rows)
            x.need(i)
            stream = x[at, :].astype(jnp.float32)
            step, gain_sum = norm_back(
                gains[which : which + 1, :], total.total(i), stream, gain_sum
            )
            gx_held[at, :] = (gx1[at, :] + step).astype(gx_held.dtype)
            gx.put(i)
        gain[...] = gain_sum
        gain.put()
        jobs.finish()

    call.run(body)
    return SimpleNamespace(
        gx=gx.result,
        passed=passed.result if extra is None else None,
        gain=gain.result,
        d_wa=d_wa.result,
        carried=[job.result for job in carried],
    )


def transfers(number, jobs_of, order):
    call = Call(number)
    carried = jobs_of(call)
    jobs = Jobs(carried, order=order)

    def body():
        begin(call, None, jobs)
        jobs.finish()

    call.run(body)
    return [job.result for job in carried]


def leave_step(moved, grad, packs, turned, gains):
    call = Call(0)
    kept = [call.load(array, BLOCKS) for array in moved]
    kept_to = [call.store_from(held, held.shape, held.dtype, BLOCKS) for held in kept]
    grad = call.load(grad, BLOCKS)
    wide = call.store(grad.shape, jnp.float32, BLOCKS)
    shard, hid = packs[0].shape[0], packs[0].shape[1] // 4
    flag = call.flags(3 * len(packs))
    packs = [call.load(array) for array in packs]
    unpacked = [[call.give((shard, hid), pack.dtype) for _ in range(3)] for pack in packs]
    upright = [call.store((hid, shard), pack.dtype) for pack in packs]
    turned = [call.load(array) for array in turned]
    turned_to = [call.store(held.shape[::-1], held.dtype) for held in turned]
    gains = call.load(gains)
    gain_to = [call.store((1, shard), gains.dtype) for _ in range(4)]

    def body():
        call.start_loads()
        copies = []
        for at, pack in enumerate(packs):
            pack.need()
            for j in range(3):
                source = pack.at[:, j * hid : (j + 1) * hid]
                copies.append(
                    pltpu.make_async_copy(source, unpacked[at][j].ref, flag.at[3 * at + j])
                )
                copies[-1].start()
            upright[at][...] = pack[:, 3 * hid :].T
            upright[at].put()
        for held, target in zip(turned, turned_to):
            held.need()
            target[...] = held[...].T
            target.put()
        gains.need()
        for j, target in enumerate(gain_to):
            target[...] = gains[j : j + 1, :]
            target.put()
        rows = grad.shape[0] // BLOCKS
        for i in range(BLOCKS):
            at = pl.ds(i * rows, rows)
            grad.need(i)
            wide[at, :] = grad[at, :].astype(jnp.float32)
            wide.put(i)
            for held, target in zip(kept, kept_to):
                held.need(i)
                target.put(i)
        for copy in copies:
            copy.wait()

    call.run(body, False)
    return SimpleNamespace(
        kept=[target.result for target in kept_to],
        grad=wide.result,
        packs=[
            [part.result for part in parts] + [last.result]
            for parts, last in zip(unpacked, upright)
        ],
        turned=[target.result for target in turned_to],
        gains=[target.result.reshape(-1) for target in gain_to],
    )


def dealt_device(
    inputs,
    segment_ids,
    norm_attn_one,
    query_one,
    key_one,
    value_one,
    output_one,
    norm_ffn_one,
    gate_one,
    up_one,
    down_one,
    norm_attn_two,
    query_two,
    key_two,
    value_two,
    output_two,
    norm_ffn_two,
    gate_two,
    up_two,
    down_two,
    cotangent,
):
    parts, length, width = inputs.shape
    places = lax.axis_size(DP) * lax.axis_size(CTX)
    shard = width // places
    gain_rows = jnp.stack([norm_attn_one, norm_ffn_one, norm_attn_two, norm_ffn_two] * 2)
    half = HEAD_DIM // 2
    frequency = 10000.0 ** (-np.arange(half, dtype=np.float32) / np.float32(half))
    repeat = LANES // HEAD_DIM
    signs = np.concatenate([-np.ones(half), np.ones(half)])
    angle_row = np.zeros((8, LANES), np.float32)
    angle_row[0] = np.tile(frequency, 2 * repeat)
    angle_row[1] = np.tile(signs, repeat)

    def split(array):
        return array.reshape(places, shard, array.shape[-1])

    def deal(array):
        return array.reshape(parts, length, width)

    def opening(call):
        return Opening(
            call,
            inputs,
            segment_ids,
            (
                (query_one, key_one, value_one, output_one, gate_one.T, up_one.T, down_one),
                (query_two, key_two, value_two, output_two, gate_two.T, up_two.T, down_two),
            ),
            gain_rows,
            jnp.asarray(angle_row),
            places,
        )

    attn_one = attention_layer(
        1,
        None,
        None,
        None,
        None,
        0,
        None,
        lambda c, start: [Gather(c, held, places) for held in start.shards_one],
        opening,
        26.0,
    )
    start = attn_one.start
    x, wa_one, gains = start.deal.result, start.gather.result, start.gains.result
    tables = [table.result for table in start.tables()]
    ffn_one_w = attn_one.carried
    wa_two_shard = start.wa_two.result
    shards_two = [held.result for held in start.shards_two]
    ffn_one = feed_forward_layer(
        2,
        attn_one.x1,
        *ffn_one_w,
        gains,
        1,
        lambda c: [Gather(c, wa_two_shard, places), Gather(c, shards_two[0], places)],
        30.0,
    )
    wa_two, gate_two_w = ffn_one.carried
    attn_two = attention_layer(
        3,
        ffn_one.y,
        attn_one.v,
        wa_two,
        gains,
        2,
        tables,
        lambda c, start: [Gather(c, array, places) for array in shards_two[1:]],
        span=26.0,
    )
    ffn_two_w = (gate_two_w, *attn_two.carried)
    ffn_two = feed_forward_layer(
        4,
        attn_two.x1,
        *ffn_two_w,
        gains,
        3,
        lambda c: [Deal(c, cotangent, True), Deal(c, deal(ffn_one.y_low))],
        90.0,
    )
    out_one = ffn_two.carried[1]
    back_ffn_two = feed_forward_back(
        5,
        ffn_two.carried[0],
        attn_two.x1,
        ffn_two,
        *ffn_two_w,
        gains,
        3,
        lambda c, down_sum: [down_sum, Deal(c, deal(ffn_two.y_low), True)],
        36.0,
    )
    down_g2, out_two = back_ffn_two.carried

    def ffn_grads(back):
        return lambda c: [Scatter(c, split(array)) for array in (back.d_gate, back.d_up)]

    back_attn_two = attention_back(
        6,
        back_ffn_two.gx1,
        ffn_one.y,
        attn_two,
        None,
        wa_two,
        gains,
        2,
        tables,
        ffn_grads(back_ffn_two),
    )
    back_ffn_one = feed_forward_back(
        7,
        back_attn_two.gx,
        attn_one.x1,
        ffn_one,
        *ffn_one_w,
        gains,
        1,
        lambda c, down_sum: [Scatter(c, split(back_attn_two.d_wa)), down_sum],
        40.0,
    )
    packed_two, down_g1 = back_ffn_one.carried
    back_attn_one = attention_back(
        8,
        back_ffn_one.gx1,
        x,
        attn_one,
        back_attn_two.passed,
        wa_one,
        gains,
        0,
        tables,
        ffn_grads(back_ffn_one),
    )
    gain_grads = jnp.concatenate(
        [back_attn_one.gain, back_ffn_one.gain, back_attn_two.gain, back_ffn_two.gain] * 2
    )
    gain_grads = jnp.transpose(gain_grads.reshape(-1, places, shard), (1, 0, 2))
    gain_shards, packed_one, grad = transfers(
        9,
        lambda c: [
            Scatter(c, gain_grads),
            Scatter(c, split(back_attn_one.d_wa)),
            Deal(c, deal(back_attn_one.gx)),
        ],
        (1, 0, 2, 0, 1, 0, 2, 2, 0, 1, 2, 2, 2, 1),
    )
    final = leave_step(
        (out_one, out_two),
        grad,
        (packed_one, packed_two),
        back_attn_one.carried + [down_g1] + back_attn_two.carried + [down_g2],
        gain_shards,
    )
    gate_g1, up_g1, down_g1, gate_g2, up_g2, down_g2 = final.turned
    return (
        deal(final.kept[0]),
        deal(final.kept[1]),
        deal(final.grad),
        final.gains[0],
        *final.packs[0],
        final.gains[1],
        gate_g1.T,
        up_g1.T,
        down_g1,
        final.gains[2],
        *final.packs[1],
        final.gains[3],
        gate_g2.T,
        up_g2.T,
        down_g2,
    )


def solution(mesh):
    placed = (
        P(DP, CTX, None),
        P(DP, None),
        P((DP, CTX)),
        P((DP, CTX), MP),
        P((DP, CTX), MP),
        P((DP, CTX), MP),
        P(MP, (DP, CTX)),
        P((DP, CTX)),
        P((DP, CTX), MP),
        P((DP, CTX), MP),
        P(MP, (DP, CTX)),
        P((DP, CTX)),
        P((DP, CTX), MP),
        P((DP, CTX), MP),
        P((DP, CTX), MP),
        P(MP, (DP, CTX)),
        P((DP, CTX)),
        P((DP, CTX), MP),
        P((DP, CTX), MP),
        P(MP, (DP, CTX)),
        P(DP, CTX, None),
    )
    sizes = dict(mesh.shape)

    def per_device(*operands):
        fits = sizes[DP] == 2 and sizes[MP] == 4 and operands[0].shape[0] == sizes[CTX]
        return (dealt_device if fits else on_device)(*operands)

    return jax.shard_map(
        per_device,
        mesh=mesh,
        in_specs=placed,
        out_specs=(
            P(DP, CTX, None),
            P(DP, CTX, None),
            P(DP, CTX, None),
            P((DP, CTX)),
            P((DP, CTX), MP),
            P((DP, CTX), MP),
            P((DP, CTX), MP),
            P(MP, (DP, CTX)),
            P((DP, CTX)),
            P((DP, CTX), MP),
            P((DP, CTX), MP),
            P(MP, (DP, CTX)),
            P((DP, CTX)),
            P((DP, CTX), MP),
            P((DP, CTX), MP),
            P((DP, CTX), MP),
            P(MP, (DP, CTX)),
            P((DP, CTX)),
            P((DP, CTX), MP),
            P((DP, CTX), MP),
            P(MP, (DP, CTX)),
        ),
        check_vma=False,
    )
```

```python
import functools
import math
from types import SimpleNamespace

import jax
import jax.numpy as jnp
import numpy as np
from jax import lax
from jax.experimental import pallas as pl
from jax.experimental.pallas import tpu as pltpu
from jax.sharding import PartitionSpec as P

MESH = pl.DeviceIdType.MESH

HEAD_DIM = 64
DP, CTX, MP = "dp", "ctx", "mp"


epsilon = 1e-05
neg_large = -1e30


def project(left_operand, right_operand):
    return jnp.einsum(
        "sbd,de->sbe", left_operand, right_operand, preferred_element_type=jnp.float32
    )


def project_back(left_operand, right_operand):
    return jnp.einsum(
        "sbe,de->sbd", left_operand, right_operand, preferred_element_type=jnp.float32
    )


def weight_term(left_operand, right_operand):
    return jnp.einsum(
        "sbd,sbe->de", left_operand, right_operand, preferred_element_type=jnp.float32
    )


def head_sum_kernel(
    chunks, x_ref, o_ref, near, half_sum, far, send_a, recv_a, send_b, recv_b, send_c, recv_c
):
    dp, ctx, mp = (lax.axis_index(name) for name in (DP, CTX, MP))
    side = lax.rem(mp, 2)
    pair = (dp, ctx, mp + 1 - 2 * side)
    cross = (dp, ctx, lax.rem(mp + 2, 4))
    barrier = pltpu.get_barrier_semaphore()
    for peer in (pair, cross):
        pl.semaphore_signal(barrier, inc=1, device_id=peer, device_id_type=MESH)
    pl.semaphore_wait(barrier, 2)
    rows = x_ref.shape[0] // chunks
    half = rows // 2

    def copy(source, target, send, recv, i, peer):
        return pltpu.make_async_remote_copy(
            src_ref=source,
            dst_ref=target,
            send_sem=send.at[i],
            recv_sem=recv.at[i],
            device_id=peer,
            device_id_type=MESH,
        )

    def first(i):
        theirs = x_ref.at[pl.ds(i * rows + (1 - side) * half, half)]
        return copy(theirs, near.at[i], send_a, recv_a, i, pair)

    def second(i):
        return copy(half_sum.at[i], far.at[i], send_b, recv_b, i, cross)

    def third(i):
        mine = o_ref.at[pl.ds(i * rows + side * half, half)]
        return copy(mine, mine, send_c, recv_c, i, pair)

    for i in range(chunks):
        first(i).start()
    for i in range(chunks):
        first(i).wait()
        mine = x_ref[pl.ds(i * rows + side * half, half)].astype(jnp.float32)
        half_sum[i] = (mine + near[i].astype(jnp.float32)).astype(jnp.bfloat16)
        second(i).start()
    for i in range(chunks):
        second(i).wait()
        total = half_sum[i].astype(jnp.float32) + far[i].astype(jnp.float32)
        o_ref[pl.ds(i * rows + side * half, half)] = total.astype(jnp.bfloat16)
        third(i).start()
    for i in range(chunks):
        third(i).wait()


def head_sum(partial_sum, number):
    flat = partial_sum.astype(jnp.bfloat16).reshape(-1, partial_sum.shape[-1])
    count, width = flat.shape
    chunks = 4
    half = count // chunks // 2
    total = pl.pallas_call(
        functools.partial(head_sum_kernel, chunks),
        out_shape=jax.ShapeDtypeStruct((count, width), jnp.bfloat16),
        in_specs=[pl.BlockSpec(memory_space=pltpu.VMEM)],
        out_specs=pl.BlockSpec(memory_space=pltpu.VMEM),
        scratch_shapes=[pltpu.VMEM((chunks, half, width), jnp.bfloat16)] * 3
        + [pltpu.SemaphoreType.DMA((chunks,))] * 6,
        compiler_params=pltpu.CompilerParams(
            collective_id=0, has_side_effects=True, vmem_limit_bytes=32 << 20
        ),
    )(flat)
    return total.reshape(partial_sum.shape).astype(jnp.float32)


def head_total(partial_sum):
    return head_sum(partial_sum, 0)


def head_back(partial_sum):
    return head_sum(partial_sum, 0)


def rotary_tables(first_place, count_of_rows):
    half_width = HEAD_DIM // 2
    frequency = 10000.0 ** (-jnp.arange(half_width, dtype=jnp.float32) / half_width)
    places = (first_place + jnp.arange(count_of_rows, dtype=jnp.int32)).astype(jnp.float32)
    angles = places[:, None] * frequency[None, :]
    return (jnp.cos(angles)[None, :, None, :], jnp.sin(angles)[None, :, None, :])


def rotate(split_heads, cosine, sine_table):
    half_width = HEAD_DIM // 2
    first_half = split_heads[..., :half_width]
    second_half = split_heads[..., half_width:]
    return jnp.concatenate(
        [
            first_half * cosine - second_half * sine_table,
            first_half * sine_table + second_half * cosine,
        ],
        axis=-1,
    )


def rotate_back(split_heads, cosine, sine_table):
    half_width = HEAD_DIM // 2
    first_half = split_heads[..., :half_width]
    second_half = split_heads[..., half_width:]
    return jnp.concatenate(
        [
            first_half * cosine + second_half * sine_table,
            second_half * cosine - first_half * sine_table,
        ],
        axis=-1,
    )


def norm_forward(stream, gain_row):
    inverse = lax.rsqrt(jnp.mean(stream * stream, axis=-1, keepdims=True) + epsilon)
    normed = (stream * inverse * gain_row.astype(jnp.float32)).astype(jnp.bfloat16)
    return (normed, inverse)


def norm_backward(grad_normed, stream, inverse, gain_row):
    scaled = stream * inverse
    grad_scaled = grad_normed * gain_row.astype(jnp.float32)
    gain_grad = jnp.sum(grad_normed * scaled, axis=(0, 1))
    grad_stream = inverse * (
        grad_scaled - scaled * jnp.mean(grad_scaled * scaled, axis=-1, keepdims=True)
    )
    return (grad_stream, gain_grad)


def block_grads(
    query_block,
    grad_block,
    lse_block,
    delta_block,
    query_places,
    query_document_ids,
    key_block,
    value_block,
    key_places,
    key_segments,
):
    score_scale = HEAD_DIM ** (-0.5)
    scores = (
        jnp.einsum("sqhe,skhe->shqk", query_block, key_block, preferred_element_type=jnp.float32)
        * score_scale
    )
    visible = (
        (key_places[None, :] <= query_places[:, None])[None]
        & (key_segments[:, None, :] == query_document_ids[:, :, None])
    )[:, None]
    probabilities = jnp.where(visible, jnp.exp(scores - lse_block[..., None]), 0.0)
    grad_probs = jnp.einsum(
        "sqhe,skhe->shqk", grad_block, value_block, preferred_element_type=jnp.float32
    )
    grad_scores = (probabilities * (grad_probs - delta_block[..., None]) * score_scale).astype(
        jnp.bfloat16
    )
    query_grad = jnp.einsum(
        "shqk,skhe->sqhe", grad_scores, key_block, preferred_element_type=jnp.float32
    )
    key_grad = jnp.einsum(
        "shqk,sqhe->skhe", grad_scores, query_block, preferred_element_type=jnp.float32
    )
    value_grad = jnp.einsum(
        "shqk,sqhe->skhe",
        probabilities.astype(jnp.bfloat16),
        grad_block,
        preferred_element_type=jnp.float32,
    )
    return (query_grad, key_grad, value_grad)


def attend_forward(queries, key_rows, value_rows, segments, query_places):
    seq_count, count_of_rows, head_count, head_width = queries.shape
    score_scale = head_width ** (-0.5)
    query_document_ids = lax.dynamic_slice_in_dim(segments, query_places[0], count_of_rows, 1)
    last_query = query_places[count_of_rows - 1]
    initial = (
        jnp.full((seq_count, head_count, count_of_rows), neg_large, jnp.float32),
        jnp.zeros((seq_count, head_count, count_of_rows), jnp.float32),
        jnp.zeros((seq_count, count_of_rows, head_count, head_width), jnp.float32),
    )
    key_piece = lax.all_gather(key_rows, CTX, axis=1, tiled=True)
    value_piece = lax.all_gather(value_rows, CTX, axis=1, tiled=True)
    piece_rows = key_piece.shape[1]
    block_rows = math.gcd(piece_rows, 512)
    key_split = key_piece.reshape(seq_count, piece_rows, head_count, head_width)
    value_split = value_piece.reshape(seq_count, piece_rows, head_count, head_width)

    def absorb_visit(running, block_index):
        first_key = block_index * block_rows

        def absorb_compute(current):
            row_max, row_total, weighted = current
            key_block = lax.dynamic_slice_in_dim(key_split, first_key, block_rows, 1)
            value_block = lax.dynamic_slice_in_dim(value_split, first_key, block_rows, 1)
            key_places = first_key + jnp.arange(block_rows, dtype=jnp.int32)
            key_segments = lax.dynamic_slice_in_dim(segments, first_key, block_rows, 1)
            scores = (
                jnp.einsum(
                    "sqhe,skhe->shqk", queries, key_block, preferred_element_type=jnp.float32
                )
                * score_scale
            )
            visible = (
                (key_places[None, :] <= query_places[:, None])[None]
                & (key_segments[:, None, :] == query_document_ids[:, :, None])
            )[:, None]
            new_max = jnp.maximum(row_max, jnp.max(jnp.where(visible, scores, neg_large), axis=-1))
            exponent = jnp.where(visible, jnp.exp(scores - new_max[..., None]), 0.0)
            factor = jnp.exp(row_max - new_max)
            new_total = row_total * factor + jnp.sum(exponent, axis=-1)
            update = jnp.einsum(
                "shqk,skhe->sqhe",
                exponent.astype(jnp.bfloat16),
                value_block,
                preferred_element_type=jnp.float32,
            )
            new_weighted = weighted * jnp.transpose(factor, (0, 2, 1))[..., None] + update
            return (new_max, new_total, new_weighted)

        def absorb_keep(current):
            return current

        return (lax.cond(first_key <= last_query, absorb_compute, absorb_keep, running), None)

    result, unused = lax.scan(
        absorb_visit, initial, jnp.arange(piece_rows // block_rows, dtype=jnp.int32)
    )
    row_max, row_total, weighted = result
    attended = weighted / jnp.transpose(row_total, (0, 2, 1))[..., None]
    return (attended, row_max + jnp.log(row_total))


def attend_back_gather(
    queries, grad_attended, log_normalizer, row_delta, key_rows, value_rows, segments, query_places
):
    seq_count, count_of_rows, head_count, head_width = queries.shape
    query_document_ids = lax.dynamic_slice_in_dim(segments, query_places[0], count_of_rows, 1)
    last_query = query_places[count_of_rows - 1]
    all_keys, all_values = (
        lax.all_gather(key_rows, CTX, axis=1, tiled=True),
        lax.all_gather(value_rows, CTX, axis=1, tiled=True),
    )
    length = all_keys.shape[1]
    block_rows = math.gcd(length, 512)
    key_split = all_keys.reshape(seq_count, length, head_count, head_width)
    value_split = all_values.reshape(seq_count, length, head_count, head_width)
    initial = (
        jnp.zeros((seq_count, count_of_rows, head_count, head_width), jnp.float32),
        jnp.zeros((seq_count, length, head_count, head_width), jnp.float32),
        jnp.zeros((seq_count, length, head_count, head_width), jnp.float32),
    )

    def attend_visit(state_now, block_index):
        first_key = block_index * block_rows

        def attend_compute(current):
            query_acc, key_acc, value_acc = current
            key_block = lax.dynamic_slice_in_dim(key_split, first_key, block_rows, 1)
            value_block = lax.dynamic_slice_in_dim(value_split, first_key, block_rows, 1)
            key_places = first_key + jnp.arange(block_rows, dtype=jnp.int32)
            key_segments = lax.dynamic_slice_in_dim(segments, first_key, block_rows, 1)
            query_part, key_part, value_part = block_grads(
                queries,
                grad_attended,
                log_normalizer,
                row_delta,
                query_places,
                query_document_ids,
                key_block,
                value_block,
                key_places,
                key_segments,
            )
            key_acc = lax.dynamic_update_slice_in_dim(key_acc, key_part, first_key, 1)
            value_acc = lax.dynamic_update_slice_in_dim(value_acc, value_part, first_key, 1)
            return (query_acc + query_part, key_acc, value_acc)

        def attend_keep(current):
            return current

        return (lax.cond(first_key <= last_query, attend_compute, attend_keep, state_now), None)

    totals, unused = lax.scan(
        attend_visit, initial, jnp.arange(length // block_rows, dtype=jnp.int32)
    )
    query_grad, key_grad, value_grad = totals
    key_home, value_home = (
        lax.psum_scatter(
            key_grad.reshape(seq_count, length, -1).astype(jnp.bfloat16),
            CTX,
            scatter_dimension=1,
            tiled=True,
        ).astype(jnp.float32),
        lax.psum_scatter(
            value_grad.reshape(seq_count, length, -1).astype(jnp.bfloat16),
            CTX,
            scatter_dimension=1,
            tiled=True,
        ).astype(jnp.float32),
    )
    split_shape = (seq_count, count_of_rows, head_count, head_width)
    return (query_grad, key_home.reshape(split_shape), value_home.reshape(split_shape))


def forward_layer(stream, first_values, weights, segments, cosine, sine_table, query_places):
    norm_attn, w_query, w_key, w_value, w_output, norm_ffn, w_gate, w_up, w_down = weights
    seq_count, count_of_rows, model_width = stream.shape
    head_count = w_query.shape[1] // HEAD_DIM
    split_shape = (seq_count, count_of_rows, head_count, HEAD_DIM)
    normed, inverse_one = norm_forward(stream, norm_attn)
    queries = rotate(project(normed, w_query).reshape(split_shape), cosine, sine_table).astype(
        jnp.bfloat16
    )
    key_rows = (
        rotate(project(normed, w_key).reshape(split_shape), cosine, sine_table)
        .astype(jnp.bfloat16)
        .reshape(seq_count, count_of_rows, -1)
    )
    own_values = project(normed, w_value)
    if first_values is None:
        mixed = own_values.astype(jnp.bfloat16)
    else:
        mixed = (0.5 * own_values + 0.5 * first_values).astype(jnp.bfloat16)
    attended, log_normalizer = attend_forward(queries, key_rows, mixed, segments, query_places)
    attended_low = attended.reshape(seq_count, count_of_rows, -1).astype(jnp.bfloat16)
    hidden_one = stream + head_total(project(attended_low, w_output))
    normed_two, inverse_two = norm_forward(hidden_one, norm_ffn)
    gate_values = project(normed_two, w_gate)
    up_values = project(normed_two, w_up)
    activated = (jax.nn.silu(gate_values) * up_values).astype(jnp.bfloat16)
    result = hidden_one + head_total(project(activated, w_down))
    saved_state = (
        stream,
        inverse_one,
        normed,
        queries,
        key_rows,
        mixed,
        attended,
        log_normalizer,
        attended_low,
        hidden_one,
        inverse_two,
        normed_two,
        gate_values,
        up_values,
        activated,
    )
    return (result, saved_state, own_values)


def backward_layer(
    grad_out, value_extra, saved_state, weights, segments, cosine, sine_table, query_places, mixes
):
    (
        stream,
        inverse_one,
        normed,
        queries,
        key_rows,
        mixed,
        attended,
        log_normalizer,
        attended_low,
        hidden_one,
        inverse_two,
        normed_two,
        gate_values,
        up_values,
        activated,
    ) = saved_state
    norm_attn, w_query, w_key, w_value, w_output, norm_ffn, w_gate, w_up, w_down = weights
    seq_count, count_of_rows, head_count, head_width = queries.shape
    grad_branch = grad_out.astype(jnp.bfloat16)
    down_grad = weight_term(activated, grad_branch)
    grad_active = project_back(grad_branch, w_down)
    gate_sigmoid = jax.nn.sigmoid(gate_values)
    grad_gate = (
        grad_active * up_values * gate_sigmoid * (1.0 + gate_values * (1.0 - gate_sigmoid))
    ).astype(jnp.bfloat16)
    grad_up = (grad_active * gate_values * gate_sigmoid).astype(jnp.bfloat16)
    gate_grad = weight_term(normed_two, grad_gate)
    up_grad = weight_term(normed_two, grad_up)
    grad_normed_two = head_back(project_back(grad_gate, w_gate) + project_back(grad_up, w_up))
    grad_norm_two, ffn_gain_grad = norm_backward(grad_normed_two, hidden_one, inverse_two, norm_ffn)
    grad_hidden = grad_out + grad_norm_two
    grad_attn = grad_hidden.astype(jnp.bfloat16)
    output_grad = weight_term(attended_low, grad_attn)
    grad_attended = (
        project_back(grad_attn, w_output)
        .astype(jnp.bfloat16)
        .reshape(seq_count, count_of_rows, head_count, head_width)
    )
    row_delta = jnp.transpose(
        jnp.sum(grad_attended.astype(jnp.float32) * attended, axis=-1), (0, 2, 1)
    )
    query_rot, key_rot, value_mix = attend_back_gather(
        queries, grad_attended, log_normalizer, row_delta, key_rows, mixed, segments, query_places
    )
    query_low = (
        rotate_back(query_rot, cosine, sine_table)
        .astype(jnp.bfloat16)
        .reshape(seq_count, count_of_rows, -1)
    )
    key_low = (
        rotate_back(key_rot, cosine, sine_table)
        .astype(jnp.bfloat16)
        .reshape(seq_count, count_of_rows, -1)
    )
    value_mix = value_mix.reshape(seq_count, count_of_rows, -1)
    if mixes:
        value_low = (0.5 * value_mix).astype(jnp.bfloat16)
        passed_on = 0.5 * value_mix
    else:
        value_low = (value_mix + value_extra).astype(jnp.bfloat16)
        passed_on = value_extra
    query_grad = weight_term(normed, query_low)
    key_grad = weight_term(normed, key_low)
    value_grad = weight_term(normed, value_low)
    grad_normed = head_back(
        project_back(query_low, w_query)
        + project_back(key_low, w_key)
        + project_back(value_low, w_value)
    )
    grad_norm_one, attn_gain_grad = norm_backward(grad_normed, stream, inverse_one, norm_attn)
    grad_stream = grad_hidden + grad_norm_one
    grad_terms = (
        attn_gain_grad,
        query_grad,
        key_grad,
        value_grad,
        output_grad,
        ffn_gain_grad,
        gate_grad,
        up_grad,
        down_grad,
    )
    return (grad_stream, passed_on, grad_terms)


def on_device(
    inputs,
    segment_ids,
    norm_attn_one,
    query_one,
    key_one,
    value_one,
    output_one,
    norm_ffn_one,
    gate_one,
    up_one,
    down_one,
    norm_attn_two,
    query_two,
    key_two,
    value_two,
    output_two,
    norm_ffn_two,
    gate_two,
    up_two,
    down_two,
    cotangent,
):
    def gather_layer(gain_attn, query, key, value, output, gain_ffn, gate, up, down):
        both = (DP, CTX)
        packed = jnp.concatenate([query, key, value, output.T, gate, up, down.T], axis=1)
        whole = lax.all_gather(packed, both, axis=0, tiled=True)
        gains = lax.all_gather(jnp.stack([gain_attn, gain_ffn]), both, axis=1, tiled=True)
        cuts = []
        for part in (query, key, value, output.T, gate, up, down.T):
            cuts.append((cuts[-1] if cuts else 0) + part.shape[1])
        w_q, w_k, w_v, w_o, w_g, w_u, w_d = jnp.split(whole, cuts[:-1], axis=1)
        return (gains[0], w_q, w_k, w_v, w_o.T, gains[1], w_g, w_u, w_d.T)

    def scatter_layer(grads, outs):
        both = (DP, CTX)
        gain_attn, query, key, value, output, gain_ffn, gate, up, down = grads
        pieces = [query, key, value, output.T, gate, up, down.T]
        packed = jnp.concatenate([part.astype(jnp.bfloat16) for part in pieces], axis=1)
        mine = lax.psum_scatter(packed, both, scatter_dimension=0, tiled=True)
        gains = lax.psum_scatter(
            jnp.stack([gain_attn, gain_ffn]).astype(jnp.bfloat16),
            both,
            scatter_dimension=1,
            tiled=True,
        ).astype(jnp.float32)
        cuts = []
        for part in pieces:
            cuts.append((cuts[-1] if cuts else 0) + part.shape[1])
        g_q, g_k, g_v, g_o, g_g, g_u, g_d = (
            part.astype(jnp.float32) for part in jnp.split(mine, cuts[:-1], axis=1)
        )
        return (gains[0], g_q, g_k, g_v, g_o.T, gains[1], g_g, g_u, g_d.T)

    gathered = gather_layer(
        norm_attn_one,
        query_one,
        key_one,
        value_one,
        output_one,
        norm_ffn_one,
        gate_one,
        up_one,
        down_one,
    ) + gather_layer(
        norm_attn_two,
        query_two,
        key_two,
        value_two,
        output_two,
        norm_ffn_two,
        gate_two,
        up_two,
        down_two,
    )
    weights_one = gathered[:9]
    weights_two = gathered[9:]
    seq_count, count_of_rows, model_width = inputs.shape
    query_places = lax.axis_index(CTX) * count_of_rows + jnp.arange(
        count_of_rows, dtype=jnp.int32
    )
    cosine, sine_table = rotary_tables(query_places[0], count_of_rows)
    layer_one, saved_one, first_values = forward_layer(
        inputs.astype(jnp.float32), None, weights_one, segment_ids, cosine, sine_table, query_places
    )
    layer_two, saved_two, unused = forward_layer(
        layer_one, first_values, weights_two, segment_ids, cosine, sine_table, query_places
    )
    grad_middle, value_extra, grads_two = backward_layer(
        cotangent.astype(jnp.float32),
        None,
        saved_two,
        weights_two,
        segment_ids,
        cosine,
        sine_table,
        query_places,
        True,
    )
    grad_input, unused_extra, grads_one = backward_layer(
        grad_middle,
        value_extra,
        saved_one,
        weights_one,
        segment_ids,
        cosine,
        sine_table,
        query_places,
        False,
    )
    totals = scatter_layer(grads_one, None) + scatter_layer(grads_two, None)
    return (
        layer_one.astype(jnp.bfloat16),
        layer_two.astype(jnp.bfloat16),
        grad_input,
        totals[0],
        totals[1],
        totals[2],
        totals[3],
        totals[4],
        totals[5],
        totals[6],
        totals[7],
        totals[8],
        totals[9],
        totals[10],
        totals[11],
        totals[12],
        totals[13],
        totals[14],
        totals[15],
        totals[16],
        totals[17],
    )


class Raw:
    def __init__(self, call, kind, index):
        self.call, self.kind, self.index = call, kind, index

    @property
    def ref(self):
        return self.call.refs[self.kind][self.index]

    @property
    def at(self):
        return self.ref.at

    @property
    def result(self):
        return self.call.results[self.index]


def cut_rows(ref, blocks, i):
    if blocks == 1:
        return ref
    rows = ref.shape[-2] // blocks
    part = pl.ds(i * rows, rows)
    return ref.at[part] if len(ref.shape) == 2 else ref.at[:, part]


class Store:
    def __init__(self, call, held, shape, dtype, blocks):
        self.held, self.blocks = held, blocks
        self.out = call.give(shape, dtype)
        self.flag = call.flags(blocks)
        call.stores.append(self)

    def copy(self, i):
        return pltpu.make_async_copy(
            cut_rows(self.held.ref, self.blocks, i),
            cut_rows(self.out.ref, self.blocks, i),
            self.flag.at[i],
        )

    def put(self, i=None):
        for k in range(self.blocks) if i is None else (i,):
            self.copy(k).start()

    def finish(self):
        for i in range(self.blocks):
            self.copy(i).wait()

    @property
    def result(self):
        return self.out.result


class Held:
    def __init__(self, call, shape, dtype):
        self.call, self.shape, self.dtype = call, shape, dtype
        self.slot = call.scratch_slot(pltpu.VMEM(shape, dtype))
        self.source = self.out = None
        self.blocks, self.waited = 1, set()

    @property
    def ref(self):
        return self.call.refs[2][self.slot]

    @property
    def at(self):
        return self.ref.at

    def __getitem__(self, key):
        return self.ref[key]

    def __setitem__(self, key, value):
        self.ref[key] = value

    def load_copy(self, i):
        return pltpu.make_async_copy(
            cut_rows(self.source.ref, self.blocks, i),
            cut_rows(self.ref, self.blocks, i),
            self.flag.at[i],
        )

    def need(self, i=None):
        if self.source is None:
            return
        for k in range(self.blocks) if i is None or self.blocks == 1 else (i,):
            if k not in self.waited:
                self.waited.add(k)
                self.load_copy(k).wait()

    def put(self, i=None):
        self.out.put(i)

    @property
    def result(self):
        return self.out.result


class Call:
    def __init__(self, number):
        self.number = number
        self.operands, self.shapes, self.scratch = [], [], []
        self.loads, self.stores, self.jobs = [], [], []
        self.far = self.in_turn = False

    def take(self, array):
        self.operands.append(array)
        return Raw(self, 0, len(self.operands) - 1)

    def give(self, shape, dtype):
        self.shapes.append(jax.ShapeDtypeStruct(shape, dtype))
        return Raw(self, 1, len(self.shapes) - 1)

    def scratch_slot(self, kind):
        self.scratch.append(kind)
        return len(self.scratch) - 1

    def flags(self, count):
        return Raw(self, 2, self.scratch_slot(pltpu.SemaphoreType.DMA((count,))))

    def hold(self, shape, dtype):
        return Held(self, shape, dtype)

    def load(self, array, blocks=1):
        held = Held(self, array.shape, array.dtype)
        self.load_into(held, self.take(array), blocks)
        self.loads.append(held)
        return held

    def load_into(self, held, source, blocks):
        held.source, held.blocks, held.flag = source, blocks, self.flags(blocks)

    def store(self, shape, dtype, blocks=1):
        held = Held(self, shape, dtype)
        held.out = Store(self, held, shape, dtype, blocks)
        return held

    def store_from(self, held, shape, dtype, blocks=1):
        return Store(self, held, shape, dtype, blocks)

    def start_loads(self, backward=False):
        if self.in_turn:
            for held in self.loads:
                for k in range(held.blocks):
                    held.load_copy(k).start()
            return
        for k in range(max([held.blocks for held in self.loads], default=0)):
            for held in self.loads:
                if k < held.blocks:
                    held.load_copy(held.blocks - 1 - k if backward else k).start()

    def run(self, body, remote_ops=True):
        ins, outs = len(self.operands), len(self.operands) + len(self.shapes)

        def kernel(*refs):
            self.refs = (refs[:ins], refs[ins:outs], refs[outs:])
            for held in self.loads:
                held.waited = set()
            body()
            for held in self.loads:
                held.need()
            for store in self.stores:
                store.finish()

        space = pl.BlockSpec(memory_space=pltpu.HBM)
        self.results = pl.pallas_call(
            kernel,
            out_shape=tuple(self.shapes),
            in_specs=[space] * ins,
            out_specs=(space,) * len(self.shapes),
            scratch_shapes=self.scratch,
            compiler_params=pltpu.CompilerParams(
                has_side_effects=remote_ops,
                vmem_limit_bytes=62 << 20,
                collective_id=self.number if remote_ops else None,
            ),
        )(*self.operands)
        self.refs = None


class Place:
    def __init__(self):
        self.dp, self.ctx, self.mp = (lax.axis_index(a) for a in (DP, CTX, MP))
        self.ctx_size = lax.axis_size(CTX)
        self.side = lax.rem(self.mp, 2)
        self.pair = (self.dp, self.ctx, self.mp + 1 - 2 * self.side)
        self.cross = (self.dp, self.ctx, lax.rem(self.mp + 2, 4))
        self.other = (1 - self.dp, self.ctx, self.mp)

    def ahead(self, step):
        return lax.rem(self.ctx + step, self.ctx_size)

    def behind(self, step):
        return lax.rem(self.ctx + self.ctx_size - step, self.ctx_size)

    def along(self, index):
        return (self.dp, index, self.mp)

    def peers(self, far):
        peers = [self.pair, self.cross]
        if far:
            peers.append(self.other)
            peers += [self.along(self.ahead(s)) for s in range(1, self.ctx_size)]
        return peers

    def greet(self, far):
        barrier = pltpu.get_barrier_semaphore()
        for peer in self.peers(far):
            pl.semaphore_signal(barrier, inc=1, device_id=peer, device_id_type=MESH)

    def enter(self, far):
        pl.semaphore_wait(pltpu.get_barrier_semaphore(), len(self.peers(far)))


def remote(source, target, send, recv, peer):
    return pltpu.make_async_remote_copy(
        src_ref=source,
        dst_ref=target,
        send_sem=send,
        recv_sem=recv,
        device_id=peer,
        device_id_type=MESH,
    )


class HeadSum:
    def __init__(self, call, blocks, rows, width):
        self.half = rows // 2
        self.part = call.hold((blocks, rows, width), jnp.bfloat16)
        self.near, self.far, self.rest = (
            call.hold((blocks, rows // 2, width), jnp.bfloat16) for _ in range(3)
        )
        self.sa, self.ra, self.sb, self.rb, self.sc, self.rc = (
            call.flags(blocks) for _ in range(6)
        )

    def bind(self, place):
        self.place = place

    def own(self):
        return pl.ds(pl.multiple_of(self.place.side * self.half, self.half), self.half)

    def theirs(self):
        start = (1 - self.place.side) * self.half
        return pl.ds(pl.multiple_of(start, self.half), self.half)

    def first(self, i):
        source = self.part.at[i, self.theirs()]
        return remote(source, self.near.at[i], self.sa.at[i], self.ra.at[i], self.place.pair)

    def second(self, i):
        return remote(
            self.near.at[i], self.far.at[i], self.sb.at[i], self.rb.at[i], self.place.cross
        )

    def third(self, i):
        return remote(
            self.far.at[i], self.rest.at[i], self.sc.at[i], self.rc.at[i], self.place.pair
        )

    def send(self, i, partial_rows):
        self.part[i] = partial_rows.astype(jnp.bfloat16)
        self.first(i).start()

    def middle(self, i):
        self.first(i).wait()
        mine = self.part[i, self.own()].astype(jnp.float32)
        self.near[i] = (mine + self.near[i].astype(jnp.float32)).astype(jnp.bfloat16)
        self.second(i).start()

    def last(self, i):
        self.second(i).wait()
        total = self.near[i].astype(jnp.float32) + self.far[i].astype(jnp.float32)
        self.far[i] = total.astype(jnp.bfloat16)
        self.third(i).start()

    def total(self, i):
        self.third(i).wait()
        self.part[i, self.own()] = self.far[i]
        self.part[i, self.theirs()] = self.rest[i]
        return self.part[i].astype(jnp.float32)


class Gather:
    def __init__(self, call, shard, places, swap=False):
        self.parts = lax.axis_size(CTX)
        call.far = True
        if isinstance(shard, Held):
            self.shard = shard
        else:
            self.shard = call.load(shard)
            call.loads.insert(0, call.loads.pop())
        self.whole = call.give((places,) + shard.shape, shard.dtype)
        self.zs, self.zr, self.ys, self.yr = (call.flags(self.parts) for _ in range(4))
        self.l, self.ss, self.sr = (call.flags(1) for _ in range(3))
        self.relayed = self.parts == 4
        self.swap = swap and self.relayed
        self.order = (2, 1, 3) if self.relayed else tuple(range(self.parts - 1, 0, -1))
        self.steps = len(self.order)

    def bind(self, place):
        self.place, self.crossed = place, False

    def slot(self, dp, ctx):
        return self.whole.at[dp * self.parts + ctx]

    def local(self):
        p = self.place
        return pltpu.make_async_copy(self.shard.ref, self.slot(p.dp, p.ctx), self.l.at[0])

    def along(self, s):
        p = self.place
        target = self.slot(p.dp, p.ctx)
        return remote(self.shard.ref, target, self.zs.at[s], self.zr.at[s], p.along(p.ahead(s)))

    def direct(self, s, act):
        if self.relayed and s != 2:
            pl.when(self.place.ctx != (0 if s == 3 else 3))(lambda: act(self.along(s)))
        else:
            act(self.along(s))

    def relay(self, act):
        p = self.place
        block = self.slot(p.dp, p.behind(2))
        for middle, end, s in ((2, 3, 3), (1, 0, 1)):
            copy = remote(block, block, self.zs.at[0], self.zr.at[s], p.along(end))
            pl.when(p.ctx == middle)(lambda copy=copy: act(copy))

    def across(self, s):
        p = self.place
        block = self.slot(p.dp, p.behind(s))
        source = self.shard.ref if s == 0 else block
        return remote(source, block, self.ys.at[s], self.yr.at[s], p.other)

    def arrive(self, s):
        p = self.place
        block = self.slot(1 - p.dp, p.behind(s))
        return remote(block, block, self.ys.at[s], self.yr.at[s], p.other)

    def when_crossing(self, s, act):
        if self.swap and s in (1, 3):
            pl.when(lax.rem(self.place.ctx, 2) == (0 if s == 1 else 1))(act)
        else:
            act()

    def swapped(self, ctx):
        p = self.place
        block = self.slot(1 - p.dp, ctx)
        neighbour = p.ctx + 1 - 2 * lax.rem(p.ctx, 2)
        return remote(block, block, self.ss.at[0], self.sr.at[0], p.along(neighbour))

    def cross(self):
        self.crossed = True
        self.shard.need()
        self.across(0).start()

    def start(self):
        self.shard.need()
        for s in self.order:
            self.direct(s, lambda copy: copy.start())
        if not self.crossed:
            self.cross()
        self.local().start()

    def step(self, k):
        s = self.order[k]
        p = self.place
        block = self.slot(p.dp, p.behind(s))
        remote(block, block, self.zs.at[s], self.zr.at[s], p.along(p.ctx)).wait_recv()
        if self.relayed and s == 2:
            self.relay(lambda copy: copy.start())
        self.when_crossing(s, lambda: self.across(s).start())
        if self.swap and k == 0:
            self.arrive(0).wait_recv()
            self.swapped(p.ctx).start()

    def finish(self):
        p = self.place
        self.local().wait()
        for s in self.order:
            self.direct(s, lambda copy: copy.wait_send())
        if self.relayed:
            self.relay(lambda copy: copy.wait_send())

        def both(s):
            self.across(s).wait_send()
            self.arrive(s).wait_recv()

        for s in self.order:
            self.when_crossing(s, functools.partial(both, s))
        self.across(0).wait_send()
        if self.swap:
            self.swapped(p.ctx).wait_send()
            self.swapped(p.ctx + 1 - 2 * lax.rem(p.ctx, 2)).wait_recv()
        else:
            self.arrive(0).wait_recv()

    @property
    def result(self):
        whole = self.whole.result
        return whole.reshape(-1, whole.shape[-1])


class Scatter:
    def __init__(self, call, blocks, swap=False):
        self.parts = lax.axis_size(CTX)
        places, rows, width = blocks.shape
        self.dtype = blocks.dtype
        call.far = True
        self.late = isinstance(blocks, Held)
        self.blocks = blocks if self.late else call.take(blocks)
        self.out = call.store((rows, width), jnp.float32)
        if not self.late:
            self.mb = call.hold((self.parts, rows, width), blocks.dtype)
        self.yb = call.hold((self.parts, rows, width), blocks.dtype)
        self.zb = call.hold((self.parts - 1, rows, width), blocks.dtype)
        self.zs, self.zr, self.ys, self.yr = (call.flags(self.parts) for _ in range(4))
        self.l, self.ss, self.sr = (call.flags(2) for _ in range(3))
        self.relayed = self.parts == 4
        self.swap = swap and self.relayed
        self.order = (3, 1, 2, 0) if self.relayed else tuple(range(self.parts - 1, -1, -1))
        if self.relayed:
            self.rb = call.hold((rows, width), blocks.dtype)
        if self.swap:
            self.tb, self.wb = (call.hold((rows, width), blocks.dtype) for _ in range(2))
        self.steps = self.parts

    def bind(self, place):
        self.place = place

    def block_of(self, dp, ctx):
        return self.blocks.at[dp * self.parts + ctx]

    def local(self):
        mine = self.blocks.at[pl.ds(self.place.dp * self.parts, self.parts)]
        return pltpu.make_async_copy(mine, self.mb.ref, self.l.at[0])

    def local_twin(self):
        p = self.place
        return pltpu.make_async_copy(self.block_of(1 - p.dp, p.ctx), self.tb.ref, self.l.at[1])

    def swapped(self):
        p = self.place
        neighbour = p.ctx + 1 - 2 * lax.rem(p.ctx, 2)
        block = self.block_of(1 - p.dp, neighbour)
        return remote(block, self.wb.ref, self.ss.at[0], self.sr.at[0], p.along(neighbour))

    def across(self, s):
        p = self.place
        block = self.tb.ref if self.swap and s == 0 else self.block_of(1 - p.dp, p.ahead(s))
        return remote(block, self.yb.at[s], self.ys.at[s], self.yr.at[s], p.other)

    def when_crossing(self, s, act):
        if self.swap and s in (1, 3):
            pl.when(lax.rem(self.place.ctx, 2) == (1 if s == 1 else 0))(act)
        else:
            act()

    def along(self, s, act):
        p = self.place
        target = self.zb.at[s - 1]
        copy = remote(self.yb.at[s], target, self.zs.at[s], self.zr.at[s], p.along(p.ahead(s)))
        if not self.relayed or s == 2:
            act(copy)
            return
        end, middle = (0, 1) if s == 3 else (3, 2)
        way = remote(self.yb.at[s], self.rb.ref, self.zs.at[s], self.zr.at[0], p.along(middle))
        pl.when(p.ctx != end)(lambda: act(copy))
        pl.when(p.ctx == end)(lambda: act(way))

    def early(self, act):
        p = self.place
        for s, odd in ((1, 0), (3, 1)):
            block, target = self.block_of(p.dp, p.ahead(s)), self.zb.at[s - 1]
            copy = remote(block, target, self.zs.at[s], self.zr.at[s], p.along(p.ahead(s)))
            pl.when(lax.rem(p.ctx, 2) == odd)(lambda copy=copy: act(copy))

    def start(self):
        if self.swap:
            self.swapped().start()
            self.local_twin().start()
            self.early(lambda copy: copy.start())
        for s in self.order:
            if s or not self.swap:
                self.when_crossing(s, lambda s=s: self.across(s).start())
        if not self.late:
            self.local().start()

    def send_twin(self):
        self.local_twin().wait()
        self.swapped().wait()
        both = self.tb[...].astype(jnp.float32) + self.wb[...].astype(jnp.float32)
        self.tb[...] = both.astype(self.dtype)
        self.across(0).start()

    def step(self, k):
        p = self.place
        s = self.order[k]
        if k == 0:
            if not self.late:
                self.local().wait()
            if self.swap:
                self.send_twin()
        if self.late:
            mine = self.blocks[p.dp * self.parts + p.ahead(s)]
        else:
            mine = self.mb[p.ahead(s)]
        mine = mine.astype(jnp.float32)

        def add_crossed():
            self.across(s).wait()
            self.yb[s] = (mine + self.yb[s].astype(jnp.float32)).astype(self.dtype)
            if s != 2:
                self.along(s, lambda copy: copy.start())

        if s == 0:
            self.across(s).wait()
            self.out[...] = mine + self.yb[s].astype(jnp.float32)
            return
        self.when_crossing(s, add_crossed)
        if s != 2:
            return
        if self.relayed:

            def add_ends():
                way = remote(self.rb.ref, self.rb.ref, self.zs.at[0], self.zr.at[0], p.other)
                way.wait_recv()
                through = self.yb[s].astype(jnp.float32) + self.rb[...].astype(jnp.float32)
                self.yb[s] = through.astype(self.dtype)

            pl.when((p.ctx == 1) | (p.ctx == 2))(add_ends)
        self.along(s, lambda copy: copy.start())

    def finish(self):
        p = self.place

        def add(s):
            block = self.zb.at[s - 1]
            remote(block, block, self.zs.at[s], self.zr.at[s], p.other).wait_recv()
            self.out[...] += self.zb[s - 1].astype(jnp.float32)

        for s in self.order:
            if s == 0:
                continue
            self.along(s, lambda copy: copy.wait_send())
            if self.relayed and s != 2:
                pl.when(p.ctx != (3 if s == 3 else 0))(functools.partial(add, s))
            else:
                add(s)
        self.out.put()

    @property
    def result(self):
        return self.out.result


class Deal:
    def __init__(self, call, blocks, wide=False):
        self.parts, self.wide = lax.axis_size(CTX), wide
        self.share = blocks.shape[1] // (2 if wide else 4)
        call.far = True
        self.source = call.take(blocks)
        self.target = call.give(blocks.shape, blocks.dtype)
        self.held = call.hold(blocks.shape[1:], blocks.dtype)
        self.l = call.flags(2)
        self.zf, self.af, self.xf, self.bf = (
            tuple(call.flags(self.parts) for _ in range(2)) for _ in range(4)
        )
        self.steps = (self.parts - 1) * (1 if wide else 2)

    def bind(self, place):
        self.place = place
        self.own = place.side if self.wide else place.mp

    def rows(self, index):
        return pl.ds(pl.multiple_of(index * self.share, self.share), self.share)

    def local(self, k):
        p = self.place
        refs = (self.source.at[p.ctx], self.held.ref, self.target.at[p.ctx])
        return pltpu.make_async_copy(refs[k], refs[k + 1], self.l.at[k])

    def along(self, s):
        p = self.place
        rows = self.rows(self.own)
        return remote(
            self.source.at[p.ahead(s), rows],
            self.target.at[p.ctx, rows],
            self.zf[0].at[s],
            self.zf[1].at[s],
            p.along(p.ahead(s)),
        )

    def piece(self, s, index, flags, peer):
        ref = self.target.at[self.place.behind(s), self.rows(index)]
        return remote(ref, ref, flags[0].at[s], flags[1].at[s], peer)

    def start(self):
        for s in range(self.parts - 1, 0, -1):
            self.along(s).start()
        self.local(0).start()

    def step(self, k):
        p = self.place
        if k == 0:
            self.local(0).wait()
            self.local(1).start()
        if self.wide:
            s = self.parts - 1 - k
            self.piece(s, self.own, self.zf, p.along(p.ctx)).wait_recv()
            self.piece(s, self.own, self.af, p.pair).start()
            return
        s = self.parts - 1 - k % (self.parts - 1)
        far = lax.rem(p.mp + 2, 4)
        if k < self.parts - 1:
            self.piece(s, p.mp, self.zf, p.along(p.ctx)).wait_recv()
            self.piece(s, p.mp, self.xf, p.cross).start()
            self.piece(s, p.mp, self.af, p.pair).start()
        else:
            self.piece(s, far, self.xf, p.cross).wait_recv()
            self.piece(s, far, self.bf, p.pair).start()

    def finish(self):
        p = self.place
        self.local(1).wait()
        if self.wide:
            for s in range(1, self.parts):
                self.along(s).wait_send()
                self.piece(s, self.own, self.af, p.pair).wait_send()
                self.piece(s, 1 - self.own, self.af, p.pair).wait_recv()
            return
        far = lax.rem(p.mp + 2, 4)
        near = p.mp + 1 - 2 * p.side
        near_far = lax.rem(near + 2, 4)
        for s in range(1, self.parts):
            self.along(s).wait_send()
            self.piece(s, p.mp, self.xf, p.cross).wait_send()
            self.piece(s, p.mp, self.af, p.pair).wait_send()
            self.piece(s, far, self.bf, p.pair).wait_send()
            self.piece(s, near, self.af, p.pair).wait_recv()
            self.piece(s, near_far, self.bf, p.pair).wait_recv()

    @property
    def result(self):
        whole = self.target.result
        return whole.reshape(-1, whole.shape[-1])


LATE = "late"


class Jobs:
    def __init__(self, jobs, plan):
        self.jobs = list(jobs)
        self.queue = sorted(
            (times[k] if len(times) > 2 else times[0] + k * times[1], j, k)
            for j, (job, times) in enumerate(zip(self.jobs, plan))
            for k in range(job.steps)
        )
        self.at = 0

    def bind(self, place):
        self.at = 0
        for job in self.jobs:
            job.bind(place)

    def start(self):
        for job in self.jobs:
            if not getattr(job, LATE, False):
                job.start()

    def advance(self, reached):
        while self.at < len(self.queue) and self.queue[self.at][0] <= reached:
            _, j, k = self.queue[self.at]
            self.jobs[j].step(k)
            self.at += 1

    def finish(self):
        self.advance(math.inf)
        for job in self.jobs:
            job.finish()


def begin(call, total, jobs, backward=False):
    place = Place()
    if total is not None:
        total.bind(place)
    jobs.bind(place)
    place.greet(call.far)
    call.start_loads(backward)
    place.enter(call.far)
    jobs.start()


def dot_nn(a, b):
    return lax.dot_general(a, b, (((1,), (0,)), ((), ())), preferred_element_type=jnp.float32)


def dot_nt(a, b):
    return lax.dot_general(a, b, (((1,), (1,)), ((), ())), preferred_element_type=jnp.float32)


def dot_tn(a, b):
    return lax.dot_general(a, b, (((0,), (0,)), ((), ())), preferred_element_type=jnp.float32)


def lane_number(width):
    return lax.broadcasted_iota(jnp.int32, (1, width), 1)


LANES = 128
BLOCKS = 4


def turn(values, cosine, signed_sine, back):
    half = HEAD_DIM // 2
    leading = lax.rem(lane_number(LANES), HEAD_DIM) < half
    pieces = []
    for at in range(0, values.shape[1], LANES):
        piece = values[:, at : at + LANES]
        swapped = jnp.where(leading, pltpu.roll(piece, LANES - half, 1), pltpu.roll(piece, half, 1))
        moved = swapped * signed_sine
        pieces.append(piece * cosine - moved if back else piece * cosine + moved)
    return jnp.concatenate(pieces, axis=1)


def write_bias(bias, seg_col, seg_row, i, rows, keys):
    query_at = i * rows + lax.broadcasted_iota(jnp.int32, (rows, 1), 0)
    key_at = lax.broadcasted_iota(jnp.int32, (1, keys), 1)
    same = seg_col[pl.ds(i * rows, rows), :1] == seg_row[:1, :keys]
    bias[:, :keys] = jnp.where(same & (key_at <= query_at), 0.0, neg_large)


class Opening:
    def __init__(self, call, inputs, segment_ids, layers, gain_rows, angle_row, places):
        self.call, self.places = call, places
        parts, length, width = inputs.shape
        self.count = count = parts * length
        (q1, k1, v1, o1, *tall1), (q2, k2, v2, o2, *tall2) = layers
        self.shard, self.hid = shard, hid = q1.shape
        units = tall1[0].shape[0]
        low = jnp.bfloat16
        self.first = [call.load(array) for array in (q1, k1, v1, o1)]
        self.gain_rows = call.load(gain_rows)
        self.ids, self.angle = call.load(segment_ids), call.load(angle_row)
        self.tall = [call.load(array) for array in tall1]
        self.second = [call.load(array) for array in (q2, k2, v2, o2)]
        self.tall += [call.load(array) for array in tall2]
        self.shards_one = [call.hold((shard, units), low) for _ in tall1]
        self.shards_two = [call.store((shard, units), low) for _ in tall2]
        self.wa_one = call.hold((shard, 4 * hid), low)
        self.wa_two = call.store((shard, 4 * hid), low)
        self.gains_wide = call.hold(gain_rows.shape, jnp.float32)
        self.cosine, self.sine, self.seg_col = (
            call.store((count, LANES), jnp.float32, BLOCKS) for _ in range(3)
        )
        self.seg_row = call.store((8, count), jnp.float32)
        self.gather = Gather(call, self.wa_one, places)
        self.deal = Deal(call, inputs)
        self.gather_gains = Gather(call, self.gains_wide, places)
        plan = ((2.0, 0.1), (5.0, 4.0), (14.0, 6.0))
        self.jobs = Jobs([self.gather_gains, self.deal, self.gather], plan)
        self.deal.late = True
        self.x = call.hold((count, width), low)
        self.wa = call.hold((width, 4 * hid), low)
        self.gain_blocks = call.hold((places,) + gain_rows.shape, jnp.float32)
        self.gains = call.store((gain_rows.shape[0], width), jnp.float32)
        self.flag = call.flags(2 + 2 * parts)

    def tables(self):
        return (self.cosine, self.sine, self.seg_col, self.seg_row)

    def run(self, total, jobs):
        call, hid = self.call, self.hid
        place = Place()
        total.bind(place)
        self.jobs.bind(place)
        jobs.bind(place)
        place.greet(call.far)
        call.start_loads()
        place.enter(call.far)
        self.deal.start()
        for j, held in enumerate(self.first):
            held.need()
            values = held[...]
            self.wa_one[:, j * hid : (j + 1) * hid] = values.T if j == 3 else values
        self.gain_rows.need()
        self.gains_wide[...] = self.gain_rows[...].astype(jnp.float32)
        self.jobs.start()
        for tall, shard in zip(self.tall, self.shards_one + self.shards_two):
            tall.need()
            shard[...] = tall[...].T
            if shard.out is not None:
                shard.put()
        for j, held in enumerate(self.second):
            held.need()
            values = held[...]
            self.wa_two[:, j * hid : (j + 1) * hid] = values.T if j == 3 else values
        self.wa_two.put()
        for job in jobs.jobs:
            job.cross()
        self.ids.need()
        self.angle.need()
        ids = self.ids[...].astype(jnp.float32)
        mine = lax.broadcasted_iota(jnp.int32, ids.shape, 0) == place.ctx
        own = jnp.sum(jnp.where(mine, ids, 0.0), axis=0, keepdims=True)
        self.seg_row[...] = jnp.broadcast_to(own, self.seg_row.shape)
        self.seg_row.put()
        self.seg_col[...] = jnp.broadcast_to(own, (LANES, self.count)).T
        self.seg_col.put()
        rows = self.count // BLOCKS
        for i in range(BLOCKS):
            at = pl.ds(i * rows, rows)
            index = i * rows + lax.broadcasted_iota(jnp.int32, (rows, 1), 0)
            angles = index.astype(jnp.float32) * self.angle[:1, :]
            self.cosine[at, :] = jnp.cos(angles)
            self.sine[at, :] = jnp.sin(angles) * self.angle[1:2, :]
        self.cosine.put()
        self.sine.put()
        self.jobs.advance(math.inf)
        jobs.start()
        self.jobs.finish()
        shard = self.shard
        copies = [
            pltpu.make_async_copy(
                self.gather_gains.whole.ref, self.gain_blocks.ref, self.flag.at[0]
            )
        ]
        parts = self.deal.parts
        length = self.count // parts
        for k in range(parts):
            copies.append(
                pltpu.make_async_copy(
                    self.deal.target.at[k],
                    self.x.at[pl.ds(k * length, length)],
                    self.flag.at[1 + k],
                )
            )
        for k in range(self.places):
            copies.append(
                pltpu.make_async_copy(
                    self.gather.whole.at[k],
                    self.wa.at[pl.ds(k * shard, shard)],
                    self.flag.at[1 + parts],
                )
            )
        for copy in copies:
            copy.start()
        for copy in copies:
            copy.wait()
        for k in range(self.places):
            self.gains[:, k * shard : (k + 1) * shard] = self.gain_blocks[k]
        self.gains.put()


def attention_layer(number, x, first_v, wa, gains, which, tables, jobs_of, plan, opening=None):
    call = Call(number)
    if opening is None:
        start = None
        x, gains, wa = call.load(x, BLOCKS), call.load(gains), call.load(wa)
        cosine, sine, seg_col = (call.load(table, BLOCKS) for table in tables[:3])
        seg_row = call.load(tables[3])
    else:
        start = opening(call)
        x, gains, wa = start.x, start.gains, start.wa
        cosine, sine, seg_col, seg_row = start.tables()
    count, width = x.shape
    hid = wa.shape[1] // 4
    heads = hid // HEAD_DIM
    rows = count // BLOCKS
    if first_v is not None:
        first_v = call.load(first_v, BLOCKS)
    else:
        v = call.store((count, hid), jnp.float32, BLOCKS)
    x1 = call.store((count, width), jnp.float32, BLOCKS)
    h = call.store((count, width), jnp.bfloat16, BLOCKS)
    q, k, m, o = (call.store((count, hid), jnp.bfloat16, BLOCKS) for _ in range(4))
    lse = call.store((heads, count, 1), jnp.float32, BLOCKS)
    bias = call.hold((rows, count), jnp.float32)
    acc = call.hold((rows, hid), jnp.float32)
    total = HeadSum(call, BLOCKS, rows, width)
    carried = jobs_of(call, start)
    jobs = Jobs(carried, plan)

    def body():
        if start is None:
            begin(call, total, jobs)
        else:
            start.run(total, jobs)
        lane = lane_number(hid)
        for i in range(BLOCKS):
            at = pl.ds(i * rows, rows)
            x.need(i)
            gains.need()
            stream = x[at, :].astype(jnp.float32)
            inverse = lax.rsqrt(jnp.mean(stream * stream, axis=-1, keepdims=True) + epsilon)
            normed = (stream * inverse * gains[which : which + 1, :]).astype(jnp.bfloat16)
            h[at, :] = normed
            h.put(i)
            wa.need()
            projected = dot_nn(normed, wa[:, : 3 * hid])
            cosine.need(i)
            sine.need(i)
            cos, sin = cosine[at, :], sine[at, :]
            queries = turn(projected[:, :hid], cos, sin, False).astype(jnp.bfloat16)
            q[at, :] = queries * jnp.bfloat16(HEAD_DIM**-0.5)
            k[at, :] = turn(projected[:, hid : 2 * hid], cos, sin, False).astype(jnp.bfloat16)
            values = projected[:, 2 * hid :]
            if first_v is None:
                v[at, :] = values
                v.put(i)
            else:
                first_v.need(i)
                values = 0.5 * values + 0.5 * first_v[at, :]
            m[at, :] = values.astype(jnp.bfloat16)
            for held in (q, k, m):
                held.put(i)
            keys = (i + 1) * rows
            seg_col.need(i)
            seg_row.need()
            write_bias(bias, seg_col, seg_row, i, rows, keys)
            if i:
                total.middle(i - 1)
            jobs.advance((4.5, 8.0, 12.5, 18.0)[i])

            def one_head(index, unused):
                mask = lane // HEAD_DIM == index
                query = jnp.where(mask, q[at, :], jnp.bfloat16(0))
                scores = dot_nt(query, k[:keys, :]) + bias[:, :keys]
                top = jnp.max(scores, axis=-1, keepdims=True)
                exponent = jnp.exp(scores - top)
                summed = jnp.sum(exponent, axis=-1, keepdims=True)
                weighted = dot_nn(exponent.astype(jnp.bfloat16), m[:keys, :])
                acc[...] = jnp.where(mask, weighted / summed, acc[...])
                lse[index, at, :] = top + jnp.log(summed)
                return unused

            lax.fori_loop(0, heads, one_head, 0)
            attended = acc[...].astype(jnp.bfloat16)
            o[at, :] = attended
            o.put(i)
            lse.put(i)
            total.send(i, dot_nt(attended, wa[:, 3 * hid :]))
            jobs.advance((6.0, 10.5, 16.0, 22.5)[i])
        total.middle(BLOCKS - 1)
        for i in range(BLOCKS):
            total.last(i)
            jobs.advance((23.0, 24.0, 28.0, 33.0)[i])
        for i in range(BLOCKS):
            at = pl.ds(i * rows, rows)
            x1[at, :] = x[at, :].astype(jnp.float32) + total.total(i)
            x1.put(i)
        jobs.finish()

    call.run(body)
    return SimpleNamespace(
        x1=x1.result,
        h=h.result,
        q=q.result,
        k=k.result,
        m=m.result,
        o=o.result,
        lse=lse.result,
        v=v.result if first_v is None else None,
        carried=[job.result for job in carried],
        start=start,
    )


def feed_forward_layer(number, x1, gate, up, down, gains, which, jobs_of, plan):
    count, width = x1.shape
    units = gate.shape[1]
    rows = count // BLOCKS
    call = Call(number)
    x1 = call.load(x1, BLOCKS)
    gains, gate, up, down = (call.load(array) for array in (gains, gate, up, down))
    y = call.store_from(x1, (count, width), jnp.float32, BLOCKS)
    y_low, h2 = (call.store((count, width), jnp.bfloat16, BLOCKS) for _ in range(2))
    z, u, a = (call.store((count, units), jnp.bfloat16, BLOCKS) for _ in range(3))
    total = HeadSum(call, BLOCKS, rows, width)
    carried = jobs_of(call)
    jobs = Jobs(carried, plan)

    def body():
        begin(call, total, jobs)
        for i in range(BLOCKS):
            at = pl.ds(i * rows, rows)
            x1.need(i)
            gains.need()
            stream = x1[at, :]
            inverse = lax.rsqrt(jnp.mean(stream * stream, axis=-1, keepdims=True) + epsilon)
            normed = (stream * inverse * gains[which : which + 1, :]).astype(jnp.bfloat16)
            h2[at, :] = normed
            gate.need()
            gated = dot_nn(normed, gate[...])
            if i:
                total.middle(i - 1)
            jobs.advance(2.5 * i + 4.0)
            up.need()
            raised = dot_nn(normed, up[...])
            active = (gated * lax.logistic(gated) * raised).astype(jnp.bfloat16)
            z[at, :] = gated.astype(jnp.bfloat16)
            u[at, :] = raised.astype(jnp.bfloat16)
            a[at, :] = active
            for held in (h2, z, u, a):
                held.put(i)
            down.need()
            total.send(i, dot_nt(active, down[...]))
            jobs.advance(2.5 * i + 5.5)
        total.middle(BLOCKS - 1)
        for i in range(BLOCKS):
            total.last(i)
            jobs.advance(13.0 + 5.7 * i)
        for i in range(BLOCKS):
            at = pl.ds(i * rows, rows)
            result = x1[at, :] + total.total(i)
            x1[at, :] = result
            y_low[at, :] = result.astype(jnp.bfloat16)
            y.put(i)
            y_low.put(i)
        jobs.finish()

    call.run(body)
    return SimpleNamespace(
        y=y.result,
        y_low=y_low.result,
        h2=h2.result,
        z=z.result,
        u=u.result,
        a=a.result,
        carried=[job.result for job in carried],
    )


def norm_back(gain, grad, stream, gain_sum):
    inverse = lax.rsqrt(jnp.mean(stream * stream, axis=-1, keepdims=True) + epsilon)
    scaled = stream * inverse
    grad_scaled = grad * gain
    products = jnp.mean(grad_scaled * scaled, axis=-1, keepdims=True)
    gain_sum = gain_sum + jnp.sum(grad * scaled, axis=0, keepdims=True)
    return inverse * (grad_scaled - scaled * products), gain_sum


def feed_forward_back(number, gy, x1, saved, gate, up, down, gains, which, jobs_of, plan):
    count, width = x1.shape
    units = gate.shape[1]
    rows = count // BLOCKS
    call = Call(number)
    call.in_turn = True
    gy = call.load(gy, BLOCKS)
    down = call.load(down)
    z, u = call.load(saved.z, BLOCKS), call.load(saved.u, BLOCKS)
    gate, up, a, h2, gains = (call.load(w) for w in (gate, up, saved.a, saved.h2, gains))
    x1 = call.load(x1, BLOCKS)
    gx1 = call.store_from(x1, (count, width), jnp.float32, BLOCKS)
    gain = call.store((1, width), jnp.float32)
    d_gate, d_up = (call.store((width, units), jnp.bfloat16, 4) for _ in range(2))
    places = lax.axis_size(DP) * lax.axis_size(CTX)
    shard = width // places
    d_down = call.hold((places, shard, units), jnp.bfloat16)
    low = call.hold((count, width), jnp.bfloat16)
    gz, gu = (call.hold((count, units), jnp.bfloat16) for _ in range(2))
    total = HeadSum(call, BLOCKS, rows, width)
    down_sum = Scatter(call, d_down)
    carried = jobs_of(call, down_sum)
    jobs = Jobs(carried, plan)

    def body():
        begin(call, total, jobs)
        for i in range(BLOCKS):
            at = pl.ds(i * rows, rows)
            gy.need(i)
            low[at, :] = gy[at, :].astype(jnp.bfloat16)
        for i in range(BLOCKS):
            at = pl.ds(i * rows, rows)
            down.need()
            ga = dot_nn(low[at, :], down[...])
            z.need(i)
            u.need(i)
            gated = z[at, :].astype(jnp.float32)
            sigma = lax.logistic(gated)
            raised = u[at, :].astype(jnp.float32)
            slope = sigma * (1.0 + gated * (1.0 - sigma))
            gz[at, :] = (ga * raised * slope).astype(jnp.bfloat16)
            gu[at, :] = (ga * gated * sigma).astype(jnp.bfloat16)
            if i > 1:
                total.middle(i - 1)
            gate.need()
            up.need()
            total.send(i, dot_nt(gz[at, :], gate[...]) + dot_nt(gu[at, :], up[...]))
            if i == 0:
                a.need()
                for j in range(places // 2):
                    cut = slice(j * 2 * shard, (j + 1) * 2 * shard)
                    part = dot_tn(low[:, cut], a[...]).astype(jnp.bfloat16)
                    d_down[2 * j : 2 * j + 2] = part.reshape(2, shard, units)
                    if j == 0:
                        total.middle(0)
                down_sum.start()
            jobs.advance(3.0 * i + 9.0)
        total.middle(BLOCKS - 1)
        cols = width // 4
        h2.need()
        for reached, left, right, out in ((21.0, h2, gz, d_gate), (24.0, h2, gu, d_up)):
            for j in range(4):
                cut = slice(j * cols, (j + 1) * cols)
                out[cut, :] = dot_tn(left[:, cut], right[...]).astype(jnp.bfloat16)
                out.put(j)
            jobs.advance(reached)
        gains.need()
        for i in range(BLOCKS):
            total.last(i)
            jobs.advance((24.0, 24.0, 28.0, 34.0)[i])
        gain_sum = jnp.zeros((1, width), jnp.float32)
        for i in range(BLOCKS):
            at = pl.ds(i * rows, rows)
            x1.need(i)
            step, gain_sum = norm_back(
                gains[which : which + 1, :], total.total(i), x1[at, :], gain_sum
            )
            x1[at, :] = gy[at, :].astype(jnp.float32) + step
            gx1.put(i)
        gain[...] = gain_sum
        gain.put()
        jobs.finish()

    call.run(body)
    return SimpleNamespace(
        gx1=gx1.result,
        gain=gain.result,
        d_gate=d_gate.result,
        d_up=d_up.result,
        carried=[job.result for job in carried],
    )


def attention_back(number, gx1, x, saved, extra, wa, gains, which, tables, jobs_of, plan):
    count, width = x.shape
    hid = wa.shape[1] // 4
    heads = hid // HEAD_DIM
    rows = count // BLOCKS
    call = Call(number)
    gx1, wa = call.load(gx1, BLOCKS), call.load(wa)
    q, k, m, o = (
        call.load(array, blocks)
        for array, blocks in ((saved.q, BLOCKS), (saved.k, 1), (saved.m, 1), (saved.o, BLOCKS))
    )
    lse = call.load(saved.lse, BLOCKS)
    cosine, sine, seg_col = (call.load(table, BLOCKS) for table in tables[:3])
    seg_row = call.load(tables[3])
    if extra is not None:
        extra = call.load(extra, BLOCKS)
    h, gains, x = call.load(saved.h), call.load(gains), call.load(x, BLOCKS)
    if extra is not None:
        gx = call.store((count, width), jnp.bfloat16, BLOCKS)
        gx_held = gx
    else:
        gx_held = gx1
        gx = call.store_from(gx1, (count, width), jnp.float32, BLOCKS)
        passed = call.store((count, hid), jnp.float32, BLOCKS)
    gain = call.store((1, width), jnp.float32)
    d_wa = call.store((width, 4 * hid), jnp.bfloat16, 4)
    low = call.hold((count, width), jnp.bfloat16)
    bias = call.hold((rows, count), jnp.float32)
    go = call.hold((rows, hid), jnp.bfloat16)
    gq = call.hold((rows, hid), jnp.float32)
    gk, gm = (call.hold((count, hid), jnp.float32) for _ in range(2))
    g3 = call.hold((count, 3 * hid), jnp.bfloat16)
    total = HeadSum(call, BLOCKS, rows, width)
    carried = jobs_of(call)
    jobs = Jobs(carried, plan)

    def body():
        begin(call, total, jobs, True)
        lane = lane_number(hid)
        gk[...] = jnp.zeros(gk.shape, gk.dtype)
        gm[...] = jnp.zeros(gm.shape, gm.dtype)
        order = list(range(BLOCKS))[::-1]
        for turn_index, i in enumerate(order):
            at = pl.ds(i * rows, rows)
            gx1.need(i)
            low[at, :] = gx1[at, :].astype(jnp.bfloat16)
            wa.need()
            go[...] = dot_nn(low[at, :], wa[:, 3 * hid :]).astype(jnp.bfloat16)
            keys = (i + 1) * rows
            for held in (seg_row, seg_col, q, o, lse, k, m):
                held.need(i)
            write_bias(bias, seg_col, seg_row, i, rows, keys)
            gq[...] = jnp.zeros(gq.shape, gq.dtype)
            if turn_index:
                total.middle(order[turn_index - 1])

            def one_head(index, unused):
                mask = lane // HEAD_DIM == index
                zero = jnp.bfloat16(0)
                query = jnp.where(mask, q[at, :], zero)
                grad = jnp.where(mask, go[...], zero)
                both = grad.astype(jnp.float32) * o[at, :].astype(jnp.float32)
                delta = jnp.sum(both, axis=-1, keepdims=True)
                scores = dot_nt(query, k[:keys, :]) + bias[:, :keys]
                prob = jnp.exp(scores - lse[index, at, :])
                grad_prob = dot_nt(grad, m[:keys, :])
                grad_score = (prob * (grad_prob - delta)).astype(jnp.bfloat16)
                part = dot_nn(grad_score, k[:keys, :])
                gq[...] = jnp.where(mask, part, gq[...])
                gk[:keys, :] += dot_tn(grad_score, query)
                gm[:keys, :] += dot_tn(prob.astype(jnp.bfloat16), grad)
                return unused

            lax.fori_loop(0, heads, one_head, 0)
            cosine.need(i)
            sine.need(i)
            cos, sin = cosine[at, :], sine[at, :]
            values = gm[at, :]
            if extra is None:
                values = 0.5 * values
                passed[at, :] = values
                passed.put(i)
            else:
                extra.need(i)
                values = values + extra[at, :]
            back = turn(gq[...] * HEAD_DIM**-0.5, cos, sin, True)
            g3[at, :hid] = back.astype(jnp.bfloat16)
            g3[at, hid : 2 * hid] = turn(gk[at, :], cos, sin, True).astype(jnp.bfloat16)
            g3[at, 2 * hid :] = values.astype(jnp.bfloat16)
            total.send(i, dot_nt(g3[at, :], wa[:, : 3 * hid]))
            jobs.advance((11.0, 17.5, 22.0, 25.0)[turn_index])
        total.middle(order[-1])
        cols = width // 4
        h.need()
        for j in range(4):
            cut = slice(j * cols, (j + 1) * cols)
            d_wa[cut, : 3 * hid] = dot_tn(h[:, cut], g3[...]).astype(jnp.bfloat16)
            d_wa[cut, 3 * hid :] = dot_tn(low[:, cut], o[...]).astype(jnp.bfloat16)
            d_wa.put(j)
        jobs.advance(30.0)
        gains.need()
        for turn_index, i in enumerate(order):
            total.last(i)
            jobs.advance((30.0, 30.0, 32.0, 37.0)[turn_index])
        gain_sum = jnp.zeros((1, width), jnp.float32)
        for i in order:
            at = pl.ds(i * rows, rows)
            x.need(i)
            stream = x[at, :].astype(jnp.float32)
            step, gain_sum = norm_back(
                gains[which : which + 1, :], total.total(i), stream, gain_sum
            )
            gx_held[at, :] = (gx1[at, :] + step).astype(gx_held.dtype)
            gx.put(i)
        gain[...] = gain_sum
        gain.put()
        jobs.finish()

    call.run(body)
    return SimpleNamespace(
        gx=gx.result,
        passed=passed.result if extra is None else None,
        gain=gain.result,
        d_wa=d_wa.result,
        carried=[job.result for job in carried],
    )


def transfers(number, jobs_of, plan):
    call = Call(number)
    carried = jobs_of(call)
    jobs = Jobs(carried, plan)

    def body():
        begin(call, None, jobs)
        jobs.finish()

    call.run(body)
    return [job.result for job in carried]


def leave_step(moved, grad, packs, turned, gains):
    call = Call(0)
    kept = [call.load(array, BLOCKS) for array in moved]
    kept_to = [call.store_from(held, held.shape, held.dtype, BLOCKS) for held in kept]
    grad = call.load(grad, BLOCKS)
    wide = call.store(grad.shape, jnp.float32, BLOCKS)
    shard, hid = packs[0].shape[0], packs[0].shape[1] // 4
    flag = call.flags(3 * len(packs))
    packs = [call.load(array) for array in packs]
    unpacked = [[call.give((shard, hid), pack.dtype) for _ in range(3)] for pack in packs]
    upright = [call.store((hid, shard), pack.dtype) for pack in packs]
    turned = [call.load(array) for array in turned]
    turned_to = [call.store(held.shape[::-1], held.dtype) for held in turned]
    gains = call.load(gains)
    gain_to = [call.store((1, shard), gains.dtype) for _ in range(4)]

    def body():
        call.start_loads()
        copies = []
        for at, pack in enumerate(packs):
            pack.need()
            for j in range(3):
                source = pack.at[:, j * hid : (j + 1) * hid]
                copies.append(
                    pltpu.make_async_copy(source, unpacked[at][j].ref, flag.at[3 * at + j])
                )
                copies[-1].start()
            upright[at][...] = pack[:, 3 * hid :].T
            upright[at].put()
        for held, target in zip(turned, turned_to):
            held.need()
            target[...] = held[...].T
            target.put()
        gains.need()
        for j, target in enumerate(gain_to):
            target[...] = gains[j : j + 1, :]
            target.put()
        rows = grad.shape[0] // BLOCKS
        for i in range(BLOCKS):
            at = pl.ds(i * rows, rows)
            grad.need(i)
            wide[at, :] = grad[at, :].astype(jnp.float32)
            wide.put(i)
            for held, target in zip(kept, kept_to):
                held.need(i)
                target.put(i)
        for copy in copies:
            copy.wait()

    call.run(body, False)
    return SimpleNamespace(
        kept=[target.result for target in kept_to],
        grad=wide.result,
        packs=[
            [part.result for part in parts] + [last.result]
            for parts, last in zip(unpacked, upright)
        ],
        turned=[target.result for target in turned_to],
        gains=[target.result.reshape(-1) for target in gain_to],
    )


def dealt_device(
    inputs,
    segment_ids,
    norm_attn_one,
    query_one,
    key_one,
    value_one,
    output_one,
    norm_ffn_one,
    gate_one,
    up_one,
    down_one,
    norm_attn_two,
    query_two,
    key_two,
    value_two,
    output_two,
    norm_ffn_two,
    gate_two,
    up_two,
    down_two,
    cotangent,
):
    parts, length, width = inputs.shape
    places = lax.axis_size(DP) * lax.axis_size(CTX)
    shard = width // places
    gain_rows = jnp.stack([norm_attn_one, norm_ffn_one, norm_attn_two, norm_ffn_two] * 2)
    half = HEAD_DIM // 2
    frequency = 10000.0 ** (-np.arange(half, dtype=np.float32) / np.float32(half))
    repeat = LANES // HEAD_DIM
    signs = np.concatenate([-np.ones(half), np.ones(half)])
    angle_row = np.zeros((8, LANES), np.float32)
    angle_row[0] = np.tile(frequency, 2 * repeat)
    angle_row[1] = np.tile(signs, repeat)

    def split(array):
        return array.reshape(places, shard, array.shape[-1])

    def deal(array):
        return array.reshape(parts, length, width)

    def opening(call):
        return Opening(
            call,
            inputs,
            segment_ids,
            (
                (query_one, key_one, value_one, output_one, gate_one.T, up_one.T, down_one),
                (query_two, key_two, value_two, output_two, gate_two.T, up_two.T, down_two),
            ),
            gain_rows,
            jnp.asarray(angle_row),
            places,
        )

    attn_one = attention_layer(
        1,
        None,
        None,
        None,
        None,
        0,
        None,
        lambda c, start: [Gather(c, held, places) for held in start.shards_one],
        ((2.0, 4.1), (14.3, 4.1), (26.6, 4.1)),
        opening,
    )
    start = attn_one.start
    x, wa_one, gains = start.deal.result, start.gather.result, start.gains.result
    tables = [table.result for table in start.tables()]
    ffn_one_w = attn_one.carried
    wa_two_shard = start.wa_two.result
    shards_two = [held.result for held in start.shards_two]
    ffn_one = feed_forward_layer(
        2,
        attn_one.x1,
        *ffn_one_w,
        gains,
        1,
        lambda c: [Gather(c, wa_two_shard, places, True), Gather(c, shards_two[0], places)],
        ((7.0, 4.0), (20.0, 4.1)),
    )
    wa_two, gate_two_w = ffn_one.carried
    attn_two = attention_layer(
        3,
        ffn_one.y,
        attn_one.v,
        wa_two,
        gains,
        2,
        tables,
        lambda c, start: [
            Gather(c, shards_two[1], places),
            Gather(c, shards_two[2], places, True),
        ],
        ((8.0, 3.0), (18.0, 3.0)),
    )
    ffn_two_w = (gate_two_w, *attn_two.carried)
    ffn_two = feed_forward_layer(
        4,
        attn_two.x1,
        *ffn_two_w,
        gains,
        3,
        lambda c: [Deal(c, cotangent, True)],
        ((9.5, 7.3),),
    )
    back_ffn_two = feed_forward_back(
        5,
        ffn_two.carried[0],
        attn_two.x1,
        ffn_two,
        *ffn_two_w,
        gains,
        3,
        lambda c, down_sum: [down_sum, Deal(c, deal(ffn_two.y_low), True)],
        ((13.0, 4.2), (10.0, 7.3)),
    )
    down_g2, out_two = back_ffn_two.carried

    grads_plan = ((10.0, 3.0), (25.0, 3.0))

    def ffn_grads(back):
        return lambda c: [Scatter(c, split(array)) for array in (back.d_gate, back.d_up)]

    back_attn_two = attention_back(
        6,
        back_ffn_two.gx1,
        ffn_one.y,
        attn_two,
        None,
        wa_two,
        gains,
        2,
        tables,
        ffn_grads(back_ffn_two),
        grads_plan,
    )
    gate_g2, up_g2 = back_attn_two.carried
    back_ffn_one = feed_forward_back(
        7,
        back_attn_two.gx,
        attn_one.x1,
        ffn_one,
        *ffn_one_w,
        gains,
        1,
        lambda c, down_sum: [
            Scatter(c, split(back_attn_two.d_wa)),
            down_sum,
            Deal(c, deal(ffn_one.y_low)),
        ],
        ((8.0, 5.8), (30.0, 4.2), (33.0, 33.1, 33.2, 37.0, 37.1, 37.2)),
    )
    packed_two, down_g1, out_one = back_ffn_one.carried
    back_attn_one = attention_back(
        8,
        back_ffn_one.gx1,
        x,
        attn_one,
        back_attn_two.passed,
        wa_one,
        gains,
        0,
        tables,
        ffn_grads(back_ffn_one),
        grads_plan,
    )
    gain_grads = jnp.concatenate(
        [back_attn_one.gain, back_ffn_one.gain, back_attn_two.gain, back_ffn_two.gain] * 2
    )
    gain_grads = jnp.transpose(gain_grads.reshape(-1, places, shard), (1, 0, 2))
    gain_shards, packed_one, grad = transfers(
        9,
        lambda c: [
            Scatter(c, gain_grads),
            Scatter(c, split(back_attn_one.d_wa)),
            Deal(c, deal(back_attn_one.gx)),
        ],
        ((4.0, 0.1), (7.0, 5.8), (6.0, 4.0)),
    )
    final = leave_step(
        (out_one, out_two),
        grad,
        (packed_one, packed_two),
        back_attn_one.carried + [down_g1, gate_g2, up_g2, down_g2],
        gain_shards,
    )
    gate_g1, up_g1, down_g1, gate_g2, up_g2, down_g2 = final.turned
    return (
        deal(final.kept[0]),
        deal(final.kept[1]),
        deal(final.grad),
        final.gains[0],
        *final.packs[0],
        final.gains[1],
        gate_g1.T,
        up_g1.T,
        down_g1,
        final.gains[2],
        *final.packs[1],
        final.gains[3],
        gate_g2.T,
        up_g2.T,
        down_g2,
    )


def solution(mesh):
    placed = (
        P(DP, CTX, None),
        P(DP, None),
        P((DP, CTX)),
        P((DP, CTX), MP),
        P((DP, CTX), MP),
        P((DP, CTX), MP),
        P(MP, (DP, CTX)),
        P((DP, CTX)),
        P((DP, CTX), MP),
        P((DP, CTX), MP),
        P(MP, (DP, CTX)),
        P((DP, CTX)),
        P((DP, CTX), MP),
        P((DP, CTX), MP),
        P((DP, CTX), MP),
        P(MP, (DP, CTX)),
        P((DP, CTX)),
        P((DP, CTX), MP),
        P((DP, CTX), MP),
        P(MP, (DP, CTX)),
        P(DP, CTX, None),
    )
    sizes = dict(mesh.shape)

    def per_device(*operands):
        fits = sizes[DP] == 2 and sizes[MP] == 4 and operands[0].shape[0] == sizes[CTX]
        return (dealt_device if fits else on_device)(*operands)

    return jax.shard_map(
        per_device,
        mesh=mesh,
        in_specs=placed,
        out_specs=(
            P(DP, CTX, None),
            P(DP, CTX, None),
            P(DP, CTX, None),
            P((DP, CTX)),
            P((DP, CTX), MP),
            P((DP, CTX), MP),
            P((DP, CTX), MP),
            P(MP, (DP, CTX)),
            P((DP, CTX)),
            P((DP, CTX), MP),
            P((DP, CTX), MP),
            P(MP, (DP, CTX)),
            P((DP, CTX)),
            P((DP, CTX), MP),
            P((DP, CTX), MP),
            P((DP, CTX), MP),
            P(MP, (DP, CTX)),
            P((DP, CTX)),
            P((DP, CTX), MP),
            P((DP, CTX), MP),
            P(MP, (DP, CTX)),
        ),
        check_vma=False,
    )
```

```python
import functools
import math
from types import SimpleNamespace

import jax
import jax.numpy as jnp
import numpy as np
from jax import lax
from jax.experimental import pallas as pl
from jax.experimental.pallas import tpu as pltpu
from jax.sharding import PartitionSpec as P

MESH = pl.DeviceIdType.MESH

HEAD_DIM = 64
DP, CTX, MP = "dp", "ctx", "mp"


epsilon = 1e-05
neg_large = -1e30


def project(left_operand, right_operand):
    return jnp.einsum(
        "sbd,de->sbe", left_operand, right_operand, preferred_element_type=jnp.float32
    )


def project_back(left_operand, right_operand):
    return jnp.einsum(
        "sbe,de->sbd", left_operand, right_operand, preferred_element_type=jnp.float32
    )


def weight_term(left_operand, right_operand):
    return jnp.einsum(
        "sbd,sbe->de", left_operand, right_operand, preferred_element_type=jnp.float32
    )


def head_sum_kernel(
    chunks, x_ref, o_ref, near, half_sum, far, send_a, recv_a, send_b, recv_b, send_c, recv_c
):
    dp, ctx, mp = (lax.axis_index(name) for name in (DP, CTX, MP))
    side = lax.rem(mp, 2)
    pair = (dp, ctx, mp + 1 - 2 * side)
    cross = (dp, ctx, lax.rem(mp + 2, 4))
    barrier = pltpu.get_barrier_semaphore()
    for peer in (pair, cross):
        pl.semaphore_signal(barrier, inc=1, device_id=peer, device_id_type=MESH)
    pl.semaphore_wait(barrier, 2)
    rows = x_ref.shape[0] // chunks
    half = rows // 2

    def copy(source, target, send, recv, i, peer):
        return pltpu.make_async_remote_copy(
            src_ref=source,
            dst_ref=target,
            send_sem=send.at[i],
            recv_sem=recv.at[i],
            device_id=peer,
            device_id_type=MESH,
        )

    def first(i):
        theirs = x_ref.at[pl.ds(i * rows + (1 - side) * half, half)]
        return copy(theirs, near.at[i], send_a, recv_a, i, pair)

    def second(i):
        return copy(half_sum.at[i], far.at[i], send_b, recv_b, i, cross)

    def third(i):
        mine = o_ref.at[pl.ds(i * rows + side * half, half)]
        return copy(mine, mine, send_c, recv_c, i, pair)

    for i in range(chunks):
        first(i).start()
    for i in range(chunks):
        first(i).wait()
        mine = x_ref[pl.ds(i * rows + side * half, half)].astype(jnp.float32)
        half_sum[i] = (mine + near[i].astype(jnp.float32)).astype(jnp.bfloat16)
        second(i).start()
    for i in range(chunks):
        second(i).wait()
        total = half_sum[i].astype(jnp.float32) + far[i].astype(jnp.float32)
        o_ref[pl.ds(i * rows + side * half, half)] = total.astype(jnp.bfloat16)
        third(i).start()
    for i in range(chunks):
        third(i).wait()


def head_sum(partial_sum, number):
    flat = partial_sum.astype(jnp.bfloat16).reshape(-1, partial_sum.shape[-1])
    count, width = flat.shape
    chunks = 4
    half = count // chunks // 2
    total = pl.pallas_call(
        functools.partial(head_sum_kernel, chunks),
        out_shape=jax.ShapeDtypeStruct((count, width), jnp.bfloat16),
        in_specs=[pl.BlockSpec(memory_space=pltpu.VMEM)],
        out_specs=pl.BlockSpec(memory_space=pltpu.VMEM),
        scratch_shapes=[pltpu.VMEM((chunks, half, width), jnp.bfloat16)] * 3
        + [pltpu.SemaphoreType.DMA((chunks,))] * 6,
        compiler_params=pltpu.CompilerParams(
            collective_id=0, has_side_effects=True, vmem_limit_bytes=32 << 20
        ),
    )(flat)
    return total.reshape(partial_sum.shape).astype(jnp.float32)


def head_total(partial_sum):
    return head_sum(partial_sum, 0)


def head_back(partial_sum):
    return head_sum(partial_sum, 0)


def rotary_tables(first_place, count_of_rows):
    half_width = HEAD_DIM // 2
    frequency = 10000.0 ** (-jnp.arange(half_width, dtype=jnp.float32) / half_width)
    places = (first_place + jnp.arange(count_of_rows, dtype=jnp.int32)).astype(jnp.float32)
    angles = places[:, None] * frequency[None, :]
    return (jnp.cos(angles)[None, :, None, :], jnp.sin(angles)[None, :, None, :])


def rotate(split_heads, cosine, sine_table):
    half_width = HEAD_DIM // 2
    first_half = split_heads[..., :half_width]
    second_half = split_heads[..., half_width:]
    return jnp.concatenate(
        [
            first_half * cosine - second_half * sine_table,
            first_half * sine_table + second_half * cosine,
        ],
        axis=-1,
    )


def rotate_back(split_heads, cosine, sine_table):
    half_width = HEAD_DIM // 2
    first_half = split_heads[..., :half_width]
    second_half = split_heads[..., half_width:]
    return jnp.concatenate(
        [
            first_half * cosine + second_half * sine_table,
            second_half * cosine - first_half * sine_table,
        ],
        axis=-1,
    )


def norm_forward(stream, gain_row):
    inverse = lax.rsqrt(jnp.mean(stream * stream, axis=-1, keepdims=True) + epsilon)
    normed = (stream * inverse * gain_row.astype(jnp.float32)).astype(jnp.bfloat16)
    return (normed, inverse)


def norm_backward(grad_normed, stream, inverse, gain_row):
    scaled = stream * inverse
    grad_scaled = grad_normed * gain_row.astype(jnp.float32)
    gain_grad = jnp.sum(grad_normed * scaled, axis=(0, 1))
    grad_stream = inverse * (
        grad_scaled - scaled * jnp.mean(grad_scaled * scaled, axis=-1, keepdims=True)
    )
    return (grad_stream, gain_grad)


def block_grads(
    query_block,
    grad_block,
    lse_block,
    delta_block,
    query_places,
    query_document_ids,
    key_block,
    value_block,
    key_places,
    key_segments,
):
    score_scale = HEAD_DIM ** (-0.5)
    scores = (
        jnp.einsum("sqhe,skhe->shqk", query_block, key_block, preferred_element_type=jnp.float32)
        * score_scale
    )
    visible = (
        (key_places[None, :] <= query_places[:, None])[None]
        & (key_segments[:, None, :] == query_document_ids[:, :, None])
    )[:, None]
    probabilities = jnp.where(visible, jnp.exp(scores - lse_block[..., None]), 0.0)
    grad_probs = jnp.einsum(
        "sqhe,skhe->shqk", grad_block, value_block, preferred_element_type=jnp.float32
    )
    grad_scores = (probabilities * (grad_probs - delta_block[..., None]) * score_scale).astype(
        jnp.bfloat16
    )
    query_grad = jnp.einsum(
        "shqk,skhe->sqhe", grad_scores, key_block, preferred_element_type=jnp.float32
    )
    key_grad = jnp.einsum(
        "shqk,sqhe->skhe", grad_scores, query_block, preferred_element_type=jnp.float32
    )
    value_grad = jnp.einsum(
        "shqk,sqhe->skhe",
        probabilities.astype(jnp.bfloat16),
        grad_block,
        preferred_element_type=jnp.float32,
    )
    return (query_grad, key_grad, value_grad)


def attend_forward(queries, key_rows, value_rows, segments, query_places):
    seq_count, count_of_rows, head_count, head_width = queries.shape
    score_scale = head_width ** (-0.5)
    query_document_ids = lax.dynamic_slice_in_dim(segments, query_places[0], count_of_rows, 1)
    last_query = query_places[count_of_rows - 1]
    initial = (
        jnp.full((seq_count, head_count, count_of_rows), neg_large, jnp.float32),
        jnp.zeros((seq_count, head_count, count_of_rows), jnp.float32),
        jnp.zeros((seq_count, count_of_rows, head_count, head_width), jnp.float32),
    )
    key_piece = lax.all_gather(key_rows, CTX, axis=1, tiled=True)
    value_piece = lax.all_gather(value_rows, CTX, axis=1, tiled=True)
    piece_rows = key_piece.shape[1]
    block_rows = math.gcd(piece_rows, 512)
    key_split = key_piece.reshape(seq_count, piece_rows, head_count, head_width)
    value_split = value_piece.reshape(seq_count, piece_rows, head_count, head_width)

    def absorb_visit(running, block_index):
        first_key = block_index * block_rows

        def absorb_compute(current):
            row_max, row_total, weighted = current
            key_block = lax.dynamic_slice_in_dim(key_split, first_key, block_rows, 1)
            value_block = lax.dynamic_slice_in_dim(value_split, first_key, block_rows, 1)
            key_places = first_key + jnp.arange(block_rows, dtype=jnp.int32)
            key_segments = lax.dynamic_slice_in_dim(segments, first_key, block_rows, 1)
            scores = (
                jnp.einsum(
                    "sqhe,skhe->shqk", queries, key_block, preferred_element_type=jnp.float32
                )
                * score_scale
            )
            visible = (
                (key_places[None, :] <= query_places[:, None])[None]
                & (key_segments[:, None, :] == query_document_ids[:, :, None])
            )[:, None]
            new_max = jnp.maximum(row_max, jnp.max(jnp.where(visible, scores, neg_large), axis=-1))
            exponent = jnp.where(visible, jnp.exp(scores - new_max[..., None]), 0.0)
            factor = jnp.exp(row_max - new_max)
            new_total = row_total * factor + jnp.sum(exponent, axis=-1)
            update = jnp.einsum(
                "shqk,skhe->sqhe",
                exponent.astype(jnp.bfloat16),
                value_block,
                preferred_element_type=jnp.float32,
            )
            new_weighted = weighted * jnp.transpose(factor, (0, 2, 1))[..., None] + update
            return (new_max, new_total, new_weighted)

        def absorb_keep(current):
            return current

        return (lax.cond(first_key <= last_query, absorb_compute, absorb_keep, running), None)

    result, unused = lax.scan(
        absorb_visit, initial, jnp.arange(piece_rows // block_rows, dtype=jnp.int32)
    )
    row_max, row_total, weighted = result
    attended = weighted / jnp.transpose(row_total, (0, 2, 1))[..., None]
    return (attended, row_max + jnp.log(row_total))


def attend_back_gather(
    queries, grad_attended, log_normalizer, row_delta, key_rows, value_rows, segments, query_places
):
    seq_count, count_of_rows, head_count, head_width = queries.shape
    query_document_ids = lax.dynamic_slice_in_dim(segments, query_places[0], count_of_rows, 1)
    last_query = query_places[count_of_rows - 1]
    all_keys, all_values = (
        lax.all_gather(key_rows, CTX, axis=1, tiled=True),
        lax.all_gather(value_rows, CTX, axis=1, tiled=True),
    )
    length = all_keys.shape[1]
    block_rows = math.gcd(length, 512)
    key_split = all_keys.reshape(seq_count, length, head_count, head_width)
    value_split = all_values.reshape(seq_count, length, head_count, head_width)
    initial = (
        jnp.zeros((seq_count, count_of_rows, head_count, head_width), jnp.float32),
        jnp.zeros((seq_count, length, head_count, head_width), jnp.float32),
        jnp.zeros((seq_count, length, head_count, head_width), jnp.float32),
    )

    def attend_visit(state_now, block_index):
        first_key = block_index * block_rows

        def attend_compute(current):
            query_acc, key_acc, value_acc = current
            key_block = lax.dynamic_slice_in_dim(key_split, first_key, block_rows, 1)
            value_block = lax.dynamic_slice_in_dim(value_split, first_key, block_rows, 1)
            key_places = first_key + jnp.arange(block_rows, dtype=jnp.int32)
            key_segments = lax.dynamic_slice_in_dim(segments, first_key, block_rows, 1)
            query_part, key_part, value_part = block_grads(
                queries,
                grad_attended,
                log_normalizer,
                row_delta,
                query_places,
                query_document_ids,
                key_block,
                value_block,
                key_places,
                key_segments,
            )
            key_acc = lax.dynamic_update_slice_in_dim(key_acc, key_part, first_key, 1)
            value_acc = lax.dynamic_update_slice_in_dim(value_acc, value_part, first_key, 1)
            return (query_acc + query_part, key_acc, value_acc)

        def attend_keep(current):
            return current

        return (lax.cond(first_key <= last_query, attend_compute, attend_keep, state_now), None)

    totals, unused = lax.scan(
        attend_visit, initial, jnp.arange(length // block_rows, dtype=jnp.int32)
    )
    query_grad, key_grad, value_grad = totals
    key_home, value_home = (
        lax.psum_scatter(
            key_grad.reshape(seq_count, length, -1).astype(jnp.bfloat16),
            CTX,
            scatter_dimension=1,
            tiled=True,
        ).astype(jnp.float32),
        lax.psum_scatter(
            value_grad.reshape(seq_count, length, -1).astype(jnp.bfloat16),
            CTX,
            scatter_dimension=1,
            tiled=True,
        ).astype(jnp.float32),
    )
    split_shape = (seq_count, count_of_rows, head_count, head_width)
    return (query_grad, key_home.reshape(split_shape), value_home.reshape(split_shape))


def forward_layer(stream, first_values, weights, segments, cosine, sine_table, query_places):
    norm_attn, w_query, w_key, w_value, w_output, norm_ffn, w_gate, w_up, w_down = weights
    seq_count, count_of_rows, model_width = stream.shape
    head_count = w_query.shape[1] // HEAD_DIM
    split_shape = (seq_count, count_of_rows, head_count, HEAD_DIM)
    normed, inverse_one = norm_forward(stream, norm_attn)
    queries = rotate(project(normed, w_query).reshape(split_shape), cosine, sine_table).astype(
        jnp.bfloat16
    )
    key_rows = (
        rotate(project(normed, w_key).reshape(split_shape), cosine, sine_table)
        .astype(jnp.bfloat16)
        .reshape(seq_count, count_of_rows, -1)
    )
    own_values = project(normed, w_value)
    if first_values is None:
        mixed = own_values.astype(jnp.bfloat16)
    else:
        mixed = (0.5 * own_values + 0.5 * first_values).astype(jnp.bfloat16)
    attended, log_normalizer = attend_forward(queries, key_rows, mixed, segments, query_places)
    attended_low = attended.reshape(seq_count, count_of_rows, -1).astype(jnp.bfloat16)
    hidden_one = stream + head_total(project(attended_low, w_output))
    normed_two, inverse_two = norm_forward(hidden_one, norm_ffn)
    gate_values = project(normed_two, w_gate)
    up_values = project(normed_two, w_up)
    activated = (jax.nn.silu(gate_values) * up_values).astype(jnp.bfloat16)
    result = hidden_one + head_total(project(activated, w_down))
    saved_state = (
        stream,
        inverse_one,
        normed,
        queries,
        key_rows,
        mixed,
        attended,
        log_normalizer,
        attended_low,
        hidden_one,
        inverse_two,
        normed_two,
        gate_values,
        up_values,
        activated,
    )
    return (result, saved_state, own_values)


def backward_layer(
    grad_out, value_extra, saved_state, weights, segments, cosine, sine_table, query_places, mixes
):
    (
        stream,
        inverse_one,
        normed,
        queries,
        key_rows,
        mixed,
        attended,
        log_normalizer,
        attended_low,
        hidden_one,
        inverse_two,
        normed_two,
        gate_values,
        up_values,
        activated,
    ) = saved_state
    norm_attn, w_query, w_key, w_value, w_output, norm_ffn, w_gate, w_up, w_down = weights
    seq_count, count_of_rows, head_count, head_width = queries.shape
    grad_branch = grad_out.astype(jnp.bfloat16)
    down_grad = weight_term(activated, grad_branch)
    grad_active = project_back(grad_branch, w_down)
    gate_sigmoid = jax.nn.sigmoid(gate_values)
    grad_gate = (
        grad_active * up_values * gate_sigmoid * (1.0 + gate_values * (1.0 - gate_sigmoid))
    ).astype(jnp.bfloat16)
    grad_up = (grad_active * gate_values * gate_sigmoid).astype(jnp.bfloat16)
    gate_grad = weight_term(normed_two, grad_gate)
    up_grad = weight_term(normed_two, grad_up)
    grad_normed_two = head_back(project_back(grad_gate, w_gate) + project_back(grad_up, w_up))
    grad_norm_two, ffn_gain_grad = norm_backward(grad_normed_two, hidden_one, inverse_two, norm_ffn)
    grad_hidden = grad_out + grad_norm_two
    grad_attn = grad_hidden.astype(jnp.bfloat16)
    output_grad = weight_term(attended_low, grad_attn)
    grad_attended = (
        project_back(grad_attn, w_output)
        .astype(jnp.bfloat16)
        .reshape(seq_count, count_of_rows, head_count, head_width)
    )
    row_delta = jnp.transpose(
        jnp.sum(grad_attended.astype(jnp.float32) * attended, axis=-1), (0, 2, 1)
    )
    query_rot, key_rot, value_mix = attend_back_gather(
        queries, grad_attended, log_normalizer, row_delta, key_rows, mixed, segments, query_places
    )
    query_low = (
        rotate_back(query_rot, cosine, sine_table)
        .astype(jnp.bfloat16)
        .reshape(seq_count, count_of_rows, -1)
    )
    key_low = (
        rotate_back(key_rot, cosine, sine_table)
        .astype(jnp.bfloat16)
        .reshape(seq_count, count_of_rows, -1)
    )
    value_mix = value_mix.reshape(seq_count, count_of_rows, -1)
    if mixes:
        value_low = (0.5 * value_mix).astype(jnp.bfloat16)
        passed_on = 0.5 * value_mix
    else:
        value_low = (value_mix + value_extra).astype(jnp.bfloat16)
        passed_on = value_extra
    query_grad = weight_term(normed, query_low)
    key_grad = weight_term(normed, key_low)
    value_grad = weight_term(normed, value_low)
    grad_normed = head_back(
        project_back(query_low, w_query)
        + project_back(key_low, w_key)
        + project_back(value_low, w_value)
    )
    grad_norm_one, attn_gain_grad = norm_backward(grad_normed, stream, inverse_one, norm_attn)
    grad_stream = grad_hidden + grad_norm_one
    grad_terms = (
        attn_gain_grad,
        query_grad,
        key_grad,
        value_grad,
        output_grad,
        ffn_gain_grad,
        gate_grad,
        up_grad,
        down_grad,
    )
    return (grad_stream, passed_on, grad_terms)


def on_device(
    inputs,
    segment_ids,
    norm_attn_one,
    query_one,
    key_one,
    value_one,
    output_one,
    norm_ffn_one,
    gate_one,
    up_one,
    down_one,
    norm_attn_two,
    query_two,
    key_two,
    value_two,
    output_two,
    norm_ffn_two,
    gate_two,
    up_two,
    down_two,
    cotangent,
):
    def gather_layer(gain_attn, query, key, value, output, gain_ffn, gate, up, down):
        both = (DP, CTX)
        packed = jnp.concatenate([query, key, value, output.T, gate, up, down.T], axis=1)
        whole = lax.all_gather(packed, both, axis=0, tiled=True)
        gains = lax.all_gather(jnp.stack([gain_attn, gain_ffn]), both, axis=1, tiled=True)
        cuts = []
        for part in (query, key, value, output.T, gate, up, down.T):
            cuts.append((cuts[-1] if cuts else 0) + part.shape[1])
        w_q, w_k, w_v, w_o, w_g, w_u, w_d = jnp.split(whole, cuts[:-1], axis=1)
        return (gains[0], w_q, w_k, w_v, w_o.T, gains[1], w_g, w_u, w_d.T)

    def scatter_layer(grads, outs):
        both = (DP, CTX)
        gain_attn, query, key, value, output, gain_ffn, gate, up, down = grads
        pieces = [query, key, value, output.T, gate, up, down.T]
        packed = jnp.concatenate([part.astype(jnp.bfloat16) for part in pieces], axis=1)
        mine = lax.psum_scatter(packed, both, scatter_dimension=0, tiled=True)
        gains = lax.psum_scatter(
            jnp.stack([gain_attn, gain_ffn]).astype(jnp.bfloat16),
            both,
            scatter_dimension=1,
            tiled=True,
        ).astype(jnp.float32)
        cuts = []
        for part in pieces:
            cuts.append((cuts[-1] if cuts else 0) + part.shape[1])
        g_q, g_k, g_v, g_o, g_g, g_u, g_d = (
            part.astype(jnp.float32) for part in jnp.split(mine, cuts[:-1], axis=1)
        )
        return (gains[0], g_q, g_k, g_v, g_o.T, gains[1], g_g, g_u, g_d.T)

    gathered = gather_layer(
        norm_attn_one,
        query_one,
        key_one,
        value_one,
        output_one,
        norm_ffn_one,
        gate_one,
        up_one,
        down_one,
    ) + gather_layer(
        norm_attn_two,
        query_two,
        key_two,
        value_two,
        output_two,
        norm_ffn_two,
        gate_two,
        up_two,
        down_two,
    )
    weights_one = gathered[:9]
    weights_two = gathered[9:]
    seq_count, count_of_rows, model_width = inputs.shape
    query_places = lax.axis_index(CTX) * count_of_rows + jnp.arange(
        count_of_rows, dtype=jnp.int32
    )
    cosine, sine_table = rotary_tables(query_places[0], count_of_rows)
    layer_one, saved_one, first_values = forward_layer(
        inputs.astype(jnp.float32), None, weights_one, segment_ids, cosine, sine_table, query_places
    )
    layer_two, saved_two, unused = forward_layer(
        layer_one, first_values, weights_two, segment_ids, cosine, sine_table, query_places
    )
    grad_middle, value_extra, grads_two = backward_layer(
        cotangent.astype(jnp.float32),
        None,
        saved_two,
        weights_two,
        segment_ids,
        cosine,
        sine_table,
        query_places,
        True,
    )
    grad_input, unused_extra, grads_one = backward_layer(
        grad_middle,
        value_extra,
        saved_one,
        weights_one,
        segment_ids,
        cosine,
        sine_table,
        query_places,
        False,
    )
    totals = scatter_layer(grads_one, None) + scatter_layer(grads_two, None)
    return (
        layer_one.astype(jnp.bfloat16),
        layer_two.astype(jnp.bfloat16),
        grad_input,
        totals[0],
        totals[1],
        totals[2],
        totals[3],
        totals[4],
        totals[5],
        totals[6],
        totals[7],
        totals[8],
        totals[9],
        totals[10],
        totals[11],
        totals[12],
        totals[13],
        totals[14],
        totals[15],
        totals[16],
        totals[17],
    )


class Raw:
    def __init__(self, call, kind, index):
        self.call, self.kind, self.index = call, kind, index

    @property
    def ref(self):
        return self.call.refs[self.kind][self.index]

    @property
    def at(self):
        return self.ref.at

    @property
    def result(self):
        return self.call.results[self.index]


def cut_rows(ref, blocks, i):
    if blocks == 1:
        return ref
    rows = ref.shape[-2] // blocks
    part = pl.ds(i * rows, rows)
    return ref.at[part] if len(ref.shape) == 2 else ref.at[:, part]


class Store:
    def __init__(self, call, held, shape, dtype, blocks):
        self.held, self.blocks = held, blocks
        self.out = call.give(shape, dtype)
        self.flag = call.flags(blocks)
        call.stores.append(self)

    def copy(self, i):
        return pltpu.make_async_copy(
            cut_rows(self.held.ref, self.blocks, i),
            cut_rows(self.out.ref, self.blocks, i),
            self.flag.at[i],
        )

    def put(self, i=None):
        for k in range(self.blocks) if i is None else (i,):
            self.copy(k).start()

    def finish(self):
        for i in range(self.blocks):
            self.copy(i).wait()

    @property
    def result(self):
        return self.out.result


class Held:
    def __init__(self, call, shape, dtype):
        self.call, self.shape, self.dtype = call, shape, dtype
        self.slot = call.scratch_slot(pltpu.VMEM(shape, dtype))
        self.source = self.out = None
        self.blocks, self.waited = 1, set()

    @property
    def ref(self):
        return self.call.refs[2][self.slot]

    @property
    def at(self):
        return self.ref.at

    def __getitem__(self, key):
        return self.ref[key]

    def __setitem__(self, key, value):
        self.ref[key] = value

    def load_copy(self, i):
        return pltpu.make_async_copy(
            cut_rows(self.source.ref, self.blocks, i),
            cut_rows(self.ref, self.blocks, i),
            self.flag.at[i],
        )

    def need(self, i=None):
        if self.source is None:
            return
        for k in range(self.blocks) if i is None or self.blocks == 1 else (i,):
            if k not in self.waited:
                self.waited.add(k)
                self.load_copy(k).wait()

    def put(self, i=None):
        self.out.put(i)

    @property
    def result(self):
        return self.out.result


class Call:
    def __init__(self, number):
        self.number = number
        self.operands, self.shapes, self.scratch = [], [], []
        self.loads, self.stores, self.jobs = [], [], []
        self.far = self.in_turn = False

    def take(self, array):
        self.operands.append(array)
        return Raw(self, 0, len(self.operands) - 1)

    def give(self, shape, dtype):
        self.shapes.append(jax.ShapeDtypeStruct(shape, dtype))
        return Raw(self, 1, len(self.shapes) - 1)

    def scratch_slot(self, kind):
        self.scratch.append(kind)
        return len(self.scratch) - 1

    def flags(self, count):
        return Raw(self, 2, self.scratch_slot(pltpu.SemaphoreType.DMA((count,))))

    def hold(self, shape, dtype):
        return Held(self, shape, dtype)

    def load(self, array, blocks=1):
        held = Held(self, array.shape, array.dtype)
        self.load_into(held, self.take(array), blocks)
        self.loads.append(held)
        return held

    def load_into(self, held, source, blocks):
        held.source, held.blocks, held.flag = source, blocks, self.flags(blocks)

    def store(self, shape, dtype, blocks=1):
        held = Held(self, shape, dtype)
        held.out = Store(self, held, shape, dtype, blocks)
        return held

    def store_from(self, held, shape, dtype, blocks=1):
        return Store(self, held, shape, dtype, blocks)

    def start_loads(self, backward=False):
        if self.in_turn:
            for held in self.loads:
                for k in range(held.blocks):
                    held.load_copy(k).start()
            return
        for k in range(max([held.blocks for held in self.loads], default=0)):
            for held in self.loads:
                if k < held.blocks:
                    held.load_copy(held.blocks - 1 - k if backward else k).start()

    def run(self, body, remote_ops=True):
        ins, outs = len(self.operands), len(self.operands) + len(self.shapes)

        def kernel(*refs):
            self.refs = (refs[:ins], refs[ins:outs], refs[outs:])
            for held in self.loads:
                held.waited = set()
            body()
            for held in self.loads:
                held.need()
            for store in self.stores:
                store.finish()

        space = pl.BlockSpec(memory_space=pltpu.HBM)
        self.results = pl.pallas_call(
            kernel,
            out_shape=tuple(self.shapes),
            in_specs=[space] * ins,
            out_specs=(space,) * len(self.shapes),
            scratch_shapes=self.scratch,
            compiler_params=pltpu.CompilerParams(
                has_side_effects=remote_ops,
                vmem_limit_bytes=62 << 20,
                collective_id=self.number if remote_ops else None,
            ),
        )(*self.operands)
        self.refs = None


class Place:
    def __init__(self):
        self.dp, self.ctx, self.mp = (lax.axis_index(a) for a in (DP, CTX, MP))
        self.ctx_size = lax.axis_size(CTX)
        self.side = lax.rem(self.mp, 2)
        self.pair = (self.dp, self.ctx, self.mp + 1 - 2 * self.side)
        self.cross = (self.dp, self.ctx, lax.rem(self.mp + 2, 4))
        self.other = (1 - self.dp, self.ctx, self.mp)

    def ahead(self, step):
        return lax.rem(self.ctx + step, self.ctx_size)

    def behind(self, step):
        return lax.rem(self.ctx + self.ctx_size - step, self.ctx_size)

    def along(self, index):
        return (self.dp, index, self.mp)

    def peers(self, far):
        peers = [self.pair, self.cross]
        if far:
            peers.append(self.other)
            peers += [self.along(self.ahead(s)) for s in range(1, self.ctx_size)]
        return peers

    def greet(self, far):
        barrier = pltpu.get_barrier_semaphore()
        for peer in self.peers(far):
            pl.semaphore_signal(barrier, inc=1, device_id=peer, device_id_type=MESH)

    def enter(self, far):
        pl.semaphore_wait(pltpu.get_barrier_semaphore(), len(self.peers(far)))


def remote(source, target, send, recv, peer):
    return pltpu.make_async_remote_copy(
        src_ref=source,
        dst_ref=target,
        send_sem=send,
        recv_sem=recv,
        device_id=peer,
        device_id_type=MESH,
    )


class HeadSum:
    def __init__(self, call, blocks, rows, width):
        self.half = rows // 2
        self.part = call.hold((blocks, rows, width), jnp.bfloat16)
        self.near, self.far, self.rest = (
            call.hold((blocks, rows // 2, width), jnp.bfloat16) for _ in range(3)
        )
        self.sa, self.ra, self.sb, self.rb, self.sc, self.rc = (
            call.flags(blocks) for _ in range(6)
        )

    def bind(self, place):
        self.place = place

    def own(self):
        return pl.ds(pl.multiple_of(self.place.side * self.half, self.half), self.half)

    def theirs(self):
        start = (1 - self.place.side) * self.half
        return pl.ds(pl.multiple_of(start, self.half), self.half)

    def first(self, i):
        source = self.part.at[i, self.theirs()]
        return remote(source, self.near.at[i], self.sa.at[i], self.ra.at[i], self.place.pair)

    def second(self, i):
        return remote(
            self.near.at[i], self.far.at[i], self.sb.at[i], self.rb.at[i], self.place.cross
        )

    def third(self, i):
        return remote(
            self.far.at[i], self.rest.at[i], self.sc.at[i], self.rc.at[i], self.place.pair
        )

    def send(self, i, partial_rows):
        self.part[i] = partial_rows.astype(jnp.bfloat16)
        self.first(i).start()

    def middle(self, i):
        self.first(i).wait()
        mine = self.part[i, self.own()].astype(jnp.float32)
        self.near[i] = (mine + self.near[i].astype(jnp.float32)).astype(jnp.bfloat16)
        self.second(i).start()

    def last(self, i):
        self.second(i).wait()
        total = self.near[i].astype(jnp.float32) + self.far[i].astype(jnp.float32)
        self.far[i] = total.astype(jnp.bfloat16)
        self.third(i).start()

    def total(self, i):
        self.third(i).wait()
        self.part[i, self.own()] = self.far[i]
        self.part[i, self.theirs()] = self.rest[i]
        return self.part[i].astype(jnp.float32)


class QuarterSum(HeadSum):
    def __init__(self, call, blocks, rows, width):
        self.half, self.quarter = rows // 2, rows // 4
        self.part = call.hold((blocks, rows, width), jnp.bfloat16)
        self.near = call.hold((blocks, rows // 2, width), jnp.bfloat16)
        self.far = call.hold((blocks, rows // 4, width), jnp.bfloat16)
        self.out = call.store((blocks, rows // 4, width), jnp.bfloat16)
        self.sa, self.ra, self.sb, self.rb = (call.flags(blocks) for _ in range(4))

    def rows_of(self, index):
        return pl.ds(pl.multiple_of(index * self.quarter, self.quarter), self.quarter)

    def second(self, i):
        source = self.near.at[i, self.rows_of(1 - self.place.mp // 2)]
        return remote(source, self.far.at[i], self.sb.at[i], self.rb.at[i], self.place.cross)

    def last(self, i):
        self.second(i).wait()
        mine = self.near[i, self.rows_of(self.place.mp // 2)].astype(jnp.float32)
        self.out[i] = (mine + self.far[i].astype(jnp.float32)).astype(jnp.bfloat16)


class Gather:
    def __init__(self, call, shard, places, swap=False):
        self.parts = lax.axis_size(CTX)
        call.far = True
        if isinstance(shard, Held):
            self.shard = shard
        else:
            self.shard = call.load(shard)
            call.loads.insert(0, call.loads.pop())
        self.whole = call.give((places,) + shard.shape, shard.dtype)
        self.zs, self.zr, self.ys, self.yr = (call.flags(self.parts) for _ in range(4))
        self.l, self.ss, self.sr = (call.flags(1) for _ in range(3))
        self.relayed = self.parts == 4
        self.swap = swap and self.relayed
        self.order = (2, 1, 3) if self.relayed else tuple(range(self.parts - 1, 0, -1))
        self.steps = len(self.order)

    def bind(self, place):
        self.place, self.crossed = place, False

    def slot(self, dp, ctx):
        return self.whole.at[dp * self.parts + ctx]

    def local(self):
        p = self.place
        return pltpu.make_async_copy(self.shard.ref, self.slot(p.dp, p.ctx), self.l.at[0])

    def along(self, s):
        p = self.place
        target = self.slot(p.dp, p.ctx)
        return remote(self.shard.ref, target, self.zs.at[s], self.zr.at[s], p.along(p.ahead(s)))

    def direct(self, s, act):
        if self.relayed and s != 2:
            pl.when(self.place.ctx != (0 if s == 3 else 3))(lambda: act(self.along(s)))
        else:
            act(self.along(s))

    def relay(self, act):
        p = self.place
        block = self.slot(p.dp, p.behind(2))
        for middle, end, s in ((2, 3, 3), (1, 0, 1)):
            copy = remote(block, block, self.zs.at[0], self.zr.at[s], p.along(end))
            pl.when(p.ctx == middle)(lambda copy=copy: act(copy))

    def across(self, s):
        p = self.place
        block = self.slot(p.dp, p.behind(s))
        source = self.shard.ref if s == 0 else block
        return remote(source, block, self.ys.at[s], self.yr.at[s], p.other)

    def arrive(self, s):
        p = self.place
        block = self.slot(1 - p.dp, p.behind(s))
        return remote(block, block, self.ys.at[s], self.yr.at[s], p.other)

    def when_crossing(self, s, act):
        if self.swap and s in (1, 3):
            pl.when(lax.rem(self.place.ctx, 2) == (0 if s == 1 else 1))(act)
        else:
            act()

    def swapped(self, ctx):
        p = self.place
        block = self.slot(1 - p.dp, ctx)
        neighbour = p.ctx + 1 - 2 * lax.rem(p.ctx, 2)
        return remote(block, block, self.ss.at[0], self.sr.at[0], p.along(neighbour))

    def cross(self):
        self.crossed = True
        self.shard.need()
        self.across(0).start()

    def start(self):
        self.shard.need()
        for s in self.order:
            self.direct(s, lambda copy: copy.start())
        if not self.crossed:
            self.cross()
        self.local().start()

    def step(self, k):
        s = self.order[k]
        p = self.place
        block = self.slot(p.dp, p.behind(s))
        remote(block, block, self.zs.at[s], self.zr.at[s], p.along(p.ctx)).wait_recv()
        if self.relayed and s == 2:
            self.relay(lambda copy: copy.start())
        self.when_crossing(s, lambda: self.across(s).start())
        if self.swap and k == 0:
            self.arrive(0).wait_recv()
            self.swapped(p.ctx).start()

    def finish(self):
        p = self.place
        self.local().wait()
        for s in self.order:
            self.direct(s, lambda copy: copy.wait_send())
        if self.relayed:
            self.relay(lambda copy: copy.wait_send())

        def both(s):
            self.across(s).wait_send()
            self.arrive(s).wait_recv()

        for s in self.order:
            self.when_crossing(s, functools.partial(both, s))
        self.across(0).wait_send()
        if self.swap:
            self.swapped(p.ctx).wait_send()
            self.swapped(p.ctx + 1 - 2 * lax.rem(p.ctx, 2)).wait_recv()
        else:
            self.arrive(0).wait_recv()

    @property
    def result(self):
        whole = self.whole.result
        return whole.reshape(-1, whole.shape[-1])


class Scatter:
    def __init__(self, call, blocks, swap=False):
        self.parts = lax.axis_size(CTX)
        places, rows, width = blocks.shape
        self.dtype = blocks.dtype
        call.far = True
        self.late = isinstance(blocks, Held)
        self.blocks = blocks if self.late else call.take(blocks)
        self.out = call.store((rows, width), jnp.float32)
        if not self.late:
            self.mb = call.hold((self.parts, rows, width), blocks.dtype)
        self.yb = call.hold((self.parts, rows, width), blocks.dtype)
        self.zb = call.hold((self.parts - 1, rows, width), blocks.dtype)
        self.zs, self.zr, self.ys, self.yr = (call.flags(self.parts) for _ in range(4))
        self.l, self.ss, self.sr = (call.flags(2) for _ in range(3))
        self.relayed = self.parts == 4
        self.swap = swap and self.relayed
        self.order = (3, 1, 2, 0) if self.relayed else tuple(range(self.parts - 1, -1, -1))
        if self.relayed:
            self.rb = call.hold((rows, width), blocks.dtype)
        if self.swap:
            self.tb, self.wb = (call.hold((rows, width), blocks.dtype) for _ in range(2))
        self.steps = self.parts

    def bind(self, place):
        self.place = place

    def block_of(self, dp, ctx):
        return self.blocks.at[dp * self.parts + ctx]

    def local(self):
        mine = self.blocks.at[pl.ds(self.place.dp * self.parts, self.parts)]
        return pltpu.make_async_copy(mine, self.mb.ref, self.l.at[0])

    def local_twin(self):
        p = self.place
        return pltpu.make_async_copy(self.block_of(1 - p.dp, p.ctx), self.tb.ref, self.l.at[1])

    def swapped(self):
        p = self.place
        neighbour = p.ctx + 1 - 2 * lax.rem(p.ctx, 2)
        block = self.block_of(1 - p.dp, neighbour)
        return remote(block, self.wb.ref, self.ss.at[0], self.sr.at[0], p.along(neighbour))

    def across(self, s):
        p = self.place
        block = self.tb.ref if self.swap and s == 0 else self.block_of(1 - p.dp, p.ahead(s))
        return remote(block, self.yb.at[s], self.ys.at[s], self.yr.at[s], p.other)

    def when_crossing(self, s, act):
        if self.swap and s in (1, 3):
            pl.when(lax.rem(self.place.ctx, 2) == (1 if s == 1 else 0))(act)
        else:
            act()

    def along(self, s, act):
        p = self.place
        target = self.zb.at[s - 1]
        copy = remote(self.yb.at[s], target, self.zs.at[s], self.zr.at[s], p.along(p.ahead(s)))
        if not self.relayed or s == 2:
            act(copy)
            return
        end, middle = (0, 1) if s == 3 else (3, 2)
        way = remote(self.yb.at[s], self.rb.ref, self.zs.at[s], self.zr.at[0], p.along(middle))
        pl.when(p.ctx != end)(lambda: act(copy))
        pl.when(p.ctx == end)(lambda: act(way))

    def early(self, act):
        p = self.place
        for s, odd in ((1, 0), (3, 1)):
            block, target = self.block_of(p.dp, p.ahead(s)), self.zb.at[s - 1]
            copy = remote(block, target, self.zs.at[s], self.zr.at[s], p.along(p.ahead(s)))
            pl.when(lax.rem(p.ctx, 2) == odd)(lambda copy=copy: act(copy))

    def start(self):
        if self.swap:
            self.swapped().start()
            self.local_twin().start()
            self.early(lambda copy: copy.start())
        for s in self.order:
            if s or not self.swap:
                self.when_crossing(s, lambda s=s: self.across(s).start())
        if not self.late:
            self.local().start()

    def send_twin(self):
        self.local_twin().wait()
        self.swapped().wait()
        both = self.tb[...].astype(jnp.float32) + self.wb[...].astype(jnp.float32)
        self.tb[...] = both.astype(self.dtype)
        self.across(0).start()

    def step(self, k):
        p = self.place
        s = self.order[k]
        if k == 0:
            if not self.late:
                self.local().wait()
            if self.swap:
                self.send_twin()
        if self.late:
            mine = self.blocks[p.dp * self.parts + p.ahead(s)]
        else:
            mine = self.mb[p.ahead(s)]
        mine = mine.astype(jnp.float32)

        def add_crossed():
            self.across(s).wait()
            self.yb[s] = (mine + self.yb[s].astype(jnp.float32)).astype(self.dtype)
            if s != 2:
                self.along(s, lambda copy: copy.start())

        if s == 0:
            self.across(s).wait()
            self.out[...] = mine + self.yb[s].astype(jnp.float32)
            return
        self.when_crossing(s, add_crossed)
        if s != 2:
            return
        if self.relayed:

            def add_ends():
                way = remote(self.rb.ref, self.rb.ref, self.zs.at[0], self.zr.at[0], p.other)
                way.wait_recv()
                through = self.yb[s].astype(jnp.float32) + self.rb[...].astype(jnp.float32)
                self.yb[s] = through.astype(self.dtype)

            pl.when((p.ctx == 1) | (p.ctx == 2))(add_ends)
        self.along(s, lambda copy: copy.start())

    def finish(self):
        p = self.place

        def add(s):
            block = self.zb.at[s - 1]
            remote(block, block, self.zs.at[s], self.zr.at[s], p.other).wait_recv()
            self.out[...] += self.zb[s - 1].astype(jnp.float32)

        for s in self.order:
            if s == 0:
                continue
            self.along(s, lambda copy: copy.wait_send())
            if self.relayed and s != 2:
                pl.when(p.ctx != (3 if s == 3 else 0))(functools.partial(add, s))
            else:
                add(s)
        self.out.put()

    @property
    def result(self):
        return self.out.result


class Deal:
    def __init__(self, call, blocks, rows=None):
        self.parts, self.compact = lax.axis_size(CTX), rows is not None
        length, width = rows or blocks.shape[1], blocks.shape[2]
        self.share = length // 4
        call.far = True
        self.source = call.take(blocks)
        self.target = call.give((self.parts, length, width), blocks.dtype)
        self.held = call.hold(blocks.shape[1:], blocks.dtype)
        self.l = call.flags(2)
        self.zf, self.af, self.xf, self.bf = (
            tuple(call.flags(self.parts) for _ in range(2)) for _ in range(4)
        )
        self.order = list(range(self.parts - 1, 0, -1))
        if self.compact:
            self.order.insert(0, 0)
        self.steps = 2 * len(self.order)

    def bind(self, place):
        self.place = place
        if self.compact:
            x, side = place.mp // 2, place.side
            self.own, self.far = side * 2 + x, side * 2 + 1 - x
            self.near, self.near_far = (1 - side) * 2 + x, (1 - side) * 2 + 1 - x
        else:
            self.own, self.far = place.mp, lax.rem(place.mp + 2, 4)
            self.near = place.mp + 1 - 2 * place.side
            self.near_far = lax.rem(self.near + 2, 4)

    def rows(self, index):
        return pl.ds(pl.multiple_of(index * self.share, self.share), self.share)

    def local(self, k):
        p = self.place
        target = self.target.at[p.ctx]
        if self.compact:
            target = self.target.at[p.ctx, self.rows(self.own)]
        refs = (self.source.at[p.ctx], self.held.ref, target)
        return pltpu.make_async_copy(refs[k], refs[k + 1], self.l.at[k])

    def along(self, s):
        p = self.place
        rows = self.rows(self.own)
        source = self.source.at[p.ahead(s)] if self.compact else self.source.at[p.ahead(s), rows]
        target = self.target.at[p.ctx, rows]
        return remote(source, target, self.zf[0].at[s], self.zf[1].at[s], p.along(p.ahead(s)))

    def piece(self, s, index, flags, peer):
        ref = self.target.at[self.place.behind(s), self.rows(index)]
        return remote(ref, ref, flags[0].at[s], flags[1].at[s], peer)

    def start(self):
        for s in self.order:
            if s:
                self.along(s).start()
        self.local(0).start()

    def step(self, k):
        p = self.place
        if k == 0:
            self.local(0).wait()
            self.local(1).start()
        s = self.order[k % len(self.order)]
        if k < len(self.order):
            if s:
                self.piece(s, self.own, self.zf, p.along(p.ctx)).wait_recv()
            else:
                self.local(1).wait()
            self.piece(s, self.own, self.xf, p.cross).start()
            self.piece(s, self.own, self.af, p.pair).start()
        else:
            self.piece(s, self.far, self.xf, p.cross).wait_recv()
            self.piece(s, self.far, self.bf, p.pair).start()

    def finish(self):
        p = self.place
        if not self.compact:
            self.local(1).wait()
        for s in self.order:
            if s:
                self.along(s).wait_send()
            self.piece(s, self.own, self.xf, p.cross).wait_send()
            self.piece(s, self.own, self.af, p.pair).wait_send()
            self.piece(s, self.far, self.bf, p.pair).wait_send()
            self.piece(s, self.near, self.af, p.pair).wait_recv()
            self.piece(s, self.near_far, self.bf, p.pair).wait_recv()

    @property
    def result(self):
        whole = self.target.result
        return whole.reshape(-1, whole.shape[-1])


LATE = "late"


class Jobs:
    def __init__(self, jobs, plan):
        self.jobs = list(jobs)
        self.queue = sorted(
            (times[k] if len(times) > 2 else times[0] + k * times[1], j, k)
            for j, (job, times) in enumerate(zip(self.jobs, plan))
            for k in range(job.steps)
        )
        self.at = 0

    def bind(self, place):
        self.at = 0
        for job in self.jobs:
            job.bind(place)

    def start(self):
        for job in self.jobs:
            if not getattr(job, LATE, False):
                job.start()

    def advance(self, reached):
        while self.at < len(self.queue) and self.queue[self.at][0] <= reached:
            _, j, k = self.queue[self.at]
            self.jobs[j].step(k)
            self.at += 1

    def finish(self):
        self.advance(math.inf)
        for job in self.jobs:
            job.finish()


def begin(call, total, jobs, backward=False):
    place = Place()
    if total is not None:
        total.bind(place)
    jobs.bind(place)
    place.greet(call.far)
    call.start_loads(backward)
    place.enter(call.far)
    jobs.start()
    return place


def dot_nn(a, b):
    return lax.dot_general(a, b, (((1,), (0,)), ((), ())), preferred_element_type=jnp.float32)


def dot_nt(a, b):
    return lax.dot_general(a, b, (((1,), (1,)), ((), ())), preferred_element_type=jnp.float32)


def dot_tn(a, b):
    return lax.dot_general(a, b, (((0,), (0,)), ((), ())), preferred_element_type=jnp.float32)


def lane_number(width):
    return lax.broadcasted_iota(jnp.int32, (1, width), 1)


LANES = 128
BLOCKS = 4


def turn(values, cosine, signed_sine, back):
    half = HEAD_DIM // 2
    leading = lax.rem(lane_number(LANES), HEAD_DIM) < half
    pieces = []
    for at in range(0, values.shape[1], LANES):
        piece = values[:, at : at + LANES]
        swapped = jnp.where(leading, pltpu.roll(piece, LANES - half, 1), pltpu.roll(piece, half, 1))
        moved = swapped * signed_sine
        pieces.append(piece * cosine - moved if back else piece * cosine + moved)
    return jnp.concatenate(pieces, axis=1)


def write_bias(bias, seg_col, seg_row, i, rows, keys):
    query_at = i * rows + lax.broadcasted_iota(jnp.int32, (rows, 1), 0)
    key_at = lax.broadcasted_iota(jnp.int32, (1, keys), 1)
    same = seg_col[pl.ds(i * rows, rows), :1] == seg_row[:1, :keys]
    bias[:, :keys] = jnp.where(same & (key_at <= query_at), 0.0, neg_large)


class Opening:
    def __init__(self, call, inputs, segment_ids, layers, gain_rows, angle_row, places):
        self.call, self.places = call, places
        parts, length, width = inputs.shape
        self.count = count = parts * length
        (q1, k1, v1, o1, *tall1), (q2, k2, v2, o2, *tall2) = layers
        self.shard, self.hid = shard, hid = q1.shape
        units = tall1[0].shape[0]
        low = jnp.bfloat16
        self.first = [call.load(array) for array in (q1, k1, v1, o1)]
        self.gain_rows = call.load(gain_rows)
        self.ids, self.angle = call.load(segment_ids), call.load(angle_row)
        self.tall = [call.load(array) for array in tall1]
        self.second = [call.load(array) for array in (q2, k2, v2, o2)]
        self.tall += [call.load(array) for array in tall2]
        self.shards_one = [call.hold((shard, units), low) for _ in tall1]
        self.shards_two = [call.store((shard, units), low) for _ in tall2]
        self.wa_one = call.hold((shard, 4 * hid), low)
        self.wa_two = call.store((shard, 4 * hid), low)
        self.gains_wide = call.hold(gain_rows.shape, jnp.float32)
        self.cosine, self.sine, self.seg_col = (
            call.store((count, LANES), jnp.float32, BLOCKS) for _ in range(3)
        )
        self.seg_row = call.store((8, count), jnp.float32)
        self.gather = Gather(call, self.wa_one, places)
        self.deal = Deal(call, inputs)
        self.gather_gains = Gather(call, self.gains_wide, places)
        plan = ((2.0, 0.1), (5.0, 4.0), (14.0, 6.0))
        self.jobs = Jobs([self.gather_gains, self.deal, self.gather], plan)
        self.deal.late = True
        self.x = call.hold((count, width), low)
        self.wa = call.hold((width, 4 * hid), low)
        self.gain_blocks = call.hold((places,) + gain_rows.shape, jnp.float32)
        self.gains = call.store((gain_rows.shape[0], width), jnp.float32)
        self.flag = call.flags(2 + 2 * parts)

    def tables(self):
        return (self.cosine, self.sine, self.seg_col, self.seg_row)

    def run(self, total, jobs):
        call, hid = self.call, self.hid
        place = Place()
        total.bind(place)
        self.jobs.bind(place)
        jobs.bind(place)
        place.greet(call.far)
        call.start_loads()
        place.enter(call.far)
        self.deal.start()
        for j, held in enumerate(self.first):
            held.need()
            values = held[...]
            self.wa_one[:, j * hid : (j + 1) * hid] = values.T if j == 3 else values
        self.gain_rows.need()
        self.gains_wide[...] = self.gain_rows[...].astype(jnp.float32)
        self.jobs.start()
        for tall, shard in zip(self.tall, self.shards_one + self.shards_two):
            tall.need()
            shard[...] = tall[...].T
            if shard.out is not None:
                shard.put()
        for j, held in enumerate(self.second):
            held.need()
            values = held[...]
            self.wa_two[:, j * hid : (j + 1) * hid] = values.T if j == 3 else values
        self.wa_two.put()
        for job in jobs.jobs:
            job.cross()
        self.ids.need()
        self.angle.need()
        ids = self.ids[...].astype(jnp.float32)
        mine = lax.broadcasted_iota(jnp.int32, ids.shape, 0) == place.ctx
        own = jnp.sum(jnp.where(mine, ids, 0.0), axis=0, keepdims=True)
        self.seg_row[...] = jnp.broadcast_to(own, self.seg_row.shape)
        self.seg_row.put()
        self.seg_col[...] = jnp.broadcast_to(own, (LANES, self.count)).T
        self.seg_col.put()
        rows = self.count // BLOCKS
        for i in range(BLOCKS):
            at = pl.ds(i * rows, rows)
            index = i * rows + lax.broadcasted_iota(jnp.int32, (rows, 1), 0)
            angles = index.astype(jnp.float32) * self.angle[:1, :]
            self.cosine[at, :] = jnp.cos(angles)
            self.sine[at, :] = jnp.sin(angles) * self.angle[1:2, :]
        self.cosine.put()
        self.sine.put()
        self.jobs.advance(math.inf)
        jobs.start()
        self.jobs.finish()
        jobs.advance(0.5)
        shard = self.shard
        copies = [
            pltpu.make_async_copy(
                self.gather_gains.whole.ref, self.gain_blocks.ref, self.flag.at[0]
            )
        ]
        parts = self.deal.parts
        length = self.count // parts
        for k in range(parts):
            copies.append(
                pltpu.make_async_copy(
                    self.deal.target.at[k],
                    self.x.at[pl.ds(k * length, length)],
                    self.flag.at[1 + k],
                )
            )
        for k in range(self.places):
            copies.append(
                pltpu.make_async_copy(
                    self.gather.whole.at[k],
                    self.wa.at[pl.ds(k * shard, shard)],
                    self.flag.at[1 + parts],
                )
            )
        for copy in copies:
            copy.start()
        for copy in copies:
            copy.wait()
        for k in range(self.places):
            self.gains[:, k * shard : (k + 1) * shard] = self.gain_blocks[k]
        self.gains.put()


def attention_layer(number, x, first_v, wa, gains, which, tables, jobs_of, plan, opening=None):
    call = Call(number)
    if opening is None:
        start = None
        x, gains, wa = call.load(x, BLOCKS), call.load(gains), call.load(wa)
        cosine, sine, seg_col = (call.load(table, BLOCKS) for table in tables[:3])
        seg_row = call.load(tables[3])
    else:
        start = opening(call)
        x, gains, wa = start.x, start.gains, start.wa
        cosine, sine, seg_col, seg_row = start.tables()
    count, width = x.shape
    hid = wa.shape[1] // 4
    heads = hid // HEAD_DIM
    rows = count // BLOCKS
    if first_v is not None:
        first_v = call.load(first_v, BLOCKS)
    else:
        v = call.store((count, hid), jnp.float32, BLOCKS)
    x1 = call.store((count, width), jnp.float32, BLOCKS)
    h = call.store((count, width), jnp.bfloat16, BLOCKS)
    q, k, m, o = (call.store((count, hid), jnp.bfloat16, BLOCKS) for _ in range(4))
    lse = call.store((heads, count, 1), jnp.float32, BLOCKS)
    bias = call.hold((rows, count), jnp.float32)
    acc = call.hold((rows, hid), jnp.float32)
    total = HeadSum(call, BLOCKS, rows, width)
    carried = jobs_of(call, start)
    jobs = Jobs(carried, plan)

    def body():
        if start is None:
            begin(call, total, jobs)
        else:
            start.run(total, jobs)
        lane = lane_number(hid)
        for i in range(BLOCKS):
            at = pl.ds(i * rows, rows)
            x.need(i)
            gains.need()
            stream = x[at, :].astype(jnp.float32)
            inverse = lax.rsqrt(jnp.mean(stream * stream, axis=-1, keepdims=True) + epsilon)
            normed = (stream * inverse * gains[which : which + 1, :]).astype(jnp.bfloat16)
            h[at, :] = normed
            h.put(i)
            wa.need()
            projected = dot_nn(normed, wa[:, : 3 * hid])
            cosine.need(i)
            sine.need(i)
            cos, sin = cosine[at, :], sine[at, :]
            queries = turn(projected[:, :hid], cos, sin, False).astype(jnp.bfloat16)
            q[at, :] = queries * jnp.bfloat16(HEAD_DIM**-0.5)
            k[at, :] = turn(projected[:, hid : 2 * hid], cos, sin, False).astype(jnp.bfloat16)
            values = projected[:, 2 * hid :]
            if first_v is None:
                v[at, :] = values
                v.put(i)
            else:
                first_v.need(i)
                values = 0.5 * values + 0.5 * first_v[at, :]
            m[at, :] = values.astype(jnp.bfloat16)
            for held in (q, k, m):
                held.put(i)
            keys = (i + 1) * rows
            seg_col.need(i)
            seg_row.need()
            write_bias(bias, seg_col, seg_row, i, rows, keys)
            if i:
                total.middle(i - 1)
            jobs.advance((4.5, 8.0, 12.5, 18.0)[i])

            def one_head(index, unused):
                mask = lane // HEAD_DIM == index
                query = jnp.where(mask, q[at, :], jnp.bfloat16(0))
                scores = dot_nt(query, k[:keys, :]) + bias[:, :keys]
                top = jnp.max(scores, axis=-1, keepdims=True)
                exponent = jnp.exp(scores - top)
                summed = jnp.sum(exponent, axis=-1, keepdims=True)
                weighted = dot_nn(exponent.astype(jnp.bfloat16), m[:keys, :])
                acc[...] = jnp.where(mask, weighted / summed, acc[...])
                lse[index, at, :] = top + jnp.log(summed)
                return unused

            lax.fori_loop(0, heads, one_head, 0)
            attended = acc[...].astype(jnp.bfloat16)
            o[at, :] = attended
            o.put(i)
            lse.put(i)
            total.send(i, dot_nt(attended, wa[:, 3 * hid :]))
            jobs.advance((6.0, 10.5, 16.0, 22.5)[i])
        total.middle(BLOCKS - 1)
        for i in range(BLOCKS):
            total.last(i)
            jobs.advance((23.0, 24.0, 28.0, 33.0)[i])
        for i in range(BLOCKS):
            at = pl.ds(i * rows, rows)
            x1[at, :] = x[at, :].astype(jnp.float32) + total.total(i)
            x1.put(i)
        jobs.finish()

    call.run(body)
    return SimpleNamespace(
        x1=x1.result,
        h=h.result,
        q=q.result,
        k=k.result,
        m=m.result,
        o=o.result,
        lse=lse.result,
        v=v.result if first_v is None else None,
        carried=[job.result for job in carried],
        start=start,
    )


def feed_forward_layer(number, x1, gate, up, down, gains, which, jobs_of, plan):
    count, width = x1.shape
    units = gate.shape[1]
    rows = count // BLOCKS
    call = Call(number)
    x1 = call.load(x1, BLOCKS)
    gains, gate, up, down = (call.load(array) for array in (gains, gate, up, down))
    y = call.store_from(x1, (count, width), jnp.float32, BLOCKS)
    y_low, h2 = (call.store((count, width), jnp.bfloat16, BLOCKS) for _ in range(2))
    z, u, a = (call.store((count, units), jnp.bfloat16, BLOCKS) for _ in range(3))
    total = HeadSum(call, BLOCKS, rows, width)
    carried = jobs_of(call)
    jobs = Jobs(carried, plan)

    def body():
        begin(call, total, jobs)
        for i in range(BLOCKS):
            at = pl.ds(i * rows, rows)
            x1.need(i)
            gains.need()
            stream = x1[at, :]
            inverse = lax.rsqrt(jnp.mean(stream * stream, axis=-1, keepdims=True) + epsilon)
            normed = (stream * inverse * gains[which : which + 1, :]).astype(jnp.bfloat16)
            h2[at, :] = normed
            gate.need()
            gated = dot_nn(normed, gate[...])
            if i:
                total.middle(i - 1)
            jobs.advance(2.5 * i + 4.0)
            up.need()
            raised = dot_nn(normed, up[...])
            active = (gated * lax.logistic(gated) * raised).astype(jnp.bfloat16)
            z[at, :] = gated.astype(jnp.bfloat16)
            u[at, :] = raised.astype(jnp.bfloat16)
            a[at, :] = active
            for held in (h2, z, u, a):
                held.put(i)
            down.need()
            total.send(i, dot_nt(active, down[...]))
            jobs.advance(2.5 * i + 5.5)
        total.middle(BLOCKS - 1)
        for i in range(BLOCKS):
            total.last(i)
            jobs.advance(13.0 + 5.7 * i)
        for i in range(BLOCKS):
            at = pl.ds(i * rows, rows)
            result = x1[at, :] + total.total(i)
            x1[at, :] = result
            y_low[at, :] = result.astype(jnp.bfloat16)
            y.put(i)
            y_low.put(i)
        jobs.finish()

    call.run(body)
    return SimpleNamespace(
        y=y.result,
        y_low=y_low.result,
        h2=h2.result,
        z=z.result,
        u=u.result,
        a=a.result,
        carried=[job.result for job in carried],
    )


def norm_back(gain, grad, stream, gain_sum):
    inverse = lax.rsqrt(jnp.mean(stream * stream, axis=-1, keepdims=True) + epsilon)
    scaled = stream * inverse
    grad_scaled = grad * gain
    products = jnp.mean(grad_scaled * scaled, axis=-1, keepdims=True)
    gain_sum = gain_sum + jnp.sum(grad * scaled, axis=0, keepdims=True)
    return inverse * (grad_scaled - scaled * products), gain_sum


def feed_forward_back(number, gy, x1, saved, gate, up, down, gains, which, jobs_of, plan):
    count, width = x1.shape
    units = gate.shape[1]
    rows = count // BLOCKS
    call = Call(number)
    call.in_turn = True
    if saved is not None:
        gy = call.load(gy, BLOCKS)
        down = call.load(down)
        z, u = call.load(saved.z, BLOCKS), call.load(saved.u, BLOCKS)
        gate, up, a, h2, gains = (call.load(w) for w in (gate, up, saved.a, saved.h2, gains))
        x1 = call.load(x1, BLOCKS)
        later = 0.0
    else:
        x1, gains = call.load(x1, BLOCKS), call.load(gains)
        gate, up, down = (call.load(w) for w in (gate, up, down))
        gy = call.load(gy, BLOCKS)
        h2 = call.hold((count, width), jnp.bfloat16)
        z, u, a = (call.hold((count, units), jnp.bfloat16) for _ in range(3))
        quarters = QuarterSum(call, BLOCKS, rows, width)
        later = 10.0
    gx1 = call.store_from(x1, (count, width), jnp.float32, BLOCKS)
    gain = call.store((1, width), jnp.float32)
    d_gate, d_up = (call.store((width, units), jnp.bfloat16, 4) for _ in range(2))
    places = lax.axis_size(DP) * lax.axis_size(CTX)
    shard = width // places
    d_down = call.hold((places, shard, units), jnp.bfloat16)
    low = call.hold((count, width), jnp.bfloat16)
    gz, gu = (call.hold((count, units), jnp.bfloat16) for _ in range(2))
    total = HeadSum(call, BLOCKS, rows, width)
    down_sum = Scatter(call, d_down)
    carried = jobs_of(call, down_sum)
    jobs = Jobs(carried, plan)

    def forward():
        for i in range(BLOCKS):
            at = pl.ds(i * rows, rows)
            x1.need(i)
            gains.need()
            stream = x1[at, :]
            inverse = lax.rsqrt(jnp.mean(stream * stream, axis=-1, keepdims=True) + epsilon)
            normed = (stream * inverse * gains[which : which + 1, :]).astype(jnp.bfloat16)
            h2[at, :] = normed
            gate.need()
            gated = dot_nn(normed, gate[...])
            up.need()
            raised = dot_nn(normed, up[...])
            active = (gated * lax.logistic(gated) * raised).astype(jnp.bfloat16)
            z[at, :] = gated.astype(jnp.bfloat16)
            u[at, :] = raised.astype(jnp.bfloat16)
            a[at, :] = active
            down.need()
            if i:
                quarters.middle(i - 1)
            quarters.send(i, dot_nt(active, down[...]) + stream * 0.25)
        quarters.middle(BLOCKS - 1)

    def body():
        if saved is None:
            quarters.bind(begin(call, total, jobs))
            forward()
        else:
            begin(call, total, jobs)
        for i in range(BLOCKS):
            at = pl.ds(i * rows, rows)
            gy.need(i)
            low[at, :] = gy[at, :].astype(jnp.bfloat16)
        for i in range(BLOCKS):
            at = pl.ds(i * rows, rows)
            down.need()
            ga = dot_nn(low[at, :], down[...])
            z.need(i)
            u.need(i)
            gated = z[at, :].astype(jnp.float32)
            sigma = lax.logistic(gated)
            raised = u[at, :].astype(jnp.float32)
            slope = sigma * (1.0 + gated * (1.0 - sigma))
            gz[at, :] = (ga * raised * slope).astype(jnp.bfloat16)
            gu[at, :] = (ga * gated * sigma).astype(jnp.bfloat16)
            if i > 1:
                total.middle(i - 1)
            gate.need()
            up.need()
            total.send(i, dot_nt(gz[at, :], gate[...]) + dot_nt(gu[at, :], up[...]))
            if i == 0:
                a.need()
                for j in range(places // 2):
                    cut = slice(j * 2 * shard, (j + 1) * 2 * shard)
                    part = dot_tn(low[:, cut], a[...]).astype(jnp.bfloat16)
                    d_down[2 * j : 2 * j + 2] = part.reshape(2, shard, units)
                    if j == 0:
                        total.middle(0)
                down_sum.start()
            jobs.advance(3.0 * i + 9.0 + later)
        total.middle(BLOCKS - 1)
        cols = width // 4
        h2.need()
        for reached, left, right, out in ((21.0, h2, gz, d_gate), (24.0, h2, gu, d_up)):
            for j in range(4):
                cut = slice(j * cols, (j + 1) * cols)
                out[cut, :] = dot_tn(left[:, cut], right[...]).astype(jnp.bfloat16)
                out.put(j)
            jobs.advance(reached + later)
        gains.need()
        if saved is None:
            for i in range(BLOCKS):
                quarters.last(i)
            quarters.out.put()
        for i in range(BLOCKS):
            total.last(i)
            jobs.advance((24.0, 24.0, 28.0, 34.0)[i] + later)
        gain_sum = jnp.zeros((1, width), jnp.float32)
        for i in range(BLOCKS):
            at = pl.ds(i * rows, rows)
            x1.need(i)
            step, gain_sum = norm_back(
                gains[which : which + 1, :], total.total(i), x1[at, :], gain_sum
            )
            x1[at, :] = gy[at, :].astype(jnp.float32) + step
            gx1.put(i)
        gain[...] = gain_sum
        gain.put()
        jobs.finish()

    call.run(body)
    return SimpleNamespace(
        gx1=gx1.result,
        gain=gain.result,
        d_gate=d_gate.result,
        d_up=d_up.result,
        quarters=quarters.out.result if saved is None else None,
        carried=[job.result for job in carried],
    )


def attention_back(number, gx1, x, saved, extra, wa, gains, which, tables, jobs_of, plan):
    count, width = x.shape
    hid = wa.shape[1] // 4
    heads = hid // HEAD_DIM
    rows = count // BLOCKS
    call = Call(number)
    gx1, wa = call.load(gx1, BLOCKS), call.load(wa)
    q, k, m, o = (
        call.load(array, blocks)
        for array, blocks in ((saved.q, BLOCKS), (saved.k, 1), (saved.m, 1), (saved.o, BLOCKS))
    )
    lse = call.load(saved.lse, BLOCKS)
    cosine, sine, seg_col = (call.load(table, BLOCKS) for table in tables[:3])
    seg_row = call.load(tables[3])
    if extra is not None:
        extra = call.load(extra, BLOCKS)
    h, gains, x = call.load(saved.h), call.load(gains), call.load(x, BLOCKS)
    if extra is not None:
        gx = call.store((count, width), jnp.bfloat16, BLOCKS)
        gx_held = gx
    else:
        gx_held = gx1
        gx = call.store_from(gx1, (count, width), jnp.float32, BLOCKS)
        passed = call.store((count, hid), jnp.float32, BLOCKS)
    gain = call.store((1, width), jnp.float32)
    d_wa = call.store((width, 4 * hid), jnp.bfloat16, 4)
    low = call.hold((count, width), jnp.bfloat16)
    bias = call.hold((rows, count), jnp.float32)
    go = call.hold((rows, hid), jnp.bfloat16)
    gq = call.hold((rows, hid), jnp.float32)
    gk, gm = (call.hold((count, hid), jnp.float32) for _ in range(2))
    g3 = call.hold((count, 3 * hid), jnp.bfloat16)
    total = HeadSum(call, BLOCKS, rows, width)
    carried = jobs_of(call)
    jobs = Jobs(carried, plan)

    def body():
        begin(call, total, jobs, True)
        lane = lane_number(hid)
        gk[...] = jnp.zeros(gk.shape, gk.dtype)
        gm[...] = jnp.zeros(gm.shape, gm.dtype)
        order = list(range(BLOCKS))[::-1]
        for turn_index, i in enumerate(order):
            at = pl.ds(i * rows, rows)
            gx1.need(i)
            low[at, :] = gx1[at, :].astype(jnp.bfloat16)
            wa.need()
            go[...] = dot_nn(low[at, :], wa[:, 3 * hid :]).astype(jnp.bfloat16)
            keys = (i + 1) * rows
            for held in (seg_row, seg_col, q, o, lse, k, m):
                held.need(i)
            write_bias(bias, seg_col, seg_row, i, rows, keys)
            gq[...] = jnp.zeros(gq.shape, gq.dtype)
            if turn_index:
                total.middle(order[turn_index - 1])
            else:
                jobs.advance(5.0)

            def one_head(index, unused):
                mask = lane // HEAD_DIM == index
                zero = jnp.bfloat16(0)
                query = jnp.where(mask, q[at, :], zero)
                grad = jnp.where(mask, go[...], zero)
                both = grad.astype(jnp.float32) * o[at, :].astype(jnp.float32)
                delta = jnp.sum(both, axis=-1, keepdims=True)
                scores = dot_nt(query, k[:keys, :]) + bias[:, :keys]
                prob = jnp.exp(scores - lse[index, at, :])
                grad_prob = dot_nt(grad, m[:keys, :])
                grad_score = (prob * (grad_prob - delta)).astype(jnp.bfloat16)
                part = dot_nn(grad_score, k[:keys, :])
                gq[...] = jnp.where(mask, part, gq[...])
                gk[:keys, :] += dot_tn(grad_score, query)
                gm[:keys, :] += dot_tn(prob.astype(jnp.bfloat16), grad)
                return unused

            lax.fori_loop(0, heads, one_head, 0)
            cosine.need(i)
            sine.need(i)
            cos, sin = cosine[at, :], sine[at, :]
            values = gm[at, :]
            if extra is None:
                values = 0.5 * values
                passed[at, :] = values
                passed.put(i)
            else:
                extra.need(i)
                values = values + extra[at, :]
            back = turn(gq[...] * HEAD_DIM**-0.5, cos, sin, True)
            g3[at, :hid] = back.astype(jnp.bfloat16)
            g3[at, hid : 2 * hid] = turn(gk[at, :], cos, sin, True).astype(jnp.bfloat16)
            g3[at, 2 * hid :] = values.astype(jnp.bfloat16)
            total.send(i, dot_nt(g3[at, :], wa[:, : 3 * hid]))
            jobs.advance((11.0, 17.5, 22.0, 25.0)[turn_index])
        total.middle(order[-1])
        cols = width // 4
        h.need()
        for j in range(4):
            cut = slice(j * cols, (j + 1) * cols)
            d_wa[cut, : 3 * hid] = dot_tn(h[:, cut], g3[...]).astype(jnp.bfloat16)
            d_wa[cut, 3 * hid :] = dot_tn(low[:, cut], o[...]).astype(jnp.bfloat16)
            d_wa.put(j)
        jobs.advance(30.0)
        gains.need()
        for turn_index, i in enumerate(order):
            total.last(i)
            jobs.advance((30.0, 30.0, 32.0, 37.0)[turn_index])
        gain_sum = jnp.zeros((1, width), jnp.float32)
        for i in order:
            at = pl.ds(i * rows, rows)
            x.need(i)
            stream = x[at, :].astype(jnp.float32)
            step, gain_sum = norm_back(
                gains[which : which + 1, :], total.total(i), stream, gain_sum
            )
            gx_held[at, :] = (gx1[at, :] + step).astype(gx_held.dtype)
            gx.put(i)
        gain[...] = gain_sum
        gain.put()
        jobs.finish()

    call.run(body)
    return SimpleNamespace(
        gx=gx.result,
        passed=passed.result if extra is None else None,
        gain=gain.result,
        d_wa=d_wa.result,
        carried=[job.result for job in carried],
    )


def transfers(number, jobs_of, plan):
    call = Call(number)
    carried = jobs_of(call)
    jobs = Jobs(carried, plan)

    def body():
        begin(call, None, jobs)
        jobs.finish()

    call.run(body)
    return [job.result for job in carried]


def leave_step(moved, grad, packs, turned, gains):
    call = Call(0)
    kept = [call.load(array, BLOCKS) for array in moved]
    kept_to = [call.store_from(held, held.shape, held.dtype, BLOCKS) for held in kept]
    grad = call.load(grad, BLOCKS)
    wide = call.store(grad.shape, jnp.float32, BLOCKS)
    shard, hid = packs[0].shape[0], packs[0].shape[1] // 4
    flag = call.flags(3 * len(packs))
    packs = [call.load(array) for array in packs]
    unpacked = [[call.give((shard, hid), pack.dtype) for _ in range(3)] for pack in packs]
    upright = [call.store((hid, shard), pack.dtype) for pack in packs]
    turned = [call.load(array) for array in turned]
    turned_to = [call.store(held.shape[::-1], held.dtype) for held in turned]
    gains = call.load(gains)
    gain_to = [call.store((1, shard), gains.dtype) for _ in range(4)]

    def body():
        call.start_loads()
        copies = []
        for at, pack in enumerate(packs):
            pack.need()
            for j in range(3):
                source = pack.at[:, j * hid : (j + 1) * hid]
                copies.append(
                    pltpu.make_async_copy(source, unpacked[at][j].ref, flag.at[3 * at + j])
                )
                copies[-1].start()
            upright[at][...] = pack[:, 3 * hid :].T
            upright[at].put()
        for held, target in zip(turned, turned_to):
            held.need()
            target[...] = held[...].T
            target.put()
        gains.need()
        for j, target in enumerate(gain_to):
            target[...] = gains[j : j + 1, :]
            target.put()
        rows = grad.shape[0] // BLOCKS
        for i in range(BLOCKS):
            at = pl.ds(i * rows, rows)
            grad.need(i)
            wide[at, :] = grad[at, :].astype(jnp.float32)
            wide.put(i)
            for held, target in zip(kept, kept_to):
                held.need(i)
                target.put(i)
        for copy in copies:
            copy.wait()

    call.run(body, False)
    return SimpleNamespace(
        kept=[target.result for target in kept_to],
        grad=wide.result,
        packs=[
            [part.result for part in parts] + [last.result]
            for parts, last in zip(unpacked, upright)
        ],
        turned=[target.result for target in turned_to],
        gains=[target.result.reshape(-1) for target in gain_to],
    )


def dealt_device(
    inputs,
    segment_ids,
    norm_attn_one,
    query_one,
    key_one,
    value_one,
    output_one,
    norm_ffn_one,
    gate_one,
    up_one,
    down_one,
    norm_attn_two,
    query_two,
    key_two,
    value_two,
    output_two,
    norm_ffn_two,
    gate_two,
    up_two,
    down_two,
    cotangent,
):
    parts, length, width = inputs.shape
    places = lax.axis_size(DP) * lax.axis_size(CTX)
    shard = width // places
    gain_rows = jnp.stack([norm_attn_one, norm_ffn_one, norm_attn_two, norm_ffn_two] * 2)
    half = HEAD_DIM // 2
    frequency = 10000.0 ** (-np.arange(half, dtype=np.float32) / np.float32(half))
    repeat = LANES // HEAD_DIM
    signs = np.concatenate([-np.ones(half), np.ones(half)])
    angle_row = np.zeros((8, LANES), np.float32)
    angle_row[0] = np.tile(frequency, 2 * repeat)
    angle_row[1] = np.tile(signs, repeat)

    def split(array):
        return array.reshape(places, shard, array.shape[-1])

    def deal(array):
        return array.reshape(parts, length, width)

    def opening(call):
        return Opening(
            call,
            inputs,
            segment_ids,
            (
                (query_one, key_one, value_one, output_one, gate_one.T, up_one.T, down_one),
                (query_two, key_two, value_two, output_two, gate_two.T, up_two.T, down_two),
            ),
            gain_rows,
            jnp.asarray(angle_row),
            places,
        )

    attn_one = attention_layer(
        1,
        None,
        None,
        None,
        None,
        0,
        None,
        lambda c, start: [Gather(c, held, places) for held in start.shards_one],
        ((0.1, 0.2, 2.0), (5.0, 8.0, 12.0), (15.0, 18.0, 22.0)),
        opening,
    )
    start = attn_one.start
    x, wa_one, gains = start.deal.result, start.gather.result, start.gains.result
    tables = [table.result for table in start.tables()]
    ffn_one_w = attn_one.carried
    wa_two_shard = start.wa_two.result
    shards_two = [held.result for held in start.shards_two]
    ffn_one = feed_forward_layer(
        2,
        attn_one.x1,
        *ffn_one_w,
        gains,
        1,
        lambda c: [Gather(c, wa_two_shard, places, True), Gather(c, shards_two[0], places)],
        ((7.0, 4.0), (20.0, 4.1)),
    )
    wa_two, gate_two_w = ffn_one.carried
    attn_two = attention_layer(
        3,
        ffn_one.y,
        attn_one.v,
        wa_two,
        gains,
        2,
        tables,
        lambda c, start: [
            Deal(c, cotangent),
            Gather(c, shards_two[1], places),
            Gather(c, shards_two[2], places, True),
        ],
        ((8.0, 12.5, 16.0, 22.5, 22.6, 22.7), (16.0, 3.0), (26.0, 3.0)),
    )
    dealt_cotangent = attn_two.carried[0]
    ffn_two_w = (gate_two_w, *attn_two.carried[1:])
    back_ffn_two = feed_forward_back(
        4,
        dealt_cotangent,
        attn_two.x1,
        None,
        *ffn_two_w,
        gains,
        3,
        lambda c, down_sum: [down_sum],
        ((23.0, 4.2),),
    )
    (down_g2,) = back_ffn_two.carried
    grads_plan = ((10.0, 3.0), (25.0, 3.0))

    def ffn_grads(back):
        return [split(array) for array in (back.d_gate, back.d_up)]

    back_attn_two = attention_back(
        6,
        back_ffn_two.gx1,
        ffn_one.y,
        attn_two,
        None,
        wa_two,
        gains,
        2,
        tables,
        lambda c: [Scatter(c, array) for array in ffn_grads(back_ffn_two)]
        + [Deal(c, back_ffn_two.quarters, length)],
        grads_plan + ((4.9, 5.0, 11.0, 11.1, 11.2, 35.0, 35.1, 35.2),),
    )
    gate_g2, up_g2, out_two = back_attn_two.carried
    back_ffn_one = feed_forward_back(
        7,
        back_attn_two.gx,
        attn_one.x1,
        ffn_one,
        *ffn_one_w,
        gains,
        1,
        lambda c, down_sum: [
            Scatter(c, split(back_attn_two.d_wa)),
            down_sum,
            Deal(c, deal(ffn_one.y_low)),
        ],
        ((8.0, 5.8), (30.0, 4.2), (33.0, 33.1, 33.2, 37.0, 37.1, 37.2)),
    )
    packed_two, down_g1, out_one = back_ffn_one.carried
    back_attn_one = attention_back(
        8,
        back_ffn_one.gx1,
        x,
        attn_one,
        back_attn_two.passed,
        wa_one,
        gains,
        0,
        tables,
        lambda c: [Scatter(c, array) for array in ffn_grads(back_ffn_one)],
        grads_plan,
    )
    gate_g1, up_g1 = back_attn_one.carried
    gain_grads = jnp.concatenate(
        [back_attn_one.gain, back_ffn_one.gain, back_attn_two.gain, back_ffn_two.gain] * 2
    )
    gain_grads = jnp.transpose(gain_grads.reshape(-1, places, shard), (1, 0, 2))
    gain_shards, packed_one, grad = transfers(
        9,
        lambda c: [
            Scatter(c, gain_grads),
            Scatter(c, split(back_attn_one.d_wa)),
            Deal(c, deal(back_attn_one.gx)),
        ],
        ((4.0, 0.1), (7.0, 5.8), (6.0, 4.0)),
    )
    final = leave_step(
        (out_one, out_two),
        grad,
        (packed_one, packed_two),
        [gate_g1, up_g1, down_g1, gate_g2, up_g2, down_g2],
        gain_shards,
    )
    gate_g1, up_g1, down_g1, gate_g2, up_g2, down_g2 = final.turned
    return (
        deal(final.kept[0]),
        deal(final.kept[1]),
        deal(final.grad),
        final.gains[0],
        *final.packs[0],
        final.gains[1],
        gate_g1.T,
        up_g1.T,
        down_g1,
        final.gains[2],
        *final.packs[1],
        final.gains[3],
        gate_g2.T,
        up_g2.T,
        down_g2,
    )


def solution(mesh):
    placed = (
        P(DP, CTX, None),
        P(DP, None),
        P((DP, CTX)),
        P((DP, CTX), MP),
        P((DP, CTX), MP),
        P((DP, CTX), MP),
        P(MP, (DP, CTX)),
        P((DP, CTX)),
        P((DP, CTX), MP),
        P((DP, CTX), MP),
        P(MP, (DP, CTX)),
        P((DP, CTX)),
        P((DP, CTX), MP),
        P((DP, CTX), MP),
        P((DP, CTX), MP),
        P(MP, (DP, CTX)),
        P((DP, CTX)),
        P((DP, CTX), MP),
        P((DP, CTX), MP),
        P(MP, (DP, CTX)),
        P(DP, CTX, None),
    )
    sizes = dict(mesh.shape)

    def per_device(*operands):
        fits = sizes[DP] == 2 and sizes[MP] == 4 and operands[0].shape[0] == sizes[CTX]
        return (dealt_device if fits else on_device)(*operands)

    return jax.shard_map(
        per_device,
        mesh=mesh,
        in_specs=placed,
        out_specs=(
            P(DP, CTX, None),
            P(DP, CTX, None),
            P(DP, CTX, None),
            P((DP, CTX)),
            P((DP, CTX), MP),
            P((DP, CTX), MP),
            P((DP, CTX), MP),
            P(MP, (DP, CTX)),
            P((DP, CTX)),
            P((DP, CTX), MP),
            P((DP, CTX), MP),
            P(MP, (DP, CTX)),
            P((DP, CTX)),
            P((DP, CTX), MP),
            P((DP, CTX), MP),
            P((DP, CTX), MP),
            P(MP, (DP, CTX)),
            P((DP, CTX)),
            P((DP, CTX), MP),
            P((DP, CTX), MP),
            P(MP, (DP, CTX)),
        ),
        check_vma=False,
    )
```

```python
import functools
import math
from types import SimpleNamespace

import jax
import jax.numpy as jnp
import numpy as np
from jax import lax
from jax.experimental import pallas as pl
from jax.experimental.pallas import tpu as pltpu
from jax.sharding import PartitionSpec as P

MESH = pl.DeviceIdType.MESH

HEAD_DIM = 64
DP, CTX, MP = "dp", "ctx", "mp"


epsilon = 1e-05
neg_large = -1e30


def project(left_operand, right_operand):
    return jnp.einsum(
        "sbd,de->sbe", left_operand, right_operand, preferred_element_type=jnp.float32
    )


def project_back(left_operand, right_operand):
    return jnp.einsum(
        "sbe,de->sbd", left_operand, right_operand, preferred_element_type=jnp.float32
    )


def weight_term(left_operand, right_operand):
    return jnp.einsum(
        "sbd,sbe->de", left_operand, right_operand, preferred_element_type=jnp.float32
    )


def head_sum_kernel(
    chunks, x_ref, o_ref, near, half_sum, far, send_a, recv_a, send_b, recv_b, send_c, recv_c
):
    dp, ctx, mp = (lax.axis_index(name) for name in (DP, CTX, MP))
    side = lax.rem(mp, 2)
    pair = (dp, ctx, mp + 1 - 2 * side)
    cross = (dp, ctx, lax.rem(mp + 2, 4))
    barrier = pltpu.get_barrier_semaphore()
    for peer in (pair, cross):
        pl.semaphore_signal(barrier, inc=1, device_id=peer, device_id_type=MESH)
    pl.semaphore_wait(barrier, 2)
    rows = x_ref.shape[0] // chunks
    half = rows // 2

    def copy(source, target, send, recv, i, peer):
        return pltpu.make_async_remote_copy(
            src_ref=source,
            dst_ref=target,
            send_sem=send.at[i],
            recv_sem=recv.at[i],
            device_id=peer,
            device_id_type=MESH,
        )

    def first(i):
        theirs = x_ref.at[pl.ds(i * rows + (1 - side) * half, half)]
        return copy(theirs, near.at[i], send_a, recv_a, i, pair)

    def second(i):
        return copy(half_sum.at[i], far.at[i], send_b, recv_b, i, cross)

    def third(i):
        mine = o_ref.at[pl.ds(i * rows + side * half, half)]
        return copy(mine, mine, send_c, recv_c, i, pair)

    for i in range(chunks):
        first(i).start()
    for i in range(chunks):
        first(i).wait()
        mine = x_ref[pl.ds(i * rows + side * half, half)].astype(jnp.float32)
        half_sum[i] = (mine + near[i].astype(jnp.float32)).astype(jnp.bfloat16)
        second(i).start()
    for i in range(chunks):
        second(i).wait()
        total = half_sum[i].astype(jnp.float32) + far[i].astype(jnp.float32)
        o_ref[pl.ds(i * rows + side * half, half)] = total.astype(jnp.bfloat16)
        third(i).start()
    for i in range(chunks):
        third(i).wait()


def head_sum(partial_sum, number):
    flat = partial_sum.astype(jnp.bfloat16).reshape(-1, partial_sum.shape[-1])
    count, width = flat.shape
    chunks = 4
    half = count // chunks // 2
    total = pl.pallas_call(
        functools.partial(head_sum_kernel, chunks),
        out_shape=jax.ShapeDtypeStruct((count, width), jnp.bfloat16),
        in_specs=[pl.BlockSpec(memory_space=pltpu.VMEM)],
        out_specs=pl.BlockSpec(memory_space=pltpu.VMEM),
        scratch_shapes=[pltpu.VMEM((chunks, half, width), jnp.bfloat16)] * 3
        + [pltpu.SemaphoreType.DMA((chunks,))] * 6,
        compiler_params=pltpu.CompilerParams(
            collective_id=0, has_side_effects=True, vmem_limit_bytes=32 << 20
        ),
    )(flat)
    return total.reshape(partial_sum.shape).astype(jnp.float32)


def head_total(partial_sum):
    return head_sum(partial_sum, 0)


def head_back(partial_sum):
    return head_sum(partial_sum, 0)


def rotary_tables(first_place, count_of_rows):
    half_width = HEAD_DIM // 2
    frequency = 10000.0 ** (-jnp.arange(half_width, dtype=jnp.float32) / half_width)
    places = (first_place + jnp.arange(count_of_rows, dtype=jnp.int32)).astype(jnp.float32)
    angles = places[:, None] * frequency[None, :]
    return (jnp.cos(angles)[None, :, None, :], jnp.sin(angles)[None, :, None, :])


def rotate(split_heads, cosine, sine_table):
    half_width = HEAD_DIM // 2
    first_half = split_heads[..., :half_width]
    second_half = split_heads[..., half_width:]
    return jnp.concatenate(
        [
            first_half * cosine - second_half * sine_table,
            first_half * sine_table + second_half * cosine,
        ],
        axis=-1,
    )


def rotate_back(split_heads, cosine, sine_table):
    half_width = HEAD_DIM // 2
    first_half = split_heads[..., :half_width]
    second_half = split_heads[..., half_width:]
    return jnp.concatenate(
        [
            first_half * cosine + second_half * sine_table,
            second_half * cosine - first_half * sine_table,
        ],
        axis=-1,
    )


def norm_forward(stream, gain_row):
    inverse = lax.rsqrt(jnp.mean(stream * stream, axis=-1, keepdims=True) + epsilon)
    normed = (stream * inverse * gain_row.astype(jnp.float32)).astype(jnp.bfloat16)
    return (normed, inverse)


def norm_backward(grad_normed, stream, inverse, gain_row):
    scaled = stream * inverse
    grad_scaled = grad_normed * gain_row.astype(jnp.float32)
    gain_grad = jnp.sum(grad_normed * scaled, axis=(0, 1))
    grad_stream = inverse * (
        grad_scaled - scaled * jnp.mean(grad_scaled * scaled, axis=-1, keepdims=True)
    )
    return (grad_stream, gain_grad)


def block_grads(
    query_block,
    grad_block,
    lse_block,
    delta_block,
    query_places,
    query_document_ids,
    key_block,
    value_block,
    key_places,
    key_segments,
):
    score_scale = HEAD_DIM ** (-0.5)
    scores = (
        jnp.einsum("sqhe,skhe->shqk", query_block, key_block, preferred_element_type=jnp.float32)
        * score_scale
    )
    visible = (
        (key_places[None, :] <= query_places[:, None])[None]
        & (key_segments[:, None, :] == query_document_ids[:, :, None])
    )[:, None]
    probabilities = jnp.where(visible, jnp.exp(scores - lse_block[..., None]), 0.0)
    grad_probs = jnp.einsum(
        "sqhe,skhe->shqk", grad_block, value_block, preferred_element_type=jnp.float32
    )
    grad_scores = (probabilities * (grad_probs - delta_block[..., None]) * score_scale).astype(
        jnp.bfloat16
    )
    query_grad = jnp.einsum(
        "shqk,skhe->sqhe", grad_scores, key_block, preferred_element_type=jnp.float32
    )
    key_grad = jnp.einsum(
        "shqk,sqhe->skhe", grad_scores, query_block, preferred_element_type=jnp.float32
    )
    value_grad = jnp.einsum(
        "shqk,sqhe->skhe",
        probabilities.astype(jnp.bfloat16),
        grad_block,
        preferred_element_type=jnp.float32,
    )
    return (query_grad, key_grad, value_grad)


def attend_forward(queries, key_rows, value_rows, segments, query_places):
    seq_count, count_of_rows, head_count, head_width = queries.shape
    score_scale = head_width ** (-0.5)
    query_document_ids = lax.dynamic_slice_in_dim(segments, query_places[0], count_of_rows, 1)
    last_query = query_places[count_of_rows - 1]
    initial = (
        jnp.full((seq_count, head_count, count_of_rows), neg_large, jnp.float32),
        jnp.zeros((seq_count, head_count, count_of_rows), jnp.float32),
        jnp.zeros((seq_count, count_of_rows, head_count, head_width), jnp.float32),
    )
    key_piece = lax.all_gather(key_rows, CTX, axis=1, tiled=True)
    value_piece = lax.all_gather(value_rows, CTX, axis=1, tiled=True)
    piece_rows = key_piece.shape[1]
    block_rows = math.gcd(piece_rows, 512)
    key_split = key_piece.reshape(seq_count, piece_rows, head_count, head_width)
    value_split = value_piece.reshape(seq_count, piece_rows, head_count, head_width)

    def absorb_visit(running, block_index):
        first_key = block_index * block_rows

        def absorb_compute(current):
            row_max, row_total, weighted = current
            key_block = lax.dynamic_slice_in_dim(key_split, first_key, block_rows, 1)
            value_block = lax.dynamic_slice_in_dim(value_split, first_key, block_rows, 1)
            key_places = first_key + jnp.arange(block_rows, dtype=jnp.int32)
            key_segments = lax.dynamic_slice_in_dim(segments, first_key, block_rows, 1)
            scores = (
                jnp.einsum(
                    "sqhe,skhe->shqk", queries, key_block, preferred_element_type=jnp.float32
                )
                * score_scale
            )
            visible = (
                (key_places[None, :] <= query_places[:, None])[None]
                & (key_segments[:, None, :] == query_document_ids[:, :, None])
            )[:, None]
            new_max = jnp.maximum(row_max, jnp.max(jnp.where(visible, scores, neg_large), axis=-1))
            exponent = jnp.where(visible, jnp.exp(scores - new_max[..., None]), 0.0)
            factor = jnp.exp(row_max - new_max)
            new_total = row_total * factor + jnp.sum(exponent, axis=-1)
            update = jnp.einsum(
                "shqk,skhe->sqhe",
                exponent.astype(jnp.bfloat16),
                value_block,
                preferred_element_type=jnp.float32,
            )
            new_weighted = weighted * jnp.transpose(factor, (0, 2, 1))[..., None] + update
            return (new_max, new_total, new_weighted)

        def absorb_keep(current):
            return current

        return (lax.cond(first_key <= last_query, absorb_compute, absorb_keep, running), None)

    result, unused = lax.scan(
        absorb_visit, initial, jnp.arange(piece_rows // block_rows, dtype=jnp.int32)
    )
    row_max, row_total, weighted = result
    attended = weighted / jnp.transpose(row_total, (0, 2, 1))[..., None]
    return (attended, row_max + jnp.log(row_total))


def attend_back_gather(
    queries, grad_attended, log_normalizer, row_delta, key_rows, value_rows, segments, query_places
):
    seq_count, count_of_rows, head_count, head_width = queries.shape
    query_document_ids = lax.dynamic_slice_in_dim(segments, query_places[0], count_of_rows, 1)
    last_query = query_places[count_of_rows - 1]
    all_keys, all_values = (
        lax.all_gather(key_rows, CTX, axis=1, tiled=True),
        lax.all_gather(value_rows, CTX, axis=1, tiled=True),
    )
    length = all_keys.shape[1]
    block_rows = math.gcd(length, 512)
    key_split = all_keys.reshape(seq_count, length, head_count, head_width)
    value_split = all_values.reshape(seq_count, length, head_count, head_width)
    initial = (
        jnp.zeros((seq_count, count_of_rows, head_count, head_width), jnp.float32),
        jnp.zeros((seq_count, length, head_count, head_width), jnp.float32),
        jnp.zeros((seq_count, length, head_count, head_width), jnp.float32),
    )

    def attend_visit(state_now, block_index):
        first_key = block_index * block_rows

        def attend_compute(current):
            query_acc, key_acc, value_acc = current
            key_block = lax.dynamic_slice_in_dim(key_split, first_key, block_rows, 1)
            value_block = lax.dynamic_slice_in_dim(value_split, first_key, block_rows, 1)
            key_places = first_key + jnp.arange(block_rows, dtype=jnp.int32)
            key_segments = lax.dynamic_slice_in_dim(segments, first_key, block_rows, 1)
            query_part, key_part, value_part = block_grads(
                queries,
                grad_attended,
                log_normalizer,
                row_delta,
                query_places,
                query_document_ids,
                key_block,
                value_block,
                key_places,
                key_segments,
            )
            key_acc = lax.dynamic_update_slice_in_dim(key_acc, key_part, first_key, 1)
            value_acc = lax.dynamic_update_slice_in_dim(value_acc, value_part, first_key, 1)
            return (query_acc + query_part, key_acc, value_acc)

        def attend_keep(current):
            return current

        return (lax.cond(first_key <= last_query, attend_compute, attend_keep, state_now), None)

    totals, unused = lax.scan(
        attend_visit, initial, jnp.arange(length // block_rows, dtype=jnp.int32)
    )
    query_grad, key_grad, value_grad = totals
    key_home, value_home = (
        lax.psum_scatter(
            key_grad.reshape(seq_count, length, -1).astype(jnp.bfloat16),
            CTX,
            scatter_dimension=1,
            tiled=True,
        ).astype(jnp.float32),
        lax.psum_scatter(
            value_grad.reshape(seq_count, length, -1).astype(jnp.bfloat16),
            CTX,
            scatter_dimension=1,
            tiled=True,
        ).astype(jnp.float32),
    )
    split_shape = (seq_count, count_of_rows, head_count, head_width)
    return (query_grad, key_home.reshape(split_shape), value_home.reshape(split_shape))


def forward_layer(stream, first_values, weights, segments, cosine, sine_table, query_places):
    norm_attn, w_query, w_key, w_value, w_output, norm_ffn, w_gate, w_up, w_down = weights
    seq_count, count_of_rows, model_width = stream.shape
    head_count = w_query.shape[1] // HEAD_DIM
    split_shape = (seq_count, count_of_rows, head_count, HEAD_DIM)
    normed, inverse_one = norm_forward(stream, norm_attn)
    queries = rotate(project(normed, w_query).reshape(split_shape), cosine, sine_table).astype(
        jnp.bfloat16
    )
    key_rows = (
        rotate(project(normed, w_key).reshape(split_shape), cosine, sine_table)
        .astype(jnp.bfloat16)
        .reshape(seq_count, count_of_rows, -1)
    )
    own_values = project(normed, w_value)
    if first_values is None:
        mixed = own_values.astype(jnp.bfloat16)
    else:
        mixed = (0.5 * own_values + 0.5 * first_values).astype(jnp.bfloat16)
    attended, log_normalizer = attend_forward(queries, key_rows, mixed, segments, query_places)
    attended_low = attended.reshape(seq_count, count_of_rows, -1).astype(jnp.bfloat16)
    hidden_one = stream + head_total(project(attended_low, w_output))
    normed_two, inverse_two = norm_forward(hidden_one, norm_ffn)
    gate_values = project(normed_two, w_gate)
    up_values = project(normed_two, w_up)
    activated = (jax.nn.silu(gate_values) * up_values).astype(jnp.bfloat16)
    result = hidden_one + head_total(project(activated, w_down))
    saved_state = (
        stream,
        inverse_one,
        normed,
        queries,
        key_rows,
        mixed,
        attended,
        log_normalizer,
        attended_low,
        hidden_one,
        inverse_two,
        normed_two,
        gate_values,
        up_values,
        activated,
    )
    return (result, saved_state, own_values)


def backward_layer(
    grad_out, value_extra, saved_state, weights, segments, cosine, sine_table, query_places, mixes
):
    (
        stream,
        inverse_one,
        normed,
        queries,
        key_rows,
        mixed,
        attended,
        log_normalizer,
        attended_low,
        hidden_one,
        inverse_two,
        normed_two,
        gate_values,
        up_values,
        activated,
    ) = saved_state
    norm_attn, w_query, w_key, w_value, w_output, norm_ffn, w_gate, w_up, w_down = weights
    seq_count, count_of_rows, head_count, head_width = queries.shape
    grad_branch = grad_out.astype(jnp.bfloat16)
    down_grad = weight_term(activated, grad_branch)
    grad_active = project_back(grad_branch, w_down)
    gate_sigmoid = jax.nn.sigmoid(gate_values)
    grad_gate = (
        grad_active * up_values * gate_sigmoid * (1.0 + gate_values * (1.0 - gate_sigmoid))
    ).astype(jnp.bfloat16)
    grad_up = (grad_active * gate_values * gate_sigmoid).astype(jnp.bfloat16)
    gate_grad = weight_term(normed_two, grad_gate)
    up_grad = weight_term(normed_two, grad_up)
    grad_normed_two = head_back(project_back(grad_gate, w_gate) + project_back(grad_up, w_up))
    grad_norm_two, ffn_gain_grad = norm_backward(grad_normed_two, hidden_one, inverse_two, norm_ffn)
    grad_hidden = grad_out + grad_norm_two
    grad_attn = grad_hidden.astype(jnp.bfloat16)
    output_grad = weight_term(attended_low, grad_attn)
    grad_attended = (
        project_back(grad_attn, w_output)
        .astype(jnp.bfloat16)
        .reshape(seq_count, count_of_rows, head_count, head_width)
    )
    row_delta = jnp.transpose(
        jnp.sum(grad_attended.astype(jnp.float32) * attended, axis=-1), (0, 2, 1)
    )
    query_rot, key_rot, value_mix = attend_back_gather(
        queries, grad_attended, log_normalizer, row_delta, key_rows, mixed, segments, query_places
    )
    query_low = (
        rotate_back(query_rot, cosine, sine_table)
        .astype(jnp.bfloat16)
        .reshape(seq_count, count_of_rows, -1)
    )
    key_low = (
        rotate_back(key_rot, cosine, sine_table)
        .astype(jnp.bfloat16)
        .reshape(seq_count, count_of_rows, -1)
    )
    value_mix = value_mix.reshape(seq_count, count_of_rows, -1)
    if mixes:
        value_low = (0.5 * value_mix).astype(jnp.bfloat16)
        passed_on = 0.5 * value_mix
    else:
        value_low = (value_mix + value_extra).astype(jnp.bfloat16)
        passed_on = value_extra
    query_grad = weight_term(normed, query_low)
    key_grad = weight_term(normed, key_low)
    value_grad = weight_term(normed, value_low)
    grad_normed = head_back(
        project_back(query_low, w_query)
        + project_back(key_low, w_key)
        + project_back(value_low, w_value)
    )
    grad_norm_one, attn_gain_grad = norm_backward(grad_normed, stream, inverse_one, norm_attn)
    grad_stream = grad_hidden + grad_norm_one
    grad_terms = (
        attn_gain_grad,
        query_grad,
        key_grad,
        value_grad,
        output_grad,
        ffn_gain_grad,
        gate_grad,
        up_grad,
        down_grad,
    )
    return (grad_stream, passed_on, grad_terms)


def on_device(
    inputs,
    segment_ids,
    norm_attn_one,
    query_one,
    key_one,
    value_one,
    output_one,
    norm_ffn_one,
    gate_one,
    up_one,
    down_one,
    norm_attn_two,
    query_two,
    key_two,
    value_two,
    output_two,
    norm_ffn_two,
    gate_two,
    up_two,
    down_two,
    cotangent,
):
    def gather_layer(gain_attn, query, key, value, output, gain_ffn, gate, up, down):
        both = (DP, CTX)
        packed = jnp.concatenate([query, key, value, output.T, gate, up, down.T], axis=1)
        whole = lax.all_gather(packed, both, axis=0, tiled=True)
        gains = lax.all_gather(jnp.stack([gain_attn, gain_ffn]), both, axis=1, tiled=True)
        cuts = []
        for part in (query, key, value, output.T, gate, up, down.T):
            cuts.append((cuts[-1] if cuts else 0) + part.shape[1])
        w_q, w_k, w_v, w_o, w_g, w_u, w_d = jnp.split(whole, cuts[:-1], axis=1)
        return (gains[0], w_q, w_k, w_v, w_o.T, gains[1], w_g, w_u, w_d.T)

    def scatter_layer(grads, outs):
        both = (DP, CTX)
        gain_attn, query, key, value, output, gain_ffn, gate, up, down = grads
        pieces = [query, key, value, output.T, gate, up, down.T]
        packed = jnp.concatenate([part.astype(jnp.bfloat16) for part in pieces], axis=1)
        mine = lax.psum_scatter(packed, both, scatter_dimension=0, tiled=True)
        gains = lax.psum_scatter(
            jnp.stack([gain_attn, gain_ffn]).astype(jnp.bfloat16),
            both,
            scatter_dimension=1,
            tiled=True,
        ).astype(jnp.float32)
        cuts = []
        for part in pieces:
            cuts.append((cuts[-1] if cuts else 0) + part.shape[1])
        g_q, g_k, g_v, g_o, g_g, g_u, g_d = (
            part.astype(jnp.float32) for part in jnp.split(mine, cuts[:-1], axis=1)
        )
        return (gains[0], g_q, g_k, g_v, g_o.T, gains[1], g_g, g_u, g_d.T)

    gathered = gather_layer(
        norm_attn_one,
        query_one,
        key_one,
        value_one,
        output_one,
        norm_ffn_one,
        gate_one,
        up_one,
        down_one,
    ) + gather_layer(
        norm_attn_two,
        query_two,
        key_two,
        value_two,
        output_two,
        norm_ffn_two,
        gate_two,
        up_two,
        down_two,
    )
    weights_one = gathered[:9]
    weights_two = gathered[9:]
    seq_count, count_of_rows, model_width = inputs.shape
    query_places = lax.axis_index(CTX) * count_of_rows + jnp.arange(
        count_of_rows, dtype=jnp.int32
    )
    cosine, sine_table = rotary_tables(query_places[0], count_of_rows)
    layer_one, saved_one, first_values = forward_layer(
        inputs.astype(jnp.float32), None, weights_one, segment_ids, cosine, sine_table, query_places
    )
    layer_two, saved_two, unused = forward_layer(
        layer_one, first_values, weights_two, segment_ids, cosine, sine_table, query_places
    )
    grad_middle, value_extra, grads_two = backward_layer(
        cotangent.astype(jnp.float32),
        None,
        saved_two,
        weights_two,
        segment_ids,
        cosine,
        sine_table,
        query_places,
        True,
    )
    grad_input, unused_extra, grads_one = backward_layer(
        grad_middle,
        value_extra,
        saved_one,
        weights_one,
        segment_ids,
        cosine,
        sine_table,
        query_places,
        False,
    )
    totals = scatter_layer(grads_one, None) + scatter_layer(grads_two, None)
    return (
        layer_one.astype(jnp.bfloat16),
        layer_two.astype(jnp.bfloat16),
        grad_input,
        totals[0],
        totals[1],
        totals[2],
        totals[3],
        totals[4],
        totals[5],
        totals[6],
        totals[7],
        totals[8],
        totals[9],
        totals[10],
        totals[11],
        totals[12],
        totals[13],
        totals[14],
        totals[15],
        totals[16],
        totals[17],
    )


class Raw:
    def __init__(self, call, kind, index):
        self.call, self.kind, self.index = call, kind, index

    @property
    def ref(self):
        return self.call.refs[self.kind][self.index]

    @property
    def at(self):
        return self.ref.at

    @property
    def result(self):
        return self.call.results[self.index]


def cut_rows(ref, blocks, i):
    if blocks == 1:
        return ref
    rows = ref.shape[-2] // blocks
    part = pl.ds(i * rows, rows)
    return ref.at[part] if len(ref.shape) == 2 else ref.at[:, part]


class Store:
    def __init__(self, call, held, shape, dtype, blocks):
        self.held, self.blocks = held, blocks
        self.out = call.give(shape, dtype)
        self.flag = call.flags(blocks)
        call.stores.append(self)

    def copy(self, i):
        return pltpu.make_async_copy(
            cut_rows(self.held.ref, self.blocks, i),
            cut_rows(self.out.ref, self.blocks, i),
            self.flag.at[i],
        )

    def put(self, i=None):
        for k in range(self.blocks) if i is None else (i,):
            self.copy(k).start()

    def finish(self):
        for i in range(self.blocks):
            self.copy(i).wait()

    @property
    def result(self):
        return self.out.result


class Held:
    def __init__(self, call, shape, dtype):
        self.call, self.shape, self.dtype = call, shape, dtype
        self.slot = call.scratch_slot(pltpu.VMEM(shape, dtype))
        self.source = self.out = None
        self.blocks, self.waited = 1, set()

    @property
    def ref(self):
        return self.call.refs[2][self.slot]

    @property
    def at(self):
        return self.ref.at

    def __getitem__(self, key):
        return self.ref[key]

    def __setitem__(self, key, value):
        self.ref[key] = value

    def load_copy(self, i):
        return pltpu.make_async_copy(
            cut_rows(self.source.ref, self.blocks, i),
            cut_rows(self.ref, self.blocks, i),
            self.flag.at[i],
        )

    def need(self, i=None):
        if self.source is None:
            return
        for k in range(self.blocks) if i is None or self.blocks == 1 else (i,):
            if k not in self.waited:
                self.waited.add(k)
                self.load_copy(k).wait()

    def put(self, i=None):
        self.out.put(i)

    @property
    def result(self):
        return self.out.result


class Call:
    def __init__(self, number):
        self.number = number
        self.operands, self.shapes, self.scratch = [], [], []
        self.loads, self.stores, self.jobs = [], [], []
        self.far = self.in_turn = False

    def take(self, array):
        self.operands.append(array)
        return Raw(self, 0, len(self.operands) - 1)

    def give(self, shape, dtype):
        self.shapes.append(jax.ShapeDtypeStruct(shape, dtype))
        return Raw(self, 1, len(self.shapes) - 1)

    def scratch_slot(self, kind):
        self.scratch.append(kind)
        return len(self.scratch) - 1

    def flags(self, count):
        return Raw(self, 2, self.scratch_slot(pltpu.SemaphoreType.DMA((count,))))

    def hold(self, shape, dtype):
        return Held(self, shape, dtype)

    def load(self, array, blocks=1):
        held = Held(self, array.shape, array.dtype)
        self.load_into(held, self.take(array), blocks)
        self.loads.append(held)
        return held

    def load_into(self, held, source, blocks):
        held.source, held.blocks, held.flag = source, blocks, self.flags(blocks)

    def store(self, shape, dtype, blocks=1):
        held = Held(self, shape, dtype)
        held.out = Store(self, held, shape, dtype, blocks)
        return held

    def store_from(self, held, shape, dtype, blocks=1):
        return Store(self, held, shape, dtype, blocks)

    def start_loads(self, backward=False):
        if self.in_turn:
            for held in self.loads:
                for k in range(held.blocks):
                    held.load_copy(k).start()
            return
        for k in range(max([held.blocks for held in self.loads], default=0)):
            for held in self.loads:
                if k < held.blocks:
                    held.load_copy(held.blocks - 1 - k if backward else k).start()

    def run(self, body, remote_ops=True):
        ins, outs = len(self.operands), len(self.operands) + len(self.shapes)

        def kernel(*refs):
            self.refs = (refs[:ins], refs[ins:outs], refs[outs:])
            for held in self.loads:
                held.waited = set()
            body()
            for held in self.loads:
                held.need()
            for store in self.stores:
                store.finish()

        space = pl.BlockSpec(memory_space=pltpu.HBM)
        self.results = pl.pallas_call(
            kernel,
            out_shape=tuple(self.shapes),
            in_specs=[space] * ins,
            out_specs=(space,) * len(self.shapes),
            scratch_shapes=self.scratch,
            compiler_params=pltpu.CompilerParams(
                has_side_effects=remote_ops,
                vmem_limit_bytes=62 << 20,
                collective_id=self.number if remote_ops else None,
            ),
        )(*self.operands)
        self.refs = None


class Place:
    def __init__(self):
        self.dp, self.ctx, self.mp = (lax.axis_index(a) for a in (DP, CTX, MP))
        self.ctx_size = lax.axis_size(CTX)
        self.side = lax.rem(self.mp, 2)
        self.pair = (self.dp, self.ctx, self.mp + 1 - 2 * self.side)
        self.cross = (self.dp, self.ctx, lax.rem(self.mp + 2, 4))
        self.other = (1 - self.dp, self.ctx, self.mp)

    def ahead(self, step):
        return lax.rem(self.ctx + step, self.ctx_size)

    def behind(self, step):
        return lax.rem(self.ctx + self.ctx_size - step, self.ctx_size)

    def along(self, index):
        return (self.dp, index, self.mp)

    def peers(self, far):
        peers = [self.pair, self.cross]
        if far:
            peers.append(self.other)
            peers += [self.along(self.ahead(s)) for s in range(1, self.ctx_size)]
        return peers

    def greet(self, far):
        barrier = pltpu.get_barrier_semaphore()
        for peer in self.peers(far):
            pl.semaphore_signal(barrier, inc=1, device_id=peer, device_id_type=MESH)

    def enter(self, far):
        pl.semaphore_wait(pltpu.get_barrier_semaphore(), len(self.peers(far)))


def remote(source, target, send, recv, peer):
    return pltpu.make_async_remote_copy(
        src_ref=source,
        dst_ref=target,
        send_sem=send,
        recv_sem=recv,
        device_id=peer,
        device_id_type=MESH,
    )


class HeadSum:
    def __init__(self, call, blocks, rows, width):
        self.half = rows // 2
        self.part = call.hold((blocks, rows, width), jnp.bfloat16)
        self.near, self.far, self.rest = (
            call.hold((blocks, rows // 2, width), jnp.bfloat16) for _ in range(3)
        )
        self.sa, self.ra, self.sb, self.rb, self.sc, self.rc = (
            call.flags(blocks) for _ in range(6)
        )

    def bind(self, place):
        self.place = place

    def own(self):
        return pl.ds(pl.multiple_of(self.place.side * self.half, self.half), self.half)

    def theirs(self):
        start = (1 - self.place.side) * self.half
        return pl.ds(pl.multiple_of(start, self.half), self.half)

    def first(self, i):
        source = self.part.at[i, self.theirs()]
        return remote(source, self.near.at[i], self.sa.at[i], self.ra.at[i], self.place.pair)

    def second(self, i):
        return remote(
            self.near.at[i], self.far.at[i], self.sb.at[i], self.rb.at[i], self.place.cross
        )

    def third(self, i):
        return remote(
            self.far.at[i], self.rest.at[i], self.sc.at[i], self.rc.at[i], self.place.pair
        )

    def send(self, i, partial_rows):
        self.part[i] = partial_rows.astype(jnp.bfloat16)
        self.first(i).start()

    def middle(self, i):
        self.first(i).wait()
        mine = self.part[i, self.own()].astype(jnp.float32)
        self.near[i] = (mine + self.near[i].astype(jnp.float32)).astype(jnp.bfloat16)
        self.second(i).start()

    def last(self, i):
        self.second(i).wait()
        total = self.near[i].astype(jnp.float32) + self.far[i].astype(jnp.float32)
        self.far[i] = total.astype(jnp.bfloat16)
        self.third(i).start()

    def total(self, i):
        self.third(i).wait()
        self.part[i, self.own()] = self.far[i]
        self.part[i, self.theirs()] = self.rest[i]
        return self.part[i].astype(jnp.float32)


class QuarterSum(HeadSum):
    def __init__(self, call, blocks, rows, width):
        self.half, self.quarter = rows // 2, rows // 4
        self.part = call.hold((blocks, rows, width), jnp.bfloat16)
        self.near = call.hold((blocks, rows // 2, width), jnp.bfloat16)
        self.far = call.hold((blocks, rows // 4, width), jnp.bfloat16)
        self.out = call.store((blocks, rows // 4, width), jnp.bfloat16)
        self.sa, self.ra, self.sb, self.rb = (call.flags(blocks) for _ in range(4))

    def rows_of(self, index):
        return pl.ds(pl.multiple_of(index * self.quarter, self.quarter), self.quarter)

    def second(self, i):
        source = self.near.at[i, self.rows_of(1 - self.place.mp // 2)]
        return remote(source, self.far.at[i], self.sb.at[i], self.rb.at[i], self.place.cross)

    def last(self, i):
        self.second(i).wait()
        mine = self.near[i, self.rows_of(self.place.mp // 2)].astype(jnp.float32)
        self.out[i] = (mine + self.far[i].astype(jnp.float32)).astype(jnp.bfloat16)


class Gather:
    def __init__(self, call, shard, places, swap=False, land=False):
        self.parts = lax.axis_size(CTX)
        call.far = True
        if isinstance(shard, Held):
            self.shard = shard
        else:
            self.shard = call.load(shard)
            call.loads.insert(0, call.loads.pop())
        self.land = land
        whole = (places,) + shard.shape
        self.whole = (call.store if land else call.give)(whole, shard.dtype)
        self.zs, self.zr, self.ys, self.yr = (call.flags(self.parts) for _ in range(4))
        self.l, self.ss, self.sr = (call.flags(1) for _ in range(3))
        self.relayed = self.parts == 4
        self.swap = swap and self.relayed
        self.order = (2, 1, 3) if self.relayed else tuple(range(self.parts - 1, 0, -1))
        self.steps = len(self.order)

    def bind(self, place):
        self.place, self.crossed = place, False

    def slot(self, dp, ctx):
        return self.whole.at[dp * self.parts + ctx]

    def local(self):
        p = self.place
        return pltpu.make_async_copy(self.shard.ref, self.slot(p.dp, p.ctx), self.l.at[0])

    def along(self, s):
        p = self.place
        target = self.slot(p.dp, p.ctx)
        return remote(self.shard.ref, target, self.zs.at[s], self.zr.at[s], p.along(p.ahead(s)))

    def direct(self, s, act):
        if self.relayed and s != 2:
            pl.when(self.place.ctx != (0 if s == 3 else 3))(lambda: act(self.along(s)))
        else:
            act(self.along(s))

    def relay(self, act):
        p = self.place
        block = self.slot(p.dp, p.behind(2))
        for middle, end, s in ((2, 3, 3), (1, 0, 1)):
            copy = remote(block, block, self.zs.at[0], self.zr.at[s], p.along(end))
            pl.when(p.ctx == middle)(lambda copy=copy: act(copy))

    def across(self, s):
        p = self.place
        block = self.slot(p.dp, p.behind(s))
        source = self.shard.ref if s == 0 else block
        return remote(source, block, self.ys.at[s], self.yr.at[s], p.other)

    def arrive(self, s):
        p = self.place
        block = self.slot(1 - p.dp, p.behind(s))
        return remote(block, block, self.ys.at[s], self.yr.at[s], p.other)

    def when_crossing(self, s, act):
        if self.swap and s in (1, 3):
            pl.when(lax.rem(self.place.ctx, 2) == (0 if s == 1 else 1))(act)
        else:
            act()

    def swapped(self, ctx):
        p = self.place
        block = self.slot(1 - p.dp, ctx)
        neighbour = p.ctx + 1 - 2 * lax.rem(p.ctx, 2)
        return remote(block, block, self.ss.at[0], self.sr.at[0], p.along(neighbour))

    def cross(self):
        self.crossed = True
        self.shard.need()
        self.across(0).start()

    def start(self):
        self.shard.need()
        for s in self.order:
            self.direct(s, lambda copy: copy.start())
        if not self.crossed:
            self.cross()
        self.local().start()

    def step(self, k):
        s = self.order[k]
        p = self.place
        block = self.slot(p.dp, p.behind(s))
        remote(block, block, self.zs.at[s], self.zr.at[s], p.along(p.ctx)).wait_recv()
        if self.relayed and s == 2:
            self.relay(lambda copy: copy.start())
        self.when_crossing(s, lambda: self.across(s).start())
        if self.swap and k == 0:
            self.arrive(0).wait_recv()
            self.swapped(p.ctx).start()

    def finish(self):
        p = self.place
        self.local().wait()
        for s in self.order:
            self.direct(s, lambda copy: copy.wait_send())
        if self.relayed:
            self.relay(lambda copy: copy.wait_send())

        def both(s):
            self.across(s).wait_send()
            self.arrive(s).wait_recv()

        for s in self.order:
            self.when_crossing(s, functools.partial(both, s))
        self.across(0).wait_send()
        if self.swap:
            self.swapped(p.ctx).wait_send()
            self.swapped(p.ctx + 1 - 2 * lax.rem(p.ctx, 2)).wait_recv()
        else:
            self.arrive(0).wait_recv()
        if self.land:
            self.whole.put()

    @property
    def result(self):
        whole = self.whole.result
        return whole.reshape(-1, whole.shape[-1])


class Scatter:
    def __init__(self, call, blocks, swap=False):
        self.parts = lax.axis_size(CTX)
        places, rows, width = blocks.shape
        self.dtype = blocks.dtype
        call.far = True
        self.late = isinstance(blocks, Held)
        self.blocks = blocks if self.late else call.take(blocks)
        self.out = call.store((rows, width), jnp.float32)
        if not self.late:
            self.mb = call.hold((self.parts, rows, width), blocks.dtype)
        self.yb = call.hold((self.parts, rows, width), blocks.dtype)
        self.zb = call.hold((self.parts - 1, rows, width), blocks.dtype)
        self.zs, self.zr, self.ys, self.yr = (call.flags(self.parts) for _ in range(4))
        self.l, self.ss, self.sr = (call.flags(2) for _ in range(3))
        self.relayed = self.parts == 4
        self.swap = swap and self.relayed
        self.order = (3, 1, 2, 0) if self.relayed else tuple(range(self.parts - 1, -1, -1))
        if self.relayed:
            self.rb = call.hold((rows, width), blocks.dtype)
        if self.swap:
            self.tb, self.wb = (call.hold((rows, width), blocks.dtype) for _ in range(2))
        self.steps = self.parts

    def bind(self, place):
        self.place = place

    def block_of(self, dp, ctx):
        return self.blocks.at[dp * self.parts + ctx]

    def local(self):
        mine = self.blocks.at[pl.ds(self.place.dp * self.parts, self.parts)]
        return pltpu.make_async_copy(mine, self.mb.ref, self.l.at[0])

    def local_twin(self):
        p = self.place
        return pltpu.make_async_copy(self.block_of(1 - p.dp, p.ctx), self.tb.ref, self.l.at[1])

    def swapped(self):
        p = self.place
        neighbour = p.ctx + 1 - 2 * lax.rem(p.ctx, 2)
        block = self.block_of(1 - p.dp, neighbour)
        return remote(block, self.wb.ref, self.ss.at[0], self.sr.at[0], p.along(neighbour))

    def across(self, s):
        p = self.place
        block = self.tb.ref if self.swap and s == 0 else self.block_of(1 - p.dp, p.ahead(s))
        return remote(block, self.yb.at[s], self.ys.at[s], self.yr.at[s], p.other)

    def when_crossing(self, s, act):
        if self.swap and s in (1, 3):
            pl.when(lax.rem(self.place.ctx, 2) == (1 if s == 1 else 0))(act)
        else:
            act()

    def along(self, s, act):
        p = self.place
        target = self.zb.at[s - 1]
        copy = remote(self.yb.at[s], target, self.zs.at[s], self.zr.at[s], p.along(p.ahead(s)))
        if not self.relayed or s == 2:
            act(copy)
            return
        end, middle = (0, 1) if s == 3 else (3, 2)
        way = remote(self.yb.at[s], self.rb.ref, self.zs.at[s], self.zr.at[0], p.along(middle))
        pl.when(p.ctx != end)(lambda: act(copy))
        pl.when(p.ctx == end)(lambda: act(way))

    def early(self, act):
        p = self.place
        for s, odd in ((1, 0), (3, 1)):
            block, target = self.block_of(p.dp, p.ahead(s)), self.zb.at[s - 1]
            copy = remote(block, target, self.zs.at[s], self.zr.at[s], p.along(p.ahead(s)))
            pl.when(lax.rem(p.ctx, 2) == odd)(lambda copy=copy: act(copy))

    def start(self):
        if self.swap:
            self.swapped().start()
            self.local_twin().start()
            self.early(lambda copy: copy.start())
        for s in self.order:
            if s or not self.swap:
                self.when_crossing(s, lambda s=s: self.across(s).start())
        if not self.late:
            self.local().start()

    def send_twin(self):
        self.local_twin().wait()
        self.swapped().wait()
        both = self.tb[...].astype(jnp.float32) + self.wb[...].astype(jnp.float32)
        self.tb[...] = both.astype(self.dtype)
        self.across(0).start()

    def step(self, k):
        p = self.place
        s = self.order[k]
        if k == 0:
            if not self.late:
                self.local().wait()
            if self.swap:
                self.send_twin()
        if self.late:
            mine = self.blocks[p.dp * self.parts + p.ahead(s)]
        else:
            mine = self.mb[p.ahead(s)]
        mine = mine.astype(jnp.float32)

        def add_crossed():
            self.across(s).wait()
            self.yb[s] = (mine + self.yb[s].astype(jnp.float32)).astype(self.dtype)
            if s != 2:
                self.along(s, lambda copy: copy.start())

        if s == 0:
            self.across(s).wait()
            self.out[...] = mine + self.yb[s].astype(jnp.float32)
            return
        self.when_crossing(s, add_crossed)
        if s != 2:
            return
        if self.relayed:

            def add_ends():
                way = remote(self.rb.ref, self.rb.ref, self.zs.at[0], self.zr.at[0], p.other)
                way.wait_recv()
                through = self.yb[s].astype(jnp.float32) + self.rb[...].astype(jnp.float32)
                self.yb[s] = through.astype(self.dtype)

            pl.when((p.ctx == 1) | (p.ctx == 2))(add_ends)
        self.along(s, lambda copy: copy.start())

    def finish(self):
        p = self.place

        def add(s):
            block = self.zb.at[s - 1]
            remote(block, block, self.zs.at[s], self.zr.at[s], p.other).wait_recv()
            self.out[...] += self.zb[s - 1].astype(jnp.float32)

        for s in self.order:
            if s == 0:
                continue
            self.along(s, lambda copy: copy.wait_send())
            if self.relayed and s != 2:
                pl.when(p.ctx != (3 if s == 3 else 0))(functools.partial(add, s))
            else:
                add(s)
        self.out.put()

    @property
    def result(self):
        return self.out.result


class Deal:
    def __init__(self, call, blocks, rows=None, land=False):
        self.parts, self.compact = lax.axis_size(CTX), rows is not None
        length, width = rows or blocks.shape[1], blocks.shape[2]
        self.share = length // 4
        call.far = True
        self.source = call.take(blocks)
        self.land = land
        target = (self.parts, length, width)
        self.target = (call.store if land else call.give)(target, blocks.dtype)
        self.held = call.hold(blocks.shape[1:], blocks.dtype)
        self.l = call.flags(2)
        self.zf, self.af, self.xf, self.bf = (
            tuple(call.flags(self.parts) for _ in range(2)) for _ in range(4)
        )
        self.order = list(range(self.parts - 1, 0, -1))
        if self.compact:
            self.order.insert(0, 0)
        self.steps = 2 * len(self.order)

    def bind(self, place):
        self.place = place
        if self.compact:
            x, side = place.mp // 2, place.side
            self.own, self.far = side * 2 + x, side * 2 + 1 - x
            self.near, self.near_far = (1 - side) * 2 + x, (1 - side) * 2 + 1 - x
        else:
            self.own, self.far = place.mp, lax.rem(place.mp + 2, 4)
            self.near = place.mp + 1 - 2 * place.side
            self.near_far = lax.rem(self.near + 2, 4)

    def rows(self, index):
        return pl.ds(pl.multiple_of(index * self.share, self.share), self.share)

    def local(self, k):
        p = self.place
        target = self.target.at[p.ctx]
        if self.compact:
            target = self.target.at[p.ctx, self.rows(self.own)]
        refs = (self.source.at[p.ctx], self.held.ref, target)
        return pltpu.make_async_copy(refs[k], refs[k + 1], self.l.at[k])

    def along(self, s):
        p = self.place
        rows = self.rows(self.own)
        source = self.source.at[p.ahead(s)] if self.compact else self.source.at[p.ahead(s), rows]
        target = self.target.at[p.ctx, rows]
        return remote(source, target, self.zf[0].at[s], self.zf[1].at[s], p.along(p.ahead(s)))

    def piece(self, s, index, flags, peer):
        ref = self.target.at[self.place.behind(s), self.rows(index)]
        return remote(ref, ref, flags[0].at[s], flags[1].at[s], peer)

    def start(self):
        for s in self.order:
            if s:
                self.along(s).start()
        self.local(0).start()

    def step(self, k):
        p = self.place
        if k == 0:
            self.local(0).wait()
            self.local(1).start()
        s = self.order[k % len(self.order)]
        if k < len(self.order):
            if s:
                self.piece(s, self.own, self.zf, p.along(p.ctx)).wait_recv()
            else:
                self.local(1).wait()
            self.piece(s, self.own, self.xf, p.cross).start()
            self.piece(s, self.own, self.af, p.pair).start()
        else:
            self.piece(s, self.far, self.xf, p.cross).wait_recv()
            self.piece(s, self.far, self.bf, p.pair).start()

    def finish(self):
        p = self.place
        if not self.compact:
            self.local(1).wait()
        for s in self.order:
            if s:
                self.along(s).wait_send()
            self.piece(s, self.own, self.xf, p.cross).wait_send()
            self.piece(s, self.own, self.af, p.pair).wait_send()
            self.piece(s, self.far, self.bf, p.pair).wait_send()
            self.piece(s, self.near, self.af, p.pair).wait_recv()
            self.piece(s, self.near_far, self.bf, p.pair).wait_recv()
        if self.land:
            self.target.put()

    @property
    def result(self):
        whole = self.target.result
        return whole.reshape(-1, whole.shape[-1])


LATE = "late"


class Jobs:
    def __init__(self, jobs, plan):
        self.jobs = list(jobs)
        self.queue = sorted(
            (times[k] if len(times) > 2 else times[0] + k * times[1], j, k)
            for j, (job, times) in enumerate(zip(self.jobs, plan))
            for k in range(job.steps)
        )
        self.at = 0

    def bind(self, place):
        self.at = 0
        for job in self.jobs:
            job.bind(place)

    def start(self):
        for job in self.jobs:
            if not getattr(job, LATE, False):
                job.start()

    def advance(self, reached):
        while self.at < len(self.queue) and self.queue[self.at][0] <= reached:
            _, j, k = self.queue[self.at]
            self.jobs[j].step(k)
            self.at += 1

    def finish(self):
        self.advance(math.inf)
        for job in self.jobs:
            job.finish()


def begin(call, total, jobs, backward=False):
    place = Place()
    if total is not None:
        total.bind(place)
    jobs.bind(place)
    place.greet(call.far)
    call.start_loads(backward)
    place.enter(call.far)
    jobs.start()
    return place


def dot_nn(a, b):
    return lax.dot_general(a, b, (((1,), (0,)), ((), ())), preferred_element_type=jnp.float32)


def dot_nt(a, b):
    return lax.dot_general(a, b, (((1,), (1,)), ((), ())), preferred_element_type=jnp.float32)


def dot_tn(a, b):
    return lax.dot_general(a, b, (((0,), (0,)), ((), ())), preferred_element_type=jnp.float32)


def lane_number(width):
    return lax.broadcasted_iota(jnp.int32, (1, width), 1)


LANES = 128
BLOCKS = 4


def turn(values, cosine, signed_sine, back):
    half = HEAD_DIM // 2
    leading = lax.rem(lane_number(LANES), HEAD_DIM) < half
    pieces = []
    for at in range(0, values.shape[1], LANES):
        piece = values[:, at : at + LANES]
        swapped = jnp.where(leading, pltpu.roll(piece, LANES - half, 1), pltpu.roll(piece, half, 1))
        moved = swapped * signed_sine
        pieces.append(piece * cosine - moved if back else piece * cosine + moved)
    return jnp.concatenate(pieces, axis=1)


def write_bias(bias, seg_col, seg_row, i, rows, keys):
    query_at = i * rows + lax.broadcasted_iota(jnp.int32, (rows, 1), 0)
    key_at = lax.broadcasted_iota(jnp.int32, (1, keys), 1)
    same = seg_col[pl.ds(i * rows, rows), :1] == seg_row[:1, :keys]
    bias[:, :keys] = jnp.where(same & (key_at <= query_at), 0.0, neg_large)


class Stacked:
    def __init__(self, held):
        self.held, self.dtype = held, held.dtype
        blocks, rows, width = held.shape
        self.shape = (blocks * rows, width)

    def need(self, i=None):
        pass

    def __getitem__(self, key):
        rows, columns = key
        if isinstance(rows, slice):
            block = self.held[:, :, columns]
            return block.reshape(-1, block.shape[-1])
        return self.held[rows.start // self.held.shape[1], :, columns]


class Opening:
    def __init__(self, call, inputs, segment_ids, layers, gain_rows, angle_row, places):
        self.call, self.places = call, places
        parts, length, width = inputs.shape
        self.count = count = parts * length
        (q1, k1, v1, o1, *tall1), (q2, k2, v2, o2, *tall2) = layers
        self.shard, self.hid = shard, hid = q1.shape
        units = tall1[0].shape[0]
        low = jnp.bfloat16
        self.first = [call.load(array) for array in (q1, k1, v1, o1)]
        self.gain_rows = call.load(gain_rows)
        self.ids, self.angle = call.load(segment_ids), call.load(angle_row)
        self.tall = [call.load(array) for array in tall1]
        self.second = [call.load(array) for array in (q2, k2, v2, o2)]
        self.tall += [call.load(array) for array in tall2]
        self.shards_one = [call.hold((shard, units), low) for _ in tall1]
        self.shards_two = [call.store((shard, units), low) for _ in tall2]
        self.wa_one = call.hold((shard, 4 * hid), low)
        self.wa_two = call.store((shard, 4 * hid), low)
        self.gains_wide = call.hold(gain_rows.shape, jnp.float32)
        self.cosine, self.sine, self.seg_col = (
            call.store((count, LANES), jnp.float32, BLOCKS) for _ in range(3)
        )
        self.seg_row = call.store((8, count), jnp.float32)
        self.gather = Gather(call, self.wa_one, places, land=True)
        self.deal = Deal(call, inputs, land=True)
        self.gather_gains = Gather(call, self.gains_wide, places, land=True)
        plan = ((2.0, 0.1), (5.0, 4.0), (14.0, 6.0))
        self.jobs = Jobs([self.gather_gains, self.deal, self.gather], plan)
        self.deal.late = True
        self.x, self.wa = Stacked(self.deal.target), Stacked(self.gather.whole)
        self.gains = call.store((gain_rows.shape[0], width), jnp.float32)

    def tables(self):
        return (self.cosine, self.sine, self.seg_col, self.seg_row)

    def run(self, total, jobs):
        call, hid = self.call, self.hid
        place = Place()
        total.bind(place)
        self.jobs.bind(place)
        jobs.bind(place)
        place.greet(call.far)
        call.start_loads()
        place.enter(call.far)
        self.deal.start()
        for j, held in enumerate(self.first):
            held.need()
            values = held[...]
            self.wa_one[:, j * hid : (j + 1) * hid] = values.T if j == 3 else values
        self.gain_rows.need()
        self.gains_wide[...] = self.gain_rows[...].astype(jnp.float32)
        self.jobs.start()
        for tall, shard in zip(self.tall, self.shards_one + self.shards_two):
            tall.need()
            shard[...] = tall[...].T
            if shard.out is not None:
                shard.put()
        for j, held in enumerate(self.second):
            held.need()
            values = held[...]
            self.wa_two[:, j * hid : (j + 1) * hid] = values.T if j == 3 else values
        self.wa_two.put()
        for job in jobs.jobs:
            job.cross()
        self.ids.need()
        self.angle.need()
        ids = self.ids[...].astype(jnp.float32)
        mine = lax.broadcasted_iota(jnp.int32, ids.shape, 0) == place.ctx
        own = jnp.sum(jnp.where(mine, ids, 0.0), axis=0, keepdims=True)
        self.seg_row[...] = jnp.broadcast_to(own, self.seg_row.shape)
        self.seg_row.put()
        self.seg_col[...] = jnp.broadcast_to(own, (LANES, self.count)).T
        self.seg_col.put()
        rows = self.count // BLOCKS
        for i in range(BLOCKS):
            at = pl.ds(i * rows, rows)
            index = i * rows + lax.broadcasted_iota(jnp.int32, (rows, 1), 0)
            angles = index.astype(jnp.float32) * self.angle[:1, :]
            self.cosine[at, :] = jnp.cos(angles)
            self.sine[at, :] = jnp.sin(angles) * self.angle[1:2, :]
        self.cosine.put()
        self.sine.put()
        self.jobs.advance(math.inf)
        jobs.start()
        self.jobs.finish()
        jobs.advance(0.5)
        shard = self.shard
        for k in range(self.places):
            self.gains[:, k * shard : (k + 1) * shard] = self.gather_gains.whole[k]
        self.gains.put()


def attention_layer(number, x, first_v, wa, gains, which, tables, jobs_of, plan, opening=None):
    call = Call(number)
    if opening is None:
        start = None
        x, gains, wa = call.load(x, BLOCKS), call.load(gains), call.load(wa)
        cosine, sine, seg_col = (call.load(table, BLOCKS) for table in tables[:3])
        seg_row = call.load(tables[3])
    else:
        start = opening(call)
        x, gains, wa = start.x, start.gains, start.wa
        cosine, sine, seg_col, seg_row = start.tables()
    count, width = x.shape
    hid = wa.shape[1] // 4
    heads = hid // HEAD_DIM
    rows = count // BLOCKS
    if first_v is not None:
        first_v = call.load(first_v, BLOCKS)
    else:
        v = call.store((count, hid), jnp.float32, BLOCKS)
    x1 = call.store((count, width), jnp.float32, BLOCKS)
    h = call.store((count, width), jnp.bfloat16, BLOCKS)
    q, k, m, o = (call.store((count, hid), jnp.bfloat16, BLOCKS) for _ in range(4))
    lse = call.store((heads, count, 1), jnp.float32, BLOCKS)
    bias = call.hold((rows, count), jnp.float32)
    acc = call.hold((rows, hid), jnp.float32)
    total = HeadSum(call, BLOCKS, rows, width)
    carried = jobs_of(call, start)
    jobs = Jobs(carried, plan)

    def body():
        if start is None:
            begin(call, total, jobs)
        else:
            start.run(total, jobs)
        lane = lane_number(hid)
        for i in range(BLOCKS):
            at = pl.ds(i * rows, rows)
            x.need(i)
            gains.need()
            stream = x[at, :].astype(jnp.float32)
            inverse = lax.rsqrt(jnp.mean(stream * stream, axis=-1, keepdims=True) + epsilon)
            normed = (stream * inverse * gains[which : which + 1, :]).astype(jnp.bfloat16)
            h[at, :] = normed
            h.put(i)
            wa.need()
            projected = dot_nn(normed, wa[:, : 3 * hid])
            cosine.need(i)
            sine.need(i)
            cos, sin = cosine[at, :], sine[at, :]
            queries = turn(projected[:, :hid], cos, sin, False).astype(jnp.bfloat16)
            q[at, :] = queries * jnp.bfloat16(HEAD_DIM**-0.5)
            k[at, :] = turn(projected[:, hid : 2 * hid], cos, sin, False).astype(jnp.bfloat16)
            values = projected[:, 2 * hid :]
            if first_v is None:
                v[at, :] = values
                v.put(i)
            else:
                first_v.need(i)
                values = 0.5 * values + 0.5 * first_v[at, :]
            m[at, :] = values.astype(jnp.bfloat16)
            for held in (q, k, m):
                held.put(i)
            keys = (i + 1) * rows
            seg_col.need(i)
            seg_row.need()
            write_bias(bias, seg_col, seg_row, i, rows, keys)
            if i:
                total.middle(i - 1)
            jobs.advance((4.5, 8.0, 12.5, 18.0)[i])

            def one_head(index, unused):
                mask = lane // HEAD_DIM == index
                query = jnp.where(mask, q[at, :], jnp.bfloat16(0))
                scores = dot_nt(query, k[:keys, :]) + bias[:, :keys]
                top = jnp.max(scores, axis=-1, keepdims=True)
                exponent = jnp.exp(scores - top)
                summed = jnp.sum(exponent, axis=-1, keepdims=True)
                weighted = dot_nn(exponent.astype(jnp.bfloat16), m[:keys, :])
                acc[...] = jnp.where(mask, weighted / summed, acc[...])
                lse[index, at, :] = top + jnp.log(summed)
                return unused

            lax.fori_loop(0, heads, one_head, 0)
            attended = acc[...].astype(jnp.bfloat16)
            o[at, :] = attended
            o.put(i)
            lse.put(i)
            total.send(i, dot_nt(attended, wa[:, 3 * hid :]))
            jobs.advance((6.0, 10.5, 16.0, 22.5)[i])
        total.middle(BLOCKS - 1)
        for i in range(BLOCKS):
            total.last(i)
            jobs.advance((23.0, 24.0, 28.0, 33.0)[i])
        for i in range(BLOCKS):
            at = pl.ds(i * rows, rows)
            x1[at, :] = x[at, :].astype(jnp.float32) + total.total(i)
            x1.put(i)
        jobs.finish()

    call.run(body)
    return SimpleNamespace(
        x1=x1.result,
        h=h.result,
        q=q.result,
        k=k.result,
        m=m.result,
        o=o.result,
        lse=lse.result,
        v=v.result if first_v is None else None,
        carried=[job.result for job in carried],
        start=start,
    )


def feed_forward_layer(number, x1, gate, up, down, gains, which, jobs_of, plan):
    count, width = x1.shape
    units = gate.shape[1]
    rows = count // BLOCKS
    call = Call(number)
    x1 = call.load(x1, BLOCKS)
    gains, gate, up, down = (call.load(array) for array in (gains, gate, up, down))
    y = call.store_from(x1, (count, width), jnp.float32, BLOCKS)
    y_low, h2 = (call.store((count, width), jnp.bfloat16, BLOCKS) for _ in range(2))
    z, u, a = (call.store((count, units), jnp.bfloat16, BLOCKS) for _ in range(3))
    total = HeadSum(call, BLOCKS, rows, width)
    carried = jobs_of(call)
    jobs = Jobs(carried, plan)

    def body():
        begin(call, total, jobs)
        for i in range(BLOCKS):
            at = pl.ds(i * rows, rows)
            x1.need(i)
            gains.need()
            stream = x1[at, :]
            inverse = lax.rsqrt(jnp.mean(stream * stream, axis=-1, keepdims=True) + epsilon)
            normed = (stream * inverse * gains[which : which + 1, :]).astype(jnp.bfloat16)
            h2[at, :] = normed
            gate.need()
            gated = dot_nn(normed, gate[...])
            if i:
                total.middle(i - 1)
            jobs.advance(2.5 * i + 4.0)
            up.need()
            raised = dot_nn(normed, up[...])
            active = (gated * lax.logistic(gated) * raised).astype(jnp.bfloat16)
            z[at, :] = gated.astype(jnp.bfloat16)
            u[at, :] = raised.astype(jnp.bfloat16)
            a[at, :] = active
            for held in (h2, z, u, a):
                held.put(i)
            down.need()
            total.send(i, dot_nt(active, down[...]))
            jobs.advance(2.5 * i + 5.5)
        total.middle(BLOCKS - 1)
        for i in range(BLOCKS):
            total.last(i)
            jobs.advance(13.0 + 5.7 * i)
        for i in range(BLOCKS):
            at = pl.ds(i * rows, rows)
            result = x1[at, :] + total.total(i)
            x1[at, :] = result
            y_low[at, :] = result.astype(jnp.bfloat16)
            y.put(i)
            y_low.put(i)
        jobs.finish()

    call.run(body)
    return SimpleNamespace(
        y=y.result,
        y_low=y_low.result,
        h2=h2.result,
        z=z.result,
        u=u.result,
        a=a.result,
        carried=[job.result for job in carried],
    )


def norm_back(gain, grad, stream, gain_sum):
    inverse = lax.rsqrt(jnp.mean(stream * stream, axis=-1, keepdims=True) + epsilon)
    scaled = stream * inverse
    grad_scaled = grad * gain
    products = jnp.mean(grad_scaled * scaled, axis=-1, keepdims=True)
    gain_sum = gain_sum + jnp.sum(grad * scaled, axis=0, keepdims=True)
    return inverse * (grad_scaled - scaled * products), gain_sum


def feed_forward_back(number, gy, x1, saved, gate, up, down, gains, which, jobs_of, plan):
    count, width = x1.shape
    units = gate.shape[1]
    rows = count // BLOCKS
    call = Call(number)
    call.in_turn = True
    if saved is not None:
        gy = call.load(gy, BLOCKS)
        down = call.load(down)
        z, u = call.load(saved.z, BLOCKS), call.load(saved.u, BLOCKS)
        gate, up, a, h2, gains = (call.load(w) for w in (gate, up, saved.a, saved.h2, gains))
        x1 = call.load(x1, BLOCKS)
        later = 0.0
    else:
        x1, gains = call.load(x1, BLOCKS), call.load(gains)
        gate, up, down = (call.load(w) for w in (gate, up, down))
        gy = call.load(gy, BLOCKS)
        h2 = call.hold((count, width), jnp.bfloat16)
        z, u, a = (call.hold((count, units), jnp.bfloat16) for _ in range(3))
        quarters = QuarterSum(call, BLOCKS, rows, width)
        later = 10.0
    gx1 = call.store_from(x1, (count, width), jnp.float32, BLOCKS)
    gain = call.store((1, width), jnp.float32)
    d_gate, d_up = (call.store((width, units), jnp.bfloat16, 4) for _ in range(2))
    places = lax.axis_size(DP) * lax.axis_size(CTX)
    shard = width // places
    d_down = call.hold((places, shard, units), jnp.bfloat16)
    low = call.hold((count, width), jnp.bfloat16)
    gz, gu = (call.hold((count, units), jnp.bfloat16) for _ in range(2))
    total = HeadSum(call, BLOCKS, rows, width)
    down_sum = Scatter(call, d_down)
    carried = jobs_of(call, down_sum)
    jobs = Jobs(carried, plan)

    def forward():
        for i in range(BLOCKS):
            at = pl.ds(i * rows, rows)
            x1.need(i)
            gains.need()
            stream = x1[at, :]
            inverse = lax.rsqrt(jnp.mean(stream * stream, axis=-1, keepdims=True) + epsilon)
            normed = (stream * inverse * gains[which : which + 1, :]).astype(jnp.bfloat16)
            h2[at, :] = normed
            gate.need()
            gated = dot_nn(normed, gate[...])
            up.need()
            raised = dot_nn(normed, up[...])
            active = (gated * lax.logistic(gated) * raised).astype(jnp.bfloat16)
            z[at, :] = gated.astype(jnp.bfloat16)
            u[at, :] = raised.astype(jnp.bfloat16)
            a[at, :] = active
            down.need()
            if i:
                quarters.middle(i - 1)
            quarters.send(i, dot_nt(active, down[...]) + stream * 0.25)
        quarters.middle(BLOCKS - 1)

    def body():
        if saved is None:
            quarters.bind(begin(call, total, jobs))
            forward()
        else:
            begin(call, total, jobs)
        for i in range(BLOCKS):
            at = pl.ds(i * rows, rows)
            gy.need(i)
            low[at, :] = gy[at, :].astype(jnp.bfloat16)
        for i in range(BLOCKS):
            at = pl.ds(i * rows, rows)
            down.need()
            ga = dot_nn(low[at, :], down[...])
            z.need(i)
            u.need(i)
            gated = z[at, :].astype(jnp.float32)
            sigma = lax.logistic(gated)
            raised = u[at, :].astype(jnp.float32)
            slope = sigma * (1.0 + gated * (1.0 - sigma))
            gz[at, :] = (ga * raised * slope).astype(jnp.bfloat16)
            gu[at, :] = (ga * gated * sigma).astype(jnp.bfloat16)
            if i > 1:
                total.middle(i - 1)
            gate.need()
            up.need()
            total.send(i, dot_nt(gz[at, :], gate[...]) + dot_nt(gu[at, :], up[...]))
            if i == 0:
                a.need()
                for j in range(places // 2):
                    cut = slice(j * 2 * shard, (j + 1) * 2 * shard)
                    part = dot_tn(low[:, cut], a[...]).astype(jnp.bfloat16)
                    d_down[2 * j : 2 * j + 2] = part.reshape(2, shard, units)
                    if j == 0:
                        total.middle(0)
                down_sum.start()
            jobs.advance(3.0 * i + 9.0 + later)
        total.middle(BLOCKS - 1)
        cols = width // 4
        h2.need()
        for reached, left, right, out in ((21.0, h2, gz, d_gate), (24.0, h2, gu, d_up)):
            for j in range(4):
                cut = slice(j * cols, (j + 1) * cols)
                out[cut, :] = dot_tn(left[:, cut], right[...]).astype(jnp.bfloat16)
                out.put(j)
            jobs.advance(reached + later)
        gains.need()
        if saved is None:
            for i in range(BLOCKS):
                quarters.last(i)
            quarters.out.put()
        for i in range(BLOCKS):
            total.last(i)
            jobs.advance((24.0, 24.0, 28.0, 34.0)[i] + later)
        gain_sum = jnp.zeros((1, width), jnp.float32)
        for i in range(BLOCKS):
            at = pl.ds(i * rows, rows)
            x1.need(i)
            step, gain_sum = norm_back(
                gains[which : which + 1, :], total.total(i), x1[at, :], gain_sum
            )
            x1[at, :] = gy[at, :].astype(jnp.float32) + step
            gx1.put(i)
        gain[...] = gain_sum
        gain.put()
        jobs.finish()

    call.run(body)
    return SimpleNamespace(
        gx1=gx1.result,
        gain=gain.result,
        d_gate=d_gate.result,
        d_up=d_up.result,
        quarters=quarters.out.result if saved is None else None,
        carried=[job.result for job in carried],
    )


def attention_back(number, gx1, x, saved, extra, wa, gains, which, tables, jobs_of, plan):
    count, width = x.shape
    hid = wa.shape[1] // 4
    heads = hid // HEAD_DIM
    rows = count // BLOCKS
    call = Call(number)
    gx1, wa = call.load(gx1, BLOCKS), call.load(wa)
    q, k, m, o = (
        call.load(array, blocks)
        for array, blocks in ((saved.q, BLOCKS), (saved.k, 1), (saved.m, 1), (saved.o, BLOCKS))
    )
    lse = call.load(saved.lse, BLOCKS)
    cosine, sine, seg_col = (call.load(table, BLOCKS) for table in tables[:3])
    seg_row = call.load(tables[3])
    if extra is not None:
        extra = call.load(extra, BLOCKS)
    h, gains, x = call.load(saved.h), call.load(gains), call.load(x, BLOCKS)
    if extra is not None:
        gx = call.store((count, width), jnp.bfloat16, BLOCKS)
        gx_held = gx
    else:
        gx_held = gx1
        gx = call.store_from(gx1, (count, width), jnp.float32, BLOCKS)
        passed = call.store((count, hid), jnp.float32, BLOCKS)
    gain = call.store((1, width), jnp.float32)
    d_wa = call.store((width, 4 * hid), jnp.bfloat16, 4)
    low = call.hold((count, width), jnp.bfloat16)
    bias = call.hold((rows, count), jnp.float32)
    go = call.hold((rows, hid), jnp.bfloat16)
    gq = call.hold((rows, hid), jnp.float32)
    gk, gm = (call.hold((count, hid), jnp.float32) for _ in range(2))
    g3 = call.hold((count, 3 * hid), jnp.bfloat16)
    total = HeadSum(call, BLOCKS, rows, width)
    carried = jobs_of(call)
    jobs = Jobs(carried, plan)

    def body():
        begin(call, total, jobs, True)
        lane = lane_number(hid)
        gk[...] = jnp.zeros(gk.shape, gk.dtype)
        gm[...] = jnp.zeros(gm.shape, gm.dtype)
        order = list(range(BLOCKS))[::-1]
        for turn_index, i in enumerate(order):
            at = pl.ds(i * rows, rows)
            gx1.need(i)
            low[at, :] = gx1[at, :].astype(jnp.bfloat16)
            wa.need()
            go[...] = dot_nn(low[at, :], wa[:, 3 * hid :]).astype(jnp.bfloat16)
            keys = (i + 1) * rows
            for held in (seg_row, seg_col, q, o, lse, k, m):
                held.need(i)
            write_bias(bias, seg_col, seg_row, i, rows, keys)
            gq[...] = jnp.zeros(gq.shape, gq.dtype)
            if turn_index:
                total.middle(order[turn_index - 1])
            else:
                jobs.advance(5.0)

            def one_head(index, unused):
                mask = lane // HEAD_DIM == index
                zero = jnp.bfloat16(0)
                query = jnp.where(mask, q[at, :], zero)
                grad = jnp.where(mask, go[...], zero)
                both = grad.astype(jnp.float32) * o[at, :].astype(jnp.float32)
                delta = jnp.sum(both, axis=-1, keepdims=True)
                scores = dot_nt(query, k[:keys, :]) + bias[:, :keys]
                prob = jnp.exp(scores - lse[index, at, :])
                grad_prob = dot_nt(grad, m[:keys, :])
                grad_score = (prob * (grad_prob - delta)).astype(jnp.bfloat16)
                part = dot_nn(grad_score, k[:keys, :])
                gq[...] = jnp.where(mask, part, gq[...])
                gk[:keys, :] += dot_tn(grad_score, query)
                gm[:keys, :] += dot_tn(prob.astype(jnp.bfloat16), grad)
                return unused

            lax.fori_loop(0, heads, one_head, 0)
            cosine.need(i)
            sine.need(i)
            cos, sin = cosine[at, :], sine[at, :]
            values = gm[at, :]
            if extra is None:
                values = 0.5 * values
                passed[at, :] = values
                passed.put(i)
            else:
                extra.need(i)
                values = values + extra[at, :]
            back = turn(gq[...] * HEAD_DIM**-0.5, cos, sin, True)
            g3[at, :hid] = back.astype(jnp.bfloat16)
            g3[at, hid : 2 * hid] = turn(gk[at, :], cos, sin, True).astype(jnp.bfloat16)
            g3[at, 2 * hid :] = values.astype(jnp.bfloat16)
            total.send(i, dot_nt(g3[at, :], wa[:, : 3 * hid]))
            jobs.advance((11.0, 17.5, 22.0, 25.0)[turn_index])
        total.middle(order[-1])
        cols = width // 4
        h.need()
        for j in range(4):
            cut = slice(j * cols, (j + 1) * cols)
            d_wa[cut, : 3 * hid] = dot_tn(h[:, cut], g3[...]).astype(jnp.bfloat16)
            d_wa[cut, 3 * hid :] = dot_tn(low[:, cut], o[...]).astype(jnp.bfloat16)
            d_wa.put(j)
        jobs.advance(30.0)
        gains.need()
        for turn_index, i in enumerate(order):
            total.last(i)
            jobs.advance((30.0, 30.0, 32.0, 37.0)[turn_index])
        gain_sum = jnp.zeros((1, width), jnp.float32)
        for i in order:
            at = pl.ds(i * rows, rows)
            x.need(i)
            stream = x[at, :].astype(jnp.float32)
            step, gain_sum = norm_back(
                gains[which : which + 1, :], total.total(i), stream, gain_sum
            )
            gx_held[at, :] = (gx1[at, :] + step).astype(gx_held.dtype)
            gx.put(i)
        gain[...] = gain_sum
        gain.put()
        jobs.finish()

    call.run(body)
    return SimpleNamespace(
        gx=gx.result,
        passed=passed.result if extra is None else None,
        gain=gain.result,
        d_wa=d_wa.result,
        carried=[job.result for job in carried],
    )


def transfers(number, jobs_of, plan):
    call = Call(number)
    carried = jobs_of(call)
    jobs = Jobs(carried, plan)

    def body():
        begin(call, None, jobs)
        jobs.finish()

    call.run(body)
    return [job.result for job in carried]


def leave_step(moved, grad, packs, turned, gains):
    call = Call(0)
    kept = [call.load(array, BLOCKS) for array in moved]
    kept_to = [call.store_from(held, held.shape, held.dtype, BLOCKS) for held in kept]
    grad = call.load(grad, BLOCKS)
    wide = call.store(grad.shape, jnp.float32, BLOCKS)
    shard, hid = packs[0].shape[0], packs[0].shape[1] // 4
    flag = call.flags(3 * len(packs))
    packs = [call.load(array) for array in packs]
    unpacked = [[call.give((shard, hid), pack.dtype) for _ in range(3)] for pack in packs]
    upright = [call.store((hid, shard), pack.dtype) for pack in packs]
    turned = [call.load(array) for array in turned]
    turned_to = [call.store(held.shape[::-1], held.dtype) for held in turned]
    gains = call.load(gains)
    gain_to = [call.store((1, shard), gains.dtype) for _ in range(4)]

    def body():
        call.start_loads()
        copies = []
        for at, pack in enumerate(packs):
            pack.need()
            for j in range(3):
                source = pack.at[:, j * hid : (j + 1) * hid]
                copies.append(
                    pltpu.make_async_copy(source, unpacked[at][j].ref, flag.at[3 * at + j])
                )
                copies[-1].start()
            upright[at][...] = pack[:, 3 * hid :].T
            upright[at].put()
        for held, target in zip(turned, turned_to):
            held.need()
            target[...] = held[...].T
            target.put()
        gains.need()
        for j, target in enumerate(gain_to):
            target[...] = gains[j : j + 1, :]
            target.put()
        rows = grad.shape[0] // BLOCKS
        for i in range(BLOCKS):
            at = pl.ds(i * rows, rows)
            grad.need(i)
            wide[at, :] = grad[at, :].astype(jnp.float32)
            wide.put(i)
            for held, target in zip(kept, kept_to):
                held.need(i)
                target.put(i)
        for copy in copies:
            copy.wait()

    call.run(body, False)
    return SimpleNamespace(
        kept=[target.result for target in kept_to],
        grad=wide.result,
        packs=[
            [part.result for part in parts] + [last.result]
            for parts, last in zip(unpacked, upright)
        ],
        turned=[target.result for target in turned_to],
        gains=[target.result.reshape(-1) for target in gain_to],
    )


def dealt_device(
    inputs,
    segment_ids,
    norm_attn_one,
    query_one,
    key_one,
    value_one,
    output_one,
    norm_ffn_one,
    gate_one,
    up_one,
    down_one,
    norm_attn_two,
    query_two,
    key_two,
    value_two,
    output_two,
    norm_ffn_two,
    gate_two,
    up_two,
    down_two,
    cotangent,
):
    parts, length, width = inputs.shape
    places = lax.axis_size(DP) * lax.axis_size(CTX)
    shard = width // places
    gain_rows = jnp.stack([norm_attn_one, norm_ffn_one, norm_attn_two, norm_ffn_two] * 2)
    half = HEAD_DIM // 2
    frequency = 10000.0 ** (-np.arange(half, dtype=np.float32) / np.float32(half))
    repeat = LANES // HEAD_DIM
    signs = np.concatenate([-np.ones(half), np.ones(half)])
    angle_row = np.zeros((8, LANES), np.float32)
    angle_row[0] = np.tile(frequency, 2 * repeat)
    angle_row[1] = np.tile(signs, repeat)

    def split(array):
        return array.reshape(places, shard, array.shape[-1])

    def deal(array):
        return array.reshape(parts, length, width)

    def opening(call):
        return Opening(
            call,
            inputs,
            segment_ids,
            (
                (query_one, key_one, value_one, output_one, gate_one.T, up_one.T, down_one),
                (query_two, key_two, value_two, output_two, gate_two.T, up_two.T, down_two),
            ),
            gain_rows,
            jnp.asarray(angle_row),
            places,
        )

    attn_one = attention_layer(
        1,
        None,
        None,
        None,
        None,
        0,
        None,
        lambda c, start: [Gather(c, held, places) for held in start.shards_one],
        ((0.1, 0.2, 2.0), (5.0, 8.0, 12.0), (15.0, 18.0, 22.0)),
        opening,
    )
    start = attn_one.start
    x, wa_one, gains = start.deal.result, start.gather.result, start.gains.result
    tables = [table.result for table in start.tables()]
    ffn_one_w = attn_one.carried
    wa_two_shard = start.wa_two.result
    shards_two = [held.result for held in start.shards_two]
    ffn_one = feed_forward_layer(
        2,
        attn_one.x1,
        *ffn_one_w,
        gains,
        1,
        lambda c: [Gather(c, wa_two_shard, places, True), Gather(c, shards_two[0], places)],
        ((7.0, 4.0), (20.0, 4.1)),
    )
    wa_two, gate_two_w = ffn_one.carried
    attn_two = attention_layer(
        3,
        ffn_one.y,
        attn_one.v,
        wa_two,
        gains,
        2,
        tables,
        lambda c, start: [
            Deal(c, cotangent),
            Gather(c, shards_two[1], places, True),
            Gather(c, shards_two[2], places, True),
        ],
        ((8.0, 12.5, 16.0, 22.5, 22.6, 22.7), (16.0, 3.0), (26.0, 3.0)),
    )
    dealt_cotangent = attn_two.carried[0]
    ffn_two_w = (gate_two_w, *attn_two.carried[1:])
    back_ffn_two = feed_forward_back(
        4,
        dealt_cotangent,
        attn_two.x1,
        None,
        *ffn_two_w,
        gains,
        3,
        lambda c, down_sum: [down_sum],
        ((23.0, 4.2),),
    )
    (down_g2,) = back_ffn_two.carried
    grads_plan = ((10.0, 3.0), (25.0, 3.0))

    def ffn_grads(back):
        return [split(array) for array in (back.d_gate, back.d_up)]

    back_attn_two = attention_back(
        6,
        back_ffn_two.gx1,
        ffn_one.y,
        attn_two,
        None,
        wa_two,
        gains,
        2,
        tables,
        lambda c: [Scatter(c, array) for array in ffn_grads(back_ffn_two)]
        + [Deal(c, back_ffn_two.quarters, length)],
        grads_plan + ((4.9, 5.0, 11.0, 11.1, 11.2, 35.0, 35.1, 35.2),),
    )
    gate_g2, up_g2, out_two = back_attn_two.carried
    back_ffn_one = feed_forward_back(
        7,
        back_attn_two.gx,
        attn_one.x1,
        ffn_one,
        *ffn_one_w,
        gains,
        1,
        lambda c, down_sum: [
            Scatter(c, split(back_attn_two.d_wa)),
            down_sum,
            Deal(c, deal(ffn_one.y_low)),
        ],
        ((8.0, 5.8), (30.0, 4.2), (33.0, 33.1, 33.2, 37.0, 37.1, 37.2)),
    )
    packed_two, down_g1, out_one = back_ffn_one.carried
    back_attn_one = attention_back(
        8,
        back_ffn_one.gx1,
        x,
        attn_one,
        back_attn_two.passed,
        wa_one,
        gains,
        0,
        tables,
        lambda c: [Scatter(c, array) for array in ffn_grads(back_ffn_one)],
        grads_plan,
    )
    gate_g1, up_g1 = back_attn_one.carried
    gain_grads = jnp.concatenate(
        [back_attn_one.gain, back_ffn_one.gain, back_attn_two.gain, back_ffn_two.gain] * 2
    )
    gain_grads = jnp.transpose(gain_grads.reshape(-1, places, shard), (1, 0, 2))
    gain_shards, packed_one, grad = transfers(
        9,
        lambda c: [
            Scatter(c, gain_grads),
            Scatter(c, split(back_attn_one.d_wa)),
            Deal(c, deal(back_attn_one.gx)),
        ],
        ((4.0, 0.1), (7.0, 5.8), (6.0, 4.0)),
    )
    final = leave_step(
        (out_one, out_two),
        grad,
        (packed_one, packed_two),
        [gate_g1, up_g1, down_g1, gate_g2, up_g2, down_g2],
        gain_shards,
    )
    gate_g1, up_g1, down_g1, gate_g2, up_g2, down_g2 = final.turned
    return (
        deal(final.kept[0]),
        deal(final.kept[1]),
        deal(final.grad),
        final.gains[0],
        *final.packs[0],
        final.gains[1],
        gate_g1.T,
        up_g1.T,
        down_g1,
        final.gains[2],
        *final.packs[1],
        final.gains[3],
        gate_g2.T,
        up_g2.T,
        down_g2,
    )


def solution(mesh):
    placed = (
        P(DP, CTX, None),
        P(DP, None),
        P((DP, CTX)),
        P((DP, CTX), MP),
        P((DP, CTX), MP),
        P((DP, CTX), MP),
        P(MP, (DP, CTX)),
        P((DP, CTX)),
        P((DP, CTX), MP),
        P((DP, CTX), MP),
        P(MP, (DP, CTX)),
        P((DP, CTX)),
        P((DP, CTX), MP),
        P((DP, CTX), MP),
        P((DP, CTX), MP),
        P(MP, (DP, CTX)),
        P((DP, CTX)),
        P((DP, CTX), MP),
        P((DP, CTX), MP),
        P(MP, (DP, CTX)),
        P(DP, CTX, None),
    )
    sizes = dict(mesh.shape)

    def per_device(*operands):
        fits = sizes[DP] == 2 and sizes[MP] == 4 and operands[0].shape[0] == sizes[CTX] == BLOCKS
        return (dealt_device if fits else on_device)(*operands)

    return jax.shard_map(
        per_device,
        mesh=mesh,
        in_specs=placed,
        out_specs=(
            P(DP, CTX, None),
            P(DP, CTX, None),
            P(DP, CTX, None),
            P((DP, CTX)),
            P((DP, CTX), MP),
            P((DP, CTX), MP),
            P((DP, CTX), MP),
            P(MP, (DP, CTX)),
            P((DP, CTX)),
            P((DP, CTX), MP),
            P((DP, CTX), MP),
            P(MP, (DP, CTX)),
            P((DP, CTX)),
            P((DP, CTX), MP),
            P((DP, CTX), MP),
            P((DP, CTX), MP),
            P(MP, (DP, CTX)),
            P((DP, CTX)),
            P((DP, CTX), MP),
            P((DP, CTX), MP),
            P(MP, (DP, CTX)),
        ),
        check_vma=False,
    )
```

```python
import functools
import math
from types import SimpleNamespace

import jax
import jax.numpy as jnp
import numpy as np
from jax import lax
from jax.experimental import pallas as pl
from jax.experimental.pallas import tpu as pltpu
from jax.sharding import PartitionSpec as P

MESH = pl.DeviceIdType.MESH

HEAD_DIM = 64
DP, CTX, MP = "dp", "ctx", "mp"


epsilon = 1e-05
neg_large = -1e30


def project(left_operand, right_operand):
    return jnp.einsum(
        "sbd,de->sbe", left_operand, right_operand, preferred_element_type=jnp.float32
    )


def project_back(left_operand, right_operand):
    return jnp.einsum(
        "sbe,de->sbd", left_operand, right_operand, preferred_element_type=jnp.float32
    )


def weight_term(left_operand, right_operand):
    return jnp.einsum(
        "sbd,sbe->de", left_operand, right_operand, preferred_element_type=jnp.float32
    )


def head_sum_kernel(
    chunks, x_ref, o_ref, near, half_sum, far, send_a, recv_a, send_b, recv_b, send_c, recv_c
):
    dp, ctx, mp = (lax.axis_index(name) for name in (DP, CTX, MP))
    side = lax.rem(mp, 2)
    pair = (dp, ctx, mp + 1 - 2 * side)
    cross = (dp, ctx, lax.rem(mp + 2, 4))
    barrier = pltpu.get_barrier_semaphore()
    for peer in (pair, cross):
        pl.semaphore_signal(barrier, inc=1, device_id=peer, device_id_type=MESH)
    pl.semaphore_wait(barrier, 2)
    rows = x_ref.shape[0] // chunks
    half = rows // 2

    def copy(source, target, send, recv, i, peer):
        return pltpu.make_async_remote_copy(
            src_ref=source,
            dst_ref=target,
            send_sem=send.at[i],
            recv_sem=recv.at[i],
            device_id=peer,
            device_id_type=MESH,
        )

    def first(i):
        theirs = x_ref.at[pl.ds(i * rows + (1 - side) * half, half)]
        return copy(theirs, near.at[i], send_a, recv_a, i, pair)

    def second(i):
        return copy(half_sum.at[i], far.at[i], send_b, recv_b, i, cross)

    def third(i):
        mine = o_ref.at[pl.ds(i * rows + side * half, half)]
        return copy(mine, mine, send_c, recv_c, i, pair)

    for i in range(chunks):
        first(i).start()
    for i in range(chunks):
        first(i).wait()
        mine = x_ref[pl.ds(i * rows + side * half, half)].astype(jnp.float32)
        half_sum[i] = (mine + near[i].astype(jnp.float32)).astype(jnp.bfloat16)
        second(i).start()
    for i in range(chunks):
        second(i).wait()
        total = half_sum[i].astype(jnp.float32) + far[i].astype(jnp.float32)
        o_ref[pl.ds(i * rows + side * half, half)] = total.astype(jnp.bfloat16)
        third(i).start()
    for i in range(chunks):
        third(i).wait()


def head_sum(partial_sum, number):
    flat = partial_sum.astype(jnp.bfloat16).reshape(-1, partial_sum.shape[-1])
    count, width = flat.shape
    chunks = 4
    half = count // chunks // 2
    total = pl.pallas_call(
        functools.partial(head_sum_kernel, chunks),
        out_shape=jax.ShapeDtypeStruct((count, width), jnp.bfloat16),
        in_specs=[pl.BlockSpec(memory_space=pltpu.VMEM)],
        out_specs=pl.BlockSpec(memory_space=pltpu.VMEM),
        scratch_shapes=[pltpu.VMEM((chunks, half, width), jnp.bfloat16)] * 3
        + [pltpu.SemaphoreType.DMA((chunks,))] * 6,
        compiler_params=pltpu.CompilerParams(
            collective_id=0, has_side_effects=True, vmem_limit_bytes=32 << 20
        ),
    )(flat)
    return total.reshape(partial_sum.shape).astype(jnp.float32)


def head_total(partial_sum):
    return head_sum(partial_sum, 0)


def head_back(partial_sum):
    return head_sum(partial_sum, 0)


def rotary_tables(first_place, count_of_rows):
    half_width = HEAD_DIM // 2
    frequency = 10000.0 ** (-jnp.arange(half_width, dtype=jnp.float32) / half_width)
    places = (first_place + jnp.arange(count_of_rows, dtype=jnp.int32)).astype(jnp.float32)
    angles = places[:, None] * frequency[None, :]
    return (jnp.cos(angles)[None, :, None, :], jnp.sin(angles)[None, :, None, :])


def rotate(split_heads, cosine, sine_table):
    half_width = HEAD_DIM // 2
    first_half = split_heads[..., :half_width]
    second_half = split_heads[..., half_width:]
    return jnp.concatenate(
        [
            first_half * cosine - second_half * sine_table,
            first_half * sine_table + second_half * cosine,
        ],
        axis=-1,
    )


def rotate_back(split_heads, cosine, sine_table):
    half_width = HEAD_DIM // 2
    first_half = split_heads[..., :half_width]
    second_half = split_heads[..., half_width:]
    return jnp.concatenate(
        [
            first_half * cosine + second_half * sine_table,
            second_half * cosine - first_half * sine_table,
        ],
        axis=-1,
    )


def norm_forward(stream, gain_row):
    inverse = lax.rsqrt(jnp.mean(stream * stream, axis=-1, keepdims=True) + epsilon)
    normed = (stream * inverse * gain_row.astype(jnp.float32)).astype(jnp.bfloat16)
    return (normed, inverse)


def norm_backward(grad_normed, stream, inverse, gain_row):
    scaled = stream * inverse
    grad_scaled = grad_normed * gain_row.astype(jnp.float32)
    gain_grad = jnp.sum(grad_normed * scaled, axis=(0, 1))
    grad_stream = inverse * (
        grad_scaled - scaled * jnp.mean(grad_scaled * scaled, axis=-1, keepdims=True)
    )
    return (grad_stream, gain_grad)


def block_grads(
    query_block,
    grad_block,
    lse_block,
    delta_block,
    query_places,
    query_document_ids,
    key_block,
    value_block,
    key_places,
    key_segments,
):
    score_scale = HEAD_DIM ** (-0.5)
    scores = (
        jnp.einsum("sqhe,skhe->shqk", query_block, key_block, preferred_element_type=jnp.float32)
        * score_scale
    )
    visible = (
        (key_places[None, :] <= query_places[:, None])[None]
        & (key_segments[:, None, :] == query_document_ids[:, :, None])
    )[:, None]
    probabilities = jnp.where(visible, jnp.exp(scores - lse_block[..., None]), 0.0)
    grad_probs = jnp.einsum(
        "sqhe,skhe->shqk", grad_block, value_block, preferred_element_type=jnp.float32
    )
    grad_scores = (probabilities * (grad_probs - delta_block[..., None]) * score_scale).astype(
        jnp.bfloat16
    )
    query_grad = jnp.einsum(
        "shqk,skhe->sqhe", grad_scores, key_block, preferred_element_type=jnp.float32
    )
    key_grad = jnp.einsum(
        "shqk,sqhe->skhe", grad_scores, query_block, preferred_element_type=jnp.float32
    )
    value_grad = jnp.einsum(
        "shqk,sqhe->skhe",
        probabilities.astype(jnp.bfloat16),
        grad_block,
        preferred_element_type=jnp.float32,
    )
    return (query_grad, key_grad, value_grad)


def attend_forward(queries, key_rows, value_rows, segments, query_places):
    seq_count, count_of_rows, head_count, head_width = queries.shape
    score_scale = head_width ** (-0.5)
    query_document_ids = lax.dynamic_slice_in_dim(segments, query_places[0], count_of_rows, 1)
    last_query = query_places[count_of_rows - 1]
    initial = (
        jnp.full((seq_count, head_count, count_of_rows), neg_large, jnp.float32),
        jnp.zeros((seq_count, head_count, count_of_rows), jnp.float32),
        jnp.zeros((seq_count, count_of_rows, head_count, head_width), jnp.float32),
    )
    key_piece = lax.all_gather(key_rows, CTX, axis=1, tiled=True)
    value_piece = lax.all_gather(value_rows, CTX, axis=1, tiled=True)
    piece_rows = key_piece.shape[1]
    block_rows = math.gcd(piece_rows, 512)
    key_split = key_piece.reshape(seq_count, piece_rows, head_count, head_width)
    value_split = value_piece.reshape(seq_count, piece_rows, head_count, head_width)

    def absorb_visit(running, block_index):
        first_key = block_index * block_rows

        def absorb_compute(current):
            row_max, row_total, weighted = current
            key_block = lax.dynamic_slice_in_dim(key_split, first_key, block_rows, 1)
            value_block = lax.dynamic_slice_in_dim(value_split, first_key, block_rows, 1)
            key_places = first_key + jnp.arange(block_rows, dtype=jnp.int32)
            key_segments = lax.dynamic_slice_in_dim(segments, first_key, block_rows, 1)
            scores = (
                jnp.einsum(
                    "sqhe,skhe->shqk", queries, key_block, preferred_element_type=jnp.float32
                )
                * score_scale
            )
            visible = (
                (key_places[None, :] <= query_places[:, None])[None]
                & (key_segments[:, None, :] == query_document_ids[:, :, None])
            )[:, None]
            new_max = jnp.maximum(row_max, jnp.max(jnp.where(visible, scores, neg_large), axis=-1))
            exponent = jnp.where(visible, jnp.exp(scores - new_max[..., None]), 0.0)
            factor = jnp.exp(row_max - new_max)
            new_total = row_total * factor + jnp.sum(exponent, axis=-1)
            update = jnp.einsum(
                "shqk,skhe->sqhe",
                exponent.astype(jnp.bfloat16),
                value_block,
                preferred_element_type=jnp.float32,
            )
            new_weighted = weighted * jnp.transpose(factor, (0, 2, 1))[..., None] + update
            return (new_max, new_total, new_weighted)

        def absorb_keep(current):
            return current

        return (lax.cond(first_key <= last_query, absorb_compute, absorb_keep, running), None)

    result, unused = lax.scan(
        absorb_visit, initial, jnp.arange(piece_rows // block_rows, dtype=jnp.int32)
    )
    row_max, row_total, weighted = result
    attended = weighted / jnp.transpose(row_total, (0, 2, 1))[..., None]
    return (attended, row_max + jnp.log(row_total))


def attend_back_gather(
    queries, grad_attended, log_normalizer, row_delta, key_rows, value_rows, segments, query_places
):
    seq_count, count_of_rows, head_count, head_width = queries.shape
    query_document_ids = lax.dynamic_slice_in_dim(segments, query_places[0], count_of_rows, 1)
    last_query = query_places[count_of_rows - 1]
    all_keys, all_values = (
        lax.all_gather(key_rows, CTX, axis=1, tiled=True),
        lax.all_gather(value_rows, CTX, axis=1, tiled=True),
    )
    length = all_keys.shape[1]
    block_rows = math.gcd(length, 512)
    key_split = all_keys.reshape(seq_count, length, head_count, head_width)
    value_split = all_values.reshape(seq_count, length, head_count, head_width)
    initial = (
        jnp.zeros((seq_count, count_of_rows, head_count, head_width), jnp.float32),
        jnp.zeros((seq_count, length, head_count, head_width), jnp.float32),
        jnp.zeros((seq_count, length, head_count, head_width), jnp.float32),
    )

    def attend_visit(state_now, block_index):
        first_key = block_index * block_rows

        def attend_compute(current):
            query_acc, key_acc, value_acc = current
            key_block = lax.dynamic_slice_in_dim(key_split, first_key, block_rows, 1)
            value_block = lax.dynamic_slice_in_dim(value_split, first_key, block_rows, 1)
            key_places = first_key + jnp.arange(block_rows, dtype=jnp.int32)
            key_segments = lax.dynamic_slice_in_dim(segments, first_key, block_rows, 1)
            query_part, key_part, value_part = block_grads(
                queries,
                grad_attended,
                log_normalizer,
                row_delta,
                query_places,
                query_document_ids,
                key_block,
                value_block,
                key_places,
                key_segments,
            )
            key_acc = lax.dynamic_update_slice_in_dim(key_acc, key_part, first_key, 1)
            value_acc = lax.dynamic_update_slice_in_dim(value_acc, value_part, first_key, 1)
            return (query_acc + query_part, key_acc, value_acc)

        def attend_keep(current):
            return current

        return (lax.cond(first_key <= last_query, attend_compute, attend_keep, state_now), None)

    totals, unused = lax.scan(
        attend_visit, initial, jnp.arange(length // block_rows, dtype=jnp.int32)
    )
    query_grad, key_grad, value_grad = totals
    key_home, value_home = (
        lax.psum_scatter(
            key_grad.reshape(seq_count, length, -1).astype(jnp.bfloat16),
            CTX,
            scatter_dimension=1,
            tiled=True,
        ).astype(jnp.float32),
        lax.psum_scatter(
            value_grad.reshape(seq_count, length, -1).astype(jnp.bfloat16),
            CTX,
            scatter_dimension=1,
            tiled=True,
        ).astype(jnp.float32),
    )
    split_shape = (seq_count, count_of_rows, head_count, head_width)
    return (query_grad, key_home.reshape(split_shape), value_home.reshape(split_shape))


def forward_layer(stream, first_values, weights, segments, cosine, sine_table, query_places):
    norm_attn, w_query, w_key, w_value, w_output, norm_ffn, w_gate, w_up, w_down = weights
    seq_count, count_of_rows, model_width = stream.shape
    head_count = w_query.shape[1] // HEAD_DIM
    split_shape = (seq_count, count_of_rows, head_count, HEAD_DIM)
    normed, inverse_one = norm_forward(stream, norm_attn)
    queries = rotate(project(normed, w_query).reshape(split_shape), cosine, sine_table).astype(
        jnp.bfloat16
    )
    key_rows = (
        rotate(project(normed, w_key).reshape(split_shape), cosine, sine_table)
        .astype(jnp.bfloat16)
        .reshape(seq_count, count_of_rows, -1)
    )
    own_values = project(normed, w_value)
    if first_values is None:
        mixed = own_values.astype(jnp.bfloat16)
    else:
        mixed = (0.5 * own_values + 0.5 * first_values).astype(jnp.bfloat16)
    attended, log_normalizer = attend_forward(queries, key_rows, mixed, segments, query_places)
    attended_low = attended.reshape(seq_count, count_of_rows, -1).astype(jnp.bfloat16)
    hidden_one = stream + head_total(project(attended_low, w_output))
    normed_two, inverse_two = norm_forward(hidden_one, norm_ffn)
    gate_values = project(normed_two, w_gate)
    up_values = project(normed_two, w_up)
    activated = (jax.nn.silu(gate_values) * up_values).astype(jnp.bfloat16)
    result = hidden_one + head_total(project(activated, w_down))
    saved_state = (
        stream,
        inverse_one,
        normed,
        queries,
        key_rows,
        mixed,
        attended,
        log_normalizer,
        attended_low,
        hidden_one,
        inverse_two,
        normed_two,
        gate_values,
        up_values,
        activated,
    )
    return (result, saved_state, own_values)


def backward_layer(
    grad_out, value_extra, saved_state, weights, segments, cosine, sine_table, query_places, mixes
):
    (
        stream,
        inverse_one,
        normed,
        queries,
        key_rows,
        mixed,
        attended,
        log_normalizer,
        attended_low,
        hidden_one,
        inverse_two,
        normed_two,
        gate_values,
        up_values,
        activated,
    ) = saved_state
    norm_attn, w_query, w_key, w_value, w_output, norm_ffn, w_gate, w_up, w_down = weights
    seq_count, count_of_rows, head_count, head_width = queries.shape
    grad_branch = grad_out.astype(jnp.bfloat16)
    down_grad = weight_term(activated, grad_branch)
    grad_active = project_back(grad_branch, w_down)
    gate_sigmoid = jax.nn.sigmoid(gate_values)
    grad_gate = (
        grad_active * up_values * gate_sigmoid * (1.0 + gate_values * (1.0 - gate_sigmoid))
    ).astype(jnp.bfloat16)
    grad_up = (grad_active * gate_values * gate_sigmoid).astype(jnp.bfloat16)
    gate_grad = weight_term(normed_two, grad_gate)
    up_grad = weight_term(normed_two, grad_up)
    grad_normed_two = head_back(project_back(grad_gate, w_gate) + project_back(grad_up, w_up))
    grad_norm_two, ffn_gain_grad = norm_backward(grad_normed_two, hidden_one, inverse_two, norm_ffn)
    grad_hidden = grad_out + grad_norm_two
    grad_attn = grad_hidden.astype(jnp.bfloat16)
    output_grad = weight_term(attended_low, grad_attn)
    grad_attended = (
        project_back(grad_attn, w_output)
        .astype(jnp.bfloat16)
        .reshape(seq_count, count_of_rows, head_count, head_width)
    )
    row_delta = jnp.transpose(
        jnp.sum(grad_attended.astype(jnp.float32) * attended, axis=-1), (0, 2, 1)
    )
    query_rot, key_rot, value_mix = attend_back_gather(
        queries, grad_attended, log_normalizer, row_delta, key_rows, mixed, segments, query_places
    )
    query_low = (
        rotate_back(query_rot, cosine, sine_table)
        .astype(jnp.bfloat16)
        .reshape(seq_count, count_of_rows, -1)
    )
    key_low = (
        rotate_back(key_rot, cosine, sine_table)
        .astype(jnp.bfloat16)
        .reshape(seq_count, count_of_rows, -1)
    )
    value_mix = value_mix.reshape(seq_count, count_of_rows, -1)
    if mixes:
        value_low = (0.5 * value_mix).astype(jnp.bfloat16)
        passed_on = 0.5 * value_mix
    else:
        value_low = (value_mix + value_extra).astype(jnp.bfloat16)
        passed_on = value_extra
    query_grad = weight_term(normed, query_low)
    key_grad = weight_term(normed, key_low)
    value_grad = weight_term(normed, value_low)
    grad_normed = head_back(
        project_back(query_low, w_query)
        + project_back(key_low, w_key)
        + project_back(value_low, w_value)
    )
    grad_norm_one, attn_gain_grad = norm_backward(grad_normed, stream, inverse_one, norm_attn)
    grad_stream = grad_hidden + grad_norm_one
    grad_terms = (
        attn_gain_grad,
        query_grad,
        key_grad,
        value_grad,
        output_grad,
        ffn_gain_grad,
        gate_grad,
        up_grad,
        down_grad,
    )
    return (grad_stream, passed_on, grad_terms)


def on_device(
    inputs,
    segment_ids,
    norm_attn_one,
    query_one,
    key_one,
    value_one,
    output_one,
    norm_ffn_one,
    gate_one,
    up_one,
    down_one,
    norm_attn_two,
    query_two,
    key_two,
    value_two,
    output_two,
    norm_ffn_two,
    gate_two,
    up_two,
    down_two,
    cotangent,
):
    def gather_layer(gain_attn, query, key, value, output, gain_ffn, gate, up, down):
        both = (DP, CTX)
        packed = jnp.concatenate([query, key, value, output.T, gate, up, down.T], axis=1)
        whole = lax.all_gather(packed, both, axis=0, tiled=True)
        gains = lax.all_gather(jnp.stack([gain_attn, gain_ffn]), both, axis=1, tiled=True)
        cuts = []
        for part in (query, key, value, output.T, gate, up, down.T):
            cuts.append((cuts[-1] if cuts else 0) + part.shape[1])
        w_q, w_k, w_v, w_o, w_g, w_u, w_d = jnp.split(whole, cuts[:-1], axis=1)
        return (gains[0], w_q, w_k, w_v, w_o.T, gains[1], w_g, w_u, w_d.T)

    def scatter_layer(grads, outs):
        both = (DP, CTX)
        gain_attn, query, key, value, output, gain_ffn, gate, up, down = grads
        pieces = [query, key, value, output.T, gate, up, down.T]
        packed = jnp.concatenate([part.astype(jnp.bfloat16) for part in pieces], axis=1)
        mine = lax.psum_scatter(packed, both, scatter_dimension=0, tiled=True)
        gains = lax.psum_scatter(
            jnp.stack([gain_attn, gain_ffn]).astype(jnp.bfloat16),
            both,
            scatter_dimension=1,
            tiled=True,
        ).astype(jnp.float32)
        cuts = []
        for part in pieces:
            cuts.append((cuts[-1] if cuts else 0) + part.shape[1])
        g_q, g_k, g_v, g_o, g_g, g_u, g_d = (
            part.astype(jnp.float32) for part in jnp.split(mine, cuts[:-1], axis=1)
        )
        return (gains[0], g_q, g_k, g_v, g_o.T, gains[1], g_g, g_u, g_d.T)

    gathered = gather_layer(
        norm_attn_one,
        query_one,
        key_one,
        value_one,
        output_one,
        norm_ffn_one,
        gate_one,
        up_one,
        down_one,
    ) + gather_layer(
        norm_attn_two,
        query_two,
        key_two,
        value_two,
        output_two,
        norm_ffn_two,
        gate_two,
        up_two,
        down_two,
    )
    weights_one = gathered[:9]
    weights_two = gathered[9:]
    seq_count, count_of_rows, model_width = inputs.shape
    query_places = lax.axis_index(CTX) * count_of_rows + jnp.arange(
        count_of_rows, dtype=jnp.int32
    )
    cosine, sine_table = rotary_tables(query_places[0], count_of_rows)
    layer_one, saved_one, first_values = forward_layer(
        inputs.astype(jnp.float32), None, weights_one, segment_ids, cosine, sine_table, query_places
    )
    layer_two, saved_two, unused = forward_layer(
        layer_one, first_values, weights_two, segment_ids, cosine, sine_table, query_places
    )
    grad_middle, value_extra, grads_two = backward_layer(
        cotangent.astype(jnp.float32),
        None,
        saved_two,
        weights_two,
        segment_ids,
        cosine,
        sine_table,
        query_places,
        True,
    )
    grad_input, unused_extra, grads_one = backward_layer(
        grad_middle,
        value_extra,
        saved_one,
        weights_one,
        segment_ids,
        cosine,
        sine_table,
        query_places,
        False,
    )
    totals = scatter_layer(grads_one, None) + scatter_layer(grads_two, None)
    return (
        layer_one.astype(jnp.bfloat16),
        layer_two.astype(jnp.bfloat16),
        grad_input,
        totals[0],
        totals[1],
        totals[2],
        totals[3],
        totals[4],
        totals[5],
        totals[6],
        totals[7],
        totals[8],
        totals[9],
        totals[10],
        totals[11],
        totals[12],
        totals[13],
        totals[14],
        totals[15],
        totals[16],
        totals[17],
    )


class Raw:
    def __init__(self, call, kind, index):
        self.call, self.kind, self.index = call, kind, index

    @property
    def ref(self):
        return self.call.refs[self.kind][self.index]

    @property
    def at(self):
        return self.ref.at

    @property
    def result(self):
        return self.call.results[self.index]


def cut_rows(ref, blocks, i):
    if blocks == 1:
        return ref
    rows = ref.shape[-2] // blocks
    part = pl.ds(i * rows, rows)
    return ref.at[part] if len(ref.shape) == 2 else ref.at[:, part]


class Store:
    def __init__(self, call, held, shape, dtype, blocks):
        self.held, self.blocks = held, blocks
        self.out = call.give(shape, dtype)
        self.flag = call.flags(blocks)
        call.stores.append(self)

    def copy(self, i):
        return pltpu.make_async_copy(
            cut_rows(self.held.ref, self.blocks, i),
            cut_rows(self.out.ref, self.blocks, i),
            self.flag.at[i],
        )

    def put(self, i=None):
        for k in range(self.blocks) if i is None else (i,):
            self.copy(k).start()

    def finish(self):
        for i in range(self.blocks):
            self.copy(i).wait()

    @property
    def result(self):
        return self.out.result


class Held:
    def __init__(self, call, shape, dtype):
        self.call, self.shape, self.dtype = call, shape, dtype
        self.slot = call.scratch_slot(pltpu.VMEM(shape, dtype))
        self.source = self.out = None
        self.blocks, self.waited = 1, set()

    @property
    def ref(self):
        return self.call.refs[2][self.slot]

    @property
    def at(self):
        return self.ref.at

    def __getitem__(self, key):
        return self.ref[key]

    def __setitem__(self, key, value):
        self.ref[key] = value

    def load_copy(self, i):
        return pltpu.make_async_copy(
            cut_rows(self.source.ref, self.blocks, i),
            cut_rows(self.ref, self.blocks, i),
            self.flag.at[i],
        )

    def need(self, i=None):
        if self.source is None:
            return
        for k in range(self.blocks) if i is None or self.blocks == 1 else (i,):
            if k not in self.waited:
                self.waited.add(k)
                self.load_copy(k).wait()

    def put(self, i=None):
        self.out.put(i)

    @property
    def result(self):
        return self.out.result


class Call:
    def __init__(self, number):
        self.number = number
        self.operands, self.shapes, self.scratch = [], [], []
        self.loads, self.stores, self.jobs = [], [], []
        self.far = self.in_turn = False

    def take(self, array):
        self.operands.append(array)
        return Raw(self, 0, len(self.operands) - 1)

    def give(self, shape, dtype):
        self.shapes.append(jax.ShapeDtypeStruct(shape, dtype))
        return Raw(self, 1, len(self.shapes) - 1)

    def scratch_slot(self, kind):
        self.scratch.append(kind)
        return len(self.scratch) - 1

    def flags(self, count):
        return Raw(self, 2, self.scratch_slot(pltpu.SemaphoreType.DMA((count,))))

    def hold(self, shape, dtype):
        return Held(self, shape, dtype)

    def load(self, array, blocks=1):
        held = Held(self, array.shape, array.dtype)
        self.load_into(held, self.take(array), blocks)
        self.loads.append(held)
        return held

    def load_into(self, held, source, blocks):
        held.source, held.blocks, held.flag = source, blocks, self.flags(blocks)

    def store(self, shape, dtype, blocks=1):
        held = Held(self, shape, dtype)
        held.out = Store(self, held, shape, dtype, blocks)
        return held

    def store_from(self, held, shape, dtype, blocks=1):
        return Store(self, held, shape, dtype, blocks)

    def start_loads(self, backward=False):
        if self.in_turn:
            for held in self.loads:
                for k in range(held.blocks):
                    held.load_copy(k).start()
            return
        for k in range(max([held.blocks for held in self.loads], default=0)):
            for held in self.loads:
                if k < held.blocks:
                    held.load_copy(held.blocks - 1 - k if backward else k).start()

    def run(self, body, remote_ops=True):
        ins, outs = len(self.operands), len(self.operands) + len(self.shapes)

        def kernel(*refs):
            self.refs = (refs[:ins], refs[ins:outs], refs[outs:])
            for held in self.loads:
                held.waited = set()
            body()
            for held in self.loads:
                held.need()
            for store in self.stores:
                store.finish()

        space = pl.BlockSpec(memory_space=pltpu.HBM)
        self.results = pl.pallas_call(
            kernel,
            out_shape=tuple(self.shapes),
            in_specs=[space] * ins,
            out_specs=(space,) * len(self.shapes),
            scratch_shapes=self.scratch,
            compiler_params=pltpu.CompilerParams(
                has_side_effects=remote_ops,
                vmem_limit_bytes=62 << 20,
                collective_id=self.number if remote_ops else None,
            ),
        )(*self.operands)
        self.refs = None


class Place:
    def __init__(self):
        self.dp, self.ctx, self.mp = (lax.axis_index(a) for a in (DP, CTX, MP))
        self.ctx_size = lax.axis_size(CTX)
        self.side = lax.rem(self.mp, 2)
        self.pair = (self.dp, self.ctx, self.mp + 1 - 2 * self.side)
        self.cross = (self.dp, self.ctx, lax.rem(self.mp + 2, 4))
        self.other = (1 - self.dp, self.ctx, self.mp)

    def ahead(self, step):
        return lax.rem(self.ctx + step, self.ctx_size)

    def behind(self, step):
        return lax.rem(self.ctx + self.ctx_size - step, self.ctx_size)

    def along(self, index):
        return (self.dp, index, self.mp)

    def peers(self, far):
        peers = [self.pair, self.cross]
        if far:
            peers.append(self.other)
            peers += [self.along(self.ahead(s)) for s in range(1, self.ctx_size)]
        return peers

    def greet(self, far):
        barrier = pltpu.get_barrier_semaphore()
        for peer in self.peers(far):
            pl.semaphore_signal(barrier, inc=1, device_id=peer, device_id_type=MESH)

    def enter(self, far):
        pl.semaphore_wait(pltpu.get_barrier_semaphore(), len(self.peers(far)))


def remote(source, target, send, recv, peer):
    return pltpu.make_async_remote_copy(
        src_ref=source,
        dst_ref=target,
        send_sem=send,
        recv_sem=recv,
        device_id=peer,
        device_id_type=MESH,
    )


class HeadSum:
    def __init__(self, call, blocks, rows, width):
        self.half = rows // 2
        self.part = call.hold((blocks, rows, width), jnp.bfloat16)
        self.near, self.far, self.rest = (
            call.hold((blocks, rows // 2, width), jnp.bfloat16) for _ in range(3)
        )
        self.sa, self.ra, self.sb, self.rb, self.sc, self.rc = (
            call.flags(blocks) for _ in range(6)
        )

    def bind(self, place):
        self.place = place

    def own(self):
        return pl.ds(pl.multiple_of(self.place.side * self.half, self.half), self.half)

    def theirs(self):
        start = (1 - self.place.side) * self.half
        return pl.ds(pl.multiple_of(start, self.half), self.half)

    def first(self, i):
        source = self.part.at[i, self.theirs()]
        return remote(source, self.near.at[i], self.sa.at[i], self.ra.at[i], self.place.pair)

    def second(self, i):
        return remote(
            self.near.at[i], self.far.at[i], self.sb.at[i], self.rb.at[i], self.place.cross
        )

    def third(self, i):
        return remote(
            self.far.at[i], self.rest.at[i], self.sc.at[i], self.rc.at[i], self.place.pair
        )

    def send(self, i, partial_rows):
        self.part[i] = partial_rows.astype(jnp.bfloat16)
        self.first(i).start()

    def middle(self, i):
        self.first(i).wait()
        mine = self.part[i, self.own()].astype(jnp.float32)
        self.near[i] = (mine + self.near[i].astype(jnp.float32)).astype(jnp.bfloat16)
        self.second(i).start()

    def last(self, i):
        self.second(i).wait()
        total = self.near[i].astype(jnp.float32) + self.far[i].astype(jnp.float32)
        self.far[i] = total.astype(jnp.bfloat16)
        self.third(i).start()

    def total(self, i):
        self.third(i).wait()
        self.part[i, self.own()] = self.far[i]
        self.part[i, self.theirs()] = self.rest[i]
        return self.part[i].astype(jnp.float32)


class QuarterSum(HeadSum):
    def __init__(self, call, blocks, rows, width):
        self.half, self.quarter = rows // 2, rows // 4
        self.part = call.hold((blocks, rows, width), jnp.bfloat16)
        self.near = call.hold((blocks, rows // 2, width), jnp.bfloat16)
        self.far = call.hold((blocks, rows // 4, width), jnp.bfloat16)
        self.out = call.store((blocks, rows // 4, width), jnp.bfloat16)
        self.sa, self.ra, self.sb, self.rb = (call.flags(blocks) for _ in range(4))

    def rows_of(self, index):
        return pl.ds(pl.multiple_of(index * self.quarter, self.quarter), self.quarter)

    def second(self, i):
        source = self.near.at[i, self.rows_of(1 - self.place.mp // 2)]
        return remote(source, self.far.at[i], self.sb.at[i], self.rb.at[i], self.place.cross)

    def last(self, i):
        self.second(i).wait()
        mine = self.near[i, self.rows_of(self.place.mp // 2)].astype(jnp.float32)
        self.out[i] = (mine + self.far[i].astype(jnp.float32)).astype(jnp.bfloat16)


class Gather:
    def __init__(self, call, shard, places, swap=False, land=False):
        self.parts = lax.axis_size(CTX)
        call.far = True
        if isinstance(shard, Held):
            self.shard = shard
        else:
            self.shard = call.load(shard)
            call.loads.insert(0, call.loads.pop())
        self.land = land
        whole = (places,) + shard.shape
        self.whole = (call.store if land else call.give)(whole, shard.dtype)
        self.zs, self.zr, self.ys, self.yr = (call.flags(self.parts) for _ in range(4))
        self.l, self.ss, self.sr = (call.flags(1) for _ in range(3))
        self.relayed = self.parts == 4
        self.swap = swap and self.relayed
        self.order = (2, 1, 3) if self.relayed else tuple(range(self.parts - 1, 0, -1))
        self.steps = len(self.order)

    def bind(self, place):
        self.place, self.crossed = place, False

    def slot(self, dp, ctx):
        return self.whole.at[dp * self.parts + ctx]

    def local(self):
        p = self.place
        return pltpu.make_async_copy(self.shard.ref, self.slot(p.dp, p.ctx), self.l.at[0])

    def along(self, s):
        p = self.place
        target = self.slot(p.dp, p.ctx)
        return remote(self.shard.ref, target, self.zs.at[s], self.zr.at[s], p.along(p.ahead(s)))

    def direct(self, s, act):
        if self.relayed and s != 2:
            pl.when(self.place.ctx != (0 if s == 3 else 3))(lambda: act(self.along(s)))
        else:
            act(self.along(s))

    def relay(self, act):
        p = self.place
        block = self.slot(p.dp, p.behind(2))
        for middle, end, s in ((2, 3, 3), (1, 0, 1)):
            copy = remote(block, block, self.zs.at[0], self.zr.at[s], p.along(end))
            pl.when(p.ctx == middle)(lambda copy=copy: act(copy))

    def across(self, s):
        p = self.place
        block = self.slot(p.dp, p.behind(s))
        source = self.shard.ref if s == 0 else block
        return remote(source, block, self.ys.at[s], self.yr.at[s], p.other)

    def arrive(self, s):
        p = self.place
        block = self.slot(1 - p.dp, p.behind(s))
        return remote(block, block, self.ys.at[s], self.yr.at[s], p.other)

    def when_crossing(self, s, act):
        if self.swap and s in (1, 3):
            pl.when(lax.rem(self.place.ctx, 2) == (0 if s == 1 else 1))(act)
        else:
            act()

    def swapped(self, ctx):
        p = self.place
        block = self.slot(1 - p.dp, ctx)
        neighbour = p.ctx + 1 - 2 * lax.rem(p.ctx, 2)
        return remote(block, block, self.ss.at[0], self.sr.at[0], p.along(neighbour))

    def cross(self):
        self.crossed = True
        self.shard.need()
        self.across(0).start()

    def start(self):
        self.shard.need()
        for s in self.order:
            self.direct(s, lambda copy: copy.start())
        if not self.crossed:
            self.cross()
        self.local().start()

    def step(self, k):
        s = self.order[k]
        p = self.place
        block = self.slot(p.dp, p.behind(s))
        remote(block, block, self.zs.at[s], self.zr.at[s], p.along(p.ctx)).wait_recv()
        if self.relayed and s == 2:
            self.relay(lambda copy: copy.start())
        self.when_crossing(s, lambda: self.across(s).start())
        if self.swap and k == 0:
            self.arrive(0).wait_recv()
            self.swapped(p.ctx).start()

    def finish(self):
        p = self.place
        self.local().wait()
        for s in self.order:
            self.direct(s, lambda copy: copy.wait_send())
        if self.relayed:
            self.relay(lambda copy: copy.wait_send())

        def both(s):
            self.across(s).wait_send()
            self.arrive(s).wait_recv()

        for s in self.order:
            self.when_crossing(s, functools.partial(both, s))
        self.across(0).wait_send()
        if self.swap:
            self.swapped(p.ctx).wait_send()
            self.swapped(p.ctx + 1 - 2 * lax.rem(p.ctx, 2)).wait_recv()
        else:
            self.arrive(0).wait_recv()
        if self.land:
            self.whole.put()

    @property
    def result(self):
        whole = self.whole.result
        return whole.reshape(-1, whole.shape[-1])


class Scatter:
    def __init__(self, call, blocks, swap=False):
        self.parts = lax.axis_size(CTX)
        places, rows, width = blocks.shape
        self.dtype = blocks.dtype
        call.far = True
        self.late = isinstance(blocks, Held)
        self.blocks = blocks if self.late else call.take(blocks)
        self.out = call.store((rows, width), jnp.float32)
        if not self.late:
            self.mb = call.hold((self.parts, rows, width), blocks.dtype)
        self.yb = call.hold((self.parts, rows, width), blocks.dtype)
        self.zb = call.hold((self.parts - 1, rows, width), blocks.dtype)
        self.zs, self.zr, self.ys, self.yr = (call.flags(self.parts) for _ in range(4))
        self.l, self.ss, self.sr = (call.flags(2) for _ in range(3))
        self.relayed = self.parts == 4
        self.swap = swap and self.relayed
        self.order = (3, 1, 2, 0) if self.relayed else tuple(range(self.parts - 1, -1, -1))
        if self.relayed:
            self.rb = call.hold((rows, width), blocks.dtype)
        if self.swap:
            self.tb, self.wb = (call.hold((rows, width), blocks.dtype) for _ in range(2))
        self.steps = self.parts

    def bind(self, place):
        self.place = place

    def block_of(self, dp, ctx):
        return self.blocks.at[dp * self.parts + ctx]

    def local(self):
        mine = self.blocks.at[pl.ds(self.place.dp * self.parts, self.parts)]
        return pltpu.make_async_copy(mine, self.mb.ref, self.l.at[0])

    def local_twin(self):
        p = self.place
        return pltpu.make_async_copy(self.block_of(1 - p.dp, p.ctx), self.tb.ref, self.l.at[1])

    def swapped(self):
        p = self.place
        neighbour = p.ctx + 1 - 2 * lax.rem(p.ctx, 2)
        block = self.block_of(1 - p.dp, neighbour)
        return remote(block, self.wb.ref, self.ss.at[0], self.sr.at[0], p.along(neighbour))

    def across(self, s):
        p = self.place
        block = self.tb.ref if self.swap and s == 0 else self.block_of(1 - p.dp, p.ahead(s))
        return remote(block, self.yb.at[s], self.ys.at[s], self.yr.at[s], p.other)

    def when_crossing(self, s, act):
        if self.swap and s in (1, 3):
            pl.when(lax.rem(self.place.ctx, 2) == (1 if s == 1 else 0))(act)
        else:
            act()

    def along(self, s, act):
        p = self.place
        target = self.zb.at[s - 1]
        copy = remote(self.yb.at[s], target, self.zs.at[s], self.zr.at[s], p.along(p.ahead(s)))
        if not self.relayed or s == 2:
            act(copy)
            return
        end, middle = (0, 1) if s == 3 else (3, 2)
        way = remote(self.yb.at[s], self.rb.ref, self.zs.at[s], self.zr.at[0], p.along(middle))
        pl.when(p.ctx != end)(lambda: act(copy))
        pl.when(p.ctx == end)(lambda: act(way))

    def early(self, act):
        p = self.place
        for s, odd in ((1, 0), (3, 1)):
            block, target = self.block_of(p.dp, p.ahead(s)), self.zb.at[s - 1]
            copy = remote(block, target, self.zs.at[s], self.zr.at[s], p.along(p.ahead(s)))
            pl.when(lax.rem(p.ctx, 2) == odd)(lambda copy=copy: act(copy))

    def start(self):
        if self.swap:
            self.swapped().start()
            self.local_twin().start()
            self.early(lambda copy: copy.start())
        for s in self.order:
            if s or not self.swap:
                self.when_crossing(s, lambda s=s: self.across(s).start())
        if not self.late:
            self.local().start()

    def send_twin(self):
        self.local_twin().wait()
        self.swapped().wait()
        both = self.tb[...].astype(jnp.float32) + self.wb[...].astype(jnp.float32)
        self.tb[...] = both.astype(self.dtype)
        self.across(0).start()

    def step(self, k):
        p = self.place
        s = self.order[k]
        if k == 0:
            if not self.late:
                self.local().wait()
            if self.swap:
                self.send_twin()
        if self.late:
            mine = self.blocks[p.dp * self.parts + p.ahead(s)]
        else:
            mine = self.mb[p.ahead(s)]
        mine = mine.astype(jnp.float32)

        def add_crossed():
            self.across(s).wait()
            self.yb[s] = (mine + self.yb[s].astype(jnp.float32)).astype(self.dtype)
            if s != 2:
                self.along(s, lambda copy: copy.start())

        if s == 0:
            self.across(s).wait()
            self.out[...] = mine + self.yb[s].astype(jnp.float32)
            return
        self.when_crossing(s, add_crossed)
        if s != 2:
            return
        if self.relayed:

            def add_ends():
                way = remote(self.rb.ref, self.rb.ref, self.zs.at[0], self.zr.at[0], p.other)
                way.wait_recv()
                through = self.yb[s].astype(jnp.float32) + self.rb[...].astype(jnp.float32)
                self.yb[s] = through.astype(self.dtype)

            pl.when((p.ctx == 1) | (p.ctx == 2))(add_ends)
        self.along(s, lambda copy: copy.start())

    def finish(self):
        p = self.place

        def add(s):
            block = self.zb.at[s - 1]
            remote(block, block, self.zs.at[s], self.zr.at[s], p.other).wait_recv()
            self.out[...] += self.zb[s - 1].astype(jnp.float32)

        for s in self.order:
            if s == 0:
                continue
            self.along(s, lambda copy: copy.wait_send())
            if self.relayed and s != 2:
                pl.when(p.ctx != (3 if s == 3 else 0))(functools.partial(add, s))
            else:
                add(s)
        self.out.put()

    @property
    def result(self):
        return self.out.result


class Deal:
    def __init__(self, call, blocks, rows=None, land=False):
        self.parts, self.compact = lax.axis_size(CTX), rows is not None
        length, width = rows or blocks.shape[1], blocks.shape[2]
        self.share = length // 4
        call.far = True
        self.source = call.take(blocks)
        self.land = land
        target = (self.parts, length, width)
        self.target = (call.store if land else call.give)(target, blocks.dtype)
        self.held = call.hold(blocks.shape[1:], blocks.dtype)
        self.l = call.flags(2)
        self.zf, self.af, self.xf, self.bf = (
            tuple(call.flags(self.parts) for _ in range(2)) for _ in range(4)
        )
        self.order = list(range(self.parts - 1, 0, -1))
        if self.compact:
            self.order.insert(0, 0)
        self.steps = 2 * len(self.order)

    def bind(self, place):
        self.place = place
        if self.compact:
            x, side = place.mp // 2, place.side
            self.own, self.far = side * 2 + x, side * 2 + 1 - x
            self.near, self.near_far = (1 - side) * 2 + x, (1 - side) * 2 + 1 - x
        else:
            self.own, self.far = place.mp, lax.rem(place.mp + 2, 4)
            self.near = place.mp + 1 - 2 * place.side
            self.near_far = lax.rem(self.near + 2, 4)

    def rows(self, index):
        return pl.ds(pl.multiple_of(index * self.share, self.share), self.share)

    def local(self, k):
        p = self.place
        target = self.target.at[p.ctx]
        if self.compact:
            target = self.target.at[p.ctx, self.rows(self.own)]
        refs = (self.source.at[p.ctx], self.held.ref, target)
        return pltpu.make_async_copy(refs[k], refs[k + 1], self.l.at[k])

    def along(self, s):
        p = self.place
        rows = self.rows(self.own)
        source = self.source.at[p.ahead(s)] if self.compact else self.source.at[p.ahead(s), rows]
        target = self.target.at[p.ctx, rows]
        return remote(source, target, self.zf[0].at[s], self.zf[1].at[s], p.along(p.ahead(s)))

    def piece(self, s, index, flags, peer):
        ref = self.target.at[self.place.behind(s), self.rows(index)]
        return remote(ref, ref, flags[0].at[s], flags[1].at[s], peer)

    def start(self):
        for s in self.order:
            if s:
                self.along(s).start()
        self.local(0).start()

    def step(self, k):
        p = self.place
        if k == 0:
            self.local(0).wait()
            self.local(1).start()
        s = self.order[k % len(self.order)]
        if k < len(self.order):
            if s:
                self.piece(s, self.own, self.zf, p.along(p.ctx)).wait_recv()
            else:
                self.local(1).wait()
            self.piece(s, self.own, self.xf, p.cross).start()
            self.piece(s, self.own, self.af, p.pair).start()
        else:
            self.piece(s, self.far, self.xf, p.cross).wait_recv()
            self.piece(s, self.far, self.bf, p.pair).start()

    def finish(self):
        p = self.place
        if not self.compact:
            self.local(1).wait()
        for s in self.order:
            if s:
                self.along(s).wait_send()
            self.piece(s, self.own, self.xf, p.cross).wait_send()
            self.piece(s, self.own, self.af, p.pair).wait_send()
            self.piece(s, self.far, self.bf, p.pair).wait_send()
            self.piece(s, self.near, self.af, p.pair).wait_recv()
            self.piece(s, self.near_far, self.bf, p.pair).wait_recv()
        if self.land:
            self.target.put()

    @property
    def result(self):
        whole = self.target.result
        return whole.reshape(-1, whole.shape[-1])


LATE = "late"


class Jobs:
    def __init__(self, jobs, plan):
        self.jobs = list(jobs)
        self.queue = sorted(
            (times[k] if len(times) > 2 else times[0] + k * times[1], j, k)
            for j, (job, times) in enumerate(zip(self.jobs, plan))
            for k in range(job.steps)
        )
        self.at = 0

    def bind(self, place):
        self.at = 0
        for job in self.jobs:
            job.bind(place)

    def start(self):
        for job in self.jobs:
            if not getattr(job, LATE, False):
                job.start()

    def advance(self, reached):
        while self.at < len(self.queue) and self.queue[self.at][0] <= reached:
            _, j, k = self.queue[self.at]
            self.jobs[j].step(k)
            self.at += 1

    def finish(self):
        self.advance(math.inf)
        for job in self.jobs:
            job.finish()


def begin(call, total, jobs, backward=False):
    place = Place()
    if total is not None:
        total.bind(place)
    jobs.bind(place)
    place.greet(call.far)
    call.start_loads(backward)
    place.enter(call.far)
    jobs.start()
    return place


def dot_nn(a, b):
    return lax.dot_general(a, b, (((1,), (0,)), ((), ())), preferred_element_type=jnp.float32)


def dot_nt(a, b):
    return lax.dot_general(a, b, (((1,), (1,)), ((), ())), preferred_element_type=jnp.float32)


def dot_tn(a, b):
    return lax.dot_general(a, b, (((0,), (0,)), ((), ())), preferred_element_type=jnp.float32)


def lane_number(width):
    return lax.broadcasted_iota(jnp.int32, (1, width), 1)


LANES = 128
BLOCKS = 4


def turn(values, cosine, signed_sine, back):
    half = HEAD_DIM // 2
    leading = lax.rem(lane_number(LANES), HEAD_DIM) < half
    pieces = []
    for at in range(0, values.shape[1], LANES):
        piece = values[:, at : at + LANES]
        swapped = jnp.where(leading, pltpu.roll(piece, LANES - half, 1), pltpu.roll(piece, half, 1))
        moved = swapped * signed_sine
        pieces.append(piece * cosine - moved if back else piece * cosine + moved)
    return jnp.concatenate(pieces, axis=1)


def write_bias(bias, seg_col, seg_row, i, rows, keys):
    query_at = i * rows + lax.broadcasted_iota(jnp.int32, (rows, 1), 0)
    key_at = lax.broadcasted_iota(jnp.int32, (1, keys), 1)
    same = seg_col[pl.ds(i * rows, rows), :1] == seg_row[:1, :keys]
    bias[:, :keys] = jnp.where(same & (key_at <= query_at), 0.0, neg_large)


class Stacked:
    def __init__(self, held):
        self.held, self.dtype = held, held.dtype
        blocks, rows, width = held.shape
        self.shape = (blocks * rows, width)

    def need(self, i=None):
        pass

    def __getitem__(self, key):
        rows, columns = key
        if isinstance(rows, slice):
            block = self.held[:, :, columns]
            return block.reshape(-1, block.shape[-1])
        return self.held[rows.start // self.held.shape[1], :, columns]


class Opening:
    def __init__(self, call, inputs, segment_ids, layers, gain_rows, angle_row, places):
        self.call, self.places = call, places
        parts, length, width = inputs.shape
        self.count = count = parts * length
        (q1, k1, v1, o1, *tall1), (q2, k2, v2, o2, *tall2) = layers
        self.shard, self.hid = shard, hid = q1.shape
        units = tall1[0].shape[0]
        low = jnp.bfloat16
        self.first = [call.load(array) for array in (q1, k1, v1, o1)]
        self.gain_rows = call.load(gain_rows)
        self.ids, self.angle = call.load(segment_ids), call.load(angle_row)
        self.tall = [call.load(array) for array in tall1]
        self.second = [call.load(array) for array in (q2, k2, v2, o2)]
        self.tall += [call.load(array) for array in tall2]
        self.shards_one = [call.hold((shard, units), low) for _ in tall1]
        self.shards_two = [call.store((shard, units), low) for _ in tall2]
        self.wa_one = call.hold((shard, 4 * hid), low)
        self.wa_two = call.store((shard, 4 * hid), low)
        self.gains_wide = call.hold(gain_rows.shape, jnp.float32)
        self.cosine, self.sine, self.seg_col = (
            call.store((count, LANES), jnp.float32, BLOCKS) for _ in range(3)
        )
        self.seg_row = call.store((8, count), jnp.float32)
        self.gather = Gather(call, self.wa_one, places, land=True)
        self.deal = Deal(call, inputs, land=True)
        self.gather_gains = Gather(call, self.gains_wide, places, land=True)
        plan = ((2.0, 0.1), (5.0, 4.0), (14.0, 6.0))
        self.jobs = Jobs([self.gather_gains, self.deal, self.gather], plan)
        self.deal.late = True
        self.x, self.wa = Stacked(self.deal.target), Stacked(self.gather.whole)
        self.gains = call.store((gain_rows.shape[0], width), jnp.float32)

    def tables(self):
        return (self.cosine, self.sine, self.seg_col, self.seg_row)

    def run(self, total, jobs):
        call, hid = self.call, self.hid
        place = Place()
        total.bind(place)
        self.jobs.bind(place)
        jobs.bind(place)
        place.greet(call.far)
        call.start_loads()
        place.enter(call.far)
        self.deal.start()
        for j, held in enumerate(self.first):
            held.need()
            values = held[...]
            self.wa_one[:, j * hid : (j + 1) * hid] = values.T if j == 3 else values
        self.gain_rows.need()
        self.gains_wide[...] = self.gain_rows[...].astype(jnp.float32)
        self.jobs.start()
        for tall, shard in zip(self.tall, self.shards_one + self.shards_two):
            tall.need()
            shard[...] = tall[...].T
            if shard.out is not None:
                shard.put()
        for j, held in enumerate(self.second):
            held.need()
            values = held[...]
            self.wa_two[:, j * hid : (j + 1) * hid] = values.T if j == 3 else values
        self.wa_two.put()
        for job in jobs.jobs:
            job.cross()
        self.ids.need()
        self.angle.need()
        ids = self.ids[...].astype(jnp.float32)
        mine = lax.broadcasted_iota(jnp.int32, ids.shape, 0) == place.ctx
        own = jnp.sum(jnp.where(mine, ids, 0.0), axis=0, keepdims=True)
        self.seg_row[...] = jnp.broadcast_to(own, self.seg_row.shape)
        self.seg_row.put()
        self.seg_col[...] = jnp.broadcast_to(own, (LANES, self.count)).T
        self.seg_col.put()
        rows = self.count // BLOCKS
        for i in range(BLOCKS):
            at = pl.ds(i * rows, rows)
            index = i * rows + lax.broadcasted_iota(jnp.int32, (rows, 1), 0)
            angles = index.astype(jnp.float32) * self.angle[:1, :]
            self.cosine[at, :] = jnp.cos(angles)
            self.sine[at, :] = jnp.sin(angles) * self.angle[1:2, :]
        self.cosine.put()
        self.sine.put()
        self.jobs.advance(math.inf)
        jobs.start()
        self.jobs.finish()
        jobs.advance(0.5)
        shard = self.shard
        for k in range(self.places):
            self.gains[:, k * shard : (k + 1) * shard] = self.gather_gains.whole[k]
        self.gains.put()


def attention_layer(number, x, first_v, wa, gains, which, tables, jobs_of, plan, opening=None):
    call = Call(number)
    if opening is None:
        start = None
        x, gains, wa = call.load(x, BLOCKS), call.load(gains), call.load(wa)
        cosine, sine, seg_col = (call.load(table, BLOCKS) for table in tables[:3])
        seg_row = call.load(tables[3])
    else:
        start = opening(call)
        x, gains, wa = start.x, start.gains, start.wa
        cosine, sine, seg_col, seg_row = start.tables()
    count, width = x.shape
    hid = wa.shape[1] // 4
    heads = hid // HEAD_DIM
    rows = count // BLOCKS
    if first_v is not None:
        first_v = call.load(first_v, BLOCKS)
    else:
        v = call.store((count, hid), jnp.float32, BLOCKS)
    x1 = call.store((count, width), jnp.float32, BLOCKS)
    h = call.store((count, width), jnp.bfloat16, BLOCKS)
    q, k, m, o = (call.store((count, hid), jnp.bfloat16, BLOCKS) for _ in range(4))
    lse = call.store((heads, count, 1), jnp.float32, BLOCKS)
    bias = call.hold((rows, count), jnp.float32)
    acc = call.hold((rows, hid), jnp.float32)
    total = HeadSum(call, BLOCKS, rows, width)
    carried = jobs_of(call, start)
    jobs = Jobs(carried, plan)

    def body():
        if start is None:
            begin(call, total, jobs)
        else:
            start.run(total, jobs)
        lane = lane_number(hid)
        for i in range(BLOCKS):
            at = pl.ds(i * rows, rows)
            x.need(i)
            gains.need()
            stream = x[at, :].astype(jnp.float32)
            inverse = lax.rsqrt(jnp.mean(stream * stream, axis=-1, keepdims=True) + epsilon)
            normed = (stream * inverse * gains[which : which + 1, :]).astype(jnp.bfloat16)
            h[at, :] = normed
            h.put(i)
            wa.need()
            projected = dot_nn(normed, wa[:, : 3 * hid])
            cosine.need(i)
            sine.need(i)
            cos, sin = cosine[at, :], sine[at, :]
            queries = turn(projected[:, :hid], cos, sin, False).astype(jnp.bfloat16)
            q[at, :] = queries * jnp.bfloat16(HEAD_DIM**-0.5)
            k[at, :] = turn(projected[:, hid : 2 * hid], cos, sin, False).astype(jnp.bfloat16)
            values = projected[:, 2 * hid :]
            if first_v is None:
                v[at, :] = values
                v.put(i)
            else:
                first_v.need(i)
                values = 0.5 * values + 0.5 * first_v[at, :]
            m[at, :] = values.astype(jnp.bfloat16)
            for held in (q, k, m):
                held.put(i)
            keys = (i + 1) * rows
            seg_col.need(i)
            seg_row.need()
            write_bias(bias, seg_col, seg_row, i, rows, keys)
            if i:
                total.middle(i - 1)
            jobs.advance((4.5, 8.0, 12.5, 18.0)[i])

            def one_head(index, unused):
                mask = lane // HEAD_DIM == index
                query = jnp.where(mask, q[at, :], jnp.bfloat16(0))
                scores = dot_nt(query, k[:keys, :]) + bias[:, :keys]
                top = jnp.max(scores, axis=-1, keepdims=True)
                exponent = jnp.exp(scores - top)
                summed = jnp.sum(exponent, axis=-1, keepdims=True)
                weighted = dot_nn(exponent.astype(jnp.bfloat16), m[:keys, :])
                acc[...] = jnp.where(mask, weighted / summed, acc[...])
                lse[index, at, :] = top + jnp.log(summed)
                return unused

            lax.fori_loop(0, heads, one_head, 0)
            attended = acc[...].astype(jnp.bfloat16)
            o[at, :] = attended
            o.put(i)
            lse.put(i)
            total.send(i, dot_nt(attended, wa[:, 3 * hid :]))
            jobs.advance((6.0, 10.5, 16.0, 22.5)[i])
        total.middle(BLOCKS - 1)
        for i in range(BLOCKS):
            total.last(i)
            jobs.advance((23.0, 24.0, 28.0, 33.0)[i])
        for i in range(BLOCKS):
            at = pl.ds(i * rows, rows)
            x1[at, :] = x[at, :].astype(jnp.float32) + total.total(i)
            x1.put(i)
        jobs.finish()

    call.run(body)
    return SimpleNamespace(
        x1=x1.result,
        h=h.result,
        q=q.result,
        k=k.result,
        m=m.result,
        o=o.result,
        lse=lse.result,
        v=v.result if first_v is None else None,
        carried=[job.result for job in carried],
        start=start,
    )


def feed_forward_layer(number, x1, gate, up, down, gains, which, jobs_of, plan):
    count, width = x1.shape
    units = gate.shape[1]
    rows = count // BLOCKS
    call = Call(number)
    x1 = call.load(x1, BLOCKS)
    gains, gate, up, down = (call.load(array) for array in (gains, gate, up, down))
    y = call.store_from(x1, (count, width), jnp.float32, BLOCKS)
    y_low, h2 = (call.store((count, width), jnp.bfloat16, BLOCKS) for _ in range(2))
    z, u, a = (call.store((count, units), jnp.bfloat16, BLOCKS) for _ in range(3))
    total = HeadSum(call, BLOCKS, rows, width)
    carried = jobs_of(call)
    jobs = Jobs(carried, plan)

    def body():
        begin(call, total, jobs)
        for i in range(BLOCKS):
            at = pl.ds(i * rows, rows)
            x1.need(i)
            gains.need()
            stream = x1[at, :]
            inverse = lax.rsqrt(jnp.mean(stream * stream, axis=-1, keepdims=True) + epsilon)
            normed = (stream * inverse * gains[which : which + 1, :]).astype(jnp.bfloat16)
            h2[at, :] = normed
            gate.need()
            gated = dot_nn(normed, gate[...])
            if i:
                total.middle(i - 1)
            jobs.advance(2.5 * i + 4.0)
            up.need()
            raised = dot_nn(normed, up[...])
            active = (gated * lax.logistic(gated) * raised).astype(jnp.bfloat16)
            z[at, :] = gated.astype(jnp.bfloat16)
            u[at, :] = raised.astype(jnp.bfloat16)
            a[at, :] = active
            for held in (h2, z, u, a):
                held.put(i)
            down.need()
            total.send(i, dot_nt(active, down[...]))
            jobs.advance(2.5 * i + 5.5)
        total.middle(BLOCKS - 1)
        for i in range(BLOCKS):
            total.last(i)
            jobs.advance(13.0 + 5.7 * i)
        for i in range(BLOCKS):
            at = pl.ds(i * rows, rows)
            result = x1[at, :] + total.total(i)
            x1[at, :] = result
            y_low[at, :] = result.astype(jnp.bfloat16)
            y.put(i)
            y_low.put(i)
        jobs.finish()

    call.run(body)
    return SimpleNamespace(
        y=y.result,
        y_low=y_low.result,
        h2=h2.result,
        z=z.result,
        u=u.result,
        a=a.result,
        carried=[job.result for job in carried],
    )


def norm_back(gain, grad, stream, gain_sum):
    inverse = lax.rsqrt(jnp.mean(stream * stream, axis=-1, keepdims=True) + epsilon)
    scaled = stream * inverse
    grad_scaled = grad * gain
    products = jnp.mean(grad_scaled * scaled, axis=-1, keepdims=True)
    gain_sum = gain_sum + jnp.sum(grad * scaled, axis=0, keepdims=True)
    return inverse * (grad_scaled - scaled * products), gain_sum


def feed_forward_back(number, gy, x1, saved, gate, up, down, gains, which, jobs_of, plan):
    count, width = x1.shape
    units = gate.shape[1]
    rows = count // BLOCKS
    call = Call(number)
    call.in_turn = True
    if saved is not None:
        gy = call.load(gy, BLOCKS)
        down = call.load(down)
        z, u = call.load(saved.z, BLOCKS), call.load(saved.u, BLOCKS)
        gate, up, a, h2, gains = (call.load(w) for w in (gate, up, saved.a, saved.h2, gains))
        x1 = call.load(x1, BLOCKS)
        later = 0.0
    else:
        x1, gains = call.load(x1, BLOCKS), call.load(gains)
        gate, up, down = (call.load(w) for w in (gate, up, down))
        gy = call.load(gy, BLOCKS)
        h2 = call.hold((count, width), jnp.bfloat16)
        z, u, a = (call.hold((count, units), jnp.bfloat16) for _ in range(3))
        quarters = QuarterSum(call, BLOCKS, rows, width)
        later = 10.0
    gx1 = call.store_from(x1, (count, width), jnp.float32, BLOCKS)
    gain = call.store((1, width), jnp.float32)
    d_gate, d_up = (call.store((width, units), jnp.bfloat16, 4) for _ in range(2))
    places = lax.axis_size(DP) * lax.axis_size(CTX)
    shard = width // places
    d_down = call.hold((places, shard, units), jnp.bfloat16)
    low = call.hold((count, width), jnp.bfloat16)
    gz, gu = (call.hold((count, units), jnp.bfloat16) for _ in range(2))
    total = HeadSum(call, BLOCKS, rows, width)
    down_sum = Scatter(call, d_down)
    carried = jobs_of(call, down_sum)
    jobs = Jobs(carried, plan)

    def forward():
        for i in range(BLOCKS):
            at = pl.ds(i * rows, rows)
            x1.need(i)
            gains.need()
            stream = x1[at, :]
            inverse = lax.rsqrt(jnp.mean(stream * stream, axis=-1, keepdims=True) + epsilon)
            normed = (stream * inverse * gains[which : which + 1, :]).astype(jnp.bfloat16)
            h2[at, :] = normed
            gate.need()
            gated = dot_nn(normed, gate[...])
            up.need()
            raised = dot_nn(normed, up[...])
            active = (gated * lax.logistic(gated) * raised).astype(jnp.bfloat16)
            z[at, :] = gated.astype(jnp.bfloat16)
            u[at, :] = raised.astype(jnp.bfloat16)
            a[at, :] = active
            down.need()
            if i:
                quarters.middle(i - 1)
            quarters.send(i, dot_nt(active, down[...]) + stream * 0.25)
        quarters.middle(BLOCKS - 1)

    def body():
        if saved is None:
            quarters.bind(begin(call, total, jobs))
            forward()
        else:
            begin(call, total, jobs)
        for i in range(BLOCKS):
            at = pl.ds(i * rows, rows)
            gy.need(i)
            low[at, :] = gy[at, :].astype(jnp.bfloat16)
        for i in range(BLOCKS):
            at = pl.ds(i * rows, rows)
            down.need()
            ga = dot_nn(low[at, :], down[...])
            z.need(i)
            u.need(i)
            gated = z[at, :].astype(jnp.float32)
            sigma = lax.logistic(gated)
            raised = u[at, :].astype(jnp.float32)
            slope = sigma * (1.0 + gated * (1.0 - sigma))
            gz[at, :] = (ga * raised * slope).astype(jnp.bfloat16)
            gu[at, :] = (ga * gated * sigma).astype(jnp.bfloat16)
            if i > 1:
                total.middle(i - 1)
            gate.need()
            up.need()
            total.send(i, dot_nt(gz[at, :], gate[...]) + dot_nt(gu[at, :], up[...]))
            if i == 0:
                a.need()
                for j in range(places // 2):
                    cut = slice(j * 2 * shard, (j + 1) * 2 * shard)
                    part = dot_tn(low[:, cut], a[...]).astype(jnp.bfloat16)
                    d_down[2 * j : 2 * j + 2] = part.reshape(2, shard, units)
                    if j == 0:
                        total.middle(0)
                down_sum.start()
            jobs.advance(3.0 * i + 9.0 + later)
        total.middle(BLOCKS - 1)
        cols = width // 4
        h2.need()
        for reached, left, right, out in ((21.0, h2, gz, d_gate), (24.0, h2, gu, d_up)):
            for j in range(4):
                cut = slice(j * cols, (j + 1) * cols)
                out[cut, :] = dot_tn(left[:, cut], right[...]).astype(jnp.bfloat16)
                out.put(j)
            jobs.advance(reached + later)
        gains.need()
        if saved is None:
            for i in range(BLOCKS):
                quarters.last(i)
            quarters.out.put()
        for i in range(BLOCKS):
            total.last(i)
            jobs.advance((24.0, 24.0, 28.0, 34.0)[i] + later)
        gain_sum = jnp.zeros((1, width), jnp.float32)
        for i in range(BLOCKS):
            at = pl.ds(i * rows, rows)
            x1.need(i)
            step, gain_sum = norm_back(
                gains[which : which + 1, :], total.total(i), x1[at, :], gain_sum
            )
            x1[at, :] = gy[at, :].astype(jnp.float32) + step
            gx1.put(i)
        gain[...] = gain_sum
        gain.put()
        jobs.finish()

    call.run(body)
    return SimpleNamespace(
        gx1=gx1.result,
        gain=gain.result,
        d_gate=d_gate.result,
        d_up=d_up.result,
        quarters=quarters.out.result if saved is None else None,
        carried=[job.result for job in carried],
    )


def attention_back(number, gx1, x, saved, extra, wa, gains, which, tables, jobs_of, plan):
    count, width = x.shape
    hid = wa.shape[1] // 4
    heads = hid // HEAD_DIM
    rows = count // BLOCKS
    call = Call(number)
    gx1, wa = call.load(gx1, BLOCKS), call.load(wa)
    q, k, m, o = (
        call.load(array, blocks)
        for array, blocks in ((saved.q, BLOCKS), (saved.k, 1), (saved.m, 1), (saved.o, BLOCKS))
    )
    lse = call.load(saved.lse, BLOCKS)
    cosine, sine, seg_col = (call.load(table, BLOCKS) for table in tables[:3])
    seg_row = call.load(tables[3])
    if extra is not None:
        extra = call.load(extra, BLOCKS)
    h, gains, x = call.load(saved.h), call.load(gains), call.load(x, BLOCKS)
    if extra is not None:
        gx = call.store((count, width), jnp.bfloat16, BLOCKS)
        gx_held = gx
    else:
        gx_held = gx1
        gx = call.store_from(gx1, (count, width), jnp.float32, BLOCKS)
        passed = call.store((count, hid), jnp.float32, BLOCKS)
    gain = call.store((1, width), jnp.float32)
    d_wa = call.store((width, 4 * hid), jnp.bfloat16, 4)
    low = call.hold((count, width), jnp.bfloat16)
    bias = call.hold((rows, count), jnp.float32)
    go = call.hold((rows, hid), jnp.bfloat16)
    gq = call.hold((rows, hid), jnp.float32)
    gk, gm = (call.hold((count, hid), jnp.float32) for _ in range(2))
    g3 = call.hold((count, 3 * hid), jnp.bfloat16)
    total = HeadSum(call, BLOCKS, rows, width)
    carried = jobs_of(call)
    jobs = Jobs(carried, plan)

    def body():
        begin(call, total, jobs, True)
        lane = lane_number(hid)
        gk[...] = jnp.zeros(gk.shape, gk.dtype)
        gm[...] = jnp.zeros(gm.shape, gm.dtype)
        order = list(range(BLOCKS))[::-1]
        for turn_index, i in enumerate(order):
            at = pl.ds(i * rows, rows)
            gx1.need(i)
            low[at, :] = gx1[at, :].astype(jnp.bfloat16)
            wa.need()
            go[...] = dot_nn(low[at, :], wa[:, 3 * hid :]).astype(jnp.bfloat16)
            keys = (i + 1) * rows
            for held in (seg_row, seg_col, q, o, lse, k, m):
                held.need(i)
            write_bias(bias, seg_col, seg_row, i, rows, keys)
            gq[...] = jnp.zeros(gq.shape, gq.dtype)
            if turn_index:
                total.middle(order[turn_index - 1])
            else:
                jobs.advance(5.0)

            def one_head(index, unused):
                mask = lane // HEAD_DIM == index
                zero = jnp.bfloat16(0)
                query = jnp.where(mask, q[at, :], zero)
                grad = jnp.where(mask, go[...], zero)
                both = grad.astype(jnp.float32) * o[at, :].astype(jnp.float32)
                delta = jnp.sum(both, axis=-1, keepdims=True)
                scores = dot_nt(query, k[:keys, :]) + bias[:, :keys]
                prob = jnp.exp(scores - lse[index, at, :])
                grad_prob = dot_nt(grad, m[:keys, :])
                grad_score = (prob * (grad_prob - delta)).astype(jnp.bfloat16)
                part = dot_nn(grad_score, k[:keys, :])
                gq[...] = jnp.where(mask, part, gq[...])
                gk[:keys, :] += dot_tn(grad_score, query)
                gm[:keys, :] += dot_tn(prob.astype(jnp.bfloat16), grad)
                return unused

            lax.fori_loop(0, heads, one_head, 0)
            cosine.need(i)
            sine.need(i)
            cos, sin = cosine[at, :], sine[at, :]
            values = gm[at, :]
            if extra is None:
                values = 0.5 * values
                passed[at, :] = values
                passed.put(i)
            else:
                extra.need(i)
                values = values + extra[at, :]
            back = turn(gq[...] * HEAD_DIM**-0.5, cos, sin, True)
            g3[at, :hid] = back.astype(jnp.bfloat16)
            g3[at, hid : 2 * hid] = turn(gk[at, :], cos, sin, True).astype(jnp.bfloat16)
            g3[at, 2 * hid :] = values.astype(jnp.bfloat16)
            total.send(i, dot_nt(g3[at, :], wa[:, : 3 * hid]))
            jobs.advance((11.0, 17.5, 22.0, 25.0)[turn_index])
        total.middle(order[-1])
        cols = width // 4
        h.need()
        for j in range(4):
            cut = slice(j * cols, (j + 1) * cols)
            d_wa[cut, : 3 * hid] = dot_tn(h[:, cut], g3[...]).astype(jnp.bfloat16)
            d_wa[cut, 3 * hid :] = dot_tn(low[:, cut], o[...]).astype(jnp.bfloat16)
            d_wa.put(j)
        jobs.advance(30.0)
        gains.need()
        for turn_index, i in enumerate(order):
            total.last(i)
            jobs.advance((30.0, 30.0, 32.0, 37.0)[turn_index])
        gain_sum = jnp.zeros((1, width), jnp.float32)
        for i in order:
            at = pl.ds(i * rows, rows)
            x.need(i)
            stream = x[at, :].astype(jnp.float32)
            step, gain_sum = norm_back(
                gains[which : which + 1, :], total.total(i), stream, gain_sum
            )
            gx_held[at, :] = (gx1[at, :] + step).astype(gx_held.dtype)
            gx.put(i)
        gain[...] = gain_sum
        gain.put()
        jobs.finish()

    call.run(body)
    return SimpleNamespace(
        gx=gx.result,
        passed=passed.result if extra is None else None,
        gain=gain.result,
        d_wa=d_wa.result,
        carried=[job.result for job in carried],
    )


def transfers(number, jobs_of, plan):
    call = Call(number)
    carried = jobs_of(call)
    jobs = Jobs(carried, plan)

    def body():
        begin(call, None, jobs)
        jobs.finish()

    call.run(body)
    return [job.result for job in carried]


def leave_step(moved, grad, packs, turned, gains):
    call = Call(0)
    kept = [call.load(array, BLOCKS) for array in moved]
    kept_to = [call.store_from(held, held.shape, held.dtype, BLOCKS) for held in kept]
    grad = call.load(grad, BLOCKS)
    wide = call.store(grad.shape, jnp.float32, BLOCKS)
    shard, hid = packs[0].shape[0], packs[0].shape[1] // 4
    flag = call.flags(3 * len(packs))
    packs = [call.load(array) for array in packs]
    unpacked = [[call.give((shard, hid), pack.dtype) for _ in range(3)] for pack in packs]
    upright = [call.store((hid, shard), pack.dtype) for pack in packs]
    turned = [call.load(array) for array in turned]
    turned_to = [call.store(held.shape[::-1], held.dtype) for held in turned]
    gains = call.load(gains)
    gain_to = [call.store((1, shard), gains.dtype) for _ in range(4)]

    def body():
        call.start_loads()
        copies = []
        for at, pack in enumerate(packs):
            pack.need()
            for j in range(3):
                source = pack.at[:, j * hid : (j + 1) * hid]
                copies.append(
                    pltpu.make_async_copy(source, unpacked[at][j].ref, flag.at[3 * at + j])
                )
                copies[-1].start()
            upright[at][...] = pack[:, 3 * hid :].T
            upright[at].put()
        for held, target in zip(turned, turned_to):
            held.need()
            target[...] = held[...].T
            target.put()
        gains.need()
        for j, target in enumerate(gain_to):
            target[...] = gains[j : j + 1, :]
            target.put()
        rows = grad.shape[0] // BLOCKS
        for i in range(BLOCKS):
            at = pl.ds(i * rows, rows)
            grad.need(i)
            wide[at, :] = grad[at, :].astype(jnp.float32)
            wide.put(i)
            for held, target in zip(kept, kept_to):
                held.need(i)
                target.put(i)
        for copy in copies:
            copy.wait()

    call.run(body, False)
    return SimpleNamespace(
        kept=[target.result for target in kept_to],
        grad=wide.result,
        packs=[
            [part.result for part in parts] + [last.result]
            for parts, last in zip(unpacked, upright)
        ],
        turned=[target.result for target in turned_to],
        gains=[target.result.reshape(-1) for target in gain_to],
    )


def dealt_device(
    inputs,
    segment_ids,
    norm_attn_one,
    query_one,
    key_one,
    value_one,
    output_one,
    norm_ffn_one,
    gate_one,
    up_one,
    down_one,
    norm_attn_two,
    query_two,
    key_two,
    value_two,
    output_two,
    norm_ffn_two,
    gate_two,
    up_two,
    down_two,
    cotangent,
):
    parts, length, width = inputs.shape
    places = lax.axis_size(DP) * lax.axis_size(CTX)
    shard = width // places
    gain_rows = jnp.stack([norm_attn_one, norm_ffn_one, norm_attn_two, norm_ffn_two] * 2)
    half = HEAD_DIM // 2
    frequency = 10000.0 ** (-np.arange(half, dtype=np.float32) / np.float32(half))
    repeat = LANES // HEAD_DIM
    signs = np.concatenate([-np.ones(half), np.ones(half)])
    angle_row = np.zeros((8, LANES), np.float32)
    angle_row[0] = np.tile(frequency, 2 * repeat)
    angle_row[1] = np.tile(signs, repeat)

    def split(array):
        return array.reshape(places, shard, array.shape[-1])

    def deal(array):
        return array.reshape(parts, length, width)

    def opening(call):
        return Opening(
            call,
            inputs,
            segment_ids,
            (
                (query_one, key_one, value_one, output_one, gate_one.T, up_one.T, down_one),
                (query_two, key_two, value_two, output_two, gate_two.T, up_two.T, down_two),
            ),
            gain_rows,
            jnp.asarray(angle_row),
            places,
        )

    attn_one = attention_layer(
        1,
        None,
        None,
        None,
        None,
        0,
        None,
        lambda c, start: [Gather(c, held, places) for held in start.shards_one],
        ((0.1, 0.2, 2.0), (5.0, 8.0, 12.0), (15.0, 18.0, 22.0)),
        opening,
    )
    start = attn_one.start
    x, wa_one, gains = start.deal.result, start.gather.result, start.gains.result
    tables = [table.result for table in start.tables()]
    ffn_one_w = attn_one.carried
    wa_two_shard = start.wa_two.result
    shards_two = [held.result for held in start.shards_two]
    ffn_one = feed_forward_layer(
        2,
        attn_one.x1,
        *ffn_one_w,
        gains,
        1,
        lambda c: [Gather(c, wa_two_shard, places, True), Gather(c, shards_two[0], places)],
        ((7.0, 4.0), (20.0, 4.1)),
    )
    wa_two, gate_two_w = ffn_one.carried
    attn_two = attention_layer(
        3,
        ffn_one.y,
        attn_one.v,
        wa_two,
        gains,
        2,
        tables,
        lambda c, start: [
            Deal(c, cotangent),
            Gather(c, shards_two[1], places, True),
            Gather(c, shards_two[2], places, True),
        ],
        ((8.0, 12.5, 16.0, 22.5, 22.6, 22.7), (16.0, 3.0), (26.0, 3.0)),
    )
    dealt_cotangent = attn_two.carried[0]
    ffn_two_w = (gate_two_w, *attn_two.carried[1:])
    back_ffn_two = feed_forward_back(
        4,
        dealt_cotangent,
        attn_two.x1,
        None,
        *ffn_two_w,
        gains,
        3,
        lambda c, down_sum: [down_sum],
        ((23.0, 4.2),),
    )
    (down_g2,) = back_ffn_two.carried
    grads_plan = ((10.0, 3.0), (25.0, 3.0))

    def ffn_grads(back):
        return [split(array) for array in (back.d_gate, back.d_up)]

    back_attn_two = attention_back(
        6,
        back_ffn_two.gx1,
        ffn_one.y,
        attn_two,
        None,
        wa_two,
        gains,
        2,
        tables,
        lambda c: [Scatter(c, array) for array in ffn_grads(back_ffn_two)]
        + [Deal(c, back_ffn_two.quarters, length)],
        grads_plan + ((4.9, 5.0, 11.0, 11.1, 11.2, 35.0, 35.1, 35.2),),
    )
    gate_g2, up_g2, out_two = back_attn_two.carried
    back_ffn_one = feed_forward_back(
        7,
        back_attn_two.gx,
        attn_one.x1,
        ffn_one,
        *ffn_one_w,
        gains,
        1,
        lambda c, down_sum: [
            Scatter(c, split(back_attn_two.d_wa)),
            down_sum,
            Deal(c, deal(ffn_one.y_low)),
        ],
        ((8.0, 5.8), (30.0, 4.2), (33.0, 33.1, 33.2, 37.0, 37.1, 37.2)),
    )
    packed_two, down_g1, out_one = back_ffn_one.carried
    back_attn_one = attention_back(
        8,
        back_ffn_one.gx1,
        x,
        attn_one,
        back_attn_two.passed,
        wa_one,
        gains,
        0,
        tables,
        lambda c: [Scatter(c, array) for array in ffn_grads(back_ffn_one)],
        ((11.0, 3.5), (24.0, 6.0)),
    )
    gate_g1, up_g1 = back_attn_one.carried
    gain_grads = jnp.concatenate(
        [back_attn_one.gain, back_ffn_one.gain, back_attn_two.gain, back_ffn_two.gain] * 2
    )
    gain_grads = jnp.transpose(gain_grads.reshape(-1, places, shard), (1, 0, 2))
    gain_shards, packed_one, grad = transfers(
        9,
        lambda c: [
            Scatter(c, gain_grads),
            Scatter(c, split(back_attn_one.d_wa)),
            Deal(c, deal(back_attn_one.gx)),
        ],
        ((4.0, 0.1), (7.0, 5.8), (6.0, 4.0)),
    )
    final = leave_step(
        (out_one, out_two),
        grad,
        (packed_one, packed_two),
        [gate_g1, up_g1, down_g1, gate_g2, up_g2, down_g2],
        gain_shards,
    )
    gate_g1, up_g1, down_g1, gate_g2, up_g2, down_g2 = final.turned
    return (
        deal(final.kept[0]),
        deal(final.kept[1]),
        deal(final.grad),
        final.gains[0],
        *final.packs[0],
        final.gains[1],
        gate_g1.T,
        up_g1.T,
        down_g1,
        final.gains[2],
        *final.packs[1],
        final.gains[3],
        gate_g2.T,
        up_g2.T,
        down_g2,
    )


def solution(mesh):
    placed = (
        P(DP, CTX, None),
        P(DP, None),
        P((DP, CTX)),
        P((DP, CTX), MP),
        P((DP, CTX), MP),
        P((DP, CTX), MP),
        P(MP, (DP, CTX)),
        P((DP, CTX)),
        P((DP, CTX), MP),
        P((DP, CTX), MP),
        P(MP, (DP, CTX)),
        P((DP, CTX)),
        P((DP, CTX), MP),
        P((DP, CTX), MP),
        P((DP, CTX), MP),
        P(MP, (DP, CTX)),
        P((DP, CTX)),
        P((DP, CTX), MP),
        P((DP, CTX), MP),
        P(MP, (DP, CTX)),
        P(DP, CTX, None),
    )
    sizes = dict(mesh.shape)

    def per_device(*operands):
        fits = sizes[DP] == 2 and sizes[MP] == 4 and operands[0].shape[0] == sizes[CTX] == BLOCKS
        return (dealt_device if fits else on_device)(*operands)

    return jax.shard_map(
        per_device,
        mesh=mesh,
        in_specs=placed,
        out_specs=(
            P(DP, CTX, None),
            P(DP, CTX, None),
            P(DP, CTX, None),
            P((DP, CTX)),
            P((DP, CTX), MP),
            P((DP, CTX), MP),
            P((DP, CTX), MP),
            P(MP, (DP, CTX)),
            P((DP, CTX)),
            P((DP, CTX), MP),
            P((DP, CTX), MP),
            P(MP, (DP, CTX)),
            P((DP, CTX)),
            P((DP, CTX), MP),
            P((DP, CTX), MP),
            P((DP, CTX), MP),
            P(MP, (DP, CTX)),
            P((DP, CTX)),
            P((DP, CTX), MP),
            P((DP, CTX), MP),
            P(MP, (DP, CTX)),
        ),
        check_vma=False,
    )
```
